32 devices in a mesh: row: 4 (over y, x), seq: 8 (over z, core).
Axes of the slice: x: 2, y: 2, z: 4, core: 2. Of those that a mesh axis runs over, the one named last changes fastest.
Arguments:
- tokens: bfloat16 [8192, 768], P(('row', 'seq')), may hold values from -6 to 6
- lengths: int32 [4, 4], P('row'), may hold values from 1 to 1280, 2048 in all within a row
- w_query: bfloat16 [768, 768], replicated, may hold values from -0.21875 to 0.21875
- w_key: bfloat16 [768, 768], replicated, may hold values from -0.21875 to 0.21875
- w_value: bfloat16 [768, 768], replicated, may hold values from -0.21875 to 0.21875
- w_out: bfloat16 [768, 768], replicated, may hold values from -0.21875 to 0.21875
- w_up: bfloat16 [768, 3072], replicated, may hold values from -0.21875 to 0.21875
- w_down: bfloat16 [3072, 768], replicated, may hold values from -0.109375 to 0.109375
- gain_attend: float32 [768], replicated, may hold values from 0.5 to 1.5
- gain_inner: float32 [768], replicated, may hold values from 0.5 to 1.5
- gain_feed: float32 [768], replicated, may hold values from 0.5 to 1.5
- gain_hidden: float32 [3072], replicated, may hold values from 0.5 to 1.5
- cotangent: bfloat16 [8192, 768], P(('row', 'seq')), may hold values from -6 to 6
Outputs:
- result: bfloat16 [8192, 768], P(('row', 'seq'))
- grad_input: bfloat16 [8192, 768], P(('row', 'seq'))
- grad_query: float32 [589824], P(('row', 'seq'))
- grad_key: float32 [589824], P(('row', 'seq'))
- grad_value: float32 [589824], P(('row', 'seq'))
- grad_out: float32 [589824], P(('row', 'seq'))
- grad_up: float32 [2359296], P(('row', 'seq'))
- grad_down: float32 [2359296], P(('row', 'seq'))
- grad_gains: float32 [5376], P(('row', 'seq'))
The draws below stay inside these ranges and needn't reach their ends.
Inputs may be any that keep to these rules, and one draw needn't show every extreme that they name: The 4 lengths of each row sum to 2048; the longest is exactly 1280.
All inputs are finite; a program needn't handle non-finite values.
Results may differ from the reference program's by a relative error of at most 0.015.
Values may be sent and summed in bfloat16 or wider, within the bound.
No kernel may reach another device: no remote copies, remote signals or barrier semaphores. Data moves between devices by JAX's collectives and lax.ppermute only.
A program may use at most 192 MiB of HBM per device.

```python
import math
from functools import partial
from functools import reduce
import jax
import jax.numpy as jnp
import numpy as np
from jax import lax

D = 768
HEADS = 12
FF = 3072
SEQ_DEV = 256
SEGMENT = 2048
PATTERNS = 5
DOCS = 4
ROWS = 4
SEQLEN = 2048
TOKENS = 8192


def raised(drawn, rng, source, target, parts, factor):
    def block_of(position):
        return (jnp.arange(drawn.shape[position]) // (drawn.shape[position] // parts)).reshape((-1,) + (1,) * (drawn.ndim - 1 - position))

    first = jax.random.permutation(rng, parts)[block_of(target)]
    second = (block_of(target) + parts // 2) % parts
    return jnp.where((block_of(source) == first) | (block_of(source) == second), factor * drawn, drawn)


def block_levels(rng, dims, shards, smallest, high):
    gain = 1.0
    for axis_at, parts in shards:
        heights = jax.random.uniform(jax.random.fold_in(jax.random.fold_in(rng, 6), axis_at), (parts,), jnp.float32, smallest / len(shards), high / len(shards))
        gain = gain * jnp.repeat(jnp.exp(heights), dims[axis_at] // parts).reshape((-1,) + (1,) * (len(dims) - 1 - axis_at))
    return gain


def profile(number_of, total, most, skew):
    portions = [(1 << 20) // math.isqrt(standing ** skew) + 1 for standing in range(2, number_of + 1)]
    surplus, holding = total - most - (number_of - 1), [1] * (number_of - 1)
    while surplus > 0:
        candidates = [i for i in range(number_of - 1) if holding[i] < most]
        whole, budget = sum([portions[i] for i in candidates]), surplus
        for i in candidates:
            extra = min(most - holding[i], max(1, budget * portions[i] // whole), surplus)
            holding[i] = holding[i] + extra
            surplus = surplus - extra
    return np.array([most] + holding)


def uneven_parts(key, count, total, bound, skew):
    if count == 2:
        one = jax.random.randint(key, (), max(1, total - bound), min(bound, total - 1) + 1)
        return jnp.stack([one, total - one])
    sizes = jnp.asarray(profile(count, total, bound, skew), jnp.int32)
    twos = (count - 1) // 2
    source_of, taker = sizes[1:1 + 2 * twos:2], sizes[2:2 + 2 * twos:2]
    slack = jnp.minimum(source_of - 1, bound - taker)
    moved = jax.random.randint(jax.random.fold_in(key, 1), (twos,), 0, 1 << 20) % (slack + 1)
    sizes = sizes.at[1:1 + 2 * twos:2].set(source_of - moved).at[2:2 + 2 * twos:2].set(taker + moved)
    return sizes[jax.random.permutation(jax.random.fold_in(key, 2), count)]


def gaussian(rng, shape, scale, bound, cuts=(), held_as=jnp.bfloat16):
    loudness = block_levels(rng, shape, cuts, -0.22, 0.18) if cuts else 1.0
    drawn = jax.random.normal(rng, shape, jnp.float32) * scale * loudness
    return jnp.minimum(jnp.maximum(drawn, -bound), bound).astype(held_as)


def gaussian_with(stream_key, extent, scale, reach, cuts, heavy, kind=jnp.bfloat16):
    values = scale * jax.random.normal(stream_key, extent, jnp.float32)
    if cuts:
        values = values * block_levels(stream_key, extent, cuts, -0.22, 0.18)
    return jnp.clip(raised(values, jax.random.fold_in(stream_key, 3), *heavy), -reach, reach).astype(kind)


def setup_inputs(seed: int = 0) -> dict:
    key_of = jax.random.split(jax.random.key(seed), 14)
    tokens = gaussian_with(key_of[0], (TOKENS, D), 1.0, 6.0, ((0, 32),), (0, 1, 32, 2.75))
    lengths = jax.vmap(lambda own: uneven_parts(own, DOCS, SEQLEN, SEQLEN - 3 * SEQ_DEV, 0))(jax.random.split(key_of[1], ROWS)).reshape((ROWS, DOCS)).astype(jnp.int32)
    w_query = gaussian(key_of[2], (D, D), D ** -0.5, 0.21875)
    w_key = gaussian(key_of[3], (D, D), D ** -0.5, 0.21875)
    w_value = gaussian(key_of[4], (D, D), D ** -0.5, 0.21875)
    w_out = gaussian(key_of[5], (D, D), D ** -0.5, 0.21875)
    w_up = gaussian(key_of[6], (D, FF), D ** -0.5, 0.21875)
    w_down = gaussian(key_of[7], (FF, D), FF ** -0.5, 0.109375)
    gain_attend = jnp.clip(1.0 + 0.1 * jax.random.normal(key_of[8], (D,), jnp.float32), 0.5, 1.5)
    gain_inner = jnp.clip(1.0 + 0.1 * jax.random.normal(key_of[9], (D,), jnp.float32), 0.5, 1.5)
    gain_feed = jnp.clip(1.0 + 0.1 * jax.random.normal(key_of[10], (D,), jnp.float32), 0.5, 1.5)
    gain_hidden = jnp.clip(1.0 + 0.1 * jax.random.normal(key_of[11], (FF,), jnp.float32), 0.5, 1.5)
    cotangent = gaussian_with(key_of[12], (TOKENS, D), 1.0, 6.0, ((0, 32),), (0, 1, 32, 2.75))
    return dict(tokens=tokens, lengths=lengths, w_query=w_query, w_key=w_key, w_value=w_value, w_out=w_out, w_up=w_up, w_down=w_down, gain_attend=gain_attend, gain_inner=gain_inner, gain_feed=gain_feed, gain_hidden=gain_hidden, cotangent=cotangent)


@jax.custom_vjp
def low(v):
    return lax.optimization_barrier(v.astype(jnp.bfloat16)).astype(jnp.float32)

@jax.custom_vjp
def low_back(v):
    return v

def low_keep(v):
    return (low(v), None)

def low_pass(kept, grad):
    return (grad,)

def back_keep(v):
    return (v, None)

def back_low(kept, grad):
    return (low(grad),)
low.defvjp(low_keep, low_pass)
low_back.defvjp(back_keep, back_low)
big_negative = -1e+30
highest = lax.Precision.HIGHEST

def layer_norm(values, gain_vector):
    centre = lax.optimization_barrier(jnp.mean(values, axis=-1, keepdims=True))
    shifted = values - centre
    variance = lax.optimization_barrier(jnp.mean(shifted * shifted, axis=-1, keepdims=True))
    return shifted * lax.rsqrt(variance + 1e-05) * gain_vector

def matmul(left_side, right_side):
    return jnp.dot(left_side, right_side, precision=highest)

def selector(stride):
    return jnp.arange(stride)[:, None] == (jnp.arange(HEADS) % stride)[None, :]

def segment_attend(score_scale, inputs):
    query_set, key_set, value_set, doc_ids = inputs
    scores = low_back(jnp.einsum('qhd,khd->hqk', query_set, key_set, precision=highest) * score_scale)
    doc_rows = doc_ids[..., 0].T
    rank_ids = jnp.arange(query_set.shape[0])
    allowed = (doc_rows[:, :, None] == doc_rows[:, None, :]) & (rank_ids[:, None] >= rank_ids[None, :])[None]
    scores = jnp.where(allowed, scores, big_negative)
    row_peak = lax.optimization_barrier(jnp.max(scores, axis=-1))
    weights = jnp.where(allowed, jnp.exp(scores - row_peak[..., None]), 0.0)
    row_total = lax.optimization_barrier(jnp.sum(weights, axis=-1))
    mixed = jnp.einsum('hqk,khd->qhd', low(weights), value_set, precision=highest)
    return (row_peak.T, row_total.T, mixed)

def attend_row(query_all, key_all, value_all, doc_bounds):
    seq_len = query_all.shape[0]
    query_all = query_all.reshape(seq_len, HEADS, -1)
    key_all = key_all.reshape(seq_len, HEADS, -1)
    value_all = value_all.reshape(seq_len, HEADS, -1)
    score_scale = query_all.shape[-1] ** (-0.5)
    doc_line = lax.optimization_barrier(jnp.sum((jnp.arange(seq_len)[:, None] >= doc_bounds[None, :]).astype(jnp.int32), axis=-1))
    doc_full = jnp.broadcast_to(doc_line[:, None, None], (seq_len, HEADS, 1))
    peaks = []
    totals = []
    mixes = []
    for pattern in range(PATTERNS):
        stride = 2 ** pattern
        span = min(SEGMENT * stride, seq_len)
        part_rows = span // stride
        pieces = seq_len // span
        chosen = selector(stride)

        def squeeze(values_in):
            shaped = values_in.reshape(pieces, part_rows, stride, HEADS, values_in.shape[-1])
            return lax.optimization_barrier(jnp.sum(jnp.where(chosen[None, None, :, :, None], shaped, jnp.zeros((), values_in.dtype)), axis=2))

        def spread(values_in, fill_value):
            widened = jnp.where(chosen[None, None, :, :, None], values_in[:, :, None], jnp.asarray(fill_value, values_in.dtype))
            return widened.reshape(seq_len, HEADS, values_in.shape[-1])
        row_peak, row_total, mixed = lax.map(jax.checkpoint(partial(segment_attend, score_scale)), (squeeze(query_all), squeeze(key_all), squeeze(value_all), squeeze(doc_full)))
        peaks.append(spread(row_peak[..., None], big_negative)[..., 0])
        totals.append(spread(row_total[..., None], 0.0)[..., 0])
        mixes.append(spread(mixed, 0.0))
    best_peak = reduce(jnp.maximum, peaks)
    weight_sum = sum((totals[pattern] * jnp.exp(peaks[pattern] - best_peak) for pattern in range(PATTERNS)))
    mixed_sum = sum((mixes[pattern] * jnp.exp(peaks[pattern] - best_peak)[..., None] for pattern in range(PATTERNS)))
    return (mixed_sum / weight_sum[..., None]).reshape(seq_len, -1)

def row_forward(params, inputs):
    x_row, doc_bounds = inputs
    w_query, w_key, w_value, w_out, w_up, w_down, gain_attend, gain_inner, gain_feed, gain_hidden = params
    normed = low(layer_norm(x_row, gain_attend))
    query_all = low(low_back(matmul(normed, w_query)))
    key_all = low(low_back(matmul(normed, w_key)))
    value_all = low(low_back(matmul(normed, w_value)))
    attended = low_back(attend_row(query_all, key_all, value_all, doc_bounds))
    inner_out = low(layer_norm(attended, gain_inner))
    middle = x_row + low_back(matmul(inner_out, w_out))
    normed_two = low(layer_norm(middle, gain_feed))
    hidden_pre = low_back(matmul(normed_two, w_up))
    hidden = low(layer_norm(jax.nn.gelu(hidden_pre, approximate=True), gain_hidden))
    return middle + matmul(hidden, w_down)

def reference(tokens, lengths, w_query, w_key, w_value, w_out, w_up, w_down, gain_attend, gain_inner, gain_feed, gain_hidden, cotangent):
    doc_bounds = jnp.cumsum(lengths, axis=1)[:, :-1]
    floats = tuple((weight_in.astype(jnp.float32) for weight_in in (w_query, w_key, w_value, w_out, w_up, w_down, gain_attend, gain_inner, gain_feed, gain_hidden)))

    def whole(x_all, params):
        rows_in = x_all.reshape(ROWS, SEQLEN, D)
        return lax.map(jax.checkpoint(partial(row_forward, params)), (rows_in, doc_bounds)).reshape(TOKENS, D)
    result, pullback = jax.vjp(whole, tokens.astype(jnp.float32), floats)
    grad_x, grad_params = pullback(cotangent.astype(jnp.float32))
    factor = TOKENS ** (-0.5)
    flats = [grad_one.reshape(-1) * factor for grad_one in grad_params[:6]]
    gains_all = jnp.concatenate([grad_one * factor for grad_one in grad_params[6:]])
    return (result.astype(jnp.bfloat16), grad_x.astype(jnp.bfloat16), flats[0], flats[1], flats[2], flats[3], flats[4], flats[5], gains_all)
```

```python
from functools import partial
from functools import reduce
import math

import jax
import jax.numpy as jnp
from jax import lax
from jax.experimental import pallas as pl
from jax.experimental.pallas import tpu as pltpu
from jax.sharding import PartitionSpec as P

HEADS = 12
SEGMENT = 2048
PATTERNS = 5


big_negative = -1e30


def shifted_2(shard, axis, by):
    length = lax.axis_size(axis)
    pairs = [(i, i + by) for i in range(length) if 0 <= i + by < length]
    return lax.ppermute(shard, axis, pairs)


def shifted_3(value, axis, steps):
    count = lax.axis_size(axis)
    pairs = [(source, (source + steps) % count) for source in range(count)]
    return lax.ppermute(value, axis, pairs)


def layer_norm(values, gain_vector):
    centre = jnp.mean(values, axis=-1, keepdims=True)
    shifted = values - centre
    variance = jnp.mean(shifted * shifted, axis=-1, keepdims=True)
    return shifted * lax.rsqrt(variance + 1e-05) * gain_vector


def hidden_norm(hidden_pre, gain_vector):
    return layer_norm(jax.nn.gelu(hidden_pre, approximate=True), gain_vector)


def selector(stride, head_count):
    return jnp.arange(stride)[:, None] == (jnp.arange(head_count) % stride)[None, :]


def compact(full_array, stride):
    length_in, head_count, inner_size = full_array.shape
    shaped = full_array.reshape(length_in // stride, stride, head_count, inner_size)
    picked = jnp.where(
        selector(stride, head_count)[None, :, :, None], shaped, jnp.zeros((), full_array.dtype)
    )
    return jnp.sum(picked, axis=1)


def expand(part_array, stride, fill_value):
    part_rows, head_count, inner_size = part_array.shape
    widened = jnp.where(
        selector(stride, head_count)[None, :, :, None],
        part_array[:, None],
        jnp.asarray(fill_value, part_array.dtype),
    )
    return widened.reshape(part_rows * stride, head_count, inner_size)


def positions(start_pos, part_rows, stride, head_count):
    row_ids = jnp.arange(part_rows, dtype=jnp.int32)[:, None] * stride
    head_ids = (jnp.arange(head_count, dtype=jnp.int32) % stride)[None, :]
    return start_pos + row_ids + head_ids


def doc_index(places, doc_bounds):
    return jnp.sum((places[..., None] >= doc_bounds).astype(jnp.int32), axis=-1)


def block_mask(doc_query, doc_key, local_block):
    allowed = doc_query.T[:, :, None] == doc_key.T[:, None, :]
    if local_block:
        rank_ids = jnp.arange(doc_query.shape[0])
        allowed = allowed & (rank_ids[:, None] >= rank_ids[None, :])[None]
    return allowed


def forward_block(query_part, key_part, value_part, allowed, score_scale):
    scores = (
        jnp.einsum("qhd,khd->hqk", query_part, key_part, preferred_element_type=jnp.float32)
        * score_scale
    )
    scores = jnp.where(allowed, scores, big_negative)
    row_peak = jnp.max(scores, axis=-1)
    weights = jnp.where(allowed, jnp.exp(scores - row_peak[..., None]), 0.0)
    row_total = jnp.sum(weights, axis=-1)
    mixed = jnp.einsum(
        "hqk,khd->qhd", weights.astype(jnp.bfloat16), value_part, preferred_element_type=jnp.float32
    )
    return (row_peak.T, row_total.T, mixed)


def merge(carried, new_block):
    best_peak = jnp.maximum(carried[0], new_block[0])
    keep_factor = jnp.exp(carried[0] - best_peak)
    take_factor = jnp.exp(new_block[0] - best_peak)
    new_total = carried[1] * keep_factor + new_block[1] * take_factor
    new_mixed = carried[2] * keep_factor[..., None] + new_block[2] * take_factor[..., None]
    return (best_peak, new_total, new_mixed)


def backward_block(
    query_part, grad_part, lse_part, delta_part, key_part, value_part, allowed, score_scale
):
    scores = (
        jnp.einsum("qhd,khd->hqk", query_part, key_part, preferred_element_type=jnp.float32)
        * score_scale
    )
    probs = jnp.where(allowed, jnp.exp(scores - lse_part.T[:, :, None]), 0.0)
    dots = jnp.einsum("qhd,khd->hqk", grad_part, value_part, preferred_element_type=jnp.float32)
    grad_scores = (probs * (dots - delta_part.T[:, :, None])).astype(jnp.bfloat16)
    query_grad = (
        jnp.einsum("hqk,khd->qhd", grad_scores, key_part, preferred_element_type=jnp.float32)
        * score_scale
    )
    key_grad = (
        jnp.einsum("hqk,qhd->khd", grad_scores, query_part, preferred_element_type=jnp.float32)
        * score_scale
    )
    value_grad = jnp.einsum(
        "hqk,qhd->khd", probs.astype(jnp.bfloat16), grad_part, preferred_element_type=jnp.float32
    )
    return (query_grad, key_grad, value_grad)


def keep_state(carried):
    return carried


def ring_local(
    tokens,
    lengths,
    w_query,
    w_key,
    w_value,
    w_out,
    w_up,
    w_down,
    gain_attend,
    gain_inner,
    gain_feed,
    gain_hidden,
    cotangent,
):
    block_rows, model_width = tokens.shape
    head_count = HEADS
    head_size = model_width // head_count
    score_scale = head_size ** (-0.5)
    seq_devices = lax.axis_size("seq")
    all_devices = seq_devices * lax.axis_size("row")
    my_index = lax.axis_index("seq")
    seq_total = block_rows * seq_devices
    doc_bounds = jnp.cumsum(lengths[0])[:-1]
    patterns = [
        (2**pattern, min(SEGMENT * 2**pattern, seq_total) // block_rows)
        for pattern in range(PATTERNS)
    ]
    near_ids = [0, 1]
    far_ids = list(range(2, PATTERNS))
    reach = patterns[1][1]
    far_rows = [block_rows // patterns[pattern][0] for pattern in far_ids]
    far_starts = [sum(far_rows[:slot_id]) for slot_id in range(len(far_ids))]
    far_total = sum(far_rows)

    def key_docs(pattern, source):
        stride = patterns[pattern][0]
        return doc_index(
            positions(source * block_rows, block_rows // stride, stride, head_count), doc_bounds
        )

    def is_live(pattern, cycle_step):
        group_size = patterns[pattern][1]
        return (cycle_step < group_size) & (my_index % group_size >= cycle_step)

    source_x = tokens.astype(jnp.float32)
    normed, attend_back = jax.vjp(layer_norm, source_x, gain_attend)
    normed_b = normed.astype(jnp.bfloat16)
    query_b = jnp.dot(normed_b, w_query, preferred_element_type=jnp.float32).astype(jnp.bfloat16)
    key_b = jnp.dot(normed_b, w_key, preferred_element_type=jnp.float32).astype(jnp.bfloat16)
    value_b = jnp.dot(normed_b, w_value, preferred_element_type=jnp.float32).astype(jnp.bfloat16)
    query_heads = query_b.reshape(block_rows, head_count, head_size)
    key_heads = key_b.reshape(block_rows, head_count, head_size)
    value_heads = value_b.reshape(block_rows, head_count, head_size)
    query_parts = [compact(query_heads, stride) for stride, group_size in patterns]
    key_parts = [compact(key_heads, stride) for stride, group_size in patterns]
    value_parts = [compact(value_heads, stride) for stride, group_size in patterns]
    own_docs = [key_docs(pattern, my_index) for pattern in range(PATTERNS)]
    states = [
        forward_block(
            query_parts[pattern],
            key_parts[pattern],
            value_parts[pattern],
            block_mask(own_docs[pattern], own_docs[pattern], True),
            score_scale,
        )
        for pattern in range(PATTERNS)
    ]

    def unpack_near(key_block):
        key_full = key_block[:, :model_width].reshape(block_rows, head_count, head_size)
        value_full = key_block[:, model_width:].reshape(block_rows, head_count, head_size)
        return (key_full, value_full)

    def near_fold_parts(pattern, key_part, value_part, source, carried):
        new_block = forward_block(
            query_parts[pattern],
            key_part,
            value_part,
            block_mask(own_docs[pattern], key_docs(pattern, source), False),
            score_scale,
        )
        return merge(carried, new_block)

    def near_fold(pattern, key_full, value_full, source, carried):
        stride = patterns[pattern][0]
        return near_fold_parts(
            pattern, compact(key_full, stride), compact(value_full, stride), source, carried
        )

    pair_block = jnp.concatenate([key_b, value_b], axis=1)
    kept_blocks = jnp.zeros((max(reach - 1, 1), block_rows, 2 * model_width), jnp.bfloat16)

    def near_forward(cycle_step, loop_state):
        key_block, near_now, kept_store = loop_state
        key_block = shifted_2(key_block, "seq", 1)
        key_full, value_full = unpack_near(key_block)
        new_states = []
        for pattern in near_ids:
            new_states.append(
                lax.cond(
                    is_live(pattern, cycle_step),
                    partial(near_fold, pattern, key_full, value_full, my_index - cycle_step),
                    keep_state,
                    near_now[pattern],
                )
            )
        return (key_block, tuple(new_states), kept_store)

    _, near_states, kept_blocks = lax.fori_loop(
        1, reach, near_forward, (pair_block, (states[0], states[1]), kept_blocks)
    )
    far_block = jnp.concatenate(
        [
            jnp.concatenate(
                [
                    key_parts[pattern].reshape(rows_here, model_width),
                    value_parts[pattern].reshape(rows_here, model_width),
                ],
                axis=1,
            )
            for pattern, rows_here in zip(far_ids, far_rows)
        ],
        axis=0,
    )

    def unpack_far(key_block, slot_id):
        rows_here = far_rows[slot_id]
        row_begin = far_starts[slot_id]
        piece_rows = key_block[row_begin : row_begin + rows_here]
        key_part = piece_rows[:, :model_width].reshape(rows_here, head_count, head_size)
        value_part = piece_rows[:, model_width:].reshape(rows_here, head_count, head_size)
        return (key_part, value_part)

    def far_fold(pattern, key_part, value_part, source, carried):
        new_block = forward_block(
            query_parts[pattern],
            key_part,
            value_part,
            block_mask(own_docs[pattern], key_docs(pattern, source), False),
            score_scale,
        )
        return merge(carried, new_block)

    def far_update(far_now, key_block, cycle_step):
        new_states = []
        for slot_id, pattern in enumerate(far_ids):
            key_part, value_part = unpack_far(key_block, slot_id)
            new_states.append(
                lax.cond(
                    is_live(pattern, cycle_step),
                    partial(far_fold, pattern, key_part, value_part, my_index - cycle_step),
                    keep_state,
                    far_now[slot_id],
                )
            )
        return tuple(new_states)

    far_states = tuple((states[pattern] for pattern in far_ids))

    def far_forward(cycle_step, loop_state):
        key_block, far_now = loop_state
        key_block = shifted_2(key_block, "seq", 1)
        return (key_block, far_update(far_now, key_block, cycle_step))

    _, far_states = lax.fori_loop(1, seq_devices, far_forward, (far_block, far_states))
    ordered = list(near_states) + list(far_states)
    peaks = [
        expand(ordered[pattern][0][..., None], patterns[pattern][0], big_negative)[..., 0]
        for pattern in range(PATTERNS)
    ]
    best_peak = reduce(jnp.maximum, peaks)
    weight_sum = jnp.zeros((block_rows, head_count), jnp.float32)
    mixed_sum = jnp.zeros((block_rows, head_count, head_size), jnp.float32)
    for pattern in range(PATTERNS):
        stride = patterns[pattern][0]
        factor = jnp.exp(peaks[pattern] - best_peak)
        weight_sum = (
            weight_sum + expand(ordered[pattern][1][..., None], stride, 0.0)[..., 0] * factor
        )
        mixed_sum = mixed_sum + expand(ordered[pattern][2], stride, 0.0) * factor[..., None]
    attended = mixed_sum / weight_sum[..., None]
    log_total = best_peak + jnp.log(weight_sum)
    inner_out, inner_back = jax.vjp(
        layer_norm, attended.reshape(block_rows, model_width), gain_inner
    )
    inner_b = inner_out.astype(jnp.bfloat16)
    middle = source_x + jnp.dot(inner_b, w_out, preferred_element_type=jnp.float32)
    normed_two, feed_back = jax.vjp(layer_norm, middle, gain_feed)
    normed_two_b = normed_two.astype(jnp.bfloat16)
    hidden_pre = jnp.dot(normed_two_b, w_up, preferred_element_type=jnp.float32)
    hidden, hidden_back = jax.vjp(hidden_norm, hidden_pre, gain_hidden)
    hidden_b = hidden.astype(jnp.bfloat16)
    result = (middle + jnp.dot(hidden_b, w_down, preferred_element_type=jnp.float32)).astype(
        jnp.bfloat16
    )
    grad_down = jnp.einsum("tf,tg->fg", hidden_b, cotangent, preferred_element_type=jnp.float32)
    grad_hidden = jnp.einsum("tg,fg->tf", cotangent, w_down, preferred_element_type=jnp.float32)
    grad_pre, grad_gain_hidden = hidden_back(grad_hidden)
    grad_pre_b = grad_pre.astype(jnp.bfloat16)
    grad_up = jnp.einsum("tf,tg->fg", normed_two_b, grad_pre_b, preferred_element_type=jnp.float32)
    grad_normed_two = jnp.einsum("tg,fg->tf", grad_pre_b, w_up, preferred_element_type=jnp.float32)
    grad_middle_part, grad_gain_feed = feed_back(grad_normed_two)
    grad_middle = cotangent.astype(jnp.float32) + grad_middle_part
    grad_middle_b = grad_middle.astype(jnp.bfloat16)
    grad_out = jnp.einsum("tf,tg->fg", inner_b, grad_middle_b, preferred_element_type=jnp.float32)
    grad_inner = jnp.einsum("tg,fg->tf", grad_middle_b, w_out, preferred_element_type=jnp.float32)
    grad_attended, grad_gain_inner = inner_back(grad_inner)
    grad_heads = grad_attended.astype(jnp.bfloat16).reshape(block_rows, head_count, head_size)
    delta_rows = jnp.sum(grad_heads.astype(jnp.float32) * attended, axis=-1)
    grad_parts = [compact(grad_heads, stride) for stride, group_size in patterns]
    lse_parts = [compact(log_total[..., None], stride)[..., 0] for stride, group_size in patterns]
    delta_parts = [
        compact(delta_rows[..., None], stride)[..., 0] for stride, group_size in patterns
    ]
    query_grads = []
    home_keys = []
    home_values = []
    for pattern in range(PATTERNS):
        part_query, part_key, part_value = backward_block(
            query_parts[pattern],
            grad_parts[pattern],
            lse_parts[pattern],
            delta_parts[pattern],
            key_parts[pattern],
            value_parts[pattern],
            block_mask(own_docs[pattern], own_docs[pattern], True),
            score_scale,
        )
        query_grads.append(part_query)
        home_keys.append(part_key)
        home_values.append(part_value)

    def fetch_full(key_block):
        return shifted_2(key_block, "seq", 1)

    def near_grad(pattern, key_full, value_full, source, operands):
        query_grad, travel = operands
        stride = patterns[pattern][0]
        part_query, part_key, part_value = backward_block(
            query_parts[pattern],
            grad_parts[pattern],
            lse_parts[pattern],
            delta_parts[pattern],
            compact(key_full, stride),
            compact(value_full, stride),
            block_mask(own_docs[pattern], key_docs(pattern, source), False),
            score_scale,
        )
        spread_rows = jnp.concatenate(
            [
                expand(part_key, stride, 0.0).reshape(block_rows, model_width),
                expand(part_value, stride, 0.0).reshape(block_rows, model_width),
            ],
            axis=1,
        )
        return (query_grad + part_query, travel + spread_rows)

    def near_backward(cycle_step, loop_state):
        key_block, grads_now, travel = loop_state
        key_block = fetch_full(key_block)
        travel = shifted_3(travel.astype(jnp.bfloat16), "seq", 1).astype(travel.dtype)
        key_full, value_full = unpack_near(key_block)
        new_grads = list(grads_now)
        for pattern in near_ids:
            new_grads[pattern], travel = lax.cond(
                is_live(pattern, cycle_step),
                partial(near_grad, pattern, key_full, value_full, my_index - cycle_step),
                keep_state,
                (new_grads[pattern], travel),
            )
        return (key_block, tuple(new_grads), travel)

    own_key_near = expand(home_keys[0], 1, 0.0) + expand(home_keys[1], 2, 0.0)
    own_value_near = expand(home_values[0], 1, 0.0) + expand(home_values[1], 2, 0.0)
    near_start = jnp.concatenate(
        [
            own_key_near.reshape(block_rows, model_width),
            own_value_near.reshape(block_rows, model_width),
        ],
        axis=1,
    )
    _, near_query, travel_near = lax.fori_loop(
        1, reach, near_backward, (pair_block, (query_grads[0], query_grads[1]), near_start)
    )
    near_home = shifted_3(travel_near.astype(jnp.bfloat16), "seq", 1 - reach).astype(
        travel_near.dtype
    )
    near_key_add = near_home[:, :model_width].reshape(block_rows, head_count, head_size)
    near_value_add = near_home[:, model_width:].reshape(block_rows, head_count, head_size)

    def far_grad(slot_id, key_part, value_part, source, operands):
        query_grad, travel = operands
        pattern = far_ids[slot_id]
        rows_here = far_rows[slot_id]
        row_begin = far_starts[slot_id]
        part_query, part_key, part_value = backward_block(
            query_parts[pattern],
            grad_parts[pattern],
            lse_parts[pattern],
            delta_parts[pattern],
            key_part,
            value_part,
            block_mask(own_docs[pattern], key_docs(pattern, source), False),
            score_scale,
        )
        spread_rows = jnp.concatenate(
            [part_key.reshape(rows_here, model_width), part_value.reshape(rows_here, model_width)],
            axis=1,
        )
        return (
            query_grad + part_query,
            travel.at[row_begin : row_begin + rows_here].add(spread_rows),
        )

    def far_back_update(grads_now, travel, key_block, cycle_step):
        new_grads = list(grads_now)
        for slot_id, pattern in enumerate(far_ids):
            key_part, value_part = unpack_far(key_block, slot_id)
            new_grads[slot_id], travel = lax.cond(
                is_live(pattern, cycle_step),
                partial(far_grad, slot_id, key_part, value_part, my_index - cycle_step),
                keep_state,
                (new_grads[slot_id], travel),
            )
        return (tuple(new_grads), travel)

    far_query = tuple((query_grads[pattern] for pattern in far_ids))
    far_empty = jnp.zeros((far_total, 2 * model_width), jnp.float32)

    def far_send(travel):
        return shifted_3(travel.astype(jnp.bfloat16), "seq", 1).astype(travel.dtype)

    def far_backward(cycle_step, loop_state):
        key_block, grads_now, travel = loop_state
        key_block = shifted_2(key_block, "seq", 1)
        travel = far_send(travel)
        grads_now, travel = far_back_update(grads_now, travel, key_block, cycle_step)
        return (key_block, grads_now, travel)

    _, far_query, travel_far = lax.fori_loop(
        1, seq_devices, far_backward, (far_block, far_query, far_empty)
    )
    far_home = far_send(travel_far)
    all_query = list(near_query) + list(far_query)
    query_grad = jnp.zeros((block_rows, head_count, head_size), jnp.float32)
    key_grad = near_key_add
    value_grad = near_value_add
    for pattern in range(PATTERNS):
        stride = patterns[pattern][0]
        query_grad = query_grad + expand(all_query[pattern], stride, 0.0)
    for pattern in far_ids:
        stride = patterns[pattern][0]
        key_grad = key_grad + expand(home_keys[pattern], stride, 0.0)
        value_grad = value_grad + expand(home_values[pattern], stride, 0.0)
    for slot_id, pattern in enumerate(far_ids):
        stride = patterns[pattern][0]
        rows_here = far_rows[slot_id]
        row_begin = far_starts[slot_id]
        piece_rows = far_home[row_begin : row_begin + rows_here]
        key_grad = key_grad + expand(
            piece_rows[:, :model_width].reshape(rows_here, head_count, head_size), stride, 0.0
        )
        value_grad = value_grad + expand(
            piece_rows[:, model_width:].reshape(rows_here, head_count, head_size), stride, 0.0
        )
    grad_query_b = query_grad.reshape(block_rows, model_width).astype(jnp.bfloat16)
    grad_key_b = key_grad.reshape(block_rows, model_width).astype(jnp.bfloat16)
    grad_value_b = value_grad.reshape(block_rows, model_width).astype(jnp.bfloat16)
    grad_w_query = jnp.einsum(
        "tf,tg->fg", normed_b, grad_query_b, preferred_element_type=jnp.float32
    )
    grad_w_key = jnp.einsum("tf,tg->fg", normed_b, grad_key_b, preferred_element_type=jnp.float32)
    grad_w_value = jnp.einsum(
        "tf,tg->fg", normed_b, grad_value_b, preferred_element_type=jnp.float32
    )
    grad_normed = jnp.einsum("tg,fg->tf", grad_query_b, w_query, preferred_element_type=jnp.float32)
    grad_normed = grad_normed + jnp.einsum(
        "tg,fg->tf", grad_key_b, w_key, preferred_element_type=jnp.float32
    )
    grad_normed = grad_normed + jnp.einsum(
        "tg,fg->tf", grad_value_b, w_value, preferred_element_type=jnp.float32
    )
    grad_x_part, grad_gain_attend = attend_back(grad_normed)
    grad_input = (grad_middle + grad_x_part).astype(jnp.bfloat16)
    gains_all = jnp.concatenate(
        [grad_gain_attend, grad_gain_inner, grad_gain_feed, grad_gain_hidden]
    )
    summed = (
        lax.psum_scatter(grad_w_query.reshape(-1), ("row", "seq"), scatter_dimension=0, tiled=True),
        lax.psum_scatter(grad_w_key.reshape(-1), ("row", "seq"), scatter_dimension=0, tiled=True),
        lax.psum_scatter(grad_w_value.reshape(-1), ("row", "seq"), scatter_dimension=0, tiled=True),
        lax.psum_scatter(grad_out.reshape(-1), ("row", "seq"), scatter_dimension=0, tiled=True),
        lax.psum_scatter(grad_up.reshape(-1), ("row", "seq"), scatter_dimension=0, tiled=True),
        lax.psum_scatter(grad_down.reshape(-1), ("row", "seq"), scatter_dimension=0, tiled=True),
        lax.psum_scatter(gains_all, ("row", "seq"), scatter_dimension=0, tiled=True),
    )
    factor = 1.0 / math.sqrt(block_rows * all_devices)
    return (result, grad_input) + tuple((summed_part * factor for summed_part in summed))


def trailing_classes(places, head_ids):
    offsets = places[None, :] - head_ids[:, None]
    return [(offsets % 2**level == 0) for level in range(1, PATTERNS)]


def split_log(level):
    remaining = math.log((level + 1) / level)
    pieces = []
    for _ in range(3):
        piece = float(jnp.bfloat16.dtype.type(remaining))
        pieces.append(piece)
        remaining -= piece
    return pieces


def query_extra(places, head_ids, width):
    rows = []
    for level, member in enumerate(trailing_classes(places, head_ids), start=1):
        for piece in split_log(level):
            rows.append(jnp.where(member, piece, 0.0))
    stacked = jnp.stack(rows, axis=1).astype(jnp.bfloat16)
    return jnp.pad(stacked, ((0, 0), (0, width - stacked.shape[1]), (0, 0)))


def key_extra(places, head_ids, width):
    rows = []
    for member in trailing_classes(places, head_ids):
        rows += [member] * 3
    stacked = jnp.stack(rows, axis=2).astype(jnp.bfloat16)
    return jnp.pad(stacked, ((0, 0), (0, 0), (0, width - stacked.shape[2])))


def pair_mask(query_start, key_start, doc_line, block):
    query_place = query_start + lax.broadcasted_iota(jnp.int32, (1, block), 1)
    key_place = key_start + lax.broadcasted_iota(jnp.int32, (block, 1), 0)
    return (key_place <= query_place) & (key_place >= doc_line)


def attend_kernel(
    heads, block, key_blocks, meta, doc_ref, q_ref, k_ref, vt_ref, o_ref, ob_ref, lse_ref, m_ref, l_ref
):
    step = pl.program_id(0)
    steps = pl.num_programs(0)
    query_start = meta[step]
    doc_first = meta[steps + key_blocks + step]
    doc_line = doc_ref[...]
    m_ref[...] = jnp.full_like(m_ref, big_negative)
    l_ref[...] = jnp.zeros_like(l_ref)
    o_ref[...] = jnp.zeros_like(o_ref)

    def body(slot, carry):
        key_start = meta[steps + slot]

        @pl.when((key_start <= query_start) & (key_start + block > doc_first))
        def _():
            span = pl.ds(pl.multiple_of(slot * block, block), block)
            allowed = pair_mask(query_start, key_start, doc_line, block)
            for head in range(heads):
                scores = jnp.dot(
                    k_ref[head, span, :], q_ref[head], preferred_element_type=jnp.float32
                )
                scores = jnp.where(allowed, scores, big_negative)
                old_peak = m_ref[head]
                new_peak = jnp.maximum(old_peak, jnp.max(scores, axis=0, keepdims=True))
                weights = jnp.exp(scores - new_peak)
                fade = jnp.exp(old_peak - new_peak)
                m_ref[head] = new_peak
                l_ref[head] = l_ref[head] * fade + jnp.sum(weights, axis=0, keepdims=True)
                o_ref[head] = o_ref[head] * fade + jnp.dot(
                    vt_ref[head, :, span],
                    weights.astype(jnp.bfloat16),
                    preferred_element_type=jnp.float32,
                )

        return carry

    lax.fori_loop(0, key_blocks, body, 0)
    for head in range(heads):
        total = l_ref[head]
        mixed = o_ref[head] / total
        o_ref[head] = mixed
        ob_ref[0, head] = mixed.astype(jnp.bfloat16)
        lse_ref[head] = m_ref[head] + jnp.log(total)


def attend_back_kernel(
    heads,
    block,
    key_blocks,
    scale,
    meta,
    doc_ref,
    q_ref,
    g_ref,
    o_ref,
    lse_ref,
    k_ref,
    kt_ref,
    v_ref,
    dq_ref,
    dk_ref,
    dv_ref,
    acc_ref,
):
    step = pl.program_id(0)
    steps = pl.num_programs(0)
    query_start = meta[step]
    doc_first = meta[steps + key_blocks + step]
    doc_line = doc_ref[...]
    size = g_ref.shape[1]

    @pl.when(step == 0)
    def _():
        dk_ref[...] = jnp.zeros_like(dk_ref)
        dv_ref[...] = jnp.zeros_like(dv_ref)

    acc_ref[...] = jnp.zeros_like(acc_ref)

    def body(slot, carry):
        key_start = meta[steps + slot]

        @pl.when((key_start <= query_start) & (key_start + block > doc_first))
        def _():
            span = pl.ds(pl.multiple_of(slot * block, block), block)
            allowed = pair_mask(query_start, key_start, doc_line, block)
            for head in range(heads):
                grad = g_ref[head]
                delta = jnp.sum(grad.astype(jnp.float32) * o_ref[head], axis=0, keepdims=True)
                scores = jnp.dot(
                    k_ref[head, span, :], q_ref[head], preferred_element_type=jnp.float32
                )
                probs = jnp.where(allowed, jnp.exp(scores - lse_ref[head]), 0.0)
                dots = jnp.dot(v_ref[head, span, :], grad, preferred_element_type=jnp.float32)
                grad_scores = (probs * (dots - delta)).astype(jnp.bfloat16)
                dv_ref[head, :, span] += lax.dot_general(
                    grad,
                    probs.astype(jnp.bfloat16),
                    (((1,), (1,)), ((), ())),
                    preferred_element_type=jnp.float32,
                )
                dk_ref[head, :, span] += lax.dot_general(
                    q_ref[head, :size],
                    grad_scores,
                    (((1,), (1,)), ((), ())),
                    preferred_element_type=jnp.float32,
                )
                acc_ref[head] += jnp.dot(
                    kt_ref[head, :, span], grad_scores, preferred_element_type=jnp.float32
                )

        return carry

    lax.fori_loop(0, key_blocks, body, 0)
    dq_ref[...] = (acc_ref[...] * scale).astype(dq_ref.dtype)


def whole(shape):
    return pl.BlockSpec(shape, lambda *index: (0,) * len(shape))


def attend(meta, doc_line, q_ext, k_ext, v_t, block):
    heads, width, queries = q_ext.shape
    keys, size = k_ext.shape[1], v_t.shape[1]
    steps, key_blocks = queries // block, keys // block
    return pl.pallas_call(
        partial(attend_kernel, heads, block, key_blocks),
        grid_spec=pltpu.PrefetchScalarGridSpec(
            num_scalar_prefetch=1,
            grid=(steps,),
            in_specs=[
                pl.BlockSpec((1, block), lambda i, meta: (0, i)),
                pl.BlockSpec((heads, width, block), lambda i, meta: (0, 0, i)),
                whole(k_ext.shape),
                whole(v_t.shape),
            ],
            out_specs=[
                pl.BlockSpec((heads, size, block), lambda i, meta: (0, 0, i)),
                pl.BlockSpec((1, heads, size, block), lambda i, meta: (i, 0, 0, 0)),
                pl.BlockSpec((heads, 1, block), lambda i, meta: (0, 0, i)),
            ],
            scratch_shapes=[
                pltpu.VMEM((heads, 1, block), jnp.float32),
                pltpu.VMEM((heads, 1, block), jnp.float32),
            ],
        ),
        out_shape=[
            jax.ShapeDtypeStruct((heads, size, queries), jnp.float32),
            jax.ShapeDtypeStruct((steps, heads, size, block), jnp.bfloat16),
            jax.ShapeDtypeStruct((heads, 1, queries), jnp.float32),
        ],
        compiler_params=pltpu.CompilerParams(vmem_limit_bytes=24 << 20),
        name="attend",
    )(meta, doc_line, q_ext, k_ext, v_t)


def attend_back(meta, doc_line, q_ext, grad_t, mixed, lse, k_ext, k_t, value, block, scale):
    heads, width, queries = q_ext.shape
    keys, size = k_ext.shape[1], k_t.shape[1]
    steps, key_blocks = queries // block, keys // block
    return pl.pallas_call(
        partial(attend_back_kernel, heads, block, key_blocks, scale),
        grid_spec=pltpu.PrefetchScalarGridSpec(
            num_scalar_prefetch=1,
            grid=(steps,),
            in_specs=[
                pl.BlockSpec((1, block), lambda i, meta: (0, i)),
                pl.BlockSpec((heads, width, block), lambda i, meta: (0, 0, i)),
                pl.BlockSpec((heads, size, block), lambda i, meta: (0, 0, i)),
                pl.BlockSpec((heads, size, block), lambda i, meta: (0, 0, i)),
                pl.BlockSpec((heads, 1, block), lambda i, meta: (0, 0, i)),
                whole(k_ext.shape),
                whole(k_t.shape),
                whole(value.shape),
            ],
            out_specs=[
                pl.BlockSpec((heads, size, block), lambda i, meta: (0, 0, i)),
                whole(k_t.shape),
                whole(k_t.shape),
            ],
            scratch_shapes=[pltpu.VMEM((heads, size, block), jnp.float32)],
        ),
        out_shape=[
            jax.ShapeDtypeStruct((heads, size, queries), jnp.bfloat16),
            jax.ShapeDtypeStruct((heads, size, keys), jnp.float32),
            jax.ShapeDtypeStruct((heads, size, keys), jnp.float32),
        ],
        compiler_params=pltpu.CompilerParams(vmem_limit_bytes=32 << 20),
        name="attend_back",
    )(meta, doc_line, q_ext, grad_t, mixed, lse, k_ext, k_t, value)


def chip_shift(value, steps):
    count = lax.axis_size("seq")
    return lax.ppermute(value, "seq", [(i, (i + 2 * steps) % count) for i in range(count)])


def core_swap(value):
    return lax.ppermute(value, "seq", [(i, i ^ 1) for i in range(lax.axis_size("seq"))])


def row_swap(value, bit):
    return lax.ppermute(value, "row", [(i, i ^ bit) for i in range(lax.axis_size("row"))])


def pick(array, index, axis):
    return lax.dynamic_index_in_dim(array, index, axis, keepdims=False)


def rolled(blocks, start):
    count = blocks.shape[0]
    return lax.dynamic_slice_in_dim(jnp.concatenate([blocks, blocks], axis=0), start, count, axis=0)


def sent(array):
    return array.astype(jnp.bfloat16)


def core_sum(grid, core):
    other = core_swap(sent(pick(grid, 1 - core, 2)))
    return pick(grid, core, 2).astype(jnp.float32) + other.astype(jnp.float32)


def row_sum(grid, row):
    def stage(part, bit_value):
        return pick(part, bit_value, 0), sent(pick(part, 1 - bit_value, 0))

    half = grid.shape[2] // 2
    low_bit, high_bit = row % 2, row // 2
    shaped = grid.reshape((2, 2) + grid.shape[1:])
    first, second = shaped[:, :, :, :half], shaped[:, :, :, half:]
    keep, send = pick(first, low_bit, 1), sent(pick(first, 1 - low_bit, 1))
    first = keep + row_swap(send, 1).astype(jnp.float32)
    keep, send = pick(second, high_bit, 0), sent(pick(second, 1 - high_bit, 0))
    second = keep + row_swap(send, 2).astype(jnp.float32)
    keep, send = pick(first, high_bit, 0), sent(pick(first, 1 - high_bit, 0))
    first = keep + row_swap(send, 2).astype(jnp.float32)
    keep, send = pick(second, low_bit, 0), sent(pick(second, 1 - low_bit, 0))
    second = keep + row_swap(send, 1).astype(jnp.float32)
    return jnp.concatenate([first, second], axis=1)


def chip_sum(grid, chip):
    count = grid.shape[0]
    total = pick(grid, chip, 0)
    for step in range(1, count):
        piece = sent(pick(grid, (chip + step) % count, 0))
        total = total + chip_shift(piece, step).astype(jnp.float32)
    return total


def fast_local(
    tokens,
    lengths,
    w_query,
    w_key,
    w_value,
    w_out,
    w_up,
    w_down,
    gain_attend,
    gain_inner,
    gain_feed,
    gain_hidden,
    cotangent,
):
    block, model_width = tokens.shape
    size = model_width // HEADS
    scale = size ** (-0.5)
    seq_devices, row_devices = lax.axis_size("seq"), lax.axis_size("row")
    chips = seq_devices // 2
    heads = HEADS // chips
    share = heads * size
    position, row = lax.axis_index("seq"), lax.axis_index("row")
    chip, core = position // 2, position % 2
    bounds = jnp.cumsum(lengths[0])[:-1]
    factor = 1.0 / math.sqrt(block * seq_devices * row_devices)

    source_x = tokens.astype(jnp.float32)
    normed, attend_norm_back = jax.vjp(layer_norm, source_x, gain_attend)
    normed_b = normed.astype(jnp.bfloat16)
    own_blocks = [normed_b] + [chip_shift(normed_b, step) for step in range(1, chips)]
    own_normed = jnp.concatenate(own_blocks, axis=0)
    all_normed = jnp.concatenate([own_normed, core_swap(own_normed)], axis=0)

    chip_ids = (chip - jnp.arange(chips, dtype=jnp.int32)) % chips
    query_starts = block * (2 * chip_ids + core)
    key_starts = jnp.concatenate([query_starts, block * (2 * chip_ids + 1 - core)])
    in_block = jnp.arange(block, dtype=jnp.int32)[None, :]
    query_places = (query_starts[:, None] + in_block).reshape(-1)
    key_places = (key_starts[:, None] + in_block).reshape(-1)
    doc_line = jnp.max(jnp.where(bounds[:, None] <= query_places[None, :], bounds[:, None], 0), axis=0)
    meta = jnp.concatenate([query_starts, key_starts, doc_line.reshape(chips, block)[:, 0]])
    doc_line = doc_line[None, :]
    head_ids = heads * chip + jnp.arange(heads, dtype=jnp.int32)

    def columns(weight):
        return lax.dynamic_slice_in_dim(weight, chip * share, share, axis=1)

    wq, wk, wv = columns(w_query), columns(w_key), columns(w_value)

    def feature_major(weight, rows):
        out = lax.dot_general(weight, rows, (((0,), (1,)), ((), ())), preferred_element_type=jnp.float32)
        return out.astype(jnp.bfloat16).reshape(heads, size, rows.shape[0])

    def token_major(weight, rows):
        out = jnp.dot(rows, weight, preferred_element_type=jnp.float32).astype(jnp.bfloat16)
        return out.reshape(rows.shape[0], heads, size).transpose(1, 0, 2)

    q_t = feature_major(wq, own_normed) * jnp.bfloat16(scale)
    k_t = feature_major(wk, all_normed)
    v_t = feature_major(wv, all_normed)
    k_r = token_major(wk, all_normed)
    v_r = token_major(wv, all_normed)
    q_ext = jnp.concatenate([q_t, query_extra(query_places, head_ids, size)], axis=1)
    k_ext = jnp.concatenate([k_r, key_extra(key_places, head_ids, size)], axis=2)

    mixed, mixed_b, lse = attend(meta, doc_line, q_ext, k_ext, v_t, block)
    mixed_b = mixed_b.reshape(chips, share, block)
    back = [mixed_b[0]] + [chip_shift(mixed_b[step], -step) for step in range(1, chips)]
    attended = rolled(jnp.stack(back), (chips - chip) % chips).reshape(model_width, block).T
    attended = attended.astype(jnp.float32)

    inner_out, inner_back = jax.vjp(layer_norm, attended, gain_inner)
    inner_b = inner_out.astype(jnp.bfloat16)
    middle = source_x + jnp.dot(inner_b, w_out, preferred_element_type=jnp.float32)
    normed_two, feed_back = jax.vjp(layer_norm, middle, gain_feed)
    normed_two_b = normed_two.astype(jnp.bfloat16)
    hidden_pre = jnp.dot(normed_two_b, w_up, preferred_element_type=jnp.float32)
    hidden, hidden_back = jax.vjp(hidden_norm, hidden_pre, gain_hidden)
    hidden_b = hidden.astype(jnp.bfloat16)
    result = (middle + jnp.dot(hidden_b, w_down, preferred_element_type=jnp.float32)).astype(
        jnp.bfloat16
    )
    grad_down = jnp.einsum("tf,tg->fg", hidden_b, cotangent, preferred_element_type=jnp.float32)
    grad_hidden = jnp.einsum("tg,fg->tf", cotangent, w_down, preferred_element_type=jnp.float32)
    grad_pre, grad_gain_hidden = hidden_back(grad_hidden)
    grad_pre_b = grad_pre.astype(jnp.bfloat16)
    grad_up = jnp.einsum("tf,tg->fg", normed_two_b, grad_pre_b, preferred_element_type=jnp.float32)
    grad_normed_two = jnp.einsum("tg,fg->tf", grad_pre_b, w_up, preferred_element_type=jnp.float32)
    grad_middle_part, grad_gain_feed = feed_back(grad_normed_two)
    grad_middle = cotangent.astype(jnp.float32) + grad_middle_part
    grad_middle_b = grad_middle.astype(jnp.bfloat16)
    grad_out = jnp.einsum("tf,tg->fg", inner_b, grad_middle_b, preferred_element_type=jnp.float32)
    grad_inner = jnp.einsum("tg,fg->tf", grad_middle_b, w_out, preferred_element_type=jnp.float32)
    grad_attended, grad_gain_inner = inner_back(grad_inner)

    def placed(grad):
        rows, width = grad.shape
        per = rows // (row_devices * seq_devices)
        grid = sent(grad).reshape(row_devices, chips, 2, per, width)
        return core_sum(grid, core)

    def finish(grid):
        return chip_sum(row_sum(grid, row), chip)

    down_part, up_part, out_part = placed(grad_down), placed(grad_up), placed(grad_out)

    grad_chunks = rolled(grad_attended.astype(jnp.bfloat16).T.reshape(chips, share, block), chip)
    grad_blocks = [grad_chunks[0]] + [chip_shift(grad_chunks[step], step) for step in range(1, chips)]
    grad_t = jnp.concatenate(grad_blocks, axis=1).reshape(heads, size, chips * block)
    dq, dk, dv = attend_back(
        meta, doc_line, q_ext, grad_t, mixed, lse, k_ext, k_t, v_r, block, scale
    )
    mine = chips * block
    pair = jnp.stack([dk, dv]).reshape(2 * share, 2 * mine)
    pair_mine = pair[:, :mine] + core_swap(sent(pair[:, mine:])).astype(jnp.float32)
    grads_t = jnp.concatenate([dq.reshape(share, mine), sent(pair_mine)], axis=0)

    own_grad = lax.dot_general(
        own_normed, grads_t, (((0,), (1,)), ((), ())), preferred_element_type=jnp.float32
    )
    per = model_width // (row_devices * seq_devices)
    home = [grads_t[:, :block]] + [
        chip_shift(grads_t[:, step * block : (step + 1) * block], -step) for step in range(1, chips)
    ]
    home = rolled(jnp.stack(home), (chips - chip) % chips).reshape(chips, 3, share, block)
    grad_normed = jnp.zeros((block, model_width), jnp.float32)
    for index, weight in enumerate((w_query, w_key, w_value)):
        grad_normed = grad_normed + lax.dot_general(
            home[:, index].reshape(model_width, block),
            weight,
            (((0,), (1,)), ((), ())),
            preferred_element_type=jnp.float32,
        )
    grad_x_part, grad_gain_attend = attend_norm_back(grad_normed)
    grad_input = (grad_middle + grad_x_part).astype(jnp.bfloat16)

    heads_grid = core_sum(sent(own_grad).reshape(row_devices, chips, 2, per, 3 * share), core)
    heads_grid = row_sum(heads_grid, row)
    home = [pick(heads_grid, chip, 0)] + [
        chip_shift(pick(heads_grid, (chip + step) % chips, 0), step) for step in range(1, chips)
    ]
    home = rolled(jnp.stack(home)[::-1], (chips - 1 - chip) % chips)
    home = home.reshape(chips, per, 3, share).transpose(2, 1, 0, 3).reshape(3, per * model_width)

    gains_all = jnp.concatenate(
        [grad_gain_attend, grad_gain_inner, grad_gain_feed, grad_gain_hidden]
    )
    gains_part = lax.psum_scatter(gains_all, ("row", "seq"), scatter_dimension=0, tiled=True)
    outs = (
        result,
        grad_input,
        home[0] * factor,
        home[1] * factor,
        home[2] * factor,
        finish(out_part).reshape(-1) * factor,
        finish(up_part).reshape(-1) * factor,
        finish(down_part).reshape(-1) * factor,
        gains_part * factor,
    )
    return outs


def local(*arrays):
    seq_devices, row_devices = lax.axis_size("seq"), lax.axis_size("row")
    block, seq_total = arrays[0].shape[0], arrays[0].shape[0] * lax.axis_size("seq")
    one_segment = seq_total <= SEGMENT and block % 2 ** (PATTERNS - 1) == 0
    even = seq_devices % 2 == 0 and HEADS % max(seq_devices // 2, 1) == 0
    if one_segment and even and row_devices == 4:
        return fast_local(*arrays)
    return ring_local(*arrays)


def solution(mesh):
    return jax.shard_map(
        local,
        mesh=mesh,
        in_specs=(
            P(("row", "seq"), None),
            P("row", None),
            P(),
            P(),
            P(),
            P(),
            P(),
            P(),
            P(),
            P(),
            P(),
            P(),
            P(("row", "seq"), None),
        ),
        out_specs=(
            P(("row", "seq"), None),
            P(("row", "seq"), None),
            P(("row", "seq")),
            P(("row", "seq")),
            P(("row", "seq")),
            P(("row", "seq")),
            P(("row", "seq")),
            P(("row", "seq")),
            P(("row", "seq")),
        ),
        check_vma=False,
    )
```

```python
from functools import partial
from functools import reduce
import math

import jax
import jax.numpy as jnp
import numpy as np
from jax import lax
from jax.experimental import pallas as pl
from jax.experimental.pallas import tpu as pltpu
from jax.sharding import PartitionSpec as P

HEADS = 12
SEGMENT = 2048
PATTERNS = 5


big_negative = -1e30


def shifted_2(shard, axis, by):
    length = lax.axis_size(axis)
    pairs = [(i, i + by) for i in range(length) if 0 <= i + by < length]
    return lax.ppermute(shard, axis, pairs)


def shifted_3(value, axis, steps):
    count = lax.axis_size(axis)
    pairs = [(source, (source + steps) % count) for source in range(count)]
    return lax.ppermute(value, axis, pairs)


def layer_norm(values, gain_vector):
    centre = jnp.mean(values, axis=-1, keepdims=True)
    shifted = values - centre
    variance = jnp.mean(shifted * shifted, axis=-1, keepdims=True)
    return shifted * lax.rsqrt(variance + 1e-05) * gain_vector


def hidden_norm(hidden_pre, gain_vector):
    return layer_norm(jax.nn.gelu(hidden_pre, approximate=True), gain_vector)


def selector(stride, head_count):
    return jnp.arange(stride)[:, None] == (jnp.arange(head_count) % stride)[None, :]


def compact(full_array, stride):
    length_in, head_count, inner_size = full_array.shape
    shaped = full_array.reshape(length_in // stride, stride, head_count, inner_size)
    picked = jnp.where(
        selector(stride, head_count)[None, :, :, None], shaped, jnp.zeros((), full_array.dtype)
    )
    return jnp.sum(picked, axis=1)


def expand(part_array, stride, fill_value):
    part_rows, head_count, inner_size = part_array.shape
    widened = jnp.where(
        selector(stride, head_count)[None, :, :, None],
        part_array[:, None],
        jnp.asarray(fill_value, part_array.dtype),
    )
    return widened.reshape(part_rows * stride, head_count, inner_size)


def positions(start_pos, part_rows, stride, head_count):
    row_ids = jnp.arange(part_rows, dtype=jnp.int32)[:, None] * stride
    head_ids = (jnp.arange(head_count, dtype=jnp.int32) % stride)[None, :]
    return start_pos + row_ids + head_ids


def doc_index(places, doc_bounds):
    return jnp.sum((places[..., None] >= doc_bounds).astype(jnp.int32), axis=-1)


def block_mask(doc_query, doc_key, local_block):
    allowed = doc_query.T[:, :, None] == doc_key.T[:, None, :]
    if local_block:
        rank_ids = jnp.arange(doc_query.shape[0])
        allowed = allowed & (rank_ids[:, None] >= rank_ids[None, :])[None]
    return allowed


def forward_block(query_part, key_part, value_part, allowed, score_scale):
    scores = (
        jnp.einsum("qhd,khd->hqk", query_part, key_part, preferred_element_type=jnp.float32)
        * score_scale
    )
    scores = jnp.where(allowed, scores, big_negative)
    row_peak = jnp.max(scores, axis=-1)
    weights = jnp.where(allowed, jnp.exp(scores - row_peak[..., None]), 0.0)
    row_total = jnp.sum(weights, axis=-1)
    mixed = jnp.einsum(
        "hqk,khd->qhd", weights.astype(jnp.bfloat16), value_part, preferred_element_type=jnp.float32
    )
    return (row_peak.T, row_total.T, mixed)


def merge(carried, new_block):
    best_peak = jnp.maximum(carried[0], new_block[0])
    keep_factor = jnp.exp(carried[0] - best_peak)
    take_factor = jnp.exp(new_block[0] - best_peak)
    new_total = carried[1] * keep_factor + new_block[1] * take_factor
    new_mixed = carried[2] * keep_factor[..., None] + new_block[2] * take_factor[..., None]
    return (best_peak, new_total, new_mixed)


def backward_block(
    query_part, grad_part, lse_part, delta_part, key_part, value_part, allowed, score_scale
):
    scores = (
        jnp.einsum("qhd,khd->hqk", query_part, key_part, preferred_element_type=jnp.float32)
        * score_scale
    )
    probs = jnp.where(allowed, jnp.exp(scores - lse_part.T[:, :, None]), 0.0)
    dots = jnp.einsum("qhd,khd->hqk", grad_part, value_part, preferred_element_type=jnp.float32)
    grad_scores = (probs * (dots - delta_part.T[:, :, None])).astype(jnp.bfloat16)
    query_grad = (
        jnp.einsum("hqk,khd->qhd", grad_scores, key_part, preferred_element_type=jnp.float32)
        * score_scale
    )
    key_grad = (
        jnp.einsum("hqk,qhd->khd", grad_scores, query_part, preferred_element_type=jnp.float32)
        * score_scale
    )
    value_grad = jnp.einsum(
        "hqk,qhd->khd", probs.astype(jnp.bfloat16), grad_part, preferred_element_type=jnp.float32
    )
    return (query_grad, key_grad, value_grad)


def keep_state(carried):
    return carried


def ring_local(
    tokens,
    lengths,
    w_query,
    w_key,
    w_value,
    w_out,
    w_up,
    w_down,
    gain_attend,
    gain_inner,
    gain_feed,
    gain_hidden,
    cotangent,
):
    block_rows, model_width = tokens.shape
    head_count = HEADS
    head_size = model_width // head_count
    score_scale = head_size ** (-0.5)
    seq_devices = lax.axis_size("seq")
    all_devices = seq_devices * lax.axis_size("row")
    my_index = lax.axis_index("seq")
    seq_total = block_rows * seq_devices
    doc_bounds = jnp.cumsum(lengths[0])[:-1]
    patterns = [
        (2**pattern, min(SEGMENT * 2**pattern, seq_total) // block_rows)
        for pattern in range(PATTERNS)
    ]
    near_ids = [0, 1]
    far_ids = list(range(2, PATTERNS))
    reach = patterns[1][1]
    far_rows = [block_rows // patterns[pattern][0] for pattern in far_ids]
    far_starts = [sum(far_rows[:slot_id]) for slot_id in range(len(far_ids))]
    far_total = sum(far_rows)

    def key_docs(pattern, source):
        stride = patterns[pattern][0]
        return doc_index(
            positions(source * block_rows, block_rows // stride, stride, head_count), doc_bounds
        )

    def is_live(pattern, cycle_step):
        group_size = patterns[pattern][1]
        return (cycle_step < group_size) & (my_index % group_size >= cycle_step)

    source_x = tokens.astype(jnp.float32)
    normed, attend_back = jax.vjp(layer_norm, source_x, gain_attend)
    normed_b = normed.astype(jnp.bfloat16)
    query_b = jnp.dot(normed_b, w_query, preferred_element_type=jnp.float32).astype(jnp.bfloat16)
    key_b = jnp.dot(normed_b, w_key, preferred_element_type=jnp.float32).astype(jnp.bfloat16)
    value_b = jnp.dot(normed_b, w_value, preferred_element_type=jnp.float32).astype(jnp.bfloat16)
    query_heads = query_b.reshape(block_rows, head_count, head_size)
    key_heads = key_b.reshape(block_rows, head_count, head_size)
    value_heads = value_b.reshape(block_rows, head_count, head_size)
    query_parts = [compact(query_heads, stride) for stride, group_size in patterns]
    key_parts = [compact(key_heads, stride) for stride, group_size in patterns]
    value_parts = [compact(value_heads, stride) for stride, group_size in patterns]
    own_docs = [key_docs(pattern, my_index) for pattern in range(PATTERNS)]
    states = [
        forward_block(
            query_parts[pattern],
            key_parts[pattern],
            value_parts[pattern],
            block_mask(own_docs[pattern], own_docs[pattern], True),
            score_scale,
        )
        for pattern in range(PATTERNS)
    ]

    def unpack_near(key_block):
        key_full = key_block[:, :model_width].reshape(block_rows, head_count, head_size)
        value_full = key_block[:, model_width:].reshape(block_rows, head_count, head_size)
        return (key_full, value_full)

    def near_fold_parts(pattern, key_part, value_part, source, carried):
        new_block = forward_block(
            query_parts[pattern],
            key_part,
            value_part,
            block_mask(own_docs[pattern], key_docs(pattern, source), False),
            score_scale,
        )
        return merge(carried, new_block)

    def near_fold(pattern, key_full, value_full, source, carried):
        stride = patterns[pattern][0]
        return near_fold_parts(
            pattern, compact(key_full, stride), compact(value_full, stride), source, carried
        )

    pair_block = jnp.concatenate([key_b, value_b], axis=1)
    kept_blocks = jnp.zeros((max(reach - 1, 1), block_rows, 2 * model_width), jnp.bfloat16)

    def near_forward(cycle_step, loop_state):
        key_block, near_now, kept_store = loop_state
        key_block = shifted_2(key_block, "seq", 1)
        key_full, value_full = unpack_near(key_block)
        new_states = []
        for pattern in near_ids:
            new_states.append(
                lax.cond(
                    is_live(pattern, cycle_step),
                    partial(near_fold, pattern, key_full, value_full, my_index - cycle_step),
                    keep_state,
                    near_now[pattern],
                )
            )
        return (key_block, tuple(new_states), kept_store)

    _, near_states, kept_blocks = lax.fori_loop(
        1, reach, near_forward, (pair_block, (states[0], states[1]), kept_blocks)
    )
    far_block = jnp.concatenate(
        [
            jnp.concatenate(
                [
                    key_parts[pattern].reshape(rows_here, model_width),
                    value_parts[pattern].reshape(rows_here, model_width),
                ],
                axis=1,
            )
            for pattern, rows_here in zip(far_ids, far_rows)
        ],
        axis=0,
    )

    def unpack_far(key_block, slot_id):
        rows_here = far_rows[slot_id]
        row_begin = far_starts[slot_id]
        piece_rows = key_block[row_begin : row_begin + rows_here]
        key_part = piece_rows[:, :model_width].reshape(rows_here, head_count, head_size)
        value_part = piece_rows[:, model_width:].reshape(rows_here, head_count, head_size)
        return (key_part, value_part)

    def far_fold(pattern, key_part, value_part, source, carried):
        new_block = forward_block(
            query_parts[pattern],
            key_part,
            value_part,
            block_mask(own_docs[pattern], key_docs(pattern, source), False),
            score_scale,
        )
        return merge(carried, new_block)

    def far_update(far_now, key_block, cycle_step):
        new_states = []
        for slot_id, pattern in enumerate(far_ids):
            key_part, value_part = unpack_far(key_block, slot_id)
            new_states.append(
                lax.cond(
                    is_live(pattern, cycle_step),
                    partial(far_fold, pattern, key_part, value_part, my_index - cycle_step),
                    keep_state,
                    far_now[slot_id],
                )
            )
        return tuple(new_states)

    far_states = tuple((states[pattern] for pattern in far_ids))

    def far_forward(cycle_step, loop_state):
        key_block, far_now = loop_state
        key_block = shifted_2(key_block, "seq", 1)
        return (key_block, far_update(far_now, key_block, cycle_step))

    _, far_states = lax.fori_loop(1, seq_devices, far_forward, (far_block, far_states))
    ordered = list(near_states) + list(far_states)
    peaks = [
        expand(ordered[pattern][0][..., None], patterns[pattern][0], big_negative)[..., 0]
        for pattern in range(PATTERNS)
    ]
    best_peak = reduce(jnp.maximum, peaks)
    weight_sum = jnp.zeros((block_rows, head_count), jnp.float32)
    mixed_sum = jnp.zeros((block_rows, head_count, head_size), jnp.float32)
    for pattern in range(PATTERNS):
        stride = patterns[pattern][0]
        factor = jnp.exp(peaks[pattern] - best_peak)
        weight_sum = (
            weight_sum + expand(ordered[pattern][1][..., None], stride, 0.0)[..., 0] * factor
        )
        mixed_sum = mixed_sum + expand(ordered[pattern][2], stride, 0.0) * factor[..., None]
    attended = mixed_sum / weight_sum[..., None]
    log_total = best_peak + jnp.log(weight_sum)
    inner_out, inner_back = jax.vjp(
        layer_norm, attended.reshape(block_rows, model_width), gain_inner
    )
    inner_b = inner_out.astype(jnp.bfloat16)
    middle = source_x + jnp.dot(inner_b, w_out, preferred_element_type=jnp.float32)
    normed_two, feed_back = jax.vjp(layer_norm, middle, gain_feed)
    normed_two_b = normed_two.astype(jnp.bfloat16)
    hidden_pre = jnp.dot(normed_two_b, w_up, preferred_element_type=jnp.float32)
    hidden, hidden_back = jax.vjp(hidden_norm, hidden_pre, gain_hidden)
    hidden_b = hidden.astype(jnp.bfloat16)
    result = (middle + jnp.dot(hidden_b, w_down, preferred_element_type=jnp.float32)).astype(
        jnp.bfloat16
    )
    grad_down = jnp.einsum("tf,tg->fg", hidden_b, cotangent, preferred_element_type=jnp.float32)
    grad_hidden = jnp.einsum("tg,fg->tf", cotangent, w_down, preferred_element_type=jnp.float32)
    grad_pre, grad_gain_hidden = hidden_back(grad_hidden)
    grad_pre_b = grad_pre.astype(jnp.bfloat16)
    grad_up = jnp.einsum("tf,tg->fg", normed_two_b, grad_pre_b, preferred_element_type=jnp.float32)
    grad_normed_two = jnp.einsum("tg,fg->tf", grad_pre_b, w_up, preferred_element_type=jnp.float32)
    grad_middle_part, grad_gain_feed = feed_back(grad_normed_two)
    grad_middle = cotangent.astype(jnp.float32) + grad_middle_part
    grad_middle_b = grad_middle.astype(jnp.bfloat16)
    grad_out = jnp.einsum("tf,tg->fg", inner_b, grad_middle_b, preferred_element_type=jnp.float32)
    grad_inner = jnp.einsum("tg,fg->tf", grad_middle_b, w_out, preferred_element_type=jnp.float32)
    grad_attended, grad_gain_inner = inner_back(grad_inner)
    grad_heads = grad_attended.astype(jnp.bfloat16).reshape(block_rows, head_count, head_size)
    delta_rows = jnp.sum(grad_heads.astype(jnp.float32) * attended, axis=-1)
    grad_parts = [compact(grad_heads, stride) for stride, group_size in patterns]
    lse_parts = [compact(log_total[..., None], stride)[..., 0] for stride, group_size in patterns]
    delta_parts = [
        compact(delta_rows[..., None], stride)[..., 0] for stride, group_size in patterns
    ]
    query_grads = []
    home_keys = []
    home_values = []
    for pattern in range(PATTERNS):
        part_query, part_key, part_value = backward_block(
            query_parts[pattern],
            grad_parts[pattern],
            lse_parts[pattern],
            delta_parts[pattern],
            key_parts[pattern],
            value_parts[pattern],
            block_mask(own_docs[pattern], own_docs[pattern], True),
            score_scale,
        )
        query_grads.append(part_query)
        home_keys.append(part_key)
        home_values.append(part_value)

    def fetch_full(key_block):
        return shifted_2(key_block, "seq", 1)

    def near_grad(pattern, key_full, value_full, source, operands):
        query_grad, travel = operands
        stride = patterns[pattern][0]
        part_query, part_key, part_value = backward_block(
            query_parts[pattern],
            grad_parts[pattern],
            lse_parts[pattern],
            delta_parts[pattern],
            compact(key_full, stride),
            compact(value_full, stride),
            block_mask(own_docs[pattern], key_docs(pattern, source), False),
            score_scale,
        )
        spread_rows = jnp.concatenate(
            [
                expand(part_key, stride, 0.0).reshape(block_rows, model_width),
                expand(part_value, stride, 0.0).reshape(block_rows, model_width),
            ],
            axis=1,
        )
        return (query_grad + part_query, travel + spread_rows)

    def near_backward(cycle_step, loop_state):
        key_block, grads_now, travel = loop_state
        key_block = fetch_full(key_block)
        travel = shifted_3(travel.astype(jnp.bfloat16), "seq", 1).astype(travel.dtype)
        key_full, value_full = unpack_near(key_block)
        new_grads = list(grads_now)
        for pattern in near_ids:
            new_grads[pattern], travel = lax.cond(
                is_live(pattern, cycle_step),
                partial(near_grad, pattern, key_full, value_full, my_index - cycle_step),
                keep_state,
                (new_grads[pattern], travel),
            )
        return (key_block, tuple(new_grads), travel)

    own_key_near = expand(home_keys[0], 1, 0.0) + expand(home_keys[1], 2, 0.0)
    own_value_near = expand(home_values[0], 1, 0.0) + expand(home_values[1], 2, 0.0)
    near_start = jnp.concatenate(
        [
            own_key_near.reshape(block_rows, model_width),
            own_value_near.reshape(block_rows, model_width),
        ],
        axis=1,
    )
    _, near_query, travel_near = lax.fori_loop(
        1, reach, near_backward, (pair_block, (query_grads[0], query_grads[1]), near_start)
    )
    near_home = shifted_3(travel_near.astype(jnp.bfloat16), "seq", 1 - reach).astype(
        travel_near.dtype
    )
    near_key_add = near_home[:, :model_width].reshape(block_rows, head_count, head_size)
    near_value_add = near_home[:, model_width:].reshape(block_rows, head_count, head_size)

    def far_grad(slot_id, key_part, value_part, source, operands):
        query_grad, travel = operands
        pattern = far_ids[slot_id]
        rows_here = far_rows[slot_id]
        row_begin = far_starts[slot_id]
        part_query, part_key, part_value = backward_block(
            query_parts[pattern],
            grad_parts[pattern],
            lse_parts[pattern],
            delta_parts[pattern],
            key_part,
            value_part,
            block_mask(own_docs[pattern], key_docs(pattern, source), False),
            score_scale,
        )
        spread_rows = jnp.concatenate(
            [part_key.reshape(rows_here, model_width), part_value.reshape(rows_here, model_width)],
            axis=1,
        )
        return (
            query_grad + part_query,
            travel.at[row_begin : row_begin + rows_here].add(spread_rows),
        )

    def far_back_update(grads_now, travel, key_block, cycle_step):
        new_grads = list(grads_now)
        for slot_id, pattern in enumerate(far_ids):
            key_part, value_part = unpack_far(key_block, slot_id)
            new_grads[slot_id], travel = lax.cond(
                is_live(pattern, cycle_step),
                partial(far_grad, slot_id, key_part, value_part, my_index - cycle_step),
                keep_state,
                (new_grads[slot_id], travel),
            )
        return (tuple(new_grads), travel)

    far_query = tuple((query_grads[pattern] for pattern in far_ids))
    far_empty = jnp.zeros((far_total, 2 * model_width), jnp.float32)

    def far_send(travel):
        return shifted_3(travel.astype(jnp.bfloat16), "seq", 1).astype(travel.dtype)

    def far_backward(cycle_step, loop_state):
        key_block, grads_now, travel = loop_state
        key_block = shifted_2(key_block, "seq", 1)
        travel = far_send(travel)
        grads_now, travel = far_back_update(grads_now, travel, key_block, cycle_step)
        return (key_block, grads_now, travel)

    _, far_query, travel_far = lax.fori_loop(
        1, seq_devices, far_backward, (far_block, far_query, far_empty)
    )
    far_home = far_send(travel_far)
    all_query = list(near_query) + list(far_query)
    query_grad = jnp.zeros((block_rows, head_count, head_size), jnp.float32)
    key_grad = near_key_add
    value_grad = near_value_add
    for pattern in range(PATTERNS):
        stride = patterns[pattern][0]
        query_grad = query_grad + expand(all_query[pattern], stride, 0.0)
    for pattern in far_ids:
        stride = patterns[pattern][0]
        key_grad = key_grad + expand(home_keys[pattern], stride, 0.0)
        value_grad = value_grad + expand(home_values[pattern], stride, 0.0)
    for slot_id, pattern in enumerate(far_ids):
        stride = patterns[pattern][0]
        rows_here = far_rows[slot_id]
        row_begin = far_starts[slot_id]
        piece_rows = far_home[row_begin : row_begin + rows_here]
        key_grad = key_grad + expand(
            piece_rows[:, :model_width].reshape(rows_here, head_count, head_size), stride, 0.0
        )
        value_grad = value_grad + expand(
            piece_rows[:, model_width:].reshape(rows_here, head_count, head_size), stride, 0.0
        )
    grad_query_b = query_grad.reshape(block_rows, model_width).astype(jnp.bfloat16)
    grad_key_b = key_grad.reshape(block_rows, model_width).astype(jnp.bfloat16)
    grad_value_b = value_grad.reshape(block_rows, model_width).astype(jnp.bfloat16)
    grad_w_query = jnp.einsum(
        "tf,tg->fg", normed_b, grad_query_b, preferred_element_type=jnp.float32
    )
    grad_w_key = jnp.einsum("tf,tg->fg", normed_b, grad_key_b, preferred_element_type=jnp.float32)
    grad_w_value = jnp.einsum(
        "tf,tg->fg", normed_b, grad_value_b, preferred_element_type=jnp.float32
    )
    grad_normed = jnp.einsum("tg,fg->tf", grad_query_b, w_query, preferred_element_type=jnp.float32)
    grad_normed = grad_normed + jnp.einsum(
        "tg,fg->tf", grad_key_b, w_key, preferred_element_type=jnp.float32
    )
    grad_normed = grad_normed + jnp.einsum(
        "tg,fg->tf", grad_value_b, w_value, preferred_element_type=jnp.float32
    )
    grad_x_part, grad_gain_attend = attend_back(grad_normed)
    grad_input = (grad_middle + grad_x_part).astype(jnp.bfloat16)
    gains_all = jnp.concatenate(
        [grad_gain_attend, grad_gain_inner, grad_gain_feed, grad_gain_hidden]
    )
    summed = (
        lax.psum_scatter(grad_w_query.reshape(-1), ("row", "seq"), scatter_dimension=0, tiled=True),
        lax.psum_scatter(grad_w_key.reshape(-1), ("row", "seq"), scatter_dimension=0, tiled=True),
        lax.psum_scatter(grad_w_value.reshape(-1), ("row", "seq"), scatter_dimension=0, tiled=True),
        lax.psum_scatter(grad_out.reshape(-1), ("row", "seq"), scatter_dimension=0, tiled=True),
        lax.psum_scatter(grad_up.reshape(-1), ("row", "seq"), scatter_dimension=0, tiled=True),
        lax.psum_scatter(grad_down.reshape(-1), ("row", "seq"), scatter_dimension=0, tiled=True),
        lax.psum_scatter(gains_all, ("row", "seq"), scatter_dimension=0, tiled=True),
    )
    factor = 1.0 / math.sqrt(block_rows * all_devices)
    return (result, grad_input) + tuple((summed_part * factor for summed_part in summed))


def split_log(level):
    remaining = math.log((level + 1) / level)
    pieces = []
    for _ in range(3):
        piece = float(jnp.bfloat16.dtype.type(remaining))
        pieces.append(piece)
        remaining -= piece
    return pieces


def extra_features(heads, size, lanes):
    masks, owners, query_values, key_values = [], [], [], []
    for head in range(heads):
        for lane in range(lanes):
            level, piece = divmod(lane - size, 3)
            used = size <= lane < size + 3 * (PATTERNS - 1)
            masks.append(2 ** (level + 1) - 1 if used else 0)
            owners.append(head)
            query_values.append(split_log(level + 1)[piece] if used else 0.0)
            key_values.append(1.0 if used else 0.0)
    return (
        np.array(masks, np.int32),
        np.array(owners, np.int32),
        np.array(query_values, np.float32),
        np.array(key_values, np.float32),
    )


def nt_dot(left, right):
    return lax.dot_general(
        left, right, (((1,), (1,)), ((), ())), preferred_element_type=jnp.float32
    )


def nn_dot(left, right):
    return jnp.dot(left, right, preferred_element_type=jnp.float32)


def project_kernel(
    blocks, own, scale, meta, *refs
):
    normed = refs[:blocks]
    wq_ref, wk_ref, wv_ref, row_ref, col_ref, row_value, col_value = refs[blocks : blocks + 7]
    q_ref, k_ref, vt_ref = refs[blocks + 7 :]
    length = normed[0].shape[0]
    for index in range(blocks):
        rows = normed[index][...]
        start = meta[own + index]
        span = slice(index * length, (index + 1) * length)
        place = start + lax.broadcasted_iota(jnp.int32, (length, 1), 0)
        extra = jnp.where(
            ((place - col_ref[1:2]) & col_ref[0:1]) == 0, col_value[...], 0.0
        )
        k_ref[span, :] = (nn_dot(rows, wk_ref[...]) + extra).astype(jnp.bfloat16)
        vt_ref[:, span] = nt_dot(wv_ref[...], rows).astype(jnp.bfloat16)
        if index < own:
            place = start + lax.broadcasted_iota(jnp.int32, (1, length), 1)
            extra = jnp.where(
                ((place - row_ref[:, 1:2]) & row_ref[:, 0:1]) == 0, row_value[...], 0.0
            )
            query = nt_dot(wq_ref[...], rows).astype(jnp.bfloat16).astype(jnp.float32)
            q_ref[:, span] = (query * scale + extra).astype(jnp.bfloat16)


def project(meta, normed, wq, wk, wv, row_info, col_info, row_value, col_value, own, scale):
    blocks, length = len(normed), normed[0].shape[0]
    wide, share = wk.shape[1], wv.shape[0]
    vmem = pl.BlockSpec(memory_space=pltpu.VMEM)
    return pl.pallas_call(
        partial(project_kernel, blocks, own, scale),
        in_specs=[pl.BlockSpec(memory_space=pltpu.SMEM)] + [vmem] * (blocks + 7),
        out_specs=[vmem] * 3,
        out_shape=[
            jax.ShapeDtypeStruct((wide, own * length), jnp.bfloat16),
            jax.ShapeDtypeStruct((blocks * length, wide), jnp.bfloat16),
            jax.ShapeDtypeStruct((share, blocks * length), jnp.bfloat16),
        ],
        compiler_params=pltpu.CompilerParams(vmem_limit_bytes=32 << 20),
        name="project",
    )(meta, *normed, wq, wk, wv, row_info, col_info, row_value, col_value)


def project_back_kernel(blocks, *refs):
    normed = refs[:blocks]
    wk_ref, wv_ref, kt_ref, v_ref = refs[blocks:]
    length = normed[0].shape[0]
    for index in range(blocks):
        rows = normed[index][...]
        span = slice(index * length, (index + 1) * length)
        kt_ref[:, span] = nt_dot(wk_ref[...], rows).astype(jnp.bfloat16)
        v_ref[span, :] = nn_dot(rows, wv_ref[...]).astype(jnp.bfloat16)


def project_back(normed, wk, wv):
    blocks, length = len(normed), normed[0].shape[0]
    vmem = pl.BlockSpec(memory_space=pltpu.VMEM)
    return pl.pallas_call(
        partial(project_back_kernel, blocks),
        in_specs=[vmem] * (blocks + 2),
        out_specs=[vmem] * 2,
        out_shape=[
            jax.ShapeDtypeStruct((wk.shape[0], blocks * length), jnp.bfloat16),
            jax.ShapeDtypeStruct((blocks * length, wv.shape[1]), jnp.bfloat16),
        ],
        compiler_params=pltpu.CompilerParams(vmem_limit_bytes=32 << 20),
        cost_estimate=pl.CostEstimate(flops=3 * 10**9, bytes_accessed=6 << 20, transcendentals=0),
        name="project_back",
    )(*normed, wk, wv)


def pair_mask(query_start, key_start, doc_line, block):
    query_place = query_start + lax.broadcasted_iota(jnp.int32, (1, block), 1)
    key_place = key_start + lax.broadcasted_iota(jnp.int32, (block, 1), 0)
    return (key_place <= query_place) & (key_place >= doc_line)


def attend_kernel(
    heads, block, key_blocks, meta, doc_ref, q_ref, k_ref, vt_ref, o_ref, ob_ref, lse_ref, m_ref, l_ref
):
    step = pl.program_id(0)
    steps = pl.num_programs(0)
    query_start = meta[step]
    doc_first = meta[steps + key_blocks + step]
    doc_line = doc_ref[...]
    size = o_ref.shape[0] // heads
    lanes = q_ref.shape[0] // heads
    m_ref[...] = jnp.full_like(m_ref, big_negative)
    l_ref[...] = jnp.zeros_like(l_ref)
    o_ref[...] = jnp.zeros_like(o_ref)

    def body(slot, carry):
        key_start = meta[steps + slot]

        @pl.when((key_start <= query_start) & (key_start + block > doc_first))
        def _():
            span = pl.ds(pl.multiple_of(slot * block, block), block)
            allowed = pair_mask(query_start, key_start, doc_line, block)
            for head in range(heads):
                wide = slice(head * lanes, (head + 1) * lanes)
                rows = slice(head * size, (head + 1) * size)
                scores = nn_dot(k_ref[span, wide], q_ref[wide, :])
                scores = jnp.where(allowed, scores, big_negative)
                old_peak = m_ref[head]
                new_peak = jnp.maximum(old_peak, jnp.max(scores, axis=0, keepdims=True))
                weights = jnp.exp(scores - new_peak)
                fade = jnp.exp(old_peak - new_peak)
                m_ref[head] = new_peak
                l_ref[head] = l_ref[head] * fade + jnp.sum(weights, axis=0, keepdims=True)
                o_ref[rows, :] = o_ref[rows, :] * fade + nn_dot(
                    vt_ref[rows, span], weights.astype(jnp.bfloat16)
                )

        return carry

    lax.fori_loop(0, key_blocks, body, 0)
    for head in range(heads):
        rows = slice(head * size, (head + 1) * size)
        total = l_ref[head]
        mixed = o_ref[rows, :] / total
        o_ref[rows, :] = mixed
        ob_ref[0, rows, :] = mixed.astype(jnp.bfloat16)
        lse_ref[head] = m_ref[head] + jnp.log(total)


def attend_back_kernel(
    heads,
    block,
    key_blocks,
    scale,
    meta,
    doc_ref,
    q_ref,
    g_ref,
    o_ref,
    lse_ref,
    k_ref,
    kt_ref,
    v_ref,
    dq_ref,
    dk_ref,
    dv_ref,
    acc_ref,
):
    step = pl.program_id(0)
    steps = pl.num_programs(0)
    query_start = meta[step]
    doc_first = meta[steps + key_blocks + step]
    doc_line = doc_ref[...]
    size = g_ref.shape[0] // heads
    lanes = q_ref.shape[0] // heads

    @pl.when(step == 0)
    def _():
        dk_ref[...] = jnp.zeros_like(dk_ref)
        dv_ref[...] = jnp.zeros_like(dv_ref)

    acc_ref[...] = jnp.zeros_like(acc_ref)

    def body(slot, carry):
        key_start = meta[steps + slot]

        @pl.when((key_start <= query_start) & (key_start + block > doc_first))
        def _():
            span = pl.ds(pl.multiple_of(slot * block, block), block)
            allowed = pair_mask(query_start, key_start, doc_line, block)
            for head in range(heads):
                wide = slice(head * lanes, (head + 1) * lanes)
                rows = slice(head * size, (head + 1) * size)
                grad = g_ref[rows, :]
                delta = jnp.sum(grad.astype(jnp.float32) * o_ref[rows, :], axis=0, keepdims=True)
                scores = nn_dot(k_ref[span, wide], q_ref[wide, :])
                probs = jnp.where(allowed, jnp.exp(scores - lse_ref[head]), 0.0)
                dots = nn_dot(v_ref[span, head * lanes : head * lanes + size], grad)
                grad_scores = (probs * (dots - delta)).astype(jnp.bfloat16)
                dv_ref[rows, span] += nt_dot(grad, probs.astype(jnp.bfloat16))
                query = q_ref[head * lanes : head * lanes + size, :]
                dk_ref[rows, span] += nt_dot(query, grad_scores)
                acc_ref[rows, :] += nn_dot(kt_ref[rows, span], grad_scores)

        return carry

    lax.fori_loop(0, key_blocks, body, 0)
    dq_ref[...] = (acc_ref[...] * scale).astype(dq_ref.dtype)


def whole(shape):
    return pl.BlockSpec(shape, lambda *index: (0,) * len(shape))


def attend(meta, doc_line, q_ext, k_ext, v_t, heads, block):
    wide, queries = q_ext.shape
    share, keys = v_t.shape
    steps, key_blocks = queries // block, keys // block
    return pl.pallas_call(
        partial(attend_kernel, heads, block, key_blocks),
        grid_spec=pltpu.PrefetchScalarGridSpec(
            num_scalar_prefetch=1,
            grid=(steps,),
            in_specs=[
                pl.BlockSpec((1, block), lambda i, meta: (0, i)),
                pl.BlockSpec((wide, block), lambda i, meta: (0, i)),
                whole(k_ext.shape),
                whole(v_t.shape),
            ],
            out_specs=[
                pl.BlockSpec((share, block), lambda i, meta: (0, i)),
                pl.BlockSpec((1, share, block), lambda i, meta: (i, 0, 0)),
                pl.BlockSpec((heads, 1, block), lambda i, meta: (0, 0, i)),
            ],
            scratch_shapes=[
                pltpu.VMEM((heads, 1, block), jnp.float32),
                pltpu.VMEM((heads, 1, block), jnp.float32),
            ],
        ),
        out_shape=[
            jax.ShapeDtypeStruct((share, queries), jnp.float32),
            jax.ShapeDtypeStruct((steps, share, block), jnp.bfloat16),
            jax.ShapeDtypeStruct((heads, 1, queries), jnp.float32),
        ],
        compiler_params=pltpu.CompilerParams(vmem_limit_bytes=24 << 20),
        cost_estimate=pl.CostEstimate(flops=8 * 10**9, bytes_accessed=8 << 20, transcendentals=0),
        name="attend",
    )(meta, doc_line, q_ext, k_ext, v_t)


def attend_back(meta, doc_line, q_ext, grad_t, mixed, lse, k_ext, k_t, v_ext, heads, block, scale):
    wide, queries = q_ext.shape
    share, keys = k_t.shape
    steps, key_blocks = queries // block, keys // block
    return pl.pallas_call(
        partial(attend_back_kernel, heads, block, key_blocks, scale),
        grid_spec=pltpu.PrefetchScalarGridSpec(
            num_scalar_prefetch=1,
            grid=(steps,),
            in_specs=[
                pl.BlockSpec((1, block), lambda i, meta: (0, i)),
                pl.BlockSpec((wide, block), lambda i, meta: (0, i)),
                pl.BlockSpec((share, block), lambda i, meta: (0, i)),
                pl.BlockSpec((share, block), lambda i, meta: (0, i)),
                pl.BlockSpec((heads, 1, block), lambda i, meta: (0, 0, i)),
                whole(k_ext.shape),
                whole(k_t.shape),
                whole(v_ext.shape),
            ],
            out_specs=[
                pl.BlockSpec((share, block), lambda i, meta: (0, i)),
                whole(k_t.shape),
                whole(k_t.shape),
            ],
            scratch_shapes=[pltpu.VMEM((share, block), jnp.float32)],
        ),
        out_shape=[
            jax.ShapeDtypeStruct((share, queries), jnp.bfloat16),
            jax.ShapeDtypeStruct((share, keys), jnp.float32),
            jax.ShapeDtypeStruct((share, keys), jnp.float32),
        ],
        compiler_params=pltpu.CompilerParams(vmem_limit_bytes=32 << 20),
        cost_estimate=pl.CostEstimate(flops=10**6, bytes_accessed=1 << 10, transcendentals=0),
        name="attend_back",
    )(meta, doc_line, q_ext, grad_t, mixed, lse, k_ext, k_t, v_ext)


def norm_parts(values):
    shifted = values - jnp.mean(values, axis=-1, keepdims=True)
    rate = lax.rsqrt(jnp.mean(shifted * shifted, axis=-1, keepdims=True) + 1e-05)
    return shifted * rate, rate


def norm_back(grad, hat, rate, gain):
    scaled = grad * gain
    mean_scaled = jnp.mean(scaled, axis=-1, keepdims=True)
    mean_product = jnp.mean(scaled * hat, axis=-1, keepdims=True)
    return (
        rate * (scaled - mean_scaled - hat * mean_product),
        jnp.sum(grad * hat, axis=0, keepdims=True),
    )


def middle_kernel(
    chips,
    tiles,
    per,
    position,
    *refs,
):
    mixed = refs[:chips]
    (
        tokens_ref,
        cot_ref,
        wout_ref,
        wup_ref,
        wdown_ref,
        perm_ref,
        ginner_ref,
        gfeed_ref,
        ghidden_ref,
        result_ref,
        gmid_ref,
    ) = refs[chips : chips + 11]
    go_refs = refs[chips + 11 : 2 * chips + 11]
    (
        down_keep,
        down_send,
        flat_keep,
        flat_send,
        dinner_ref,
        dfeed_ref,
        dhidden_ref,
        swap_ref,
        mid_ref,
        z_ref,
        zhat_ref,
        h2_ref,
        hat_ref,
        h2p_ref,
        act_ref,
        slope_ref,
        dact_ref,
        acc_ref,
        stat_ref,
        down_tile,
        flat_tile,
        down_sem,
        flat_sem,
    ) = refs[2 * chips + 11 :]
    step = pl.program_id(0)
    chip, core = position[0], position[1]
    block, model_width = tokens_ref.shape
    share = model_width // chips
    tile = wdown_ref.shape[0]
    hidden = tile * tiles
    root = math.sqrt(2.0 / math.pi)
    phase, index = step // tiles, step % tiles
    slot = lax.rem(index, 2)
    chunks = down_keep.shape[0]
    group = down_tile.shape[1]
    flat = model_width // (2 * chunks)

    def down_copies(where, tile_index):
        area = pl.ds(group * tile_index, group)
        return [
            pltpu.make_async_copy(
                down_tile.at[where, :, side], target.at[area], down_sem.at[where, which]
            )
            for which, (side, target) in enumerate(((core, down_keep), (1 - core, down_send)))
        ]

    def flat_copies(where, first_row):
        area = (slice(None), pl.ds(first_row, flat))
        return [
            pltpu.make_async_copy(
                flat_tile.at[where, which], target.at[area], flat_sem.at[where, which]
            )
            for which, target in enumerate((flat_keep, flat_send))
        ]

    def fill_flat(where, grad):
        for which in range(2):
            for chunk in range(chunks):
                first = (which * chunks + chunk) * flat
                flat_tile[where, which, chunk] = grad[first : first + flat].astype(jnp.bfloat16)

    @pl.when(step == 0)
    def _():
        for near in range(chips):
            start = pl.multiple_of(share * lax.rem(chip + near, chips), share)
            swap_ref[pl.ds(start, share), :] = mixed[near][...].astype(jnp.float32)
        zhat, zrate = norm_parts(swap_ref[...].T)
        zhat_ref[...] = zhat
        stat_ref[0] = jnp.broadcast_to(zrate, stat_ref.shape[1:])
        z = (zhat * ginner_ref[...]).astype(jnp.bfloat16)
        z_ref[...] = z
        mid = tokens_ref[...].astype(jnp.float32) + nn_dot(z, wout_ref[...])
        mid_ref[...] = mid
        hat, rate = norm_parts(mid)
        hat_ref[...] = hat
        stat_ref[1] = jnp.broadcast_to(rate, stat_ref.shape[1:])
        h2 = (hat * gfeed_ref[...]).astype(jnp.bfloat16)
        h2_ref[...] = h2
        h2p_ref[...] = nt_dot(perm_ref[...], h2).astype(jnp.bfloat16)

    @pl.when(phase == 0)
    def _():
        u = nn_dot(h2_ref[...], wup_ref[...])
        squared = u * u
        bend = jnp.tanh(root * (u + 0.044715 * u * squared))
        value = 0.5 * u * (1.0 + bend)
        slope_ref[index] = 0.5 * (1.0 + bend) + 0.5 * u * (1.0 - bend * bend) * root * (
            1.0 + 3.0 * 0.044715 * squared
        )
        act_ref[index] = value

        @pl.when(index == 0)
        def _():
            stat_ref[2] = jnp.broadcast_to(
                jnp.mean(value, axis=-1, keepdims=True), stat_ref.shape[1:]
            )
            stat_ref[3] = jnp.zeros_like(stat_ref[3])
            stat_ref[4] = jnp.zeros_like(stat_ref[4])

        off = value - stat_ref[2][:, :1]
        stat_ref[3] += jnp.broadcast_to(
            jnp.sum(off, axis=-1, keepdims=True), stat_ref.shape[1:]
        )
        stat_ref[4] += jnp.broadcast_to(
            jnp.sum(off * off, axis=-1, keepdims=True), stat_ref.shape[1:]
        )

    @pl.when(step == tiles)
    def _():
        drift = stat_ref[3] / hidden
        stat_ref[2] = stat_ref[2] + drift
        stat_ref[4] = lax.rsqrt(jnp.maximum(stat_ref[4] / hidden - drift * drift, 0.0) + 1e-05)
        stat_ref[5] = jnp.zeros_like(stat_ref[5])
        stat_ref[6] = jnp.zeros_like(stat_ref[6])
        acc_ref[...] = mid_ref[...]

    @pl.when(phase == 1)
    def _():
        gain = ghidden_ref[...]
        hat = (act_ref[index] - stat_ref[2][:, :1]) * stat_ref[4][:, :1]
        act_ref[index] = hat
        act = (hat * gain).astype(jnp.bfloat16)
        cot = cot_ref[...]
        acc_ref[...] += nn_dot(act, wdown_ref[...])
        grad = nt_dot(cot, wdown_ref[...])
        dhidden_ref[...] = jnp.sum(grad * hat, axis=0, keepdims=True)
        scaled = grad * gain
        dact_ref[index] = scaled
        stat_ref[5] += jnp.broadcast_to(
            jnp.sum(scaled, axis=-1, keepdims=True), stat_ref.shape[1:]
        )
        stat_ref[6] += jnp.broadcast_to(
            jnp.sum(scaled * hat, axis=-1, keepdims=True), stat_ref.shape[1:]
        )
        grad = lax.dot_general(
            act, cot, (((0,), (0,)), ((), ())), preferred_element_type=jnp.float32
        )

        @pl.when(index >= 2)
        def _():
            for copy in down_copies(slot, index - 2):
                copy.wait()

        for part in range(group):
            for side in range(2):
                first = (2 * part + side) * per
                down_tile[slot, part, side] = grad[first : first + per].astype(jnp.bfloat16)
        for copy in down_copies(slot, index):
            copy.start()

    @pl.when(step == 2 * tiles)
    def _():
        result_ref[...] = acc_ref[...].astype(jnp.bfloat16)
        acc_ref[...] = jnp.zeros_like(acc_ref)

    @pl.when(phase == 2)
    def _():
        inner = dact_ref[index] - (stat_ref[5][:, :1] + act_ref[index] * stat_ref[6][:, :1]) / hidden
        pre = (stat_ref[4][:, :1] * inner * slope_ref[index]).astype(jnp.bfloat16)
        grad = nn_dot(h2p_ref[...], pre)

        @pl.when(index >= 2)
        def _():
            for copy in flat_copies(slot, flat * (index - 2)):
                copy.wait()

        fill_flat(slot, grad)
        for copy in flat_copies(slot, flat * index):
            copy.start()

        acc_ref[...] += nt_dot(pre, wup_ref[...])

    @pl.when(step == 3 * tiles - 1)
    def _():
        back, dfeed = norm_back(acc_ref[...], hat_ref[...], stat_ref[1][:, :1], gfeed_ref[...])
        dfeed_ref[...] = dfeed
        gmid = cot_ref[...].astype(jnp.float32) + back
        gmid_ref[...] = gmid
        gmid_b = gmid.astype(jnp.bfloat16)
        zp = nt_dot(perm_ref[...], z_ref[...]).astype(jnp.bfloat16)
        fill_flat(2, nn_dot(zp, gmid_b))
        for copy in flat_copies(2, flat * tiles):
            copy.start()
        go, dinner = norm_back(
            nt_dot(gmid_b, wout_ref[...]), zhat_ref[...], stat_ref[0][:, :1], ginner_ref[...]
        )
        dinner_ref[...] = dinner
        swap_ref[...] = go.T
        for near in range(chips):
            start = pl.multiple_of(share * lax.rem(chip + near, chips), share)
            go_refs[near][...] = swap_ref[pl.ds(start, share), :].astype(jnp.bfloat16)
        for late in range(tiles - min(tiles, 2), tiles):
            for copy in down_copies(late % 2, late) + flat_copies(late % 2, flat * late):
                copy.wait()
        for copy in flat_copies(2, flat * tiles):
            copy.wait()


def middle(position, mixed, tokens, cotangent, w_out, w_up, w_down, perm, gains, per):
    chips = len(mixed)
    block, model_width = tokens.shape
    hidden = w_up.shape[1]
    tile = model_width
    tiles = hidden // tile
    share = model_width // chips
    chunks, last = hidden // (2 * per), tiles - 1
    flat, group = model_width // (2 * chunks), chunks // tiles
    down_out = jax.ShapeDtypeStruct((chunks, per, model_width), jnp.bfloat16)
    flat_out = jax.ShapeDtypeStruct((chunks, flat * (tiles + 1), model_width), jnp.bfloat16)

    def up_index(i, pos):
        return (0, jnp.where(i < tiles, i, jnp.where(i < 2 * tiles, last, i - 2 * tiles)))

    def down_index(i, pos):
        return (jnp.clip(i - tiles, 0, last), 0)

    def hidden_index(i, pos):
        return (0, jnp.clip(i - tiles, 0, last))

    def f32(*shape):
        return pltpu.VMEM(shape, jnp.float32)

    def b16(*shape):
        return pltpu.VMEM(shape, jnp.bfloat16)

    square = (model_width, model_width)
    row = (1, model_width)
    return pl.pallas_call(
        partial(middle_kernel, chips, tiles, per),
        grid_spec=pltpu.PrefetchScalarGridSpec(
            num_scalar_prefetch=1,
            grid=(3 * tiles,),
            in_specs=[whole((share, block))] * chips
            + [
                whole((block, model_width)),
                whole((block, model_width)),
                whole(square),
                pl.BlockSpec((model_width, tile), up_index),
                pl.BlockSpec((tile, model_width), down_index),
                whole(square),
                whole(row),
                whole(row),
                pl.BlockSpec((1, tile), hidden_index),
            ],
            out_specs=[whole((block, model_width)), whole((block, model_width))]
            + [whole((share, block))] * chips
            + [
                pl.BlockSpec(memory_space=pl.ANY),
                pl.BlockSpec(memory_space=pl.ANY),
                pl.BlockSpec(memory_space=pl.ANY),
                pl.BlockSpec(memory_space=pl.ANY),
                whole(row),
                whole(row),
                pl.BlockSpec((1, tile), hidden_index),
            ],
            scratch_shapes=[
                f32(model_width, block),
                f32(block, model_width),
                b16(block, model_width),
                f32(block, model_width),
                b16(block, model_width),
                f32(block, model_width),
                b16(model_width, block),
                f32(tiles, block, tile),
                f32(tiles, block, tile),
                f32(tiles, block, tile),
                f32(block, model_width),
                f32(7, block, 128),
                b16(2, group, 2, per, model_width),
                b16(3, 2, chunks, flat, model_width),
                pltpu.SemaphoreType.DMA((2, 2)),
                pltpu.SemaphoreType.DMA((3, 2)),
            ],
        ),
        out_shape=[
            jax.ShapeDtypeStruct((block, model_width), jnp.bfloat16),
            jax.ShapeDtypeStruct((block, model_width), jnp.float32),
        ]
        + [jax.ShapeDtypeStruct((share, block), jnp.bfloat16)] * chips
        + [
            down_out,
            down_out,
            flat_out,
            flat_out,
            jax.ShapeDtypeStruct(row, jnp.float32),
            jax.ShapeDtypeStruct(row, jnp.float32),
            jax.ShapeDtypeStruct((1, hidden), jnp.float32),
        ],
        compiler_params=pltpu.CompilerParams(vmem_limit_bytes=56 << 20),
        cost_estimate=pl.CostEstimate(flops=16 * 10**9, bytes_accessed=40 << 20, transcendentals=0),
        name="middle",
    )(position, *mixed, tokens, cotangent, w_out, w_up, w_down, perm, *gains)


def final_kernel(chips, position, *refs):
    homes = refs[:chips]
    (
        tokens_ref,
        gmid_ref,
        wq_ref,
        wk_ref,
        wv_ref,
        gain_ref,
        out_ref,
        swap_ref,
    ) = refs[chips:]
    chip = position[0]
    block, model_width = tokens_ref.shape
    share = model_width // chips
    total = jnp.zeros((block, model_width), jnp.float32)
    for index, weight in enumerate((wq_ref, wk_ref, wv_ref)):
        for near in range(chips):
            start = pl.multiple_of(share * lax.rem(chip + near, chips), share)
            swap_ref[pl.ds(start, share), :] = homes[near][
                index * share : (index + 1) * share, :
            ].astype(jnp.float32)
        total = total + nt_dot(swap_ref[...].T.astype(jnp.bfloat16), weight[...])
    hat, rate = norm_parts(tokens_ref[...].astype(jnp.float32))
    back = norm_back(total, hat, rate, gain_ref[...])[0]
    out_ref[...] = (gmid_ref[...] + back).astype(jnp.bfloat16)


def final(position, homes, tokens, gmid, w_query, w_key, w_value, gain):
    block, model_width = tokens.shape
    vmem = pl.BlockSpec(memory_space=pltpu.VMEM)
    return pl.pallas_call(
        partial(final_kernel, len(homes)),
        in_specs=[pl.BlockSpec(memory_space=pltpu.SMEM)] + [vmem] * (len(homes) + 6),
        out_specs=vmem,
        out_shape=jax.ShapeDtypeStruct((block, model_width), jnp.bfloat16),
        scratch_shapes=[pltpu.VMEM((model_width, block), jnp.float32)],
        compiler_params=pltpu.CompilerParams(vmem_limit_bytes=24 << 20),
        name="final",
    )(position, *homes, tokens, gmid, w_query, w_key, w_value, gain)


def chip_shift(value, steps):
    count = lax.axis_size("seq")
    return lax.ppermute(value, "seq", [(i, (i + 2 * steps) % count) for i in range(count)])


def seq_swap(value, bit):
    return lax.ppermute(value, "seq", [(i, i ^ bit) for i in range(lax.axis_size("seq"))])


def row_swap(value, bit):
    return lax.ppermute(value, "row", [(i, i ^ bit) for i in range(lax.axis_size("row"))])


def pick(array, index, axis):
    return lax.dynamic_index_in_dim(array, index, axis, keepdims=False)


def rolled(blocks, start):
    count = blocks.shape[0]
    return lax.dynamic_slice_in_dim(jnp.concatenate([blocks, blocks], axis=0), start, count, axis=0)


def sent(array):
    return array.astype(jnp.bfloat16)


def wide(array):
    return array.astype(jnp.float32)


def total_of(*terms):
    result = wide(terms[0])
    for term in terms[1:]:
        result = result + wide(term)
    return sent(result)


def corner(term, low, high, second):
    half = term.shape[1] // 2
    rest = term.shape[2:]
    shaped = term.reshape((2, 2) + term.shape[1:])
    starts = (0 if high is None else high, 0 if low is None else low, half * second)
    sizes = (2 if high is None else 1, 2 if low is None else 1, half)
    part = lax.dynamic_slice(shaped, starts + (0,) * len(rest), sizes + rest)
    return part.reshape((2, half) + rest)


def row_first(terms, row):
    low_bit, high_bit = row % 2, row // 2
    low = row_swap(total_of(*[corner(term, 1 - low_bit, None, 0) for term in terms]), 1)
    high = row_swap(total_of(*[corner(term, None, 1 - high_bit, 1) for term in terms]), 2)
    return low, high


def row_middle(terms, low, high, row):
    low_bit, high_bit = row % 2, row // 2
    return (
        total_of(*[corner(term, low_bit, None, 0) for term in terms], low),
        total_of(*[corner(term, None, high_bit, 1) for term in terms], high),
    )


def row_second(first, second, row):
    low_bit, high_bit = row % 2, row // 2
    low = row_swap(pick(first, 1 - high_bit, 0), 2)
    high = row_swap(pick(second, 1 - low_bit, 0), 1)
    return jnp.concatenate(
        [total_of(pick(first, high_bit, 0), low), total_of(pick(second, low_bit, 0), high)], axis=0
    )


def fast_local(
    tokens,
    lengths,
    w_query,
    w_key,
    w_value,
    w_out,
    w_up,
    w_down,
    gain_attend,
    gain_inner,
    gain_feed,
    gain_hidden,
    cotangent,
):
    block, model_width = tokens.shape
    hidden = w_up.shape[1]
    size = model_width // HEADS
    lanes = 2 * size
    scale = size ** (-0.5)
    seq_devices, row_devices = lax.axis_size("seq"), lax.axis_size("row")
    chips = seq_devices // 2
    heads = HEADS // chips
    share = heads * size
    spread = heads * lanes
    parts = row_devices * seq_devices
    position, row = lax.axis_index("seq"), lax.axis_index("row")
    chip, core = position // 2, position % 2
    place = jnp.stack([chip, core]).astype(jnp.int32)
    bounds = jnp.cumsum(lengths[0])[:-1]
    factor = 1.0 / math.sqrt(block * parts)

    normed_b = layer_norm(tokens.astype(jnp.float32), gain_attend).astype(jnp.bfloat16)
    own = [normed_b] + [chip_shift(normed_b, step) for step in range(1, chips)]

    chip_ids = (chip - jnp.arange(chips, dtype=jnp.int32)) % chips
    query_starts = block * (2 * chip_ids + core)
    key_starts = jnp.concatenate([query_starts, block * (2 * chip_ids + 1 - core)])
    in_block = jnp.arange(block, dtype=jnp.int32)[None, :]
    query_places = (query_starts[:, None] + in_block).reshape(-1)
    doc_line = jnp.max(jnp.where(bounds[:, None] <= query_places[None, :], bounds[:, None], 0), axis=0)
    meta = jnp.concatenate([query_starts, key_starts, doc_line.reshape(chips, block)[:, 0]])
    doc_line = doc_line[None, :]

    feature = jnp.arange(model_width, dtype=jnp.int32)
    wide_lane = jnp.arange(spread, dtype=jnp.int32)
    source = chip * share + wide_lane // lanes * size + wide_lane % lanes
    pick_wide = ((feature[:, None] == source[None, :]) & (wide_lane % lanes < size)[None, :]).astype(
        jnp.bfloat16
    )
    narrow = chip * share + jnp.arange(share, dtype=jnp.int32)
    pick_narrow = (feature[:, None] == narrow[None, :]).astype(jnp.bfloat16)

    def picked(weight, choice):
        return sent(nn_dot(weight, choice))

    def picked_rows(weight, choice):
        return sent(
            lax.dot_general(
                choice, weight, (((0,), (1,)), ((), ())), preferred_element_type=jnp.float32
            )
        )

    per = model_width // parts
    order = jnp.arange(model_width, dtype=jnp.int32)
    chunk, inside = order // per, order % per
    chunks = parts // 2
    parity = jnp.where(chunk < chunks, core, 1 - core)
    wanted = (2 * (chunk % chunks) + parity) * per + inside
    perm = (wanted[:, None] == feature[None, :]).astype(jnp.bfloat16)

    masks, owners, query_values, key_values = extra_features(heads, size, lanes)
    head_ids = heads * chip + jnp.asarray(owners)
    info = jnp.stack([jnp.asarray(masks), head_ids])
    early = (
        jnp.concatenate([query_starts, key_starts]),
        meta,
        doc_line,
        perm,
        picked_rows(w_query, pick_wide),
        picked(w_key, pick_wide),
        picked_rows(w_value, pick_narrow),
        picked_rows(w_key, pick_narrow),
        picked(w_value, pick_wide),
        jnp.concatenate([picked(weight, pick_narrow) for weight in (w_query, w_key, w_value)], axis=1),
        info,
        info.T,
        gain_attend[None, :],
        gain_inner[None, :],
        gain_feed[None, :],
        gain_hidden[None, :],
        place,
    )
    own[1], early = lax.optimization_barrier((own[1], early))
    starts, meta, doc_line, perm, wq_wide, wk_wide, wv_rows, wk_rows, wv_wide, w_own = early[:10]
    info, info_t, gain_first, gain_inner, gain_feed, gain_hidden, place = early[10:]
    sibling = [seq_swap(rows, 1) for rows in own]
    q_ext, k_ext, v_t = project(
        starts,
        own + sibling,
        wq_wide,
        wk_wide,
        wv_rows,
        info_t,
        info,
        jnp.asarray(query_values)[:, None],
        jnp.asarray(key_values)[None, :],
        chips,
        scale,
    )
    mixed, mixed_b, lse = attend(meta, doc_line, q_ext, k_ext, v_t, heads, block)
    back = [mixed_b[0]] + [chip_shift(mixed_b[step], -step) for step in range(1, chips)]

    own_normed = jnp.concatenate(own, axis=0)
    k_t, v_ext = project_back(own + sibling, wk_rows, wv_wide)
    normed_p = sent(nt_dot(perm, own_normed))
    weights_p = sent(nn_dot(perm, w_own))
    back, k_t, v_ext, normed_p, weights_p = lax.optimization_barrier(
        (back, k_t, v_ext, normed_p, weights_p)
    )

    outs = middle(
        place,
        back,
        tokens,
        cotangent,
        w_out,
        w_up,
        w_down,
        perm,
        (gain_inner, gain_feed, gain_hidden),
        hidden // parts,
    )
    result, grad_middle = outs[:2]
    go = outs[2 : 2 + chips]
    keep_a, send_a, keep_b, send_b, dinner, dfeed, dhidden = outs[2 + chips :]

    def gridded(array):
        return array.reshape((row_devices, chips) + array.shape[1:])

    other_a, other_b = seq_swap(send_a, 1), seq_swap(send_b, 1)
    grad_t = jnp.concatenate(
        [go[0]] + [chip_shift(go[step], step) for step in range(1, chips)], axis=1
    )
    grad_t, keep_a, other_a, keep_b, other_b = lax.optimization_barrier(
        (grad_t, keep_a, other_a, keep_b, other_b)
    )
    terms_a, terms_b = [gridded(keep_a), gridded(other_a)], [gridded(keep_b), gridded(other_b)]
    low_a, high_a = row_first(terms_a, row)
    dq, dk, dv = attend_back(
        meta, doc_line, q_ext, grad_t, mixed, lse, k_ext, k_t, v_ext, heads, block, scale
    )
    dq, dk, dv, low_a, high_a, keep_b, other_b = lax.optimization_barrier(
        (dq, dk, dv, low_a, high_a, keep_b, other_b)
    )
    terms_b = [gridded(keep_b), gridded(other_b)]
    low_b, high_b = row_first(terms_b, row)
    mine = chips * block
    pair = jnp.concatenate([dk, dv], axis=0)
    pair_mine = pair[:, :mine] + wide(seq_swap(sent(pair[:, mine:]), 1))
    grads_t = jnp.concatenate([dq, sent(pair_mine)], axis=0)

    home = [grads_t[:, :block]] + [
        chip_shift(grads_t[:, step * block : (step + 1) * block], -step) for step in range(1, chips)
    ]

    own_grad = nt_dot(normed_p, grads_t)
    dattend = jnp.sum(own_grad * wide(weights_p), axis=1).reshape(2, parts // 2, 1, per)
    dattend = jnp.where(core == 0, dattend, dattend[::-1])
    dattend = jnp.concatenate([dattend[0], dattend[1]], axis=1).reshape(1, model_width)
    dattend = dattend / gain_first
    gains_all = jnp.concatenate([dattend, dinner, dfeed, dhidden], axis=1)

    gains_share = gains_all.shape[1] // parts
    gains_rows = -(-gains_share // 128)
    gains_all = gains_all.reshape(parts // 2, 2, gains_share)
    gains_all = jnp.where(core == 0, gains_all, gains_all[:, ::-1]).transpose(1, 0, 2)
    gains_all = jnp.pad(gains_all, ((0, 0), (0, 0), (0, gains_rows * 128 - gains_share)))
    gains_all = jnp.pad(
        gains_all.reshape(parts, gains_rows, 128), ((0, 0), (0, per - gains_rows), (0, 0))
    ).reshape(model_width, 128)
    gap = jnp.zeros((model_width, model_width - 128 - 3 * share), jnp.float32)
    packed = sent(jnp.concatenate([own_grad, gap, gains_all], axis=1))
    half = model_width // 2
    mine_grad = packed[:half].reshape(parts // 2, per, model_width)
    other_grad = seq_swap(packed[half:].reshape(parts // 2, per, model_width), 1)
    low_a, high_a, low_b, high_b, mine_grad, other_grad, home[1] = lax.optimization_barrier(
        (low_a, high_a, low_b, high_b, mine_grad, other_grad, home[1])
    )
    heads_terms = [gridded(mine_grad), gridded(other_grad)]
    first, second = row_middle(terms_b, low_b, high_b, row)
    stage_a = row_second(*row_middle(terms_a, low_a, high_a, row), row)
    heads_first, heads_second = row_middle(heads_terms, *row_first(heads_terms, row), row)
    home, stage_a, first, second, heads_first, heads_second = lax.optimization_barrier(
        (home, stage_a, first, second, heads_first, heads_second)
    )
    grad_input = final(
        place, home, tokens, grad_middle, w_query, w_key, w_value, gain_first
    )
    stage_b = row_second(
        jnp.concatenate([first, heads_first], axis=2),
        jnp.concatenate([second, heads_second], axis=2),
        row,
    )

    def from_chips(stage):
        return [pick(stage, chip, 0)] + [
            chip_shift(pick(stage, (chip + step) % chips, 0), step) for step in range(1, chips)
        ]

    total_a = sum(wide(part) for part in from_chips(stage_a)) * factor
    arrived = from_chips(stage_b)
    ends = stage_b.shape[1] - per
    total_b = sum(wide(part[:ends]) for part in arrived) * factor
    gains_part = sum(wide(part[ends : ends + gains_rows, -128:]) for part in arrived) * factor
    gains_part = gains_part.reshape(-1)[:gains_share]
    home = jnp.stack([part[ends:, : 3 * share] for part in arrived[::-1]])
    home = rolled(home, (chips - 1 - chip) % chips)
    home = wide(home.reshape(chips, per, 3, share)).transpose(2, 1, 0, 3)
    home = home.reshape(3, per * model_width) * factor

    tiles = hidden // model_width
    done_up = total_b[: per * tiles].reshape(tiles, per, model_width)
    return (
        result,
        grad_input,
        home[0],
        home[1],
        home[2],
        total_b[per * tiles :].reshape(-1),
        done_up.transpose(1, 0, 2).reshape(-1),
        total_a.reshape(-1),
        gains_part,
    )


def local(*arrays):
    seq_devices, row_devices = lax.axis_size("seq"), lax.axis_size("row")
    block = arrays[0].shape[0]
    one_segment = block * seq_devices <= SEGMENT and block % 2 ** (PATTERNS - 1) == 0
    if one_segment and seq_devices in (2, 4, 8) and row_devices == 4:
        return fast_local(*arrays)
    return ring_local(*arrays)


def solution(mesh):
    return jax.shard_map(
        local,
        mesh=mesh,
        in_specs=(
            P(("row", "seq"), None),
            P("row", None),
            P(),
            P(),
            P(),
            P(),
            P(),
            P(),
            P(),
            P(),
            P(),
            P(),
            P(("row", "seq"), None),
        ),
        out_specs=(
            P(("row", "seq"), None),
            P(("row", "seq"), None),
            P(("row", "seq")),
            P(("row", "seq")),
            P(("row", "seq")),
            P(("row", "seq")),
            P(("row", "seq")),
            P(("row", "seq")),
            P(("row", "seq")),
        ),
        check_vma=False,
    )
```

```python
from functools import partial
from functools import reduce
import math

import jax
import jax.numpy as jnp
import numpy as np
from jax import lax
from jax.experimental import pallas as pl
from jax.experimental.pallas import tpu as pltpu
from jax.sharding import PartitionSpec as P

HEADS = 12
SEGMENT = 2048
PATTERNS = 5


big_negative = -1e30


def shifted_2(shard, axis, by):
    length = lax.axis_size(axis)
    pairs = [(i, i + by) for i in range(length) if 0 <= i + by < length]
    return lax.ppermute(shard, axis, pairs)


def shifted_3(value, axis, steps):
    count = lax.axis_size(axis)
    pairs = [(source, (source + steps) % count) for source in range(count)]
    return lax.ppermute(value, axis, pairs)


def layer_norm(values, gain_vector):
    centre = jnp.mean(values, axis=-1, keepdims=True)
    shifted = values - centre
    variance = jnp.mean(shifted * shifted, axis=-1, keepdims=True)
    return shifted * lax.rsqrt(variance + 1e-05) * gain_vector


def hidden_norm(hidden_pre, gain_vector):
    return layer_norm(jax.nn.gelu(hidden_pre, approximate=True), gain_vector)


def selector(stride, head_count):
    return jnp.arange(stride)[:, None] == (jnp.arange(head_count) % stride)[None, :]


def compact(full_array, stride):
    length_in, head_count, inner_size = full_array.shape
    shaped = full_array.reshape(length_in // stride, stride, head_count, inner_size)
    picked = jnp.where(
        selector(stride, head_count)[None, :, :, None], shaped, jnp.zeros((), full_array.dtype)
    )
    return jnp.sum(picked, axis=1)


def expand(part_array, stride, fill_value):
    part_rows, head_count, inner_size = part_array.shape
    widened = jnp.where(
        selector(stride, head_count)[None, :, :, None],
        part_array[:, None],
        jnp.asarray(fill_value, part_array.dtype),
    )
    return widened.reshape(part_rows * stride, head_count, inner_size)


def positions(start_pos, part_rows, stride, head_count):
    row_ids = jnp.arange(part_rows, dtype=jnp.int32)[:, None] * stride
    head_ids = (jnp.arange(head_count, dtype=jnp.int32) % stride)[None, :]
    return start_pos + row_ids + head_ids


def doc_index(places, doc_bounds):
    return jnp.sum((places[..., None] >= doc_bounds).astype(jnp.int32), axis=-1)


def block_mask(doc_query, doc_key, local_block):
    allowed = doc_query.T[:, :, None] == doc_key.T[:, None, :]
    if local_block:
        rank_ids = jnp.arange(doc_query.shape[0])
        allowed = allowed & (rank_ids[:, None] >= rank_ids[None, :])[None]
    return allowed


def forward_block(query_part, key_part, value_part, allowed, score_scale):
    scores = (
        jnp.einsum("qhd,khd->hqk", query_part, key_part, preferred_element_type=jnp.float32)
        * score_scale
    )
    scores = jnp.where(allowed, scores, big_negative)
    row_peak = jnp.max(scores, axis=-1)
    weights = jnp.where(allowed, jnp.exp(scores - row_peak[..., None]), 0.0)
    row_total = jnp.sum(weights, axis=-1)
    mixed = jnp.einsum(
        "hqk,khd->qhd", weights.astype(jnp.bfloat16), value_part, preferred_element_type=jnp.float32
    )
    return (row_peak.T, row_total.T, mixed)


def merge(carried, new_block):
    best_peak = jnp.maximum(carried[0], new_block[0])
    keep_factor = jnp.exp(carried[0] - best_peak)
    take_factor = jnp.exp(new_block[0] - best_peak)
    new_total = carried[1] * keep_factor + new_block[1] * take_factor
    new_mixed = carried[2] * keep_factor[..., None] + new_block[2] * take_factor[..., None]
    return (best_peak, new_total, new_mixed)


def backward_block(
    query_part, grad_part, lse_part, delta_part, key_part, value_part, allowed, score_scale
):
    scores = (
        jnp.einsum("qhd,khd->hqk", query_part, key_part, preferred_element_type=jnp.float32)
        * score_scale
    )
    probs = jnp.where(allowed, jnp.exp(scores - lse_part.T[:, :, None]), 0.0)
    dots = jnp.einsum("qhd,khd->hqk", grad_part, value_part, preferred_element_type=jnp.float32)
    grad_scores = (probs * (dots - delta_part.T[:, :, None])).astype(jnp.bfloat16)
    query_grad = (
        jnp.einsum("hqk,khd->qhd", grad_scores, key_part, preferred_element_type=jnp.float32)
        * score_scale
    )
    key_grad = (
        jnp.einsum("hqk,qhd->khd", grad_scores, query_part, preferred_element_type=jnp.float32)
        * score_scale
    )
    value_grad = jnp.einsum(
        "hqk,qhd->khd", probs.astype(jnp.bfloat16), grad_part, preferred_element_type=jnp.float32
    )
    return (query_grad, key_grad, value_grad)


def keep_state(carried):
    return carried


def ring_local(
    tokens,
    lengths,
    w_query,
    w_key,
    w_value,
    w_out,
    w_up,
    w_down,
    gain_attend,
    gain_inner,
    gain_feed,
    gain_hidden,
    cotangent,
):
    block_rows, model_width = tokens.shape
    head_count = HEADS
    head_size = model_width // head_count
    score_scale = head_size ** (-0.5)
    seq_devices = lax.axis_size("seq")
    all_devices = seq_devices * lax.axis_size("row")
    my_index = lax.axis_index("seq")
    seq_total = block_rows * seq_devices
    doc_bounds = jnp.cumsum(lengths[0])[:-1]
    patterns = [
        (2**pattern, min(SEGMENT * 2**pattern, seq_total) // block_rows)
        for pattern in range(PATTERNS)
    ]
    near_ids = [0, 1]
    far_ids = list(range(2, PATTERNS))
    reach = patterns[1][1]
    far_rows = [block_rows // patterns[pattern][0] for pattern in far_ids]
    far_starts = [sum(far_rows[:slot_id]) for slot_id in range(len(far_ids))]
    far_total = sum(far_rows)

    def key_docs(pattern, source):
        stride = patterns[pattern][0]
        return doc_index(
            positions(source * block_rows, block_rows // stride, stride, head_count), doc_bounds
        )

    def is_live(pattern, cycle_step):
        group_size = patterns[pattern][1]
        return (cycle_step < group_size) & (my_index % group_size >= cycle_step)

    source_x = tokens.astype(jnp.float32)
    normed, attend_back = jax.vjp(layer_norm, source_x, gain_attend)
    normed_b = normed.astype(jnp.bfloat16)
    query_b = jnp.dot(normed_b, w_query, preferred_element_type=jnp.float32).astype(jnp.bfloat16)
    key_b = jnp.dot(normed_b, w_key, preferred_element_type=jnp.float32).astype(jnp.bfloat16)
    value_b = jnp.dot(normed_b, w_value, preferred_element_type=jnp.float32).astype(jnp.bfloat16)
    query_heads = query_b.reshape(block_rows, head_count, head_size)
    key_heads = key_b.reshape(block_rows, head_count, head_size)
    value_heads = value_b.reshape(block_rows, head_count, head_size)
    query_parts = [compact(query_heads, stride) for stride, group_size in patterns]
    key_parts = [compact(key_heads, stride) for stride, group_size in patterns]
    value_parts = [compact(value_heads, stride) for stride, group_size in patterns]
    own_docs = [key_docs(pattern, my_index) for pattern in range(PATTERNS)]
    states = [
        forward_block(
            query_parts[pattern],
            key_parts[pattern],
            value_parts[pattern],
            block_mask(own_docs[pattern], own_docs[pattern], True),
            score_scale,
        )
        for pattern in range(PATTERNS)
    ]

    def unpack_near(key_block):
        key_full = key_block[:, :model_width].reshape(block_rows, head_count, head_size)
        value_full = key_block[:, model_width:].reshape(block_rows, head_count, head_size)
        return (key_full, value_full)

    def near_fold_parts(pattern, key_part, value_part, source, carried):
        new_block = forward_block(
            query_parts[pattern],
            key_part,
            value_part,
            block_mask(own_docs[pattern], key_docs(pattern, source), False),
            score_scale,
        )
        return merge(carried, new_block)

    def near_fold(pattern, key_full, value_full, source, carried):
        stride = patterns[pattern][0]
        return near_fold_parts(
            pattern, compact(key_full, stride), compact(value_full, stride), source, carried
        )

    pair_block = jnp.concatenate([key_b, value_b], axis=1)
    kept_blocks = jnp.zeros((max(reach - 1, 1), block_rows, 2 * model_width), jnp.bfloat16)

    def near_forward(cycle_step, loop_state):
        key_block, near_now, kept_store = loop_state
        key_block = shifted_2(key_block, "seq", 1)
        key_full, value_full = unpack_near(key_block)
        new_states = []
        for pattern in near_ids:
            new_states.append(
                lax.cond(
                    is_live(pattern, cycle_step),
                    partial(near_fold, pattern, key_full, value_full, my_index - cycle_step),
                    keep_state,
                    near_now[pattern],
                )
            )
        return (key_block, tuple(new_states), kept_store)

    _, near_states, kept_blocks = lax.fori_loop(
        1, reach, near_forward, (pair_block, (states[0], states[1]), kept_blocks)
    )
    far_block = jnp.concatenate(
        [
            jnp.concatenate(
                [
                    key_parts[pattern].reshape(rows_here, model_width),
                    value_parts[pattern].reshape(rows_here, model_width),
                ],
                axis=1,
            )
            for pattern, rows_here in zip(far_ids, far_rows)
        ],
        axis=0,
    )

    def unpack_far(key_block, slot_id):
        rows_here = far_rows[slot_id]
        row_begin = far_starts[slot_id]
        piece_rows = key_block[row_begin : row_begin + rows_here]
        key_part = piece_rows[:, :model_width].reshape(rows_here, head_count, head_size)
        value_part = piece_rows[:, model_width:].reshape(rows_here, head_count, head_size)
        return (key_part, value_part)

    def far_fold(pattern, key_part, value_part, source, carried):
        new_block = forward_block(
            query_parts[pattern],
            key_part,
            value_part,
            block_mask(own_docs[pattern], key_docs(pattern, source), False),
            score_scale,
        )
        return merge(carried, new_block)

    def far_update(far_now, key_block, cycle_step):
        new_states = []
        for slot_id, pattern in enumerate(far_ids):
            key_part, value_part = unpack_far(key_block, slot_id)
            new_states.append(
                lax.cond(
                    is_live(pattern, cycle_step),
                    partial(far_fold, pattern, key_part, value_part, my_index - cycle_step),
                    keep_state,
                    far_now[slot_id],
                )
            )
        return tuple(new_states)

    far_states = tuple((states[pattern] for pattern in far_ids))

    def far_forward(cycle_step, loop_state):
        key_block, far_now = loop_state
        key_block = shifted_2(key_block, "seq", 1)
        return (key_block, far_update(far_now, key_block, cycle_step))

    _, far_states = lax.fori_loop(1, seq_devices, far_forward, (far_block, far_states))
    ordered = list(near_states) + list(far_states)
    peaks = [
        expand(ordered[pattern][0][..., None], patterns[pattern][0], big_negative)[..., 0]
        for pattern in range(PATTERNS)
    ]
    best_peak = reduce(jnp.maximum, peaks)
    weight_sum = jnp.zeros((block_rows, head_count), jnp.float32)
    mixed_sum = jnp.zeros((block_rows, head_count, head_size), jnp.float32)
    for pattern in range(PATTERNS):
        stride = patterns[pattern][0]
        factor = jnp.exp(peaks[pattern] - best_peak)
        weight_sum = (
            weight_sum + expand(ordered[pattern][1][..., None], stride, 0.0)[..., 0] * factor
        )
        mixed_sum = mixed_sum + expand(ordered[pattern][2], stride, 0.0) * factor[..., None]
    attended = mixed_sum / weight_sum[..., None]
    log_total = best_peak + jnp.log(weight_sum)
    inner_out, inner_back = jax.vjp(
        layer_norm, attended.reshape(block_rows, model_width), gain_inner
    )
    inner_b = inner_out.astype(jnp.bfloat16)
    middle = source_x + jnp.dot(inner_b, w_out, preferred_element_type=jnp.float32)
    normed_two, feed_back = jax.vjp(layer_norm, middle, gain_feed)
    normed_two_b = normed_two.astype(jnp.bfloat16)
    hidden_pre = jnp.dot(normed_two_b, w_up, preferred_element_type=jnp.float32)
    hidden, hidden_back = jax.vjp(hidden_norm, hidden_pre, gain_hidden)
    hidden_b = hidden.astype(jnp.bfloat16)
    result = (middle + jnp.dot(hidden_b, w_down, preferred_element_type=jnp.float32)).astype(
        jnp.bfloat16
    )
    grad_down = jnp.einsum("tf,tg->fg", hidden_b, cotangent, preferred_element_type=jnp.float32)
    grad_hidden = jnp.einsum("tg,fg->tf", cotangent, w_down, preferred_element_type=jnp.float32)
    grad_pre, grad_gain_hidden = hidden_back(grad_hidden)
    grad_pre_b = grad_pre.astype(jnp.bfloat16)
    grad_up = jnp.einsum("tf,tg->fg", normed_two_b, grad_pre_b, preferred_element_type=jnp.float32)
    grad_normed_two = jnp.einsum("tg,fg->tf", grad_pre_b, w_up, preferred_element_type=jnp.float32)
    grad_middle_part, grad_gain_feed = feed_back(grad_normed_two)
    grad_middle = cotangent.astype(jnp.float32) + grad_middle_part
    grad_middle_b = grad_middle.astype(jnp.bfloat16)
    grad_out = jnp.einsum("tf,tg->fg", inner_b, grad_middle_b, preferred_element_type=jnp.float32)
    grad_inner = jnp.einsum("tg,fg->tf", grad_middle_b, w_out, preferred_element_type=jnp.float32)
    grad_attended, grad_gain_inner = inner_back(grad_inner)
    grad_heads = grad_attended.astype(jnp.bfloat16).reshape(block_rows, head_count, head_size)
    delta_rows = jnp.sum(grad_heads.astype(jnp.float32) * attended, axis=-1)
    grad_parts = [compact(grad_heads, stride) for stride, group_size in patterns]
    lse_parts = [compact(log_total[..., None], stride)[..., 0] for stride, group_size in patterns]
    delta_parts = [
        compact(delta_rows[..., None], stride)[..., 0] for stride, group_size in patterns
    ]
    query_grads = []
    home_keys = []
    home_values = []
    for pattern in range(PATTERNS):
        part_query, part_key, part_value = backward_block(
            query_parts[pattern],
            grad_parts[pattern],
            lse_parts[pattern],
            delta_parts[pattern],
            key_parts[pattern],
            value_parts[pattern],
            block_mask(own_docs[pattern], own_docs[pattern], True),
            score_scale,
        )
        query_grads.append(part_query)
        home_keys.append(part_key)
        home_values.append(part_value)

    def fetch_full(key_block):
        return shifted_2(key_block, "seq", 1)

    def near_grad(pattern, key_full, value_full, source, operands):
        query_grad, travel = operands
        stride = patterns[pattern][0]
        part_query, part_key, part_value = backward_block(
            query_parts[pattern],
            grad_parts[pattern],
            lse_parts[pattern],
            delta_parts[pattern],
            compact(key_full, stride),
            compact(value_full, stride),
            block_mask(own_docs[pattern], key_docs(pattern, source), False),
            score_scale,
        )
        spread_rows = jnp.concatenate(
            [
                expand(part_key, stride, 0.0).reshape(block_rows, model_width),
                expand(part_value, stride, 0.0).reshape(block_rows, model_width),
            ],
            axis=1,
        )
        return (query_grad + part_query, travel + spread_rows)

    def near_backward(cycle_step, loop_state):
        key_block, grads_now, travel = loop_state
        key_block = fetch_full(key_block)
        travel = shifted_3(travel.astype(jnp.bfloat16), "seq", 1).astype(travel.dtype)
        key_full, value_full = unpack_near(key_block)
        new_grads = list(grads_now)
        for pattern in near_ids:
            new_grads[pattern], travel = lax.cond(
                is_live(pattern, cycle_step),
                partial(near_grad, pattern, key_full, value_full, my_index - cycle_step),
                keep_state,
                (new_grads[pattern], travel),
            )
        return (key_block, tuple(new_grads), travel)

    own_key_near = expand(home_keys[0], 1, 0.0) + expand(home_keys[1], 2, 0.0)
    own_value_near = expand(home_values[0], 1, 0.0) + expand(home_values[1], 2, 0.0)
    near_start = jnp.concatenate(
        [
            own_key_near.reshape(block_rows, model_width),
            own_value_near.reshape(block_rows, model_width),
        ],
        axis=1,
    )
    _, near_query, travel_near = lax.fori_loop(
        1, reach, near_backward, (pair_block, (query_grads[0], query_grads[1]), near_start)
    )
    near_home = shifted_3(travel_near.astype(jnp.bfloat16), "seq", 1 - reach).astype(
        travel_near.dtype
    )
    near_key_add = near_home[:, :model_width].reshape(block_rows, head_count, head_size)
    near_value_add = near_home[:, model_width:].reshape(block_rows, head_count, head_size)

    def far_grad(slot_id, key_part, value_part, source, operands):
        query_grad, travel = operands
        pattern = far_ids[slot_id]
        rows_here = far_rows[slot_id]
        row_begin = far_starts[slot_id]
        part_query, part_key, part_value = backward_block(
            query_parts[pattern],
            grad_parts[pattern],
            lse_parts[pattern],
            delta_parts[pattern],
            key_part,
            value_part,
            block_mask(own_docs[pattern], key_docs(pattern, source), False),
            score_scale,
        )
        spread_rows = jnp.concatenate(
            [part_key.reshape(rows_here, model_width), part_value.reshape(rows_here, model_width)],
            axis=1,
        )
        return (
            query_grad + part_query,
            travel.at[row_begin : row_begin + rows_here].add(spread_rows),
        )

    def far_back_update(grads_now, travel, key_block, cycle_step):
        new_grads = list(grads_now)
        for slot_id, pattern in enumerate(far_ids):
            key_part, value_part = unpack_far(key_block, slot_id)
            new_grads[slot_id], travel = lax.cond(
                is_live(pattern, cycle_step),
                partial(far_grad, slot_id, key_part, value_part, my_index - cycle_step),
                keep_state,
                (new_grads[slot_id], travel),
            )
        return (tuple(new_grads), travel)

    far_query = tuple((query_grads[pattern] for pattern in far_ids))
    far_empty = jnp.zeros((far_total, 2 * model_width), jnp.float32)

    def far_send(travel):
        return shifted_3(travel.astype(jnp.bfloat16), "seq", 1).astype(travel.dtype)

    def far_backward(cycle_step, loop_state):
        key_block, grads_now, travel = loop_state
        key_block = shifted_2(key_block, "seq", 1)
        travel = far_send(travel)
        grads_now, travel = far_back_update(grads_now, travel, key_block, cycle_step)
        return (key_block, grads_now, travel)

    _, far_query, travel_far = lax.fori_loop(
        1, seq_devices, far_backward, (far_block, far_query, far_empty)
    )
    far_home = far_send(travel_far)
    all_query = list(near_query) + list(far_query)
    query_grad = jnp.zeros((block_rows, head_count, head_size), jnp.float32)
    key_grad = near_key_add
    value_grad = near_value_add
    for pattern in range(PATTERNS):
        stride = patterns[pattern][0]
        query_grad = query_grad + expand(all_query[pattern], stride, 0.0)
    for pattern in far_ids:
        stride = patterns[pattern][0]
        key_grad = key_grad + expand(home_keys[pattern], stride, 0.0)
        value_grad = value_grad + expand(home_values[pattern], stride, 0.0)
    for slot_id, pattern in enumerate(far_ids):
        stride = patterns[pattern][0]
        rows_here = far_rows[slot_id]
        row_begin = far_starts[slot_id]
        piece_rows = far_home[row_begin : row_begin + rows_here]
        key_grad = key_grad + expand(
            piece_rows[:, :model_width].reshape(rows_here, head_count, head_size), stride, 0.0
        )
        value_grad = value_grad + expand(
            piece_rows[:, model_width:].reshape(rows_here, head_count, head_size), stride, 0.0
        )
    grad_query_b = query_grad.reshape(block_rows, model_width).astype(jnp.bfloat16)
    grad_key_b = key_grad.reshape(block_rows, model_width).astype(jnp.bfloat16)
    grad_value_b = value_grad.reshape(block_rows, model_width).astype(jnp.bfloat16)
    grad_w_query = jnp.einsum(
        "tf,tg->fg", normed_b, grad_query_b, preferred_element_type=jnp.float32
    )
    grad_w_key = jnp.einsum("tf,tg->fg", normed_b, grad_key_b, preferred_element_type=jnp.float32)
    grad_w_value = jnp.einsum(
        "tf,tg->fg", normed_b, grad_value_b, preferred_element_type=jnp.float32
    )
    grad_normed = jnp.einsum("tg,fg->tf", grad_query_b, w_query, preferred_element_type=jnp.float32)
    grad_normed = grad_normed + jnp.einsum(
        "tg,fg->tf", grad_key_b, w_key, preferred_element_type=jnp.float32
    )
    grad_normed = grad_normed + jnp.einsum(
        "tg,fg->tf", grad_value_b, w_value, preferred_element_type=jnp.float32
    )
    grad_x_part, grad_gain_attend = attend_back(grad_normed)
    grad_input = (grad_middle + grad_x_part).astype(jnp.bfloat16)
    gains_all = jnp.concatenate(
        [grad_gain_attend, grad_gain_inner, grad_gain_feed, grad_gain_hidden]
    )
    summed = (
        lax.psum_scatter(grad_w_query.reshape(-1), ("row", "seq"), scatter_dimension=0, tiled=True),
        lax.psum_scatter(grad_w_key.reshape(-1), ("row", "seq"), scatter_dimension=0, tiled=True),
        lax.psum_scatter(grad_w_value.reshape(-1), ("row", "seq"), scatter_dimension=0, tiled=True),
        lax.psum_scatter(grad_out.reshape(-1), ("row", "seq"), scatter_dimension=0, tiled=True),
        lax.psum_scatter(grad_up.reshape(-1), ("row", "seq"), scatter_dimension=0, tiled=True),
        lax.psum_scatter(grad_down.reshape(-1), ("row", "seq"), scatter_dimension=0, tiled=True),
        lax.psum_scatter(gains_all, ("row", "seq"), scatter_dimension=0, tiled=True),
    )
    factor = 1.0 / math.sqrt(block_rows * all_devices)
    return (result, grad_input) + tuple((summed_part * factor for summed_part in summed))


def split_log(level):
    remaining = math.log((level + 1) / level)
    pieces = []
    for _ in range(3):
        piece = float(jnp.bfloat16.dtype.type(remaining))
        pieces.append(piece)
        remaining -= piece
    return pieces


def extra_features(heads, size, lanes):
    masks, owners, query_values, key_values = [], [], [], []
    for head in range(heads):
        for lane in range(lanes):
            level, piece = divmod(lane - size, 3)
            used = size <= lane < size + 3 * (PATTERNS - 1)
            masks.append(2 ** (level + 1) - 1 if used else 0)
            owners.append(head)
            query_values.append(split_log(level + 1)[piece] if used else 0.0)
            key_values.append(1.0 if used else 0.0)
    return (
        np.array(masks, np.int32),
        np.array(owners, np.int32),
        np.array(query_values, np.float32),
        np.array(key_values, np.float32),
    )


def nt_dot(left, right):
    return lax.dot_general(
        left, right, (((1,), (1,)), ((), ())), preferred_element_type=jnp.float32
    )


def nn_dot(left, right):
    return jnp.dot(left, right, preferred_element_type=jnp.float32)


def call_whole(kernel, out_shape, name, scalars, *arrays, in_specs=None, scratch=(), cost=None, limit=12):
    return pl.pallas_call(
        kernel,
        grid_spec=pltpu.PrefetchScalarGridSpec(
            num_scalar_prefetch=1,
            grid=(1,),
            in_specs=in_specs or [whole(array.shape) for array in arrays],
            out_specs=[whole(out.shape) for out in out_shape],
            scratch_shapes=list(scratch),
        ),
        out_shape=list(out_shape),
        compiler_params=pltpu.CompilerParams(vmem_limit_bytes=limit << 20),
        cost_estimate=cost,
        name=name,
    )(scalars, *arrays)


def norm_kernel(unused, rows_ref, gain_ref, out_ref):
    out_ref[...] = (norm_parts(rows_ref[...].astype(jnp.float32))[0] * gain_ref[...]).astype(
        jnp.bfloat16
    )


def project_kernel(
    blocks, own, scale, meta, *refs
):
    normed = refs[:blocks]
    wq_ref, wk_ref, wv_ref, row_ref, col_ref, row_value, col_value = refs[blocks : blocks + 7]
    q_ref, k_ref, vt_ref = refs[blocks + 7 :]
    length = normed[0].shape[0]
    for index in range(blocks):
        rows = normed[index][...]
        start = meta[own + index]
        span = slice(index * length, (index + 1) * length)
        place = start + lax.broadcasted_iota(jnp.int32, (length, 1), 0)
        extra = jnp.where(
            ((place - col_ref[1:2]) & col_ref[0:1]) == 0, col_value[...], 0.0
        )
        k_ref[span, :] = (nn_dot(rows, wk_ref[...]) + extra).astype(jnp.bfloat16)
        vt_ref[:, span] = nt_dot(wv_ref[...], rows).astype(jnp.bfloat16)
        if index < own:
            place = start + lax.broadcasted_iota(jnp.int32, (1, length), 1)
            extra = jnp.where(
                ((place - row_ref[:, 1:2]) & row_ref[:, 0:1]) == 0, row_value[...], 0.0
            )
            query = nt_dot(wq_ref[...], rows).astype(jnp.bfloat16).astype(jnp.float32)
            q_ref[:, span] = (query * scale + extra).astype(jnp.bfloat16)


def project(meta, normed, wq, wk, wv, row_info, col_info, row_value, col_value, own, scale):
    blocks, length = len(normed), normed[0].shape[0]
    wide, share = wk.shape[1], wv.shape[0]
    return call_whole(
        partial(project_kernel, blocks, own, scale),
        [
            jax.ShapeDtypeStruct((wide, own * length), jnp.bfloat16),
            jax.ShapeDtypeStruct((blocks * length, wide), jnp.bfloat16),
            jax.ShapeDtypeStruct((share, blocks * length), jnp.bfloat16),
        ],
        "project",
        meta,
        *normed,
        wq,
        wk,
        wv,
        row_info,
        col_info,
        row_value,
        col_value,
        limit=20,
    )


def project_back_kernel(blocks, unused, *refs):
    normed = refs[:blocks]
    wk_ref, wv_ref, kt_ref, v_ref = refs[blocks:]
    length = normed[0].shape[0]
    for index in range(blocks):
        rows = normed[index][...]
        span = slice(index * length, (index + 1) * length)
        kt_ref[:, span] = nt_dot(wk_ref[...], rows).astype(jnp.bfloat16)
        v_ref[span, :] = nn_dot(rows, wv_ref[...]).astype(jnp.bfloat16)


def project_back(scalars, normed, wk, wv):
    blocks, length = len(normed), normed[0].shape[0]
    return call_whole(
        partial(project_back_kernel, blocks),
        [
            jax.ShapeDtypeStruct((wk.shape[0], blocks * length), jnp.bfloat16),
            jax.ShapeDtypeStruct((blocks * length, wv.shape[1]), jnp.bfloat16),
        ],
        "project_back",
        scalars,
        *normed,
        wk,
        wv,
        cost=pl.CostEstimate(flops=3 * 10**9, bytes_accessed=6 << 20, transcendentals=0),
    )


def pair_mask(query_start, key_start, doc_line, block):
    query_place = query_start + lax.broadcasted_iota(jnp.int32, (1, block), 1)
    key_place = key_start + lax.broadcasted_iota(jnp.int32, (block, 1), 0)
    return (key_place <= query_place) & (key_place >= doc_line)


def attend_kernel(
    heads, block, key_blocks, meta, doc_ref, q_ref, k_ref, vt_ref, o_ref, ob_ref, lse_ref, m_ref, l_ref
):
    step = pl.program_id(0)
    steps = pl.num_programs(0)
    query_start = meta[step]
    doc_first = meta[steps + key_blocks + step]
    doc_line = doc_ref[...]
    size = o_ref.shape[0] // heads
    lanes = q_ref.shape[0] // heads
    m_ref[...] = jnp.full_like(m_ref, big_negative)
    l_ref[...] = jnp.zeros_like(l_ref)
    o_ref[...] = jnp.zeros_like(o_ref)

    def body(slot, carry):
        key_start = meta[steps + slot]

        @pl.when((key_start <= query_start) & (key_start + block > doc_first))
        def _():
            span = pl.ds(pl.multiple_of(slot * block, block), block)
            allowed = pair_mask(query_start, key_start, doc_line, block)
            for head in range(heads):
                wide = slice(head * lanes, (head + 1) * lanes)
                rows = slice(head * size, (head + 1) * size)
                scores = nn_dot(k_ref[span, wide], q_ref[wide, :])
                scores = jnp.where(allowed, scores, big_negative)
                old_peak = m_ref[head]
                new_peak = jnp.maximum(old_peak, jnp.max(scores, axis=0, keepdims=True))
                weights = jnp.exp(scores - new_peak)
                fade = jnp.exp(old_peak - new_peak)
                m_ref[head] = new_peak
                l_ref[head] = l_ref[head] * fade + jnp.sum(weights, axis=0, keepdims=True)
                o_ref[rows, :] = o_ref[rows, :] * fade + nn_dot(
                    vt_ref[rows, span], weights.astype(jnp.bfloat16)
                )

        return carry

    lax.fori_loop(0, key_blocks, body, 0)
    for head in range(heads):
        rows = slice(head * size, (head + 1) * size)
        total = l_ref[head]
        mixed = o_ref[rows, :] / total
        o_ref[rows, :] = mixed
        ob_ref[0, rows, :] = mixed.astype(jnp.bfloat16)
        lse_ref[head] = m_ref[head] + jnp.log(total)


def attend_back_kernel(
    heads,
    block,
    key_blocks,
    scale,
    meta,
    doc_ref,
    q_ref,
    g_ref,
    o_ref,
    lse_ref,
    k_ref,
    kt_ref,
    v_ref,
    dq_ref,
    mine_ref,
    other_ref,
    acc_ref,
    pair_ref,
):
    step = pl.program_id(0)
    steps = pl.num_programs(0)
    query_start = meta[step]
    doc_first = meta[steps + key_blocks + step]
    doc_line = doc_ref[...]
    size = g_ref.shape[0] // heads
    lanes = q_ref.shape[0] // heads

    share = g_ref.shape[0]

    @pl.when(step == 0)
    def _():
        pair_ref[...] = jnp.zeros_like(pair_ref)

    acc_ref[...] = jnp.zeros_like(acc_ref)

    def body(slot, carry):
        key_start = meta[steps + slot]

        @pl.when((key_start <= query_start) & (key_start + block > doc_first))
        def _():
            span = pl.ds(pl.multiple_of(slot * block, block), block)
            allowed = pair_mask(query_start, key_start, doc_line, block)
            for head in range(heads):
                wide = slice(head * lanes, (head + 1) * lanes)
                rows = slice(head * size, (head + 1) * size)
                grad = g_ref[rows, :]
                delta = jnp.sum(grad.astype(jnp.float32) * o_ref[rows, :], axis=0, keepdims=True)
                scores = nn_dot(k_ref[span, wide], q_ref[wide, :])
                probs = jnp.where(allowed, jnp.exp(scores - lse_ref[head]), 0.0)
                dots = nn_dot(v_ref[span, head * lanes : head * lanes + size], grad)
                grad_scores = (probs * (dots - delta)).astype(jnp.bfloat16)
                value_rows = slice(share + head * size, share + (head + 1) * size)
                pair_ref[value_rows, span] += nt_dot(grad, probs.astype(jnp.bfloat16))
                query = q_ref[head * lanes : head * lanes + size, :]
                pair_ref[rows, span] += nt_dot(query, grad_scores)
                acc_ref[rows, :] += nn_dot(kt_ref[rows, span], grad_scores)

        return carry

    lax.fori_loop(0, key_blocks, body, 0)
    dq_ref[...] = (acc_ref[...] * scale).astype(dq_ref.dtype)

    @pl.when(step == steps - 1)
    def _():
        half = mine_ref.shape[1]
        mine_ref[...] = pair_ref[:, :half]
        other_ref[...] = pair_ref[:, half:].astype(jnp.bfloat16)


def whole(shape):
    return pl.BlockSpec(shape, lambda *index: (0,) * len(shape))


def attend(meta, doc_line, q_ext, k_ext, v_t, heads, block):
    wide, queries = q_ext.shape
    share, keys = v_t.shape
    steps, key_blocks = queries // block, keys // block
    return pl.pallas_call(
        partial(attend_kernel, heads, block, key_blocks),
        grid_spec=pltpu.PrefetchScalarGridSpec(
            num_scalar_prefetch=1,
            grid=(steps,),
            in_specs=[
                pl.BlockSpec((1, block), lambda i, meta: (0, i)),
                pl.BlockSpec((wide, block), lambda i, meta: (0, i)),
                whole(k_ext.shape),
                whole(v_t.shape),
            ],
            out_specs=[
                pl.BlockSpec((share, block), lambda i, meta: (0, i)),
                pl.BlockSpec((1, share, block), lambda i, meta: (i, 0, 0)),
                pl.BlockSpec((heads, 1, block), lambda i, meta: (0, 0, i)),
            ],
            scratch_shapes=[
                pltpu.VMEM((heads, 1, block), jnp.float32),
                pltpu.VMEM((heads, 1, block), jnp.float32),
            ],
        ),
        out_shape=[
            jax.ShapeDtypeStruct((share, queries), jnp.float32),
            jax.ShapeDtypeStruct((steps, share, block), jnp.bfloat16),
            jax.ShapeDtypeStruct((heads, 1, queries), jnp.float32),
        ],
        compiler_params=pltpu.CompilerParams(vmem_limit_bytes=12 << 20),
        cost_estimate=pl.CostEstimate(flops=8 * 10**9, bytes_accessed=8 << 20, transcendentals=0),
        name="attend",
    )(meta, doc_line, q_ext, k_ext, v_t)


def attend_back(meta, doc_line, q_ext, grad_t, mixed, lse, k_ext, k_t, v_ext, heads, block, scale):
    wide, queries = q_ext.shape
    share, keys = k_t.shape
    steps, key_blocks = queries // block, keys // block
    return pl.pallas_call(
        partial(attend_back_kernel, heads, block, key_blocks, scale),
        grid_spec=pltpu.PrefetchScalarGridSpec(
            num_scalar_prefetch=1,
            grid=(steps,),
            in_specs=[
                pl.BlockSpec((1, block), lambda i, meta: (0, i)),
                pl.BlockSpec((wide, block), lambda i, meta: (0, i)),
                pl.BlockSpec((share, block), lambda i, meta: (0, i)),
                pl.BlockSpec((share, block), lambda i, meta: (0, i)),
                pl.BlockSpec((heads, 1, block), lambda i, meta: (0, 0, i)),
                whole(k_ext.shape),
                whole(k_t.shape),
                whole(v_ext.shape),
            ],
            out_specs=[
                pl.BlockSpec((share, block), lambda i, meta: (0, i)),
                whole((2 * share, keys // 2)),
                whole((2 * share, keys // 2)),
            ],
            scratch_shapes=[
                pltpu.VMEM((share, block), jnp.float32),
                pltpu.VMEM((2 * share, keys), jnp.float32),
            ],
        ),
        out_shape=[
            jax.ShapeDtypeStruct((share, queries), jnp.bfloat16),
            jax.ShapeDtypeStruct((2 * share, keys // 2), jnp.float32),
            jax.ShapeDtypeStruct((2 * share, keys // 2), jnp.bfloat16),
        ],
        compiler_params=pltpu.CompilerParams(vmem_limit_bytes=20 << 20),
        cost_estimate=pl.CostEstimate(flops=10**6, bytes_accessed=1 << 10, transcendentals=0),
        name="attend_back",
    )(meta, doc_line, q_ext, grad_t, mixed, lse, k_ext, k_t, v_ext)


def join_kernel(chips, unused, dq_ref, mine_ref, other_ref, *out_refs):
    share = dq_ref.shape[0]
    block = dq_ref.shape[1] // chips
    for step in range(chips):
        span = slice(step * block, (step + 1) * block)
        pair = (mine_ref[:, span] + other_ref[:, span].astype(jnp.float32)).astype(jnp.bfloat16)
        out_refs[step][:share, :] = dq_ref[:, span]
        out_refs[step][share:, :] = pair


def join_parts(scalars, dq, mine, other, chips):
    rows, block = dq.shape[0] + mine.shape[0], dq.shape[1] // chips
    return call_whole(
        partial(join_kernel, chips),
        [jax.ShapeDtypeStruct((rows, block), jnp.bfloat16)] * chips,
        "join",
        scalars,
        dq,
        mine,
        other,
    )


def norm_parts(values):
    shifted = values - jnp.mean(values, axis=-1, keepdims=True)
    rate = lax.rsqrt(jnp.mean(shifted * shifted, axis=-1, keepdims=True) + 1e-05)
    return shifted * rate, rate


def norm_back(grad, hat, rate, gain):
    scaled = grad * gain
    mean_scaled = jnp.mean(scaled, axis=-1, keepdims=True)
    mean_product = jnp.mean(scaled * hat, axis=-1, keepdims=True)
    return (
        rate * (scaled - mean_scaled - hat * mean_product),
        jnp.sum(grad * hat, axis=0, keepdims=True),
    )


def middle_kernel(
    chips,
    tiles,
    per,
    position,
    *refs,
):
    mixed = refs[:chips]
    (
        tokens_ref,
        cot_ref,
        wout_ref,
        wup_ref,
        wdown_ref,
        perm_ref,
        ginner_ref,
        gfeed_ref,
        ghidden_ref,
        result_ref,
        gmid_ref,
    ) = refs[chips : chips + 11]
    go_refs = refs[chips + 11 : 2 * chips + 11]
    (
        down_keep,
        down_send,
        flat_keep,
        flat_send,
        dinner_ref,
        dfeed_ref,
        dhidden_ref,
        swap_ref,
        mid_ref,
        z_ref,
        zhat_ref,
        h2_ref,
        hat_ref,
        h2p_ref,
        act_ref,
        slope_ref,
        dact_ref,
        acc_ref,
        stat_ref,
        down_tile,
        flat_tile,
        down_sem,
        flat_sem,
    ) = refs[2 * chips + 11 :]
    step = pl.program_id(0)
    chip, core = position[0], position[1]
    block, model_width = tokens_ref.shape
    share = model_width // chips
    tile = wdown_ref.shape[0]
    hidden = tile * tiles
    root = math.sqrt(2.0 / math.pi)
    phase, index = step // tiles, step % tiles
    slot = lax.rem(index, 2)
    chunks = down_keep.shape[0]
    group = down_tile.shape[1]
    flat = model_width // (2 * chunks)

    def down_copies(where, tile_index):
        area = pl.ds(group * tile_index, group)
        return [
            pltpu.make_async_copy(
                down_tile.at[where, :, side], target.at[area], down_sem.at[where, which]
            )
            for which, (side, target) in enumerate(((core, down_keep), (1 - core, down_send)))
        ]

    def flat_copies(where, first_row):
        area = (slice(None), pl.ds(first_row, flat))
        return [
            pltpu.make_async_copy(
                flat_tile.at[where, which], target.at[area], flat_sem.at[where, which]
            )
            for which, target in enumerate((flat_keep, flat_send))
        ]

    def fill_flat(where, grad):
        for which in range(2):
            for chunk in range(chunks):
                first = (which * chunks + chunk) * flat
                flat_tile[where, which, chunk] = grad[first : first + flat].astype(jnp.bfloat16)

    @pl.when(step == 0)
    def _():
        for near in range(chips):
            start = pl.multiple_of(share * lax.rem(chip + near, chips), share)
            swap_ref[pl.ds(start, share), :] = mixed[near][...].astype(jnp.float32)
        zhat, zrate = norm_parts(swap_ref[...].T)
        zhat_ref[...] = zhat
        stat_ref[0] = jnp.broadcast_to(zrate, stat_ref.shape[1:])
        z = (zhat * ginner_ref[...]).astype(jnp.bfloat16)
        z_ref[...] = z
        mid = tokens_ref[...].astype(jnp.float32) + nn_dot(z, wout_ref[...])
        mid_ref[...] = mid
        hat, rate = norm_parts(mid)
        hat_ref[...] = hat
        stat_ref[1] = jnp.broadcast_to(rate, stat_ref.shape[1:])
        h2 = (hat * gfeed_ref[...]).astype(jnp.bfloat16)
        h2_ref[...] = h2
        h2p_ref[...] = nt_dot(perm_ref[...], h2).astype(jnp.bfloat16)

    @pl.when(phase == 0)
    def _():
        u = nn_dot(h2_ref[...], wup_ref[...])
        squared = u * u
        bend = jnp.tanh(root * (u + 0.044715 * u * squared))
        value = 0.5 * u * (1.0 + bend)
        slope_ref[index] = 0.5 * (1.0 + bend) + 0.5 * u * (1.0 - bend * bend) * root * (
            1.0 + 3.0 * 0.044715 * squared
        )
        act_ref[index] = value

        @pl.when(index == 0)
        def _():
            stat_ref[2] = jnp.broadcast_to(
                jnp.mean(value, axis=-1, keepdims=True), stat_ref.shape[1:]
            )
            stat_ref[3] = jnp.zeros_like(stat_ref[3])
            stat_ref[4] = jnp.zeros_like(stat_ref[4])

        off = value - stat_ref[2][:, :1]
        stat_ref[3] += jnp.broadcast_to(
            jnp.sum(off, axis=-1, keepdims=True), stat_ref.shape[1:]
        )
        stat_ref[4] += jnp.broadcast_to(
            jnp.sum(off * off, axis=-1, keepdims=True), stat_ref.shape[1:]
        )

    @pl.when(step == tiles)
    def _():
        drift = stat_ref[3] / hidden
        stat_ref[2] = stat_ref[2] + drift
        stat_ref[4] = lax.rsqrt(jnp.maximum(stat_ref[4] / hidden - drift * drift, 0.0) + 1e-05)
        stat_ref[5] = jnp.zeros_like(stat_ref[5])
        stat_ref[6] = jnp.zeros_like(stat_ref[6])
        acc_ref[...] = mid_ref[...]

    @pl.when(phase == 1)
    def _():
        gain = ghidden_ref[...]
        hat = (act_ref[index] - stat_ref[2][:, :1]) * stat_ref[4][:, :1]
        act_ref[index] = hat
        act = (hat * gain).astype(jnp.bfloat16)
        cot = cot_ref[...]
        acc_ref[...] += nn_dot(act, wdown_ref[...])
        grad = nt_dot(cot, wdown_ref[...])
        dhidden_ref[...] = jnp.sum(grad * hat, axis=0, keepdims=True)
        scaled = grad * gain
        dact_ref[index] = scaled
        stat_ref[5] += jnp.broadcast_to(
            jnp.sum(scaled, axis=-1, keepdims=True), stat_ref.shape[1:]
        )
        stat_ref[6] += jnp.broadcast_to(
            jnp.sum(scaled * hat, axis=-1, keepdims=True), stat_ref.shape[1:]
        )
        grad = lax.dot_general(
            act, cot, (((0,), (0,)), ((), ())), preferred_element_type=jnp.float32
        )

        @pl.when(index >= 2)
        def _():
            for copy in down_copies(slot, index - 2):
                copy.wait()

        for part in range(group):
            for side in range(2):
                first = (2 * part + side) * per
                down_tile[slot, part, side] = grad[first : first + per].astype(jnp.bfloat16)
        for copy in down_copies(slot, index):
            copy.start()

    @pl.when(step == 2 * tiles)
    def _():
        result_ref[...] = acc_ref[...].astype(jnp.bfloat16)
        acc_ref[...] = jnp.zeros_like(acc_ref)

    @pl.when(phase == 2)
    def _():
        inner = dact_ref[index] - (stat_ref[5][:, :1] + act_ref[index] * stat_ref[6][:, :1]) / hidden
        pre = (stat_ref[4][:, :1] * inner * slope_ref[index]).astype(jnp.bfloat16)
        grad = nn_dot(h2p_ref[...], pre)

        @pl.when(index >= 2)
        def _():
            for copy in flat_copies(slot, flat * (index - 2)):
                copy.wait()

        fill_flat(slot, grad)
        for copy in flat_copies(slot, flat * index):
            copy.start()

        acc_ref[...] += nt_dot(pre, wup_ref[...])

    @pl.when(step == 3 * tiles - 1)
    def _():
        back, dfeed = norm_back(acc_ref[...], hat_ref[...], stat_ref[1][:, :1], gfeed_ref[...])
        dfeed_ref[...] = dfeed
        gmid = cot_ref[...].astype(jnp.float32) + back
        gmid_ref[...] = gmid
        gmid_b = gmid.astype(jnp.bfloat16)
        zp = nt_dot(perm_ref[...], z_ref[...]).astype(jnp.bfloat16)
        fill_flat(2, nn_dot(zp, gmid_b))
        for copy in flat_copies(2, flat * tiles):
            copy.start()
        go, dinner = norm_back(
            nt_dot(gmid_b, wout_ref[...]), zhat_ref[...], stat_ref[0][:, :1], ginner_ref[...]
        )
        dinner_ref[...] = dinner
        swap_ref[...] = go.T
        for near in range(chips):
            start = pl.multiple_of(share * lax.rem(chip + near, chips), share)
            go_refs[near][...] = swap_ref[pl.ds(start, share), :].astype(jnp.bfloat16)
        for late in range(tiles - min(tiles, 2), tiles):
            for copy in down_copies(late % 2, late) + flat_copies(late % 2, flat * late):
                copy.wait()
        for copy in flat_copies(2, flat * tiles):
            copy.wait()


def middle(position, mixed, tokens, cotangent, w_out, w_up, w_down, perm, gains, per):
    chips = len(mixed)
    block, model_width = tokens.shape
    hidden = w_up.shape[1]
    tile = model_width
    tiles = hidden // tile
    share = model_width // chips
    chunks, last = hidden // (2 * per), tiles - 1
    flat, group = model_width // (2 * chunks), chunks // tiles
    down_out = jax.ShapeDtypeStruct((chunks, per, model_width), jnp.bfloat16)
    flat_out = jax.ShapeDtypeStruct((chunks, flat * (tiles + 1), model_width), jnp.bfloat16)

    def up_index(i, pos):
        return (0, jnp.where(i < tiles, i, jnp.where(i < 2 * tiles, last, i - 2 * tiles)))

    def down_index(i, pos):
        return (jnp.clip(i - tiles, 0, last), 0)

    def hidden_index(i, pos):
        return (0, jnp.clip(i - tiles, 0, last))

    def f32(*shape):
        return pltpu.VMEM(shape, jnp.float32)

    def b16(*shape):
        return pltpu.VMEM(shape, jnp.bfloat16)

    square = (model_width, model_width)
    row = (1, model_width)
    return pl.pallas_call(
        partial(middle_kernel, chips, tiles, per),
        grid_spec=pltpu.PrefetchScalarGridSpec(
            num_scalar_prefetch=1,
            grid=(3 * tiles,),
            in_specs=[whole((share, block))] * chips
            + [
                whole((block, model_width)),
                whole((block, model_width)),
                whole(square),
                pl.BlockSpec((model_width, tile), up_index),
                pl.BlockSpec((tile, model_width), down_index),
                whole(square),
                whole(row),
                whole(row),
                pl.BlockSpec((1, tile), hidden_index),
            ],
            out_specs=[whole((block, model_width)), whole((block, model_width))]
            + [whole((share, block))] * chips
            + [
                pl.BlockSpec(memory_space=pl.ANY),
                pl.BlockSpec(memory_space=pl.ANY),
                pl.BlockSpec(memory_space=pl.ANY),
                pl.BlockSpec(memory_space=pl.ANY),
                whole(row),
                whole(row),
                pl.BlockSpec((1, tile), hidden_index),
            ],
            scratch_shapes=[
                f32(model_width, block),
                f32(block, model_width),
                b16(block, model_width),
                f32(block, model_width),
                b16(block, model_width),
                f32(block, model_width),
                b16(model_width, block),
                f32(tiles, block, tile),
                f32(tiles, block, tile),
                f32(tiles, block, tile),
                f32(block, model_width),
                f32(7, block, 128),
                b16(2, group, 2, per, model_width),
                b16(3, 2, chunks, flat, model_width),
                pltpu.SemaphoreType.DMA((2, 2)),
                pltpu.SemaphoreType.DMA((3, 2)),
            ],
        ),
        out_shape=[
            jax.ShapeDtypeStruct((block, model_width), jnp.bfloat16),
            jax.ShapeDtypeStruct((block, model_width), jnp.float32),
        ]
        + [jax.ShapeDtypeStruct((share, block), jnp.bfloat16)] * chips
        + [
            down_out,
            down_out,
            flat_out,
            flat_out,
            jax.ShapeDtypeStruct(row, jnp.float32),
            jax.ShapeDtypeStruct(row, jnp.float32),
            jax.ShapeDtypeStruct((1, hidden), jnp.float32),
        ],
        compiler_params=pltpu.CompilerParams(vmem_limit_bytes=44 << 20),
        cost_estimate=pl.CostEstimate(flops=16 * 10**9, bytes_accessed=40 << 20, transcendentals=0),
        name="middle",
    )(position, *mixed, tokens, cotangent, w_out, w_up, w_down, perm, *gains)


def final_kernel(chips, position, *refs):
    homes = refs[:chips]
    (
        tokens_ref,
        gmid_ref,
        wq_ref,
        wk_ref,
        wv_ref,
        gain_ref,
        out_ref,
        swap_ref,
    ) = refs[chips:]
    chip = position[0]
    block, model_width = tokens_ref.shape
    share = model_width // chips
    total = jnp.zeros((block, model_width), jnp.float32)
    for index, weight in enumerate((wq_ref, wk_ref, wv_ref)):
        for near in range(chips):
            start = pl.multiple_of(share * lax.rem(chip + near, chips), share)
            swap_ref[pl.ds(start, share), :] = homes[near][
                index * share : (index + 1) * share, :
            ].astype(jnp.float32)
        total = total + nt_dot(swap_ref[...].T.astype(jnp.bfloat16), weight[...])
    hat, rate = norm_parts(tokens_ref[...].astype(jnp.float32))
    back = norm_back(total, hat, rate, gain_ref[...])[0]
    out_ref[...] = (gmid_ref[...] + back).astype(jnp.bfloat16)


def final(position, homes, tokens, gmid, w_query, w_key, w_value, gain):
    block, model_width = tokens.shape
    return call_whole(
        partial(final_kernel, len(homes)),
        [jax.ShapeDtypeStruct((block, model_width), jnp.bfloat16)],
        "final",
        position,
        *homes,
        tokens,
        gmid,
        w_query,
        w_key,
        w_value,
        gain,
        scratch=[pltpu.VMEM((model_width, block), jnp.float32)],
    )[0]


def chip_shift(value, steps):
    count = lax.axis_size("seq")
    return lax.ppermute(value, "seq", [(i, (i + 2 * steps) % count) for i in range(count)])


def seq_swap(value, bit):
    return lax.ppermute(value, "seq", [(i, i ^ bit) for i in range(lax.axis_size("seq"))])


def row_swap(value, bit):
    return lax.ppermute(value, "row", [(i, i ^ bit) for i in range(lax.axis_size("row"))])


def sent(array):
    return array.astype(jnp.bfloat16)


def wide(array):
    return array.astype(jnp.float32)


def low_part(shape, keep):
    def index(i, bits):
        return (0, bits[2] if keep else 1 - bits[2], 0, 0, 0)

    return pl.BlockSpec((2, 1, shape[2] // 2) + shape[3:], index)


def high_part(shape, keep):
    def index(i, bits):
        return (bits[3] if keep else 1 - bits[3], 0, 1, 0, 0)

    return pl.BlockSpec((1, 2, shape[2] // 2) + shape[3:], index)


def outgoing_kernel(scalars, low_a, low_b, high_a, high_b, low_ref, high_ref):
    low_ref[...] = sent(wide(low_a[:, 0]) + wide(low_b[:, 0]))
    high_ref[...] = sent(wide(high_a[0]) + wide(high_b[0]))


def outgoing(scalars, keep, other, kept=False):
    shape = keep.shape
    out = jax.ShapeDtypeStruct((2, shape[2] // 2) + shape[3:], jnp.bfloat16)
    low, high = low_part(shape, kept), high_part(shape, kept)
    return call_whole(
        outgoing_kernel,
        [out, out],
        "kept" if kept else "outgoing",
        scalars,
        keep,
        other,
        keep,
        other,
        in_specs=[low, low, high, high],
    )


def halfway_kernel(groups, scalars, *refs):
    ins, outs = refs[: 4 * groups], refs[4 * groups :]
    low_bit, high_bit = scalars[2], scalars[3]
    low_keep, low_send, high_keep, high_send = outs
    first = 0
    for group in range(groups):
        low, high, low_in, high_in = ins[4 * group : 4 * group + 4]
        rows = slice(first, first + low.shape[2])
        for target, side in ((low_keep, high_bit), (low_send, 1 - high_bit)):
            target[:, rows] = sent(wide(low[side]) + wide(low_in[side]))
        for target, side in ((high_keep, low_bit), (high_send, 1 - low_bit)):
            target[:, rows] = sent(wide(high[side]) + wide(high_in[side]))
        first += low.shape[2]


def halfway(scalars, groups):
    arrays = [array for group in groups for array in group]
    rows = sum(group[0].shape[2] for group in groups)
    out = jax.ShapeDtypeStruct((arrays[0].shape[1], rows, arrays[0].shape[3]), jnp.bfloat16)
    return call_whole(
        partial(halfway_kernel, len(groups)), [out] * 4, "halfway", scalars, *arrays, limit=24
    )


def split_kernel(chips, groups, scalars, *refs):
    ins, outs = refs[: 4 * groups], refs[4 * groups : 4 * groups + chips]
    all_ref = refs[-1]
    half = chips // 2
    first = 0
    for group in range(groups):
        low_keep, low_in, high_keep, high_in = ins[4 * group : 4 * group + 4]
        rows = slice(first, first + low_in.shape[1])
        all_ref[:half, rows] = sent(wide(low_keep[...]) + wide(low_in[...]))
        all_ref[half:, rows] = sent(wide(high_keep[...]) + wide(high_in[...]))
        first += low_in.shape[1]
    for step in range(chips):
        outs[step][...] = all_ref[lax.rem(scalars[0] + step, chips)]


def split(scalars, groups, chips):
    arrays = [array for group in groups for array in group]
    rows = sum(group[0].shape[1] for group in groups)
    width = arrays[0].shape[2]
    return call_whole(
        partial(split_kernel, chips, len(groups)),
        [jax.ShapeDtypeStruct((rows, width), jnp.bfloat16)] * chips,
        "split",
        scalars,
        *arrays,
        scratch=[pltpu.VMEM((chips, rows, width), jnp.bfloat16)],
    )


def lay_flat(target, values, first, step):
    for piece in range(values.shape[1] // 128):
        target[pl.ds(first + piece, values.shape[0], step), :] = values[
            :, 128 * piece : 128 * (piece + 1)
        ]


def finish_kernel(chips, per, share, factor, scalars, *refs):
    arrived, heads_in, refs = refs[:chips], refs[chips : 2 * chips], refs[chips:]
    down_ref, up_ref, out_ref, query_ref, key_ref, value_ref, gains_ref, heads_ref = refs[chips:]
    width = arrived[0].shape[1]
    chip, pieces = scalars[0], width // 128
    tiles = up_ref.shape[0] * 128 // (per * width)
    down_rows = down_ref.shape[0] * 128 // width

    def total(first, rows):
        result = wide(arrived[0][first : first + rows, :])
        for part in arrived[1:]:
            result = result + wide(part[first : first + rows, :])
        return result * factor

    lay_flat(down_ref, total(0, down_rows), 0, pieces)
    for tile in range(tiles):
        lay_flat(up_ref, total(down_rows + tile * per, per), tile * pieces, tiles * pieces)
    lay_flat(out_ref, total(down_rows + tiles * per, per), 0, pieces)
    gains = wide(heads_in[0][:8, -128:])
    for part in heads_in[1:]:
        gains = gains + wide(part[:8, -128:])
    gains_ref[...] = gains * factor
    for step in range(chips):
        heads_ref[lax.rem(chip - step + chips, chips)] = wide(heads_in[step][:, : 3 * share])
    for index, target in enumerate((query_ref, key_ref, value_ref)):
        values = jnp.concatenate(
            [heads_ref[near][:, index * share : (index + 1) * share] for near in range(chips)], axis=1
        )
        lay_flat(target, values * factor, 0, pieces)


def finish(scalars, arrived, hidden, parts, per, share, factor):
    chips, width = len(arrived) // 2, arrived[0].shape[1]
    square = jax.ShapeDtypeStruct((per * width // 128, 128), jnp.float32)
    large = jax.ShapeDtypeStruct((per * hidden // 128, 128), jnp.float32)
    return call_whole(
        partial(finish_kernel, chips, per, share, factor),
        [large, large, square, square, square, square, jax.ShapeDtypeStruct((8, 128), jnp.float32)],
        "finish",
        scalars,
        *arrived,
        scratch=[pltpu.VMEM((chips, per, 3 * share), jnp.float32)],
    )


def gathered(rows, chips, chip):
    if chips != 4:
        return [rows] + [chip_shift(rows, step) for step in range(1, chips)]
    behind, ahead = chip_shift(rows, 1), chip_shift(rows, -1)
    up = [(2 * i + core, 2 * i + 2 + core) for i in (1, 2) for core in (0, 1)]
    down = [(2 * i + core, 2 * i - 2 + core) for i in (1, 2) for core in (0, 1)]
    across = jnp.where(
        chip < 2, lax.ppermute(ahead, "seq", down), lax.ppermute(behind, "seq", up)
    )
    return [rows, behind, across, ahead]


def fast_local(
    tokens,
    lengths,
    w_query,
    w_key,
    w_value,
    w_out,
    w_up,
    w_down,
    gain_attend,
    gain_inner,
    gain_feed,
    gain_hidden,
    cotangent,
):
    block, model_width = tokens.shape
    hidden = w_up.shape[1]
    size = model_width // HEADS
    lanes = 2 * size
    scale = size ** (-0.5)
    seq_devices, row_devices = lax.axis_size("seq"), lax.axis_size("row")
    chips = seq_devices // 2
    heads = HEADS // chips
    share = heads * size
    spread = heads * lanes
    parts = row_devices * seq_devices
    position, row = lax.axis_index("seq"), lax.axis_index("row")
    chip, core = position // 2, position % 2
    place = jnp.stack([chip, core, row % 2, row // 2]).astype(jnp.int32)
    bounds = jnp.cumsum(lengths[0])[:-1]
    factor = 1.0 / math.sqrt(block * parts)

    normed_b = call_whole(
        norm_kernel,
        [jax.ShapeDtypeStruct(tokens.shape, jnp.bfloat16)],
        "norm",
        jnp.zeros((1,), jnp.int32),
        tokens,
        gain_attend[None, :],
    )[0]
    own = gathered(normed_b, chips, chip)

    chip_ids = (chip - jnp.arange(chips, dtype=jnp.int32)) % chips
    query_starts = block * (2 * chip_ids + core)
    key_starts = jnp.concatenate([query_starts, block * (2 * chip_ids + 1 - core)])
    in_block = jnp.arange(block, dtype=jnp.int32)[None, :]
    query_places = (query_starts[:, None] + in_block).reshape(-1)
    doc_line = jnp.max(jnp.where(bounds[:, None] <= query_places[None, :], bounds[:, None], 0), axis=0)
    meta = jnp.concatenate([query_starts, key_starts, doc_line.reshape(chips, block)[:, 0]])
    doc_line = doc_line[None, :]

    feature = jnp.arange(model_width, dtype=jnp.int32)
    wide_lane = jnp.arange(spread, dtype=jnp.int32)
    source = chip * share + wide_lane // lanes * size + wide_lane % lanes
    pick_wide = ((feature[:, None] == source[None, :]) & (wide_lane % lanes < size)[None, :]).astype(
        jnp.bfloat16
    )
    narrow = chip * share + jnp.arange(share, dtype=jnp.int32)
    pick_narrow = (feature[:, None] == narrow[None, :]).astype(jnp.bfloat16)

    def picked(weight, choice):
        return sent(nn_dot(weight, choice))

    def picked_rows(weight, choice):
        return sent(
            lax.dot_general(
                choice, weight, (((0,), (1,)), ((), ())), preferred_element_type=jnp.float32
            )
        )

    per = model_width // parts
    order = jnp.arange(model_width, dtype=jnp.int32)
    chunk, inside = order // per, order % per
    chunks = parts // 2
    parity = jnp.where(chunk < chunks, core, 1 - core)
    wanted = (2 * (chunk % chunks) + parity) * per + inside
    perm = (wanted[:, None] == feature[None, :]).astype(jnp.bfloat16)

    masks, owners, query_values, key_values = extra_features(heads, size, lanes)
    head_ids = heads * chip + jnp.asarray(owners)
    info = jnp.stack([jnp.asarray(masks), head_ids])
    early = (
        jnp.concatenate([query_starts, key_starts]),
        meta,
        doc_line,
        perm,
        picked_rows(w_query, pick_wide),
        picked(w_key, pick_wide),
        picked_rows(w_value, pick_narrow),
        picked_rows(w_key, pick_narrow),
        picked(w_value, pick_wide),
        jnp.concatenate([picked(weight, pick_narrow) for weight in (w_query, w_key, w_value)], axis=1),
        info,
        info.T,
        gain_attend[None, :],
        gain_inner[None, :],
        gain_feed[None, :],
        gain_hidden[None, :],
        place,
    )
    own[1], early = lax.optimization_barrier((own[1], early))
    starts, meta, doc_line, perm, wq_wide, wk_wide, wv_rows, wk_rows, wv_wide, w_own = early[:10]
    info, info_t, gain_first, gain_inner, gain_feed, gain_hidden, place = early[10:]
    sibling = [seq_swap(rows, 1) for rows in own]
    q_ext, k_ext, v_t = project(
        starts,
        own + sibling,
        wq_wide,
        wk_wide,
        wv_rows,
        info_t,
        info,
        jnp.asarray(query_values)[:, None],
        jnp.asarray(key_values)[None, :],
        chips,
        scale,
    )
    mixed, mixed_b, lse = attend(meta, doc_line, q_ext, k_ext, v_t, heads, block)
    own, w_own, mixed_b = lax.optimization_barrier((own, w_own, mixed_b))
    back = [mixed_b[0]] + [chip_shift(mixed_b[step], -step) for step in range(1, chips)]

    own_normed = jnp.concatenate(own, axis=0)
    k_t, v_ext = project_back(place, own + sibling, wk_rows, wv_wide)
    normed_p = sent(nt_dot(perm, own_normed))
    weights_p = sent(nn_dot(perm, w_own))
    back, k_t, v_ext, normed_p, weights_p = lax.optimization_barrier(
        (back, k_t, v_ext, normed_p, weights_p)
    )

    outs = middle(
        place,
        back,
        tokens,
        cotangent,
        w_out,
        w_up,
        w_down,
        perm,
        (gain_inner, gain_feed, gain_hidden),
        hidden // parts,
    )
    result, grad_middle = outs[:2]
    go = outs[2 : 2 + chips]
    keep_a, send_a, keep_b, send_b, dinner, dfeed, dhidden = outs[2 + chips :]

    def gridded(array):
        return array.reshape((2, 2, chips) + array.shape[1:])

    keep_a, other_a = gridded(keep_a), gridded(seq_swap(send_a, 1))
    keep_b, other_b = gridded(keep_b), gridded(seq_swap(send_b, 1))
    out_a, out_b = outgoing(place, keep_a, other_a), outgoing(place, keep_b, other_b)
    go = [go[0]] + [chip_shift(go[step], step) for step in range(1, chips)]
    go, out_a, out_b = lax.optimization_barrier((go, out_a, out_b))
    in_a = [row_swap(out_a[0], 1), row_swap(out_a[1], 2)]
    dq, pair, other = attend_back(
        meta, doc_line, q_ext, jnp.concatenate(go, axis=1), mixed, lse, k_ext, k_t, v_ext, heads, block, scale
    )
    dq, pair, other, in_a, out_b = lax.optimization_barrier((dq, pair, other, in_a, out_b))
    in_b = [row_swap(out_b[0], 1), row_swap(out_b[1], 2)]
    grads = join_parts(place, dq, pair, seq_swap(other, 1), chips)
    home = [grads[0]] + [chip_shift(grads[step], -step) for step in range(1, chips)]
    grads, keep_a, other_a, keep_b, other_b = lax.optimization_barrier(
        (grads, keep_a, other_a, keep_b, other_b)
    )
    kept_a = outgoing(place, keep_a, other_a, True)
    kept_b = outgoing(place, keep_b, other_b, True)
    in_a, in_b, kept_a, kept_b, home[1] = lax.optimization_barrier(
        (in_a, in_b, kept_a, kept_b, home[1])
    )
    sums = halfway(place, [(*kept_a, *in_a), (*kept_b, *in_b)])
    sums, grads = lax.optimization_barrier((sums, grads))
    low_keep, low_send, high_keep, high_send = sums
    low_in, high_in = row_swap(low_send, 2), row_swap(high_send, 1)
    grads_t = jnp.concatenate(grads, axis=1)
    own_grad = nt_dot(normed_p, grads_t)
    dattend = jnp.sum(own_grad * wide(weights_p), axis=1).reshape(2, parts // 2, 1, per)
    dattend = jnp.where(core == 0, dattend, dattend[::-1])
    dattend = jnp.concatenate([dattend[0], dattend[1]], axis=1).reshape(1, model_width)
    dattend = dattend / gain_first
    gains_all = jnp.concatenate([dattend, dinner, dfeed, dhidden], axis=1)

    gains_share = gains_all.shape[1] // parts
    gains_rows = -(-gains_share // 128)
    gains_all = gains_all.reshape(parts // 2, 2, gains_share)
    gains_all = jnp.where(core == 0, gains_all, gains_all[:, ::-1]).transpose(1, 0, 2)
    gains_all = jnp.pad(gains_all, ((0, 0), (0, 0), (0, gains_rows * 128 - gains_share)))
    gains_all = jnp.pad(
        gains_all.reshape(parts, gains_rows, 128), ((0, 0), (0, per - gains_rows), (0, 0))
    ).reshape(model_width, 128)
    gap = jnp.zeros((model_width, model_width - 128 - 3 * share), jnp.float32)
    packed = sent(jnp.concatenate([own_grad, gap, gains_all], axis=1))
    half = model_width // 2
    mine_grad = packed[:half].reshape(parts // 2, per, model_width)
    send_grad = packed[half:].reshape(parts // 2, per, model_width)
    home, low_in, high_in, mine_grad, send_grad = lax.optimization_barrier(
        (home, low_in, high_in, mine_grad, send_grad)
    )
    stage = split(place, [(low_keep, low_in, high_keep, high_in)], chips)
    arrived = [stage[0]] + [chip_shift(stage[step], step) for step in range(1, chips)]
    grad_input = final(
        place, home, tokens, grad_middle, w_query, w_key, w_value, gain_first
    )
    mine_grad, other_grad = gridded(mine_grad), gridded(seq_swap(send_grad, 1))
    low, high = outgoing(place, mine_grad, other_grad)
    low_keep, low_send, high_keep, high_send = halfway(
        place,
        [(*outgoing(place, mine_grad, other_grad, True), row_swap(low, 1), row_swap(high, 2))],
    )
    stage = split(
        place, [(low_keep, row_swap(low_send, 2), high_keep, row_swap(high_send, 1))], chips
    )
    arrived += [stage[0]] + [chip_shift(stage[step], step) for step in range(1, chips)]
    down, up, out, query, key, value, gains_part = finish(
        place, arrived, hidden, parts, per, share, factor
    )
    return (
        result,
        grad_input,
        query.reshape(-1),
        key.reshape(-1),
        value.reshape(-1),
        out.reshape(-1),
        up.reshape(-1),
        down.reshape(-1),
        gains_part.reshape(-1)[:gains_share],
    )


def local(*arrays):
    seq_devices, row_devices = lax.axis_size("seq"), lax.axis_size("row")
    block = arrays[0].shape[0]
    one_segment = block * seq_devices <= SEGMENT and block % 2 ** (PATTERNS - 1) == 0
    if one_segment and seq_devices in (2, 4, 8) and row_devices == 4:
        return fast_local(*arrays)
    return ring_local(*arrays)


def solution(mesh):
    return jax.shard_map(
        local,
        mesh=mesh,
        in_specs=(
            P(("row", "seq"), None),
            P("row", None),
            P(),
            P(),
            P(),
            P(),
            P(),
            P(),
            P(),
            P(),
            P(),
            P(),
            P(("row", "seq"), None),
        ),
        out_specs=(
            P(("row", "seq"), None),
            P(("row", "seq"), None),
            P(("row", "seq")),
            P(("row", "seq")),
            P(("row", "seq")),
            P(("row", "seq")),
            P(("row", "seq")),
            P(("row", "seq")),
            P(("row", "seq")),
        ),
        check_vma=False,
    )
```

```python
from functools import partial
from functools import reduce
import math

import jax
import jax.numpy as jnp
import numpy as np
from jax import lax
from jax.experimental import pallas as pl
from jax.experimental.pallas import tpu as pltpu
from jax.sharding import PartitionSpec as P

HEADS = 12
SEGMENT = 2048
PATTERNS = 5


big_negative = -1e30


def shifted_2(shard, axis, by):
    length = lax.axis_size(axis)
    pairs = [(i, i + by) for i in range(length) if 0 <= i + by < length]
    return lax.ppermute(shard, axis, pairs)


def shifted_3(value, axis, steps):
    count = lax.axis_size(axis)
    pairs = [(source, (source + steps) % count) for source in range(count)]
    return lax.ppermute(value, axis, pairs)


def layer_norm(values, gain_vector):
    centre = jnp.mean(values, axis=-1, keepdims=True)
    shifted = values - centre
    variance = jnp.mean(shifted * shifted, axis=-1, keepdims=True)
    return shifted * lax.rsqrt(variance + 1e-05) * gain_vector


def hidden_norm(hidden_pre, gain_vector):
    return layer_norm(jax.nn.gelu(hidden_pre, approximate=True), gain_vector)


def selector(stride, head_count):
    return jnp.arange(stride)[:, None] == (jnp.arange(head_count) % stride)[None, :]


def compact(full_array, stride):
    length_in, head_count, inner_size = full_array.shape
    shaped = full_array.reshape(length_in // stride, stride, head_count, inner_size)
    picked = jnp.where(
        selector(stride, head_count)[None, :, :, None], shaped, jnp.zeros((), full_array.dtype)
    )
    return jnp.sum(picked, axis=1)


def expand(part_array, stride, fill_value):
    part_rows, head_count, inner_size = part_array.shape
    widened = jnp.where(
        selector(stride, head_count)[None, :, :, None],
        part_array[:, None],
        jnp.asarray(fill_value, part_array.dtype),
    )
    return widened.reshape(part_rows * stride, head_count, inner_size)


def positions(start_pos, part_rows, stride, head_count):
    row_ids = jnp.arange(part_rows, dtype=jnp.int32)[:, None] * stride
    head_ids = (jnp.arange(head_count, dtype=jnp.int32) % stride)[None, :]
    return start_pos + row_ids + head_ids


def doc_index(places, doc_bounds):
    return jnp.sum((places[..., None] >= doc_bounds).astype(jnp.int32), axis=-1)


def block_mask(doc_query, doc_key, local_block):
    allowed = doc_query.T[:, :, None] == doc_key.T[:, None, :]
    if local_block:
        rank_ids = jnp.arange(doc_query.shape[0])
        allowed = allowed & (rank_ids[:, None] >= rank_ids[None, :])[None]
    return allowed


def forward_block(query_part, key_part, value_part, allowed, score_scale):
    scores = (
        jnp.einsum("qhd,khd->hqk", query_part, key_part, preferred_element_type=jnp.float32)
        * score_scale
    )
    scores = jnp.where(allowed, scores, big_negative)
    row_peak = jnp.max(scores, axis=-1)
    weights = jnp.where(allowed, jnp.exp(scores - row_peak[..., None]), 0.0)
    row_total = jnp.sum(weights, axis=-1)
    mixed = jnp.einsum(
        "hqk,khd->qhd", weights.astype(jnp.bfloat16), value_part, preferred_element_type=jnp.float32
    )
    return (row_peak.T, row_total.T, mixed)


def merge(carried, new_block):
    best_peak = jnp.maximum(carried[0], new_block[0])
    keep_factor = jnp.exp(carried[0] - best_peak)
    take_factor = jnp.exp(new_block[0] - best_peak)
    new_total = carried[1] * keep_factor + new_block[1] * take_factor
    new_mixed = carried[2] * keep_factor[..., None] + new_block[2] * take_factor[..., None]
    return (best_peak, new_total, new_mixed)


def backward_block(
    query_part, grad_part, lse_part, delta_part, key_part, value_part, allowed, score_scale
):
    scores = (
        jnp.einsum("qhd,khd->hqk", query_part, key_part, preferred_element_type=jnp.float32)
        * score_scale
    )
    probs = jnp.where(allowed, jnp.exp(scores - lse_part.T[:, :, None]), 0.0)
    dots = jnp.einsum("qhd,khd->hqk", grad_part, value_part, preferred_element_type=jnp.float32)
    grad_scores = (probs * (dots - delta_part.T[:, :, None])).astype(jnp.bfloat16)
    query_grad = (
        jnp.einsum("hqk,khd->qhd", grad_scores, key_part, preferred_element_type=jnp.float32)
        * score_scale
    )
    key_grad = (
        jnp.einsum("hqk,qhd->khd", grad_scores, query_part, preferred_element_type=jnp.float32)
        * score_scale
    )
    value_grad = jnp.einsum(
        "hqk,qhd->khd", probs.astype(jnp.bfloat16), grad_part, preferred_element_type=jnp.float32
    )
    return (query_grad, key_grad, value_grad)


def keep_state(carried):
    return carried


def ring_local(
    tokens,
    lengths,
    w_query,
    w_key,
    w_value,
    w_out,
    w_up,
    w_down,
    gain_attend,
    gain_inner,
    gain_feed,
    gain_hidden,
    cotangent,
):
    block_rows, model_width = tokens.shape
    head_count = HEADS
    head_size = model_width // head_count
    score_scale = head_size ** (-0.5)
    seq_devices = lax.axis_size("seq")
    all_devices = seq_devices * lax.axis_size("row")
    my_index = lax.axis_index("seq")
    seq_total = block_rows * seq_devices
    doc_bounds = jnp.cumsum(lengths[0])[:-1]
    patterns = [
        (2**pattern, min(SEGMENT * 2**pattern, seq_total) // block_rows)
        for pattern in range(PATTERNS)
    ]
    near_ids = [0, 1]
    far_ids = list(range(2, PATTERNS))
    reach = patterns[1][1]
    far_rows = [block_rows // patterns[pattern][0] for pattern in far_ids]
    far_starts = [sum(far_rows[:slot_id]) for slot_id in range(len(far_ids))]
    far_total = sum(far_rows)

    def key_docs(pattern, source):
        stride = patterns[pattern][0]
        return doc_index(
            positions(source * block_rows, block_rows // stride, stride, head_count), doc_bounds
        )

    def is_live(pattern, cycle_step):
        group_size = patterns[pattern][1]
        return (cycle_step < group_size) & (my_index % group_size >= cycle_step)

    source_x = tokens.astype(jnp.float32)
    normed, attend_back = jax.vjp(layer_norm, source_x, gain_attend)
    normed_b = normed.astype(jnp.bfloat16)
    query_b = jnp.dot(normed_b, w_query, preferred_element_type=jnp.float32).astype(jnp.bfloat16)
    key_b = jnp.dot(normed_b, w_key, preferred_element_type=jnp.float32).astype(jnp.bfloat16)
    value_b = jnp.dot(normed_b, w_value, preferred_element_type=jnp.float32).astype(jnp.bfloat16)
    query_heads = query_b.reshape(block_rows, head_count, head_size)
    key_heads = key_b.reshape(block_rows, head_count, head_size)
    value_heads = value_b.reshape(block_rows, head_count, head_size)
    query_parts = [compact(query_heads, stride) for stride, group_size in patterns]
    key_parts = [compact(key_heads, stride) for stride, group_size in patterns]
    value_parts = [compact(value_heads, stride) for stride, group_size in patterns]
    own_docs = [key_docs(pattern, my_index) for pattern in range(PATTERNS)]
    states = [
        forward_block(
            query_parts[pattern],
            key_parts[pattern],
            value_parts[pattern],
            block_mask(own_docs[pattern], own_docs[pattern], True),
            score_scale,
        )
        for pattern in range(PATTERNS)
    ]

    def unpack_near(key_block):
        key_full = key_block[:, :model_width].reshape(block_rows, head_count, head_size)
        value_full = key_block[:, model_width:].reshape(block_rows, head_count, head_size)
        return (key_full, value_full)

    def near_fold_parts(pattern, key_part, value_part, source, carried):
        new_block = forward_block(
            query_parts[pattern],
            key_part,
            value_part,
            block_mask(own_docs[pattern], key_docs(pattern, source), False),
            score_scale,
        )
        return merge(carried, new_block)

    def near_fold(pattern, key_full, value_full, source, carried):
        stride = patterns[pattern][0]
        return near_fold_parts(
            pattern, compact(key_full, stride), compact(value_full, stride), source, carried
        )

    pair_block = jnp.concatenate([key_b, value_b], axis=1)
    kept_blocks = jnp.zeros((max(reach - 1, 1), block_rows, 2 * model_width), jnp.bfloat16)

    def near_forward(cycle_step, loop_state):
        key_block, near_now, kept_store = loop_state
        key_block = shifted_2(key_block, "seq", 1)
        key_full, value_full = unpack_near(key_block)
        new_states = []
        for pattern in near_ids:
            new_states.append(
                lax.cond(
                    is_live(pattern, cycle_step),
                    partial(near_fold, pattern, key_full, value_full, my_index - cycle_step),
                    keep_state,
                    near_now[pattern],
                )
            )
        return (key_block, tuple(new_states), kept_store)

    _, near_states, kept_blocks = lax.fori_loop(
        1, reach, near_forward, (pair_block, (states[0], states[1]), kept_blocks)
    )
    far_block = jnp.concatenate(
        [
            jnp.concatenate(
                [
                    key_parts[pattern].reshape(rows_here, model_width),
                    value_parts[pattern].reshape(rows_here, model_width),
                ],
                axis=1,
            )
            for pattern, rows_here in zip(far_ids, far_rows)
        ],
        axis=0,
    )

    def unpack_far(key_block, slot_id):
        rows_here = far_rows[slot_id]
        row_begin = far_starts[slot_id]
        piece_rows = key_block[row_begin : row_begin + rows_here]
        key_part = piece_rows[:, :model_width].reshape(rows_here, head_count, head_size)
        value_part = piece_rows[:, model_width:].reshape(rows_here, head_count, head_size)
        return (key_part, value_part)

    def far_fold(pattern, key_part, value_part, source, carried):
        new_block = forward_block(
            query_parts[pattern],
            key_part,
            value_part,
            block_mask(own_docs[pattern], key_docs(pattern, source), False),
            score_scale,
        )
        return merge(carried, new_block)

    def far_update(far_now, key_block, cycle_step):
        new_states = []
        for slot_id, pattern in enumerate(far_ids):
            key_part, value_part = unpack_far(key_block, slot_id)
            new_states.append(
                lax.cond(
                    is_live(pattern, cycle_step),
                    partial(far_fold, pattern, key_part, value_part, my_index - cycle_step),
                    keep_state,
                    far_now[slot_id],
                )
            )
        return tuple(new_states)

    far_states = tuple((states[pattern] for pattern in far_ids))

    def far_forward(cycle_step, loop_state):
        key_block, far_now = loop_state
        key_block = shifted_2(key_block, "seq", 1)
        return (key_block, far_update(far_now, key_block, cycle_step))

    _, far_states = lax.fori_loop(1, seq_devices, far_forward, (far_block, far_states))
    ordered = list(near_states) + list(far_states)
    peaks = [
        expand(ordered[pattern][0][..., None], patterns[pattern][0], big_negative)[..., 0]
        for pattern in range(PATTERNS)
    ]
    best_peak = reduce(jnp.maximum, peaks)
    weight_sum = jnp.zeros((block_rows, head_count), jnp.float32)
    mixed_sum = jnp.zeros((block_rows, head_count, head_size), jnp.float32)
    for pattern in range(PATTERNS):
        stride = patterns[pattern][0]
        factor = jnp.exp(peaks[pattern] - best_peak)
        weight_sum = (
            weight_sum + expand(ordered[pattern][1][..., None], stride, 0.0)[..., 0] * factor
        )
        mixed_sum = mixed_sum + expand(ordered[pattern][2], stride, 0.0) * factor[..., None]
    attended = mixed_sum / weight_sum[..., None]
    log_total = best_peak + jnp.log(weight_sum)
    inner_out, inner_back = jax.vjp(
        layer_norm, attended.reshape(block_rows, model_width), gain_inner
    )
    inner_b = inner_out.astype(jnp.bfloat16)
    middle = source_x + jnp.dot(inner_b, w_out, preferred_element_type=jnp.float32)
    normed_two, feed_back = jax.vjp(layer_norm, middle, gain_feed)
    normed_two_b = normed_two.astype(jnp.bfloat16)
    hidden_pre = jnp.dot(normed_two_b, w_up, preferred_element_type=jnp.float32)
    hidden, hidden_back = jax.vjp(hidden_norm, hidden_pre, gain_hidden)
    hidden_b = hidden.astype(jnp.bfloat16)
    result = (middle + jnp.dot(hidden_b, w_down, preferred_element_type=jnp.float32)).astype(
        jnp.bfloat16
    )
    grad_down = jnp.einsum("tf,tg->fg", hidden_b, cotangent, preferred_element_type=jnp.float32)
    grad_hidden = jnp.einsum("tg,fg->tf", cotangent, w_down, preferred_element_type=jnp.float32)
    grad_pre, grad_gain_hidden = hidden_back(grad_hidden)
    grad_pre_b = grad_pre.astype(jnp.bfloat16)
    grad_up = jnp.einsum("tf,tg->fg", normed_two_b, grad_pre_b, preferred_element_type=jnp.float32)
    grad_normed_two = jnp.einsum("tg,fg->tf", grad_pre_b, w_up, preferred_element_type=jnp.float32)
    grad_middle_part, grad_gain_feed = feed_back(grad_normed_two)
    grad_middle = cotangent.astype(jnp.float32) + grad_middle_part
    grad_middle_b = grad_middle.astype(jnp.bfloat16)
    grad_out = jnp.einsum("tf,tg->fg", inner_b, grad_middle_b, preferred_element_type=jnp.float32)
    grad_inner = jnp.einsum("tg,fg->tf", grad_middle_b, w_out, preferred_element_type=jnp.float32)
    grad_attended, grad_gain_inner = inner_back(grad_inner)
    grad_heads = grad_attended.astype(jnp.bfloat16).reshape(block_rows, head_count, head_size)
    delta_rows = jnp.sum(grad_heads.astype(jnp.float32) * attended, axis=-1)
    grad_parts = [compact(grad_heads, stride) for stride, group_size in patterns]
    lse_parts = [compact(log_total[..., None], stride)[..., 0] for stride, group_size in patterns]
    delta_parts = [
        compact(delta_rows[..., None], stride)[..., 0] for stride, group_size in patterns
    ]
    query_grads = []
    home_keys = []
    home_values = []
    for pattern in range(PATTERNS):
        part_query, part_key, part_value = backward_block(
            query_parts[pattern],
            grad_parts[pattern],
            lse_parts[pattern],
            delta_parts[pattern],
            key_parts[pattern],
            value_parts[pattern],
            block_mask(own_docs[pattern], own_docs[pattern], True),
            score_scale,
        )
        query_grads.append(part_query)
        home_keys.append(part_key)
        home_values.append(part_value)

    def fetch_full(key_block):
        return shifted_2(key_block, "seq", 1)

    def near_grad(pattern, key_full, value_full, source, operands):
        query_grad, travel = operands
        stride = patterns[pattern][0]
        part_query, part_key, part_value = backward_block(
            query_parts[pattern],
            grad_parts[pattern],
            lse_parts[pattern],
            delta_parts[pattern],
            compact(key_full, stride),
            compact(value_full, stride),
            block_mask(own_docs[pattern], key_docs(pattern, source), False),
            score_scale,
        )
        spread_rows = jnp.concatenate(
            [
                expand(part_key, stride, 0.0).reshape(block_rows, model_width),
                expand(part_value, stride, 0.0).reshape(block_rows, model_width),
            ],
            axis=1,
        )
        return (query_grad + part_query, travel + spread_rows)

    def near_backward(cycle_step, loop_state):
        key_block, grads_now, travel = loop_state
        key_block = fetch_full(key_block)
        travel = shifted_3(travel.astype(jnp.bfloat16), "seq", 1).astype(travel.dtype)
        key_full, value_full = unpack_near(key_block)
        new_grads = list(grads_now)
        for pattern in near_ids:
            new_grads[pattern], travel = lax.cond(
                is_live(pattern, cycle_step),
                partial(near_grad, pattern, key_full, value_full, my_index - cycle_step),
                keep_state,
                (new_grads[pattern], travel),
            )
        return (key_block, tuple(new_grads), travel)

    own_key_near = expand(home_keys[0], 1, 0.0) + expand(home_keys[1], 2, 0.0)
    own_value_near = expand(home_values[0], 1, 0.0) + expand(home_values[1], 2, 0.0)
    near_start = jnp.concatenate(
        [
            own_key_near.reshape(block_rows, model_width),
            own_value_near.reshape(block_rows, model_width),
        ],
        axis=1,
    )
    _, near_query, travel_near = lax.fori_loop(
        1, reach, near_backward, (pair_block, (query_grads[0], query_grads[1]), near_start)
    )
    near_home = shifted_3(travel_near.astype(jnp.bfloat16), "seq", 1 - reach).astype(
        travel_near.dtype
    )
    near_key_add = near_home[:, :model_width].reshape(block_rows, head_count, head_size)
    near_value_add = near_home[:, model_width:].reshape(block_rows, head_count, head_size)

    def far_grad(slot_id, key_part, value_part, source, operands):
        query_grad, travel = operands
        pattern = far_ids[slot_id]
        rows_here = far_rows[slot_id]
        row_begin = far_starts[slot_id]
        part_query, part_key, part_value = backward_block(
            query_parts[pattern],
            grad_parts[pattern],
            lse_parts[pattern],
            delta_parts[pattern],
            key_part,
            value_part,
            block_mask(own_docs[pattern], key_docs(pattern, source), False),
            score_scale,
        )
        spread_rows = jnp.concatenate(
            [part_key.reshape(rows_here, model_width), part_value.reshape(rows_here, model_width)],
            axis=1,
        )
        return (
            query_grad + part_query,
            travel.at[row_begin : row_begin + rows_here].add(spread_rows),
        )

    def far_back_update(grads_now, travel, key_block, cycle_step):
        new_grads = list(grads_now)
        for slot_id, pattern in enumerate(far_ids):
            key_part, value_part = unpack_far(key_block, slot_id)
            new_grads[slot_id], travel = lax.cond(
                is_live(pattern, cycle_step),
                partial(far_grad, slot_id, key_part, value_part, my_index - cycle_step),
                keep_state,
                (new_grads[slot_id], travel),
            )
        return (tuple(new_grads), travel)

    far_query = tuple((query_grads[pattern] for pattern in far_ids))
    far_empty = jnp.zeros((far_total, 2 * model_width), jnp.float32)

    def far_send(travel):
        return shifted_3(travel.astype(jnp.bfloat16), "seq", 1).astype(travel.dtype)

    def far_backward(cycle_step, loop_state):
        key_block, grads_now, travel = loop_state
        key_block = shifted_2(key_block, "seq", 1)
        travel = far_send(travel)
        grads_now, travel = far_back_update(grads_now, travel, key_block, cycle_step)
        return (key_block, grads_now, travel)

    _, far_query, travel_far = lax.fori_loop(
        1, seq_devices, far_backward, (far_block, far_query, far_empty)
    )
    far_home = far_send(travel_far)
    all_query = list(near_query) + list(far_query)
    query_grad = jnp.zeros((block_rows, head_count, head_size), jnp.float32)
    key_grad = near_key_add
    value_grad = near_value_add
    for pattern in range(PATTERNS):
        stride = patterns[pattern][0]
        query_grad = query_grad + expand(all_query[pattern], stride, 0.0)
    for pattern in far_ids:
        stride = patterns[pattern][0]
        key_grad = key_grad + expand(home_keys[pattern], stride, 0.0)
        value_grad = value_grad + expand(home_values[pattern], stride, 0.0)
    for slot_id, pattern in enumerate(far_ids):
        stride = patterns[pattern][0]
        rows_here = far_rows[slot_id]
        row_begin = far_starts[slot_id]
        piece_rows = far_home[row_begin : row_begin + rows_here]
        key_grad = key_grad + expand(
            piece_rows[:, :model_width].reshape(rows_here, head_count, head_size), stride, 0.0
        )
        value_grad = value_grad + expand(
            piece_rows[:, model_width:].reshape(rows_here, head_count, head_size), stride, 0.0
        )
    grad_query_b = query_grad.reshape(block_rows, model_width).astype(jnp.bfloat16)
    grad_key_b = key_grad.reshape(block_rows, model_width).astype(jnp.bfloat16)
    grad_value_b = value_grad.reshape(block_rows, model_width).astype(jnp.bfloat16)
    grad_w_query = jnp.einsum(
        "tf,tg->fg", normed_b, grad_query_b, preferred_element_type=jnp.float32
    )
    grad_w_key = jnp.einsum("tf,tg->fg", normed_b, grad_key_b, preferred_element_type=jnp.float32)
    grad_w_value = jnp.einsum(
        "tf,tg->fg", normed_b, grad_value_b, preferred_element_type=jnp.float32
    )
    grad_normed = jnp.einsum("tg,fg->tf", grad_query_b, w_query, preferred_element_type=jnp.float32)
    grad_normed = grad_normed + jnp.einsum(
        "tg,fg->tf", grad_key_b, w_key, preferred_element_type=jnp.float32
    )
    grad_normed = grad_normed + jnp.einsum(
        "tg,fg->tf", grad_value_b, w_value, preferred_element_type=jnp.float32
    )
    grad_x_part, grad_gain_attend = attend_back(grad_normed)
    grad_input = (grad_middle + grad_x_part).astype(jnp.bfloat16)
    gains_all = jnp.concatenate(
        [grad_gain_attend, grad_gain_inner, grad_gain_feed, grad_gain_hidden]
    )
    summed = (
        lax.psum_scatter(grad_w_query.reshape(-1), ("row", "seq"), scatter_dimension=0, tiled=True),
        lax.psum_scatter(grad_w_key.reshape(-1), ("row", "seq"), scatter_dimension=0, tiled=True),
        lax.psum_scatter(grad_w_value.reshape(-1), ("row", "seq"), scatter_dimension=0, tiled=True),
        lax.psum_scatter(grad_out.reshape(-1), ("row", "seq"), scatter_dimension=0, tiled=True),
        lax.psum_scatter(grad_up.reshape(-1), ("row", "seq"), scatter_dimension=0, tiled=True),
        lax.psum_scatter(grad_down.reshape(-1), ("row", "seq"), scatter_dimension=0, tiled=True),
        lax.psum_scatter(gains_all, ("row", "seq"), scatter_dimension=0, tiled=True),
    )
    factor = 1.0 / math.sqrt(block_rows * all_devices)
    return (result, grad_input) + tuple((summed_part * factor for summed_part in summed))


NO_COST = pl.CostEstimate(flops=1000, bytes_accessed=1000, transcendentals=0)


def split_log(level):
    remaining = math.log((level + 1) / level)
    pieces = []
    for _ in range(3):
        piece = float(jnp.bfloat16.dtype.type(remaining))
        pieces.append(piece)
        remaining -= piece
    return pieces


def extra_values(places, features, head, size, per_piece):
    masks, values = jnp.zeros_like(features), jnp.zeros(features.shape, jnp.float32)
    for level in range(1, PATTERNS):
        for piece, value in enumerate(split_log(level)):
            here = features == size + 3 * (level - 1) + piece
            masks = jnp.where(here, 2**level - 1, masks)
            values = jnp.where(here, value if per_piece else 1.0, values)
    return jnp.where(((places - head) & masks) == 0, values, 0.0)


def nt_dot(left, right):
    return lax.dot_general(
        left, right, (((1,), (1,)), ((), ())), preferred_element_type=jnp.float32
    )


def nn_dot(left, right):
    return jnp.dot(left, right, preferred_element_type=jnp.float32)


def call_whole(kernel, out_shape, name, scalars, *arrays, in_specs=None, scratch=(), limit=12):
    return pl.pallas_call(
        kernel,
        grid_spec=pltpu.PrefetchScalarGridSpec(
            num_scalar_prefetch=1,
            grid=(1,),
            in_specs=in_specs or [whole(array.shape) for array in arrays],
            out_specs=[whole(out.shape) for out in out_shape],
            scratch_shapes=list(scratch),
        ),
        out_shape=list(out_shape),
        compiler_params=pltpu.CompilerParams(vmem_limit_bytes=limit << 20),
        cost_estimate=NO_COST,
        name=name,
    )(scalars, *arrays)


def norm_kernel(unused, rows_ref, gain_ref, out_ref):
    out_ref[...] = (norm_parts(rows_ref[...].astype(jnp.float32))[0] * gain_ref[...]).astype(
        jnp.bfloat16
    )


def project_kernel(blocks, own, heads, scale, meta, *refs):
    normed = refs[:blocks]
    wq_ref, wk_ref, wv_ref, q_ref, k_ref, vt_ref = refs[blocks:]
    length = normed[0].shape[0]
    lanes = wk_ref.shape[1] // heads
    size = lanes // 2
    first_head = meta[blocks]
    for index in range(blocks):
        rows = normed[index][...]
        start = meta[index]
        span = slice(index * length, (index + 1) * length)
        keys = nn_dot(rows, wk_ref[...])
        vt_ref[:, span] = nt_dot(wv_ref[...], rows).astype(jnp.bfloat16)
        places = start + lax.broadcasted_iota(jnp.int32, (length, 1), 0)
        features = lax.broadcasted_iota(jnp.int32, (1, lanes), 1)
        for head in range(heads):
            wide_rows = slice(head * lanes, (head + 1) * lanes)
            extra = extra_values(places, features, first_head + head, size, False)
            k_ref[span, wide_rows] = (keys[:, wide_rows] + extra).astype(jnp.bfloat16)
        if index < own:
            queries = nt_dot(wq_ref[...], rows).astype(jnp.bfloat16).astype(jnp.float32) * scale
            places = start + lax.broadcasted_iota(jnp.int32, (1, length), 1)
            features = lax.broadcasted_iota(jnp.int32, (lanes, 1), 0)
            for head in range(heads):
                wide_rows = slice(head * lanes, (head + 1) * lanes)
                extra = extra_values(places, features, first_head + head, size, True)
                q_ref[wide_rows, span] = (queries[wide_rows] + extra).astype(jnp.bfloat16)


def project(meta, normed, wq, wk, wv, own, heads, scale):
    blocks, length = len(normed), normed[0].shape[0]
    wide, share = wk.shape[1], wv.shape[0]
    return call_whole(
        partial(project_kernel, blocks, own, heads, scale),
        [
            jax.ShapeDtypeStruct((wide, own * length), jnp.bfloat16),
            jax.ShapeDtypeStruct((blocks * length, wide), jnp.bfloat16),
            jax.ShapeDtypeStruct((share, blocks * length), jnp.bfloat16),
        ],
        "project",
        meta,
        *normed,
        wq,
        wk,
        wv,
        limit=20,
    )


def project_back_kernel(blocks, unused, *refs):
    normed = refs[:blocks]
    wk_ref, wv_ref, kt_ref, v_ref = refs[blocks:]
    length = normed[0].shape[0]
    for index in range(blocks):
        rows = normed[index][...]
        span = slice(index * length, (index + 1) * length)
        kt_ref[:, span] = nt_dot(wk_ref[...], rows).astype(jnp.bfloat16)
        v_ref[span, :] = nn_dot(rows, wv_ref[...]).astype(jnp.bfloat16)


def project_back(scalars, normed, wk, wv):
    blocks, length = len(normed), normed[0].shape[0]
    return call_whole(
        partial(project_back_kernel, blocks),
        [
            jax.ShapeDtypeStruct((wk.shape[0], blocks * length), jnp.bfloat16),
            jax.ShapeDtypeStruct((blocks * length, wv.shape[1]), jnp.bfloat16),
        ],
        "project_back",
        scalars,
        *normed,
        wk,
        wv,
    )


def pair_mask(query_start, key_start, doc_line, block):
    query_place = query_start + lax.broadcasted_iota(jnp.int32, (1, block), 1)
    key_place = key_start + lax.broadcasted_iota(jnp.int32, (block, 1), 0)
    return (key_place <= query_place) & (key_place >= doc_line)


def attend_kernel(
    heads, block, key_blocks, meta, doc_ref, q_ref, k_ref, vt_ref, o_ref, ob_ref, lse_ref, m_ref, l_ref
):
    step = pl.program_id(0)
    steps = pl.num_programs(0)
    query_start = meta[step]
    doc_first, doc_last = meta[steps + key_blocks + step], meta[2 * steps + key_blocks + step]
    doc_line = doc_ref[...]
    size = o_ref.shape[0] // heads
    lanes = q_ref.shape[0] // heads
    m_ref[...] = jnp.full_like(m_ref, big_negative)
    l_ref[...] = jnp.zeros_like(l_ref)
    o_ref[...] = jnp.zeros_like(o_ref)

    def fold(slot, allowed):
        span = pl.ds(pl.multiple_of(slot * block, block), block)
        scores = [
            nn_dot(
                k_ref[span, head * lanes : (head + 1) * lanes],
                q_ref[head * lanes : (head + 1) * lanes, :],
            )
            for head in range(heads)
        ]
        if allowed is not None:
            scores = [jnp.where(allowed, part, big_negative) for part in scores]
        for head in range(heads):
            rows = slice(head * size, (head + 1) * size)
            old_peak = m_ref[head]
            new_peak = jnp.maximum(old_peak, jnp.max(scores[head], axis=0, keepdims=True))
            weights = jnp.exp(scores[head] - new_peak)
            fade = jnp.exp(old_peak - new_peak)
            m_ref[head] = new_peak
            l_ref[head] = l_ref[head] * fade + jnp.sum(weights, axis=0, keepdims=True)
            o_ref[rows, :] = o_ref[rows, :] * fade + nn_dot(
                vt_ref[rows, span], weights.astype(jnp.bfloat16)
            )

    def body(slot, carry):
        key_start = meta[steps + slot]
        live = (key_start <= query_start) & (key_start + block > doc_first)
        full = (key_start < query_start) & (key_start >= doc_last)

        @pl.when(full)
        def _():
            fold(slot, None)

        @pl.when(live & jnp.logical_not(full))
        def _():
            fold(slot, pair_mask(query_start, key_start, doc_line, block))

        return carry

    lax.fori_loop(0, key_blocks, body, 0)
    for head in range(heads):
        rows = slice(head * size, (head + 1) * size)
        total = l_ref[head]
        mixed = o_ref[rows, :] / total
        o_ref[rows, :] = mixed
        ob_ref[0, rows, :] = mixed.astype(jnp.bfloat16)
        lse_ref[head] = m_ref[head] + jnp.log(total)


def attend_back_kernel(
    heads,
    block,
    key_blocks,
    scale,
    meta,
    doc_ref,
    q_ref,
    g_ref,
    o_ref,
    lse_ref,
    k_ref,
    kt_ref,
    v_ref,
    dq_ref,
    mine_ref,
    other_ref,
    acc_ref,
    pair_ref,
    delta_ref,
):
    step = pl.program_id(0)
    steps = pl.num_programs(0)
    query_start = meta[step]
    doc_first, doc_last = meta[steps + key_blocks + step], meta[2 * steps + key_blocks + step]
    doc_line = doc_ref[...]
    size = g_ref.shape[0] // heads
    lanes = q_ref.shape[0] // heads
    share = g_ref.shape[0]

    @pl.when(step == 0)
    def _():
        pair_ref[...] = jnp.zeros_like(pair_ref)

    acc_ref[...] = jnp.zeros_like(acc_ref)
    for head in range(heads):
        rows = slice(head * size, (head + 1) * size)
        delta_ref[head] = jnp.sum(
            g_ref[rows, :].astype(jnp.float32) * o_ref[rows, :], axis=0, keepdims=True
        )

    def fold(slot, allowed):
        span = pl.ds(pl.multiple_of(slot * block, block), block)
        probs, grad_scores = [], []
        for head in range(heads):
            wide_rows = slice(head * lanes, (head + 1) * lanes)
            rows = slice(head * size, (head + 1) * size)
            probs.append(nn_dot(k_ref[span, wide_rows], q_ref[wide_rows, :]))
            grad_scores.append(
                nn_dot(v_ref[span, head * lanes : head * lanes + size], g_ref[rows, :])
            )
        for head in range(heads):
            part = jnp.exp(probs[head] - lse_ref[head])
            if allowed is not None:
                part = jnp.where(allowed, part, 0.0)
            grad_scores[head] = (part * (grad_scores[head] - delta_ref[head])).astype(jnp.bfloat16)
            probs[head] = part.astype(jnp.bfloat16)
        for head in range(heads):
            rows = slice(head * size, (head + 1) * size)
            value_rows = slice(share + head * size, share + (head + 1) * size)
            query_rows = slice(head * lanes, head * lanes + size)
            pair_ref[value_rows, span] += nt_dot(g_ref[rows, :], probs[head])
            pair_ref[rows, span] += nt_dot(q_ref[query_rows, :], grad_scores[head])
            acc_ref[rows, :] += nn_dot(kt_ref[rows, span], grad_scores[head])

    def body(slot, carry):
        key_start = meta[steps + slot]
        live = (key_start <= query_start) & (key_start + block > doc_first)
        full = (key_start < query_start) & (key_start >= doc_last)

        @pl.when(full)
        def _():
            fold(slot, None)

        @pl.when(live & jnp.logical_not(full))
        def _():
            fold(slot, pair_mask(query_start, key_start, doc_line, block))

        return carry

    lax.fori_loop(0, key_blocks, body, 0)
    dq_ref[...] = (acc_ref[...] * scale).astype(dq_ref.dtype)

    @pl.when(step == steps - 1)
    def _():
        half = mine_ref.shape[1]
        mine_ref[...] = pair_ref[:, :half]
        other_ref[...] = pair_ref[:, half:].astype(jnp.bfloat16)


def whole(shape):
    return pl.BlockSpec(shape, lambda *index: (0,) * len(shape))


def attend(meta, doc_line, q_ext, k_ext, v_t, heads, block):
    wide, queries = q_ext.shape
    share, keys = v_t.shape
    steps, key_blocks = queries // block, keys // block
    return pl.pallas_call(
        partial(attend_kernel, heads, block, key_blocks),
        grid_spec=pltpu.PrefetchScalarGridSpec(
            num_scalar_prefetch=1,
            grid=(steps,),
            in_specs=[
                pl.BlockSpec((1, block), lambda i, meta: (0, i)),
                pl.BlockSpec((wide, block), lambda i, meta: (0, i)),
                whole(k_ext.shape),
                whole(v_t.shape),
            ],
            out_specs=[
                pl.BlockSpec((share, block), lambda i, meta: (0, i)),
                pl.BlockSpec((1, share, block), lambda i, meta: (i, 0, 0)),
                pl.BlockSpec((heads, 1, block), lambda i, meta: (0, 0, i)),
            ],
            scratch_shapes=[
                pltpu.VMEM((heads, 1, block), jnp.float32),
                pltpu.VMEM((heads, 1, block), jnp.float32),
            ],
        ),
        out_shape=[
            jax.ShapeDtypeStruct((share, queries), jnp.float32),
            jax.ShapeDtypeStruct((steps, share, block), jnp.bfloat16),
            jax.ShapeDtypeStruct((heads, 1, queries), jnp.float32),
        ],
        compiler_params=pltpu.CompilerParams(vmem_limit_bytes=12 << 20),
        cost_estimate=NO_COST,
        name="attend",
    )(meta, doc_line, q_ext, k_ext, v_t)


def attend_back(meta, doc_line, q_ext, grad_t, mixed, lse, k_ext, k_t, v_ext, heads, block, scale):
    wide, queries = q_ext.shape
    share, keys = k_t.shape
    steps, key_blocks = queries // block, keys // block
    return pl.pallas_call(
        partial(attend_back_kernel, heads, block, key_blocks, scale),
        grid_spec=pltpu.PrefetchScalarGridSpec(
            num_scalar_prefetch=1,
            grid=(steps,),
            in_specs=[
                pl.BlockSpec((1, block), lambda i, meta: (0, i)),
                pl.BlockSpec((wide, block), lambda i, meta: (0, i)),
                pl.BlockSpec((share, block), lambda i, meta: (0, i)),
                pl.BlockSpec((share, block), lambda i, meta: (0, i)),
                pl.BlockSpec((heads, 1, block), lambda i, meta: (0, 0, i)),
                whole(k_ext.shape),
                whole(k_t.shape),
                whole(v_ext.shape),
            ],
            out_specs=[
                pl.BlockSpec((share, block), lambda i, meta: (0, i)),
                whole((2 * share, keys // 2)),
                whole((2 * share, keys // 2)),
            ],
            scratch_shapes=[
                pltpu.VMEM((share, block), jnp.float32),
                pltpu.VMEM((2 * share, keys), jnp.float32),
                pltpu.VMEM((heads, 1, block), jnp.float32),
            ],
        ),
        out_shape=[
            jax.ShapeDtypeStruct((share, queries), jnp.bfloat16),
            jax.ShapeDtypeStruct((2 * share, keys // 2), jnp.float32),
            jax.ShapeDtypeStruct((2 * share, keys // 2), jnp.bfloat16),
        ],
        compiler_params=pltpu.CompilerParams(vmem_limit_bytes=20 << 20),
        cost_estimate=NO_COST,
        name="attend_back",
    )(meta, doc_line, q_ext, grad_t, mixed, lse, k_ext, k_t, v_ext)


def join_kernel(chips, unused, dq_ref, mine_ref, other_ref, *out_refs):
    share = dq_ref.shape[0]
    block = dq_ref.shape[1] // chips
    for step in range(chips):
        span = slice(step * block, (step + 1) * block)
        pair = (mine_ref[:, span] + other_ref[:, span].astype(jnp.float32)).astype(jnp.bfloat16)
        out_refs[step][:share, :] = dq_ref[:, span]
        out_refs[step][share:, :] = pair


def join_parts(scalars, dq, mine, other, chips):
    rows, block = dq.shape[0] + mine.shape[0], dq.shape[1] // chips
    return call_whole(
        partial(join_kernel, chips),
        [jax.ShapeDtypeStruct((rows, block), jnp.bfloat16)] * chips,
        "join",
        scalars,
        dq,
        mine,
        other,
    )


def head_grads_kernel(chips, per, unused, normed_ref, *refs):
    grads = refs[:chips]
    weights_ref, gain_ref, row_ref, lane_ref, late_ref, keep_ref, send_ref = refs[chips:]
    block = normed_ref.shape[1] // chips
    own = nt_dot(normed_ref[:, :block], grads[0][...])
    for step in range(1, chips):
        own = own + nt_dot(normed_ref[:, step * block : (step + 1) * block], grads[step][...])
    gains = jnp.sum(own * weights_ref[...].astype(jnp.float32), axis=1, keepdims=True)
    gains = (gains * gain_ref[...] * lane_ref[...]).astype(jnp.bfloat16)
    gains = nn_dot(row_ref[...], gains) + late_ref[...]
    chunks, _, width = keep_ref.shape
    columns = own.shape[1]
    for which, target in enumerate((keep_ref, send_ref)):
        for chunk in range(chunks):
            first = (which * chunks + chunk) * per
            rows = slice(first, first + per)
            target[chunk, :, :columns] = own[rows].astype(jnp.bfloat16)
            target[chunk, :, columns : width - 128] = jnp.zeros(
                (per, width - 128 - columns), jnp.bfloat16
            )
            target[chunk, :, width - 128 :] = gains[rows].astype(jnp.bfloat16)


def head_grads(scalars, normed_p, grads, weights_p, gain_rows, where_row, where_lane, late, per):
    width = normed_p.shape[0]
    out = jax.ShapeDtypeStruct((width // (2 * per), per, width), jnp.bfloat16)
    return call_whole(
        partial(head_grads_kernel, len(grads), per),
        [out, out],
        "head_grads",
        scalars,
        normed_p,
        *grads,
        weights_p,
        gain_rows,
        where_row,
        where_lane,
        late,
        limit=24,
    )


def norm_parts(values):
    shifted = values - jnp.mean(values, axis=-1, keepdims=True)
    rate = lax.rsqrt(jnp.mean(shifted * shifted, axis=-1, keepdims=True) + 1e-05)
    return shifted * rate, rate


def norm_back(grad, hat, rate, gain):
    scaled = grad * gain
    mean_scaled = jnp.mean(scaled, axis=-1, keepdims=True)
    mean_product = jnp.mean(scaled * hat, axis=-1, keepdims=True)
    return (
        rate * (scaled - mean_scaled - hat * mean_product),
        jnp.sum(grad * hat, axis=0, keepdims=True),
    )


def middle_kernel(chips, tiles, position, *refs):
    mixed = refs[:chips]
    tokens_ref, cot_ref, wout_ref, wup_ref, wdown_ref, ginner_ref, gfeed_ref, ghidden_ref = refs[
        chips : chips + 8
    ]
    result_ref, gmid_ref, gmid_b_ref = refs[chips + 8 : chips + 11]
    go_refs = refs[chips + 11 : 2 * chips + 11]
    (
        z_ref,
        h2_ref,
        bent_out,
        pre_out,
        dinner_ref,
        dfeed_ref,
        dhidden_ref,
        swap_ref,
        work_ref,
        column_ref,
        zhat_ref,
        hat_ref,
        act_ref,
        slope_ref,
        dact_ref,
        acc_ref,
        stat_ref,
    ) = refs[2 * chips + 11 :]
    step = pl.program_id(0)
    chip = position[0]
    block, model_width = tokens_ref.shape
    share = model_width // chips
    tile = wdown_ref.shape[0]
    hidden = tile * tiles
    root = math.sqrt(2.0 / math.pi)
    phase, index = step // tiles, step % tiles
    lanes = stat_ref.shape[2]
    groups = tile // lanes

    def by_rows(body):
        body(slice(None))

    def spread(stat):
        return jnp.concatenate([stat] * groups, axis=1)

    def gathered_lanes(values):
        total = values[:, :lanes]
        for group in range(1, groups):
            total = total + values[:, group * lanes : (group + 1) * lanes]
        return total

    def lane_sum(values):
        return jnp.broadcast_to(jnp.sum(values, axis=-1, keepdims=True), values.shape)

    def column_sums(values):
        total = values[:8]
        for first in range(8, values.shape[0], 8):
            total = total + values[first : first + 8]
        return total

    def norm_rows(values):
        shifted = values - spread(lane_sum(gathered_lanes(values)) / tile)
        rate = lax.rsqrt(lane_sum(gathered_lanes(shifted * shifted)) / tile + 1e-05)
        return shifted * spread(rate), rate

    def norm_rows_back(grad, hat, rate, gain):
        scaled = grad * gain
        mean_scaled = lane_sum(gathered_lanes(scaled)) / tile
        mean_product = lane_sum(gathered_lanes(scaled * hat)) / tile
        return spread(rate) * (scaled - spread(mean_scaled) - hat * spread(mean_product))

    @pl.when(step == 0)
    def _():
        for near in range(chips):
            start = pl.multiple_of(share * lax.rem(chip + near, chips), share)
            swap_ref[pl.ds(start, share), :] = mixed[near][...].astype(jnp.float32)
        work_ref[...] = swap_ref[...].T

        def first_norm(rows):
            zhat, zrate = norm_rows(work_ref[rows, :])
            zhat_ref[rows, :] = zhat
            stat_ref[0, rows, :] = zrate
            z_ref[rows, :] = (zhat * ginner_ref[...]).astype(jnp.bfloat16)

        by_rows(first_norm)
        work_ref[...] = nn_dot(z_ref[...], wout_ref[...])

        def second_norm(rows):
            mid = tokens_ref[rows, :].astype(jnp.float32) + work_ref[rows, :]
            acc_ref[rows, :] = mid
            hat, rate = norm_rows(mid)
            hat_ref[rows, :] = hat
            stat_ref[1, rows, :] = rate
            h2_ref[rows, :] = (hat * gfeed_ref[...]).astype(jnp.bfloat16)

        by_rows(second_norm)
        for stat in range(3, 7):
            stat_ref[stat] = jnp.zeros_like(stat_ref[stat])

    @pl.when(phase == 0)
    def _():
        work_ref[...] = nn_dot(h2_ref[...], wup_ref[...])

        def bend_rows(rows):
            u = work_ref[rows, :]
            squared = u * u
            bend = jnp.tanh(root * (u + 0.044715 * u * squared))
            act_ref[index, rows, :] = 0.5 * u * (1.0 + bend)
            slope_ref[index, rows, :] = 0.5 * (1.0 + bend) + 0.5 * u * (1.0 - bend * bend) * root * (
                1.0 + 3.0 * 0.044715 * squared
            )

        by_rows(bend_rows)

        @pl.when(index == 0)
        def _():
            def pivot(rows):
                stat_ref[2, rows, :] = lane_sum(gathered_lanes(act_ref[0, rows, :])) / tile

            by_rows(pivot)

        def sums(rows):
            off = act_ref[index, rows, :] - spread(stat_ref[2, rows, :])
            stat_ref[3, rows, :] += gathered_lanes(off)
            stat_ref[4, rows, :] += gathered_lanes(off * off)

        by_rows(sums)

    @pl.when(step == tiles)
    def _():
        drift = lane_sum(stat_ref[3]) / hidden
        stat_ref[2] = stat_ref[2] + drift
        stat_ref[4] = lax.rsqrt(
            jnp.maximum(lane_sum(stat_ref[4]) / hidden - drift * drift, 0.0) + 1e-05
        )

    @pl.when(phase == 1)
    def _():
        def hidden_rows(rows):
            hat = (act_ref[index, rows, :] - spread(stat_ref[2, rows, :])) * spread(
                stat_ref[4, rows, :]
            )
            act_ref[index, rows, :] = hat
            bent_out[rows, :] = (hat * ghidden_ref[...]).astype(jnp.bfloat16)

        by_rows(hidden_rows)
        work_ref[...] = nt_dot(cot_ref[...], wdown_ref[...])
        acc_ref[...] += nn_dot(bent_out[...], wdown_ref[...])
        column_ref[...] = jnp.zeros_like(column_ref)

        def grad_rows(rows):
            hat, grad = act_ref[index, rows, :], work_ref[rows, :]
            column_ref[...] += column_sums(grad * hat)
            scaled = grad * ghidden_ref[...]
            dact_ref[index, rows, :] = scaled
            stat_ref[5, rows, :] += gathered_lanes(scaled)
            stat_ref[6, rows, :] += gathered_lanes(scaled * hat)

        by_rows(grad_rows)
        dhidden_ref[...] = jnp.sum(column_ref[...], axis=0, keepdims=True)

    @pl.when(step == 2 * tiles)
    def _():
        result_ref[...] = acc_ref[...].astype(jnp.bfloat16)
        acc_ref[...] = jnp.zeros_like(acc_ref)
        stat_ref[5] = lane_sum(stat_ref[5]) / hidden
        stat_ref[6] = lane_sum(stat_ref[6]) / hidden

    @pl.when(phase == 2)
    def _():
        def pre_rows(rows):
            inner = (
                dact_ref[index, rows, :]
                - spread(stat_ref[5, rows, :])
                - act_ref[index, rows, :] * spread(stat_ref[6, rows, :])
            )
            pre_out[rows, :] = (
                spread(stat_ref[4, rows, :]) * inner * slope_ref[index, rows, :]
            ).astype(jnp.bfloat16)

        by_rows(pre_rows)
        acc_ref[...] += nt_dot(pre_out[...], wup_ref[...])

    @pl.when(step == 3 * tiles - 1)
    def _():
        column_ref[...] = jnp.zeros_like(column_ref)

        def middle_rows(rows):
            grad, hat = acc_ref[rows, :], hat_ref[rows, :]
            column_ref[...] += column_sums(grad * hat)
            gmid = cot_ref[rows, :].astype(jnp.float32) + norm_rows_back(
                grad, hat, stat_ref[1, rows, :], gfeed_ref[...]
            )
            gmid_ref[rows, :] = gmid
            gmid_b_ref[rows, :] = gmid.astype(jnp.bfloat16)

        by_rows(middle_rows)
        dfeed_ref[...] = jnp.sum(column_ref[...], axis=0, keepdims=True)
        work_ref[...] = nt_dot(gmid_b_ref[...], wout_ref[...])
        column_ref[...] = jnp.zeros_like(column_ref)

        def inner_rows(rows):
            grad, hat = work_ref[rows, :], zhat_ref[rows, :]
            column_ref[...] += column_sums(grad * hat)
            work_ref[rows, :] = norm_rows_back(grad, hat, stat_ref[0, rows, :], ginner_ref[...])

        by_rows(inner_rows)
        dinner_ref[...] = jnp.sum(column_ref[...], axis=0, keepdims=True)
        swap_ref[...] = work_ref[...].T
        for near in range(chips):
            start = pl.multiple_of(share * lax.rem(chip + near, chips), share)
            go_refs[near][...] = swap_ref[pl.ds(start, share), :].astype(jnp.bfloat16)


def middle(position, mixed, tokens, cotangent, w_out, w_up, w_down, gains):
    chips = len(mixed)
    block, model_width = tokens.shape
    hidden = w_up.shape[1]
    tile = model_width
    tiles = hidden // tile
    share = model_width // chips
    last = tiles - 1

    def up_index(i, pos):
        return (0, jnp.where(i < tiles, i, jnp.where(i < 2 * tiles, last, i - 2 * tiles)))

    def down_index(i, pos):
        return (jnp.clip(i - tiles, 0, last), 0)

    def hidden_index(i, pos):
        return (0, jnp.clip(i - tiles, 0, last))

    def pre_index(i, pos):
        return (0, jnp.clip(i - 2 * tiles, 0, last))

    def f32(*shape):
        return pltpu.VMEM(shape, jnp.float32)

    row, rows = (1, model_width), (block, model_width)
    narrow = jax.ShapeDtypeStruct(rows, jnp.bfloat16)
    return pl.pallas_call(
        partial(middle_kernel, chips, tiles),
        grid_spec=pltpu.PrefetchScalarGridSpec(
            num_scalar_prefetch=1,
            grid=(3 * tiles,),
            in_specs=[whole((share, block))] * chips
            + [
                whole(rows),
                whole(rows),
                whole((model_width, model_width)),
                pl.BlockSpec((model_width, tile), up_index),
                pl.BlockSpec((tile, model_width), down_index),
                whole(row),
                whole(row),
                pl.BlockSpec((1, tile), hidden_index),
            ],
            out_specs=[whole(rows)] * 3
            + [whole((share, block))] * chips
            + [
                whole(rows),
                whole(rows),
                pl.BlockSpec((block, tile), hidden_index),
                pl.BlockSpec((block, tile), pre_index),
                whole(row),
                whole(row),
                pl.BlockSpec((1, tile), hidden_index),
            ],
            scratch_shapes=[
                f32(model_width, block),
                f32(block, tile),
                f32(8, tile),
                f32(block, model_width),
                f32(block, model_width),
                f32(tiles, block, tile),
                f32(tiles, block, tile),
                f32(tiles, block, tile),
                f32(block, model_width),
                f32(7, block, 128),
            ],
        ),
        out_shape=[narrow, jax.ShapeDtypeStruct(rows, jnp.float32), narrow]
        + [jax.ShapeDtypeStruct((share, block), jnp.bfloat16)] * chips
        + [
            narrow,
            narrow,
            jax.ShapeDtypeStruct((block, hidden), jnp.bfloat16),
            jax.ShapeDtypeStruct((block, hidden), jnp.bfloat16),
            jax.ShapeDtypeStruct(row, jnp.float32),
            jax.ShapeDtypeStruct(row, jnp.float32),
            jax.ShapeDtypeStruct((1, hidden), jnp.float32),
        ],
        compiler_params=pltpu.CompilerParams(vmem_limit_bytes=36 << 20),
        cost_estimate=NO_COST,
        name="middle",
    )(position, *mixed, tokens, cotangent, w_out, w_up, w_down, *gains)


def down_kernel(per, position, bent_ref, cot_ref, keep_ref, send_ref):
    first_core = position[1] == 0
    grad = lax.dot_general(
        bent_ref[...], cot_ref[...], (((0,), (0,)), ((), ())), preferred_element_type=jnp.float32
    ).astype(jnp.bfloat16)
    for part in range(keep_ref.shape[0]):
        even = grad[2 * per * part : 2 * per * part + per]
        odd = grad[2 * per * part + per : 2 * per * (part + 1)]
        keep_ref[part] = jnp.where(first_core, even, odd)
        send_ref[part] = jnp.where(first_core, odd, even)


def down_grad(position, bent, cotangent, per):
    (block, hidden), model_width = bent.shape, cotangent.shape[1]
    tiles, chunks = hidden // model_width, hidden // (2 * per)
    out = jax.ShapeDtypeStruct((chunks, per, model_width), jnp.bfloat16)
    out_spec = pl.BlockSpec((chunks // tiles, per, model_width), lambda i, pos: (i, 0, 0))
    return pl.pallas_call(
        partial(down_kernel, per),
        grid_spec=pltpu.PrefetchScalarGridSpec(
            num_scalar_prefetch=1,
            grid=(tiles,),
            in_specs=[
                pl.BlockSpec((block, model_width), lambda i, pos: (0, i)),
                whole(cotangent.shape),
            ],
            out_specs=[out_spec, out_spec],
        ),
        out_shape=[out, out],
        compiler_params=pltpu.CompilerParams(vmem_limit_bytes=20 << 20),
        cost_estimate=NO_COST,
        name="down_grad",
    )(position, bent, cotangent)


def up_out_kernel(tiles, position, h2_ref, pre_ref, z_ref, gmid_ref, perm_ref, keep_ref, send_ref, left_ref):
    step = pl.program_id(0)
    chunks, per = keep_ref.shape[:2]

    @pl.when(step == 0)
    def _():
        left_ref[...] = nt_dot(perm_ref[...], h2_ref[...]).astype(jnp.bfloat16)

    def store(right):
        grad = nn_dot(left_ref[...], right)
        for chunk in range(chunks):
            keep_ref[chunk] = grad[chunk * per : (chunk + 1) * per].astype(jnp.bfloat16)
            first = (chunks + chunk) * per
            send_ref[chunk] = grad[first : first + per].astype(jnp.bfloat16)

    @pl.when(step < tiles)
    def _():
        store(pre_ref[...])

    @pl.when(step == tiles)
    def _():
        left_ref[...] = nt_dot(perm_ref[...], z_ref[...]).astype(jnp.bfloat16)
        store(gmid_ref[...])


def up_out_grad(position, h2, pre, z, gmid, perm, per):
    (block, hidden), model_width = pre.shape, h2.shape[1]
    tiles, chunks = hidden // model_width, model_width // (2 * per)
    out = jax.ShapeDtypeStruct((chunks, per * (tiles + 1), model_width), jnp.bfloat16)
    out_spec = pl.BlockSpec((chunks, per, model_width), lambda i, pos: (0, i, 0))
    return pl.pallas_call(
        partial(up_out_kernel, tiles),
        grid_spec=pltpu.PrefetchScalarGridSpec(
            num_scalar_prefetch=1,
            grid=(tiles + 1,),
            in_specs=[
                whole(h2.shape),
                pl.BlockSpec((block, model_width), lambda i, pos: (0, jnp.minimum(i, tiles - 1))),
                whole(z.shape),
                whole(gmid.shape),
                whole(perm.shape),
            ],
            out_specs=[out_spec, out_spec],
            scratch_shapes=[pltpu.VMEM((model_width, block), jnp.bfloat16)],
        ),
        out_shape=[out, out],
        compiler_params=pltpu.CompilerParams(vmem_limit_bytes=20 << 20),
        cost_estimate=NO_COST,
        name="up_out_grad",
    )(position, h2, pre, z, gmid, perm)


def final_kernel(chips, position, *refs):
    homes = refs[:chips]
    (
        tokens_ref,
        gmid_ref,
        wq_ref,
        wk_ref,
        wv_ref,
        gain_ref,
        out_ref,
        swap_ref,
    ) = refs[chips:]
    chip = position[0]
    block, model_width = tokens_ref.shape
    share = model_width // chips
    total = jnp.zeros((block, model_width), jnp.float32)
    for index, weight in enumerate((wq_ref, wk_ref, wv_ref)):
        for near in range(chips):
            start = pl.multiple_of(share * lax.rem(chip + near, chips), share)
            swap_ref[pl.ds(start, share), :] = homes[near][
                index * share : (index + 1) * share, :
            ].astype(jnp.float32)
        total = total + nt_dot(swap_ref[...].T.astype(jnp.bfloat16), weight[...])
    hat, rate = norm_parts(tokens_ref[...].astype(jnp.float32))
    back = norm_back(total, hat, rate, gain_ref[...])[0]
    out_ref[...] = (gmid_ref[...] + back).astype(jnp.bfloat16)


def final(position, homes, tokens, gmid, w_query, w_key, w_value, gain):
    block, model_width = tokens.shape
    return call_whole(
        partial(final_kernel, len(homes)),
        [jax.ShapeDtypeStruct((block, model_width), jnp.bfloat16)],
        "final",
        position,
        *homes,
        tokens,
        gmid,
        w_query,
        w_key,
        w_value,
        gain,
        scratch=[pltpu.VMEM((model_width, block), jnp.float32)],
    )[0]


def chip_shift(value, steps):
    count = lax.axis_size("seq")
    return lax.ppermute(value, "seq", [(i, (i + 2 * steps) % count) for i in range(count)])


def seq_swap(value, bit):
    return lax.ppermute(value, "seq", [(i, i ^ bit) for i in range(lax.axis_size("seq"))])


def row_swap(value, bit):
    return lax.ppermute(value, "row", [(i, i ^ bit) for i in range(lax.axis_size("row"))])


def sent(array):
    return array.astype(jnp.bfloat16)


def wide(array):
    return array.astype(jnp.float32)


def low_part(shape, keep):
    def index(i, bits):
        return (0, bits[2] if keep else 1 - bits[2], 0, 0, 0)

    return pl.BlockSpec((2, 1, shape[2] // 2) + shape[3:], index)


def high_part(shape, keep):
    def index(i, bits):
        return (bits[3] if keep else 1 - bits[3], 0, 1, 0, 0)

    return pl.BlockSpec((1, 2, shape[2] // 2) + shape[3:], index)


def outgoing_kernel(scalars, low_a, low_b, high_a, high_b, low_ref, high_ref):
    low_ref[...] = sent(wide(low_a[:, 0]) + wide(low_b[:, 0]))
    high_ref[...] = sent(wide(high_a[0]) + wide(high_b[0]))


def outgoing(scalars, keep, other, kept=False):
    shape = keep.shape
    out = jax.ShapeDtypeStruct((2, shape[2] // 2) + shape[3:], jnp.bfloat16)
    low, high = low_part(shape, kept), high_part(shape, kept)
    return call_whole(
        outgoing_kernel,
        [out, out],
        "kept" if kept else "outgoing",
        scalars,
        keep,
        other,
        keep,
        other,
        in_specs=[low, low, high, high],
    )


def halfway_kernel(groups, scalars, *refs):
    ins, outs = refs[: 4 * groups], refs[4 * groups :]
    low_bit, high_bit = scalars[2], scalars[3]
    low_keep, low_send, high_keep, high_send = outs
    first = 0
    for group in range(groups):
        low, high, low_in, high_in = ins[4 * group : 4 * group + 4]
        rows = slice(first, first + low.shape[2])
        for target, side in ((low_keep, high_bit), (low_send, 1 - high_bit)):
            target[:, rows] = sent(wide(low[side]) + wide(low_in[side]))
        for target, side in ((high_keep, low_bit), (high_send, 1 - low_bit)):
            target[:, rows] = sent(wide(high[side]) + wide(high_in[side]))
        first += low.shape[2]


def halfway(scalars, groups):
    arrays = [array for group in groups for array in group]
    rows = sum(group[0].shape[2] for group in groups)
    out = jax.ShapeDtypeStruct((arrays[0].shape[1], rows, arrays[0].shape[3]), jnp.bfloat16)
    return call_whole(
        partial(halfway_kernel, len(groups)), [out] * 4, "halfway", scalars, *arrays, limit=24
    )


def split_kernel(chips, groups, scalars, *refs):
    ins, outs = refs[: 4 * groups], refs[4 * groups : 4 * groups + chips]
    all_ref = refs[-1]
    half = chips // 2
    first = 0
    for group in range(groups):
        low_keep, low_in, high_keep, high_in = ins[4 * group : 4 * group + 4]
        rows = slice(first, first + low_in.shape[1])
        all_ref[:half, rows] = sent(wide(low_keep[...]) + wide(low_in[...]))
        all_ref[half:, rows] = sent(wide(high_keep[...]) + wide(high_in[...]))
        first += low_in.shape[1]
    for step in range(chips):
        outs[step][...] = all_ref[lax.rem(scalars[0] + step, chips)]


def split(scalars, groups, chips):
    arrays = [array for group in groups for array in group]
    rows = sum(group[0].shape[1] for group in groups)
    width = arrays[0].shape[2]
    return call_whole(
        partial(split_kernel, chips, len(groups)),
        [jax.ShapeDtypeStruct((rows, width), jnp.bfloat16)] * chips,
        "split",
        scalars,
        *arrays,
        scratch=[pltpu.VMEM((chips, rows, width), jnp.bfloat16)],
    )


def lay_flat(target, values, first, step):
    for piece in range(values.shape[1] // 128):
        target[pl.ds(first + piece, values.shape[0], step), :] = values[
            :, 128 * piece : 128 * (piece + 1)
        ]


def finish_kernel(chips, per, share, factor, scalars, *refs):
    arrived, heads_in, refs = refs[:chips], refs[chips : 2 * chips], refs[chips:]
    down_ref, up_ref, out_ref, query_ref, key_ref, value_ref, gains_ref, heads_ref = refs[chips:]
    width = arrived[0].shape[1]
    chip, pieces = scalars[0], width // 128
    tiles = up_ref.shape[0] * 128 // (per * width)
    down_rows = down_ref.shape[0] * 128 // width

    def total(first, rows):
        result = wide(arrived[0][first : first + rows, :])
        for part in arrived[1:]:
            result = result + wide(part[first : first + rows, :])
        return result * factor

    lay_flat(down_ref, total(0, down_rows), 0, pieces)
    for tile in range(tiles):
        lay_flat(up_ref, total(down_rows + tile * per, per), tile * pieces, tiles * pieces)
    lay_flat(out_ref, total(down_rows + tiles * per, per), 0, pieces)
    gains = wide(heads_in[0][:8, -128:])
    for part in heads_in[1:]:
        gains = gains + wide(part[:8, -128:])
    gains_ref[...] = gains * factor
    for step in range(chips):
        heads_ref[lax.rem(chip - step + chips, chips)] = wide(heads_in[step][:, : 3 * share])
    for index, target in enumerate((query_ref, key_ref, value_ref)):
        values = jnp.concatenate(
            [heads_ref[near][:, index * share : (index + 1) * share] for near in range(chips)], axis=1
        )
        lay_flat(target, values * factor, 0, pieces)


def finish(scalars, arrived, hidden, parts, per, share, factor):
    chips, width = len(arrived) // 2, arrived[0].shape[1]
    square = jax.ShapeDtypeStruct((per * width // 128, 128), jnp.float32)
    large = jax.ShapeDtypeStruct((per * hidden // 128, 128), jnp.float32)
    return call_whole(
        partial(finish_kernel, chips, per, share, factor),
        [large, large, square, square, square, square, jax.ShapeDtypeStruct((8, 128), jnp.float32)],
        "finish",
        scalars,
        *arrived,
        scratch=[pltpu.VMEM((chips, per, 3 * share), jnp.float32)],
    )


def gathered(rows, chips, chip):
    if chips != 4:
        return [rows] + [chip_shift(rows, step) for step in range(1, chips)]
    behind, ahead = chip_shift(rows, 1), chip_shift(rows, -1)
    up = [(2 * i + core, 2 * i + 2 + core) for i in (1, 2) for core in (0, 1)]
    down = [(2 * i + core, 2 * i - 2 + core) for i in (1, 2) for core in (0, 1)]
    across = jnp.where(
        chip < 2, lax.ppermute(ahead, "seq", down), lax.ppermute(behind, "seq", up)
    )
    return [rows, behind, across, ahead]


def fast_local(
    tokens,
    lengths,
    w_query,
    w_key,
    w_value,
    w_out,
    w_up,
    w_down,
    gain_attend,
    gain_inner,
    gain_feed,
    gain_hidden,
    cotangent,
):
    block, model_width = tokens.shape
    hidden = w_up.shape[1]
    size = model_width // HEADS
    lanes = 2 * size
    scale = size ** (-0.5)
    seq_devices, row_devices = lax.axis_size("seq"), lax.axis_size("row")
    chips = seq_devices // 2
    heads = HEADS // chips
    share = heads * size
    spread = heads * lanes
    parts = row_devices * seq_devices
    position, row = lax.axis_index("seq"), lax.axis_index("row")
    chip, core = position // 2, position % 2
    place = jnp.stack([chip, core, row % 2, row // 2]).astype(jnp.int32)
    bounds = jnp.cumsum(lengths[0])[:-1]
    factor = 1.0 / math.sqrt(block * parts)

    normed_b = call_whole(
        norm_kernel,
        [jax.ShapeDtypeStruct(tokens.shape, jnp.bfloat16)],
        "norm",
        jnp.zeros((1,), jnp.int32),
        tokens,
        gain_attend[None, :],
    )[0]
    own = gathered(normed_b, chips, chip)

    chip_ids = (chip - jnp.arange(chips, dtype=jnp.int32)) % chips
    query_starts = block * (2 * chip_ids + core)
    key_starts = jnp.concatenate([query_starts, block * (2 * chip_ids + 1 - core)])
    in_block = jnp.arange(block, dtype=jnp.int32)[None, :]
    query_places = (query_starts[:, None] + in_block).reshape(-1)
    doc_line = jnp.max(jnp.where(bounds[:, None] <= query_places[None, :], bounds[:, None], 0), axis=0)
    meta = jnp.concatenate(
        [query_starts, key_starts, doc_line.reshape(chips, block)[:, 0], doc_line.reshape(chips, block)[:, -1]]
    )
    doc_line = doc_line[None, :]

    feature = jnp.arange(model_width, dtype=jnp.int32)
    wide_lane = jnp.arange(spread, dtype=jnp.int32)
    source = chip * share + wide_lane // lanes * size + wide_lane % lanes
    pick_wide = ((feature[:, None] == source[None, :]) & (wide_lane % lanes < size)[None, :]).astype(
        jnp.bfloat16
    )
    narrow = chip * share + jnp.arange(share, dtype=jnp.int32)
    pick_narrow = (feature[:, None] == narrow[None, :]).astype(jnp.bfloat16)

    def picked(weight, choice):
        return sent(nn_dot(weight, choice))

    def picked_rows(weight, choice):
        return sent(
            lax.dot_general(
                choice, weight, (((0,), (1,)), ((), ())), preferred_element_type=jnp.float32
            )
        )

    per = model_width // parts
    order = jnp.arange(model_width, dtype=jnp.int32)
    chunk, inside = order // per, order % per
    chunks = parts // 2
    parity = jnp.where(chunk < chunks, core, 1 - core)
    wanted = (2 * (chunk % chunks) + parity) * per + inside
    perm = (wanted[:, None] == feature[None, :]).astype(jnp.bfloat16)

    gains_share = (3 * model_width + hidden) // parts
    gains_rows = -(-gains_share // 128)
    owner = 2 * (chunk % chunks) + parity
    first_gain = owner * gains_share + 128 * inside
    end_gain = jnp.minimum(first_gain + 128, (owner + 1) * gains_share)
    where_row = (
        (inside < gains_rows)[:, None]
        & (wanted[None, :] >= first_gain[:, None])
        & (wanted[None, :] < end_gain[:, None])
    ).astype(jnp.bfloat16)
    where_lane = (
        (wanted % gains_share % 128)[:, None] == jnp.arange(128, dtype=jnp.int32)[None, :]
    ).astype(jnp.float32)
    gain_rows = (1.0 / gain_attend).reshape(parts // 2, 2, per)
    gain_rows = jnp.where(core == 0, gain_rows, gain_rows[:, ::-1]).transpose(1, 0, 2)
    gain_rows = gain_rows.reshape(model_width, 1)
    early = (
        jnp.concatenate([query_starts, 2 * block * chip_ids + block * (1 - core), heads * chip[None]]),
        meta,
        doc_line,
        perm,
        picked_rows(w_query, pick_wide),
        picked(w_key, pick_wide),
        picked_rows(w_value, pick_narrow),
        picked_rows(w_key, pick_narrow),
        picked(w_value, pick_wide),
        jnp.concatenate([picked(weight, pick_narrow) for weight in (w_query, w_key, w_value)], axis=1),
        gain_attend[None, :],
        gain_inner[None, :],
        gain_feed[None, :],
        gain_hidden[None, :],
        place,
        where_row,
        where_lane,
        gain_rows,
    )
    own[1], early = lax.optimization_barrier((own[1], early))
    starts, meta, doc_line, perm, wq_wide, wk_wide, wv_rows, wk_rows, wv_wide, w_own = early[:10]
    gain_first, gain_inner, gain_feed, gain_hidden, place = early[10:15]
    where_row, where_lane, gain_rows = early[15:]
    sibling = [seq_swap(rows, 1) for rows in own]
    q_ext, k_ext, v_t = project(
        starts,
        own + sibling,
        wq_wide,
        wk_wide,
        wv_rows,
        chips,
        heads,
        scale,
    )
    mixed, mixed_b, lse = attend(meta, doc_line, q_ext, k_ext, v_t, heads, block)
    own, w_own, mixed_b = lax.optimization_barrier((own, w_own, mixed_b))
    back = [mixed_b[0]] + [chip_shift(mixed_b[step], -step) for step in range(1, chips)]

    own_normed = jnp.concatenate(own, axis=0)
    k_t, v_ext = project_back(place, own + sibling, wk_rows, wv_wide)
    normed_p = sent(nt_dot(perm, own_normed))
    weights_p = sent(nn_dot(perm, w_own))
    back, k_t, v_ext, normed_p, weights_p = lax.optimization_barrier(
        (back, k_t, v_ext, normed_p, weights_p)
    )

    outs = middle(
        place, back, tokens, cotangent, w_out, w_up, w_down, (gain_inner, gain_feed, gain_hidden)
    )
    result, grad_middle, gmid_b = outs[:3]
    go = outs[3 : 3 + chips]
    z, h2, bent, pre, dinner, dfeed, dhidden = outs[3 + chips :]
    go = [go[0]] + [chip_shift(go[step], step) for step in range(1, chips)]
    go[1], bent, pre = lax.optimization_barrier((go[1], bent, pre))
    keep_a, send_a = down_grad(place, bent, cotangent, hidden // parts)
    keep_b, send_b = up_out_grad(place, h2, pre, z, gmid_b, perm, per)

    gains_late = jnp.concatenate([jnp.zeros_like(dinner), dinner, dfeed, dhidden], axis=1)
    gains_late = gains_late.reshape(parts // 2, 2, gains_share)
    gains_late = jnp.where(core == 0, gains_late, gains_late[:, ::-1]).transpose(1, 0, 2)
    gains_late = jnp.pad(gains_late, ((0, 0), (0, 0), (0, gains_rows * 128 - gains_share)))
    gains_late = jnp.pad(
        gains_late.reshape(parts, gains_rows, 128), ((0, 0), (0, per - gains_rows), (0, 0))
    ).reshape(model_width, 128)

    def gridded(array):
        return array.reshape((2, 2, chips) + array.shape[1:])

    keep_a, other_a = gridded(keep_a), gridded(seq_swap(send_a, 1))
    out_a = outgoing(place, keep_a, other_a)
    kept_a = outgoing(place, keep_a, other_a, True)
    other_b = seq_swap(send_b, 1)
    go, out_a, kept_a, keep_b, send_b = lax.optimization_barrier(
        (go, out_a, kept_a, keep_b, send_b)
    )
    in_a = [row_swap(out_a[0], 1), row_swap(out_a[1], 2)]
    dq, pair, other = attend_back(
        meta, doc_line, q_ext, jnp.concatenate(go, axis=1), mixed, lse, k_ext, k_t, v_ext, heads, block, scale
    )
    dq, pair, other, in_a, keep_b, other_b = lax.optimization_barrier(
        (dq, pair, other, in_a, keep_b, other_b)
    )
    keep_b, other_b = gridded(keep_b), gridded(other_b)
    out_b = outgoing(place, keep_b, other_b)
    in_b = [row_swap(out_b[0], 1), row_swap(out_b[1], 2)]
    grads = join_parts(place, dq, pair, seq_swap(other, 1), chips)
    home = [grads[0]] + [chip_shift(grads[step], -step) for step in range(1, chips)]
    grads, keep_b, other_b = lax.optimization_barrier((grads, keep_b, other_b))
    kept_b = outgoing(place, keep_b, other_b, True)
    mine_grad, send_grad = head_grads(
        place, normed_p, grads, weights_p, gain_rows, where_row, where_lane, gains_late, per
    )
    in_a, in_b, kept_a, kept_b, home[1], mine_grad, send_grad = lax.optimization_barrier(
        (in_a, in_b, kept_a, kept_b, home[1], mine_grad, send_grad)
    )
    low_keep, low_send, high_keep, high_send = halfway(place, [(*kept_a, *in_a), (*kept_b, *in_b)])
    low_in, high_in = row_swap(low_send, 2), row_swap(high_send, 1)
    home, low_in, high_in, mine_grad, send_grad = lax.optimization_barrier(
        (home, low_in, high_in, mine_grad, send_grad)
    )
    mine_grad, other_grad = gridded(mine_grad), gridded(seq_swap(send_grad, 1))
    stage = split(place, [(low_keep, low_in, high_keep, high_in)], chips)
    arrived = [stage[0]] + [chip_shift(stage[step], step) for step in range(1, chips)]
    grad_input = final(
        place, home, tokens, grad_middle, w_query, w_key, w_value, gain_first
    )
    low, high = outgoing(place, mine_grad, other_grad)
    low_keep, low_send, high_keep, high_send = halfway(
        place,
        [(*outgoing(place, mine_grad, other_grad, True), row_swap(low, 1), row_swap(high, 2))],
    )
    stage = split(
        place, [(low_keep, row_swap(low_send, 2), high_keep, row_swap(high_send, 1))], chips
    )
    arrived += [stage[0]] + [chip_shift(stage[step], step) for step in range(1, chips)]
    down, up, out, query, key, value, gains_part = finish(
        place, arrived, hidden, parts, per, share, factor
    )
    return (
        result,
        grad_input,
        query.reshape(-1),
        key.reshape(-1),
        value.reshape(-1),
        out.reshape(-1),
        up.reshape(-1),
        down.reshape(-1),
        gains_part.reshape(-1)[:gains_share],
    )


def local(*arrays):
    seq_devices, row_devices = lax.axis_size("seq"), lax.axis_size("row")
    block = arrays[0].shape[0]
    one_segment = block * seq_devices <= SEGMENT and block % 2 ** (PATTERNS - 1) == 0
    if one_segment and seq_devices in (2, 4, 8) and row_devices == 4:
        return fast_local(*arrays)
    return ring_local(*arrays)


def solution(mesh):
    return jax.shard_map(
        local,
        mesh=mesh,
        in_specs=(
            P(("row", "seq"), None),
            P("row", None),
            P(),
            P(),
            P(),
            P(),
            P(),
            P(),
            P(),
            P(),
            P(),
            P(),
            P(("row", "seq"), None),
        ),
        out_specs=(
            P(("row", "seq"), None),
            P(("row", "seq"), None),
            P(("row", "seq")),
            P(("row", "seq")),
            P(("row", "seq")),
            P(("row", "seq")),
            P(("row", "seq")),
            P(("row", "seq")),
            P(("row", "seq")),
        ),
        check_vma=False,
    )
```

```python
from functools import partial
from functools import reduce
import math

import jax
import jax.numpy as jnp
import numpy as np
from jax import lax
from jax.experimental import pallas as pl
from jax.experimental.pallas import tpu as pltpu
from jax.sharding import PartitionSpec as P

HEADS = 12
SEGMENT = 2048
PATTERNS = 5


big_negative = -1e30


def shifted_2(shard, axis, by):
    length = lax.axis_size(axis)
    pairs = [(i, i + by) for i in range(length) if 0 <= i + by < length]
    return lax.ppermute(shard, axis, pairs)


def shifted_3(value, axis, steps):
    count = lax.axis_size(axis)
    pairs = [(source, (source + steps) % count) for source in range(count)]
    return lax.ppermute(value, axis, pairs)


def layer_norm(values, gain_vector):
    centre = jnp.mean(values, axis=-1, keepdims=True)
    shifted = values - centre
    variance = jnp.mean(shifted * shifted, axis=-1, keepdims=True)
    return shifted * lax.rsqrt(variance + 1e-05) * gain_vector


def hidden_norm(hidden_pre, gain_vector):
    return layer_norm(jax.nn.gelu(hidden_pre, approximate=True), gain_vector)


def selector(stride, head_count):
    return jnp.arange(stride)[:, None] == (jnp.arange(head_count) % stride)[None, :]


def compact(full_array, stride):
    length_in, head_count, inner_size = full_array.shape
    shaped = full_array.reshape(length_in // stride, stride, head_count, inner_size)
    picked = jnp.where(
        selector(stride, head_count)[None, :, :, None], shaped, jnp.zeros((), full_array.dtype)
    )
    return jnp.sum(picked, axis=1)


def expand(part_array, stride, fill_value):
    part_rows, head_count, inner_size = part_array.shape
    widened = jnp.where(
        selector(stride, head_count)[None, :, :, None],
        part_array[:, None],
        jnp.asarray(fill_value, part_array.dtype),
    )
    return widened.reshape(part_rows * stride, head_count, inner_size)


def positions(start_pos, part_rows, stride, head_count):
    row_ids = jnp.arange(part_rows, dtype=jnp.int32)[:, None] * stride
    head_ids = (jnp.arange(head_count, dtype=jnp.int32) % stride)[None, :]
    return start_pos + row_ids + head_ids


def doc_index(places, doc_bounds):
    return jnp.sum((places[..., None] >= doc_bounds).astype(jnp.int32), axis=-1)


def block_mask(doc_query, doc_key, local_block):
    allowed = doc_query.T[:, :, None] == doc_key.T[:, None, :]
    if local_block:
        rank_ids = jnp.arange(doc_query.shape[0])
        allowed = allowed & (rank_ids[:, None] >= rank_ids[None, :])[None]
    return allowed


def forward_block(query_part, key_part, value_part, allowed, score_scale):
    scores = (
        jnp.einsum("qhd,khd->hqk", query_part, key_part, preferred_element_type=jnp.float32)
        * score_scale
    )
    scores = jnp.where(allowed, scores, big_negative)
    row_peak = jnp.max(scores, axis=-1)
    weights = jnp.where(allowed, jnp.exp(scores - row_peak[..., None]), 0.0)
    row_total = jnp.sum(weights, axis=-1)
    mixed = jnp.einsum(
        "hqk,khd->qhd", weights.astype(jnp.bfloat16), value_part, preferred_element_type=jnp.float32
    )
    return (row_peak.T, row_total.T, mixed)


def merge(carried, new_block):
    best_peak = jnp.maximum(carried[0], new_block[0])
    keep_factor = jnp.exp(carried[0] - best_peak)
    take_factor = jnp.exp(new_block[0] - best_peak)
    new_total = carried[1] * keep_factor + new_block[1] * take_factor
    new_mixed = carried[2] * keep_factor[..., None] + new_block[2] * take_factor[..., None]
    return (best_peak, new_total, new_mixed)


def backward_block(
    query_part, grad_part, lse_part, delta_part, key_part, value_part, allowed, score_scale
):
    scores = (
        jnp.einsum("qhd,khd->hqk", query_part, key_part, preferred_element_type=jnp.float32)
        * score_scale
    )
    probs = jnp.where(allowed, jnp.exp(scores - lse_part.T[:, :, None]), 0.0)
    dots = jnp.einsum("qhd,khd->hqk", grad_part, value_part, preferred_element_type=jnp.float32)
    grad_scores = (probs * (dots - delta_part.T[:, :, None])).astype(jnp.bfloat16)
    query_grad = (
        jnp.einsum("hqk,khd->qhd", grad_scores, key_part, preferred_element_type=jnp.float32)
        * score_scale
    )
    key_grad = (
        jnp.einsum("hqk,qhd->khd", grad_scores, query_part, preferred_element_type=jnp.float32)
        * score_scale
    )
    value_grad = jnp.einsum(
        "hqk,qhd->khd", probs.astype(jnp.bfloat16), grad_part, preferred_element_type=jnp.float32
    )
    return (query_grad, key_grad, value_grad)


def keep_state(carried):
    return carried


def ring_local(
    tokens,
    lengths,
    w_query,
    w_key,
    w_value,
    w_out,
    w_up,
    w_down,
    gain_attend,
    gain_inner,
    gain_feed,
    gain_hidden,
    cotangent,
):
    block_rows, model_width = tokens.shape
    head_count = HEADS
    head_size = model_width // head_count
    score_scale = head_size ** (-0.5)
    seq_devices = lax.axis_size("seq")
    all_devices = seq_devices * lax.axis_size("row")
    my_index = lax.axis_index("seq")
    seq_total = block_rows * seq_devices
    doc_bounds = jnp.cumsum(lengths[0])[:-1]
    patterns = [
        (2**pattern, min(SEGMENT * 2**pattern, seq_total) // block_rows)
        for pattern in range(PATTERNS)
    ]
    near_ids = [0, 1]
    far_ids = list(range(2, PATTERNS))
    reach = patterns[1][1]
    far_rows = [block_rows // patterns[pattern][0] for pattern in far_ids]
    far_starts = [sum(far_rows[:slot_id]) for slot_id in range(len(far_ids))]
    far_total = sum(far_rows)

    def key_docs(pattern, source):
        stride = patterns[pattern][0]
        return doc_index(
            positions(source * block_rows, block_rows // stride, stride, head_count), doc_bounds
        )

    def is_live(pattern, cycle_step):
        group_size = patterns[pattern][1]
        return (cycle_step < group_size) & (my_index % group_size >= cycle_step)

    source_x = tokens.astype(jnp.float32)
    normed, attend_back = jax.vjp(layer_norm, source_x, gain_attend)
    normed_b = normed.astype(jnp.bfloat16)
    query_b = jnp.dot(normed_b, w_query, preferred_element_type=jnp.float32).astype(jnp.bfloat16)
    key_b = jnp.dot(normed_b, w_key, preferred_element_type=jnp.float32).astype(jnp.bfloat16)
    value_b = jnp.dot(normed_b, w_value, preferred_element_type=jnp.float32).astype(jnp.bfloat16)
    query_heads = query_b.reshape(block_rows, head_count, head_size)
    key_heads = key_b.reshape(block_rows, head_count, head_size)
    value_heads = value_b.reshape(block_rows, head_count, head_size)
    query_parts = [compact(query_heads, stride) for stride, group_size in patterns]
    key_parts = [compact(key_heads, stride) for stride, group_size in patterns]
    value_parts = [compact(value_heads, stride) for stride, group_size in patterns]
    own_docs = [key_docs(pattern, my_index) for pattern in range(PATTERNS)]
    states = [
        forward_block(
            query_parts[pattern],
            key_parts[pattern],
            value_parts[pattern],
            block_mask(own_docs[pattern], own_docs[pattern], True),
            score_scale,
        )
        for pattern in range(PATTERNS)
    ]

    def unpack_near(key_block):
        key_full = key_block[:, :model_width].reshape(block_rows, head_count, head_size)
        value_full = key_block[:, model_width:].reshape(block_rows, head_count, head_size)
        return (key_full, value_full)

    def near_fold_parts(pattern, key_part, value_part, source, carried):
        new_block = forward_block(
            query_parts[pattern],
            key_part,
            value_part,
            block_mask(own_docs[pattern], key_docs(pattern, source), False),
            score_scale,
        )
        return merge(carried, new_block)

    def near_fold(pattern, key_full, value_full, source, carried):
        stride = patterns[pattern][0]
        return near_fold_parts(
            pattern, compact(key_full, stride), compact(value_full, stride), source, carried
        )

    pair_block = jnp.concatenate([key_b, value_b], axis=1)
    kept_blocks = jnp.zeros((max(reach - 1, 1), block_rows, 2 * model_width), jnp.bfloat16)

    def near_forward(cycle_step, loop_state):
        key_block, near_now, kept_store = loop_state
        key_block = shifted_2(key_block, "seq", 1)
        key_full, value_full = unpack_near(key_block)
        new_states = []
        for pattern in near_ids:
            new_states.append(
                lax.cond(
                    is_live(pattern, cycle_step),
                    partial(near_fold, pattern, key_full, value_full, my_index - cycle_step),
                    keep_state,
                    near_now[pattern],
                )
            )
        return (key_block, tuple(new_states), kept_store)

    _, near_states, kept_blocks = lax.fori_loop(
        1, reach, near_forward, (pair_block, (states[0], states[1]), kept_blocks)
    )
    far_block = jnp.concatenate(
        [
            jnp.concatenate(
                [
                    key_parts[pattern].reshape(rows_here, model_width),
                    value_parts[pattern].reshape(rows_here, model_width),
                ],
                axis=1,
            )
            for pattern, rows_here in zip(far_ids, far_rows)
        ],
        axis=0,
    )

    def unpack_far(key_block, slot_id):
        rows_here = far_rows[slot_id]
        row_begin = far_starts[slot_id]
        piece_rows = key_block[row_begin : row_begin + rows_here]
        key_part = piece_rows[:, :model_width].reshape(rows_here, head_count, head_size)
        value_part = piece_rows[:, model_width:].reshape(rows_here, head_count, head_size)
        return (key_part, value_part)

    def far_fold(pattern, key_part, value_part, source, carried):
        new_block = forward_block(
            query_parts[pattern],
            key_part,
            value_part,
            block_mask(own_docs[pattern], key_docs(pattern, source), False),
            score_scale,
        )
        return merge(carried, new_block)

    def far_update(far_now, key_block, cycle_step):
        new_states = []
        for slot_id, pattern in enumerate(far_ids):
            key_part, value_part = unpack_far(key_block, slot_id)
            new_states.append(
                lax.cond(
                    is_live(pattern, cycle_step),
                    partial(far_fold, pattern, key_part, value_part, my_index - cycle_step),
                    keep_state,
                    far_now[slot_id],
                )
            )
        return tuple(new_states)

    far_states = tuple((states[pattern] for pattern in far_ids))

    def far_forward(cycle_step, loop_state):
        key_block, far_now = loop_state
        key_block = shifted_2(key_block, "seq", 1)
        return (key_block, far_update(far_now, key_block, cycle_step))

    _, far_states = lax.fori_loop(1, seq_devices, far_forward, (far_block, far_states))
    ordered = list(near_states) + list(far_states)
    peaks = [
        expand(ordered[pattern][0][..., None], patterns[pattern][0], big_negative)[..., 0]
        for pattern in range(PATTERNS)
    ]
    best_peak = reduce(jnp.maximum, peaks)
    weight_sum = jnp.zeros((block_rows, head_count), jnp.float32)
    mixed_sum = jnp.zeros((block_rows, head_count, head_size), jnp.float32)
    for pattern in range(PATTERNS):
        stride = patterns[pattern][0]
        factor = jnp.exp(peaks[pattern] - best_peak)
        weight_sum = (
            weight_sum + expand(ordered[pattern][1][..., None], stride, 0.0)[..., 0] * factor
        )
        mixed_sum = mixed_sum + expand(ordered[pattern][2], stride, 0.0) * factor[..., None]
    attended = mixed_sum / weight_sum[..., None]
    log_total = best_peak + jnp.log(weight_sum)
    inner_out, inner_back = jax.vjp(
        layer_norm, attended.reshape(block_rows, model_width), gain_inner
    )
    inner_b = inner_out.astype(jnp.bfloat16)
    middle = source_x + jnp.dot(inner_b, w_out, preferred_element_type=jnp.float32)
    normed_two, feed_back = jax.vjp(layer_norm, middle, gain_feed)
    normed_two_b = normed_two.astype(jnp.bfloat16)
    hidden_pre = jnp.dot(normed_two_b, w_up, preferred_element_type=jnp.float32)
    hidden, hidden_back = jax.vjp(hidden_norm, hidden_pre, gain_hidden)
    hidden_b = hidden.astype(jnp.bfloat16)
    result = (middle + jnp.dot(hidden_b, w_down, preferred_element_type=jnp.float32)).astype(
        jnp.bfloat16
    )
    grad_down = jnp.einsum("tf,tg->fg", hidden_b, cotangent, preferred_element_type=jnp.float32)
    grad_hidden = jnp.einsum("tg,fg->tf", cotangent, w_down, preferred_element_type=jnp.float32)
    grad_pre, grad_gain_hidden = hidden_back(grad_hidden)
    grad_pre_b = grad_pre.astype(jnp.bfloat16)
    grad_up = jnp.einsum("tf,tg->fg", normed_two_b, grad_pre_b, preferred_element_type=jnp.float32)
    grad_normed_two = jnp.einsum("tg,fg->tf", grad_pre_b, w_up, preferred_element_type=jnp.float32)
    grad_middle_part, grad_gain_feed = feed_back(grad_normed_two)
    grad_middle = cotangent.astype(jnp.float32) + grad_middle_part
    grad_middle_b = grad_middle.astype(jnp.bfloat16)
    grad_out = jnp.einsum("tf,tg->fg", inner_b, grad_middle_b, preferred_element_type=jnp.float32)
    grad_inner = jnp.einsum("tg,fg->tf", grad_middle_b, w_out, preferred_element_type=jnp.float32)
    grad_attended, grad_gain_inner = inner_back(grad_inner)
    grad_heads = grad_attended.astype(jnp.bfloat16).reshape(block_rows, head_count, head_size)
    delta_rows = jnp.sum(grad_heads.astype(jnp.float32) * attended, axis=-1)
    grad_parts = [compact(grad_heads, stride) for stride, group_size in patterns]
    lse_parts = [compact(log_total[..., None], stride)[..., 0] for stride, group_size in patterns]
    delta_parts = [
        compact(delta_rows[..., None], stride)[..., 0] for stride, group_size in patterns
    ]
    query_grads = []
    home_keys = []
    home_values = []
    for pattern in range(PATTERNS):
        part_query, part_key, part_value = backward_block(
            query_parts[pattern],
            grad_parts[pattern],
            lse_parts[pattern],
            delta_parts[pattern],
            key_parts[pattern],
            value_parts[pattern],
            block_mask(own_docs[pattern], own_docs[pattern], True),
            score_scale,
        )
        query_grads.append(part_query)
        home_keys.append(part_key)
        home_values.append(part_value)

    def fetch_full(key_block):
        return shifted_2(key_block, "seq", 1)

    def near_grad(pattern, key_full, value_full, source, operands):
        query_grad, travel = operands
        stride = patterns[pattern][0]
        part_query, part_key, part_value = backward_block(
            query_parts[pattern],
            grad_parts[pattern],
            lse_parts[pattern],
            delta_parts[pattern],
            compact(key_full, stride),
            compact(value_full, stride),
            block_mask(own_docs[pattern], key_docs(pattern, source), False),
            score_scale,
        )
        spread_rows = jnp.concatenate(
            [
                expand(part_key, stride, 0.0).reshape(block_rows, model_width),
                expand(part_value, stride, 0.0).reshape(block_rows, model_width),
            ],
            axis=1,
        )
        return (query_grad + part_query, travel + spread_rows)

    def near_backward(cycle_step, loop_state):
        key_block, grads_now, travel = loop_state
        key_block = fetch_full(key_block)
        travel = shifted_3(travel.astype(jnp.bfloat16), "seq", 1).astype(travel.dtype)
        key_full, value_full = unpack_near(key_block)
        new_grads = list(grads_now)
        for pattern in near_ids:
            new_grads[pattern], travel = lax.cond(
                is_live(pattern, cycle_step),
                partial(near_grad, pattern, key_full, value_full, my_index - cycle_step),
                keep_state,
                (new_grads[pattern], travel),
            )
        return (key_block, tuple(new_grads), travel)

    own_key_near = expand(home_keys[0], 1, 0.0) + expand(home_keys[1], 2, 0.0)
    own_value_near = expand(home_values[0], 1, 0.0) + expand(home_values[1], 2, 0.0)
    near_start = jnp.concatenate(
        [
            own_key_near.reshape(block_rows, model_width),
            own_value_near.reshape(block_rows, model_width),
        ],
        axis=1,
    )
    _, near_query, travel_near = lax.fori_loop(
        1, reach, near_backward, (pair_block, (query_grads[0], query_grads[1]), near_start)
    )
    near_home = shifted_3(travel_near.astype(jnp.bfloat16), "seq", 1 - reach).astype(
        travel_near.dtype
    )
    near_key_add = near_home[:, :model_width].reshape(block_rows, head_count, head_size)
    near_value_add = near_home[:, model_width:].reshape(block_rows, head_count, head_size)

    def far_grad(slot_id, key_part, value_part, source, operands):
        query_grad, travel = operands
        pattern = far_ids[slot_id]
        rows_here = far_rows[slot_id]
        row_begin = far_starts[slot_id]
        part_query, part_key, part_value = backward_block(
            query_parts[pattern],
            grad_parts[pattern],
            lse_parts[pattern],
            delta_parts[pattern],
            key_part,
            value_part,
            block_mask(own_docs[pattern], key_docs(pattern, source), False),
            score_scale,
        )
        spread_rows = jnp.concatenate(
            [part_key.reshape(rows_here, model_width), part_value.reshape(rows_here, model_width)],
            axis=1,
        )
        return (
            query_grad + part_query,
            travel.at[row_begin : row_begin + rows_here].add(spread_rows),
        )

    def far_back_update(grads_now, travel, key_block, cycle_step):
        new_grads = list(grads_now)
        for slot_id, pattern in enumerate(far_ids):
            key_part, value_part = unpack_far(key_block, slot_id)
            new_grads[slot_id], travel = lax.cond(
                is_live(pattern, cycle_step),
                partial(far_grad, slot_id, key_part, value_part, my_index - cycle_step),
                keep_state,
                (new_grads[slot_id], travel),
            )
        return (tuple(new_grads), travel)

    far_query = tuple((query_grads[pattern] for pattern in far_ids))
    far_empty = jnp.zeros((far_total, 2 * model_width), jnp.float32)

    def far_send(travel):
        return shifted_3(travel.astype(jnp.bfloat16), "seq", 1).astype(travel.dtype)

    def far_backward(cycle_step, loop_state):
        key_block, grads_now, travel = loop_state
        key_block = shifted_2(key_block, "seq", 1)
        travel = far_send(travel)
        grads_now, travel = far_back_update(grads_now, travel, key_block, cycle_step)
        return (key_block, grads_now, travel)

    _, far_query, travel_far = lax.fori_loop(
        1, seq_devices, far_backward, (far_block, far_query, far_empty)
    )
    far_home = far_send(travel_far)
    all_query = list(near_query) + list(far_query)
    query_grad = jnp.zeros((block_rows, head_count, head_size), jnp.float32)
    key_grad = near_key_add
    value_grad = near_value_add
    for pattern in range(PATTERNS):
        stride = patterns[pattern][0]
        query_grad = query_grad + expand(all_query[pattern], stride, 0.0)
    for pattern in far_ids:
        stride = patterns[pattern][0]
        key_grad = key_grad + expand(home_keys[pattern], stride, 0.0)
        value_grad = value_grad + expand(home_values[pattern], stride, 0.0)
    for slot_id, pattern in enumerate(far_ids):
        stride = patterns[pattern][0]
        rows_here = far_rows[slot_id]
        row_begin = far_starts[slot_id]
        piece_rows = far_home[row_begin : row_begin + rows_here]
        key_grad = key_grad + expand(
            piece_rows[:, :model_width].reshape(rows_here, head_count, head_size), stride, 0.0
        )
        value_grad = value_grad + expand(
            piece_rows[:, model_width:].reshape(rows_here, head_count, head_size), stride, 0.0
        )
    grad_query_b = query_grad.reshape(block_rows, model_width).astype(jnp.bfloat16)
    grad_key_b = key_grad.reshape(block_rows, model_width).astype(jnp.bfloat16)
    grad_value_b = value_grad.reshape(block_rows, model_width).astype(jnp.bfloat16)
    grad_w_query = jnp.einsum(
        "tf,tg->fg", normed_b, grad_query_b, preferred_element_type=jnp.float32
    )
    grad_w_key = jnp.einsum("tf,tg->fg", normed_b, grad_key_b, preferred_element_type=jnp.float32)
    grad_w_value = jnp.einsum(
        "tf,tg->fg", normed_b, grad_value_b, preferred_element_type=jnp.float32
    )
    grad_normed = jnp.einsum("tg,fg->tf", grad_query_b, w_query, preferred_element_type=jnp.float32)
    grad_normed = grad_normed + jnp.einsum(
        "tg,fg->tf", grad_key_b, w_key, preferred_element_type=jnp.float32
    )
    grad_normed = grad_normed + jnp.einsum(
        "tg,fg->tf", grad_value_b, w_value, preferred_element_type=jnp.float32
    )
    grad_x_part, grad_gain_attend = attend_back(grad_normed)
    grad_input = (grad_middle + grad_x_part).astype(jnp.bfloat16)
    gains_all = jnp.concatenate(
        [grad_gain_attend, grad_gain_inner, grad_gain_feed, grad_gain_hidden]
    )
    summed = (
        lax.psum_scatter(grad_w_query.reshape(-1), ("row", "seq"), scatter_dimension=0, tiled=True),
        lax.psum_scatter(grad_w_key.reshape(-1), ("row", "seq"), scatter_dimension=0, tiled=True),
        lax.psum_scatter(grad_w_value.reshape(-1), ("row", "seq"), scatter_dimension=0, tiled=True),
        lax.psum_scatter(grad_out.reshape(-1), ("row", "seq"), scatter_dimension=0, tiled=True),
        lax.psum_scatter(grad_up.reshape(-1), ("row", "seq"), scatter_dimension=0, tiled=True),
        lax.psum_scatter(grad_down.reshape(-1), ("row", "seq"), scatter_dimension=0, tiled=True),
        lax.psum_scatter(gains_all, ("row", "seq"), scatter_dimension=0, tiled=True),
    )
    factor = 1.0 / math.sqrt(block_rows * all_devices)
    return (result, grad_input) + tuple((summed_part * factor for summed_part in summed))


NO_COST = pl.CostEstimate(flops=1000, bytes_accessed=1000, transcendentals=0)
SOME_COST = pl.CostEstimate(flops=4 * 10**9, bytes_accessed=1000, transcendentals=0)
HIGH_COST = pl.CostEstimate(flops=5 * 10**10, bytes_accessed=1000, transcendentals=0)


def split_log(level):
    remaining = math.log((level + 1) / level)
    pieces = []
    for _ in range(3):
        piece = float(jnp.bfloat16.dtype.type(remaining))
        pieces.append(piece)
        remaining -= piece
    return pieces


def extra_values(places, features, head, size, per_piece):
    masks, values = jnp.zeros_like(features), jnp.zeros(features.shape, jnp.float32)
    for level in range(1, PATTERNS):
        for piece, value in enumerate(split_log(level)):
            here = features == size + 3 * (level - 1) + piece
            masks = jnp.where(here, 2**level - 1, masks)
            values = jnp.where(here, value if per_piece else 1.0, values)
    return jnp.where(((places - head) & masks) == 0, values, 0.0)


def nt_dot(left, right):
    return lax.dot_general(
        left, right, (((1,), (1,)), ((), ())), preferred_element_type=jnp.float32
    )


def nn_dot(left, right):
    return jnp.dot(left, right, preferred_element_type=jnp.float32)


def call_whole(kernel, out_shape, name, scalars, *arrays, in_specs=None, scratch=(), limit=12, cost=None):
    return pl.pallas_call(
        kernel,
        grid_spec=pltpu.PrefetchScalarGridSpec(
            num_scalar_prefetch=1,
            grid=(1,),
            in_specs=in_specs or [whole(array.shape) for array in arrays],
            out_specs=[whole(out.shape) for out in out_shape],
            scratch_shapes=list(scratch),
        ),
        out_shape=list(out_shape),
        compiler_params=pltpu.CompilerParams(vmem_limit_bytes=limit << 20),
        cost_estimate=cost or NO_COST,
        name=name,
    )(scalars, *arrays)


def after_kernel(scalars, *refs):
    for index in range(scalars.shape[0]):
        refs[-1][index] = scalars[index]


def after(scalars, arrays, cost):
    return pl.pallas_call(
        after_kernel,
        in_specs=[pl.BlockSpec(memory_space=pltpu.SMEM)]
        + [pl.BlockSpec(memory_space=pl.ANY)] * len(arrays),
        out_specs=pl.BlockSpec(memory_space=pltpu.SMEM),
        out_shape=jax.ShapeDtypeStruct(scalars.shape, scalars.dtype),
        compiler_params=pltpu.CompilerParams(vmem_limit_bytes=1 << 20),
        cost_estimate=cost,
        name="after",
    )(scalars, *arrays)


def norm_kernel(unused, rows_ref, gain_ref, out_ref):
    out_ref[...] = (norm_parts(rows_ref[...].astype(jnp.float32))[0] * gain_ref[...]).astype(
        jnp.bfloat16
    )


def project_kernel(blocks, own, heads, scale, meta, *refs):
    normed = refs[:blocks]
    wq_ref, wk_ref, wv_ref, q_ref, k_ref, vt_ref = refs[blocks:]
    length = normed[0].shape[0]
    lanes = wk_ref.shape[1] // heads
    size = lanes // 2
    first_head = meta[blocks]
    for index in range(blocks):
        rows = normed[index][...]
        start = meta[index]
        span = slice(index * length, (index + 1) * length)
        keys = nn_dot(rows, wk_ref[...])
        vt_ref[:, span] = nt_dot(wv_ref[...], rows).astype(jnp.bfloat16)
        places = start + lax.broadcasted_iota(jnp.int32, (length, 1), 0)
        features = lax.broadcasted_iota(jnp.int32, (1, lanes), 1)
        for head in range(heads):
            wide_rows = slice(head * lanes, (head + 1) * lanes)
            extra = extra_values(places, features, first_head + head, size, False)
            k_ref[span, wide_rows] = (keys[:, wide_rows] + extra).astype(jnp.bfloat16)
        if index < own:
            queries = nt_dot(wq_ref[...], rows).astype(jnp.bfloat16).astype(jnp.float32) * scale
            places = start + lax.broadcasted_iota(jnp.int32, (1, length), 1)
            features = lax.broadcasted_iota(jnp.int32, (lanes, 1), 0)
            for head in range(heads):
                wide_rows = slice(head * lanes, (head + 1) * lanes)
                extra = extra_values(places, features, first_head + head, size, True)
                q_ref[wide_rows, span] = (queries[wide_rows] + extra).astype(jnp.bfloat16)


def project(meta, normed, wq, wk, wv, own, heads, scale):
    blocks, length = len(normed), normed[0].shape[0]
    wide, share = wk.shape[1], wv.shape[0]
    return call_whole(
        partial(project_kernel, blocks, own, heads, scale),
        [
            jax.ShapeDtypeStruct((wide, own * length), jnp.bfloat16),
            jax.ShapeDtypeStruct((blocks * length, wide), jnp.bfloat16),
            jax.ShapeDtypeStruct((share, blocks * length), jnp.bfloat16),
        ],
        "project",
        meta,
        *normed,
        wq,
        wk,
        wv,
        limit=20,
    )


def project_back_kernel(blocks, unused, *refs):
    normed = refs[:blocks]
    wk_ref, wv_ref, kt_ref, v_ref = refs[blocks:]
    length = normed[0].shape[0]
    for index in range(blocks):
        rows = normed[index][...]
        span = slice(index * length, (index + 1) * length)
        kt_ref[:, span] = nt_dot(wk_ref[...], rows).astype(jnp.bfloat16)
        v_ref[span, :] = nn_dot(rows, wv_ref[...]).astype(jnp.bfloat16)


def project_back(scalars, normed, wk, wv):
    blocks, length = len(normed), normed[0].shape[0]
    return call_whole(
        partial(project_back_kernel, blocks),
        [
            jax.ShapeDtypeStruct((wk.shape[0], blocks * length), jnp.bfloat16),
            jax.ShapeDtypeStruct((blocks * length, wv.shape[1]), jnp.bfloat16),
        ],
        "project_back",
        scalars,
        *normed,
        wk,
        wv,
    )


def pair_mask(query_start, key_start, doc_line, block):
    query_place = query_start + lax.broadcasted_iota(jnp.int32, (1, block), 1)
    key_place = key_start + lax.broadcasted_iota(jnp.int32, (block, 1), 0)
    return (key_place <= query_place) & (key_place >= doc_line)


def attend_kernel(
    heads, block, key_blocks, meta, doc_ref, q_ref, k_ref, vt_ref, o_ref, lse_ref, *refs
):
    ob_refs, (m_ref, l_ref) = refs[:-2], refs[-2:]
    step = pl.program_id(0)
    steps = len(ob_refs)
    query_start = meta[step]
    doc_first, doc_last = meta[steps + key_blocks + step], meta[2 * steps + key_blocks + step]
    doc_line = doc_ref[...]
    size = o_ref.shape[0] // heads
    lanes = q_ref.shape[0] // heads
    m_ref[...] = jnp.full_like(m_ref, big_negative)
    l_ref[...] = jnp.zeros_like(l_ref)
    o_ref[...] = jnp.zeros_like(o_ref)

    def fold(slot, allowed):
        span = pl.ds(pl.multiple_of(slot * block, block), block)
        scores = [
            nn_dot(
                k_ref[span, head * lanes : (head + 1) * lanes],
                q_ref[head * lanes : (head + 1) * lanes, :],
            )
            for head in range(heads)
        ]
        if allowed is not None:
            scores = [jnp.where(allowed, part, big_negative) for part in scores]
        for head in range(heads):
            rows = slice(head * size, (head + 1) * size)
            old_peak = m_ref[head]
            new_peak = jnp.maximum(old_peak, jnp.max(scores[head], axis=0, keepdims=True))
            weights = jnp.exp(scores[head] - new_peak)
            fade = jnp.exp(old_peak - new_peak)
            m_ref[head] = new_peak
            l_ref[head] = l_ref[head] * fade + jnp.sum(weights, axis=0, keepdims=True)
            o_ref[rows, :] = o_ref[rows, :] * fade + nn_dot(
                vt_ref[rows, span], weights.astype(jnp.bfloat16)
            )

    def body(slot, carry):
        key_start = meta[steps + slot]
        live = (key_start <= query_start) & (key_start + block > doc_first)
        full = (key_start < query_start) & (key_start >= doc_last)

        @pl.when(full)
        def _():
            fold(slot, None)

        @pl.when(live & jnp.logical_not(full))
        def _():
            fold(slot, pair_mask(query_start, key_start, doc_line, block))

        return carry

    lax.fori_loop(0, key_blocks, body, 0)
    for head in range(heads):
        rows = slice(head * size, (head + 1) * size)
        total = l_ref[head]
        mixed = o_ref[rows, :] / total
        o_ref[rows, :] = mixed
        lse_ref[head] = m_ref[head] + jnp.log(total)
    for index, ob_ref in enumerate(ob_refs):

        @pl.when(step == index)
        def _(ob_ref=ob_ref):
            ob_ref[...] = o_ref[...].astype(jnp.bfloat16)


def attend_back_kernel(
    heads,
    block,
    key_blocks,
    scale,
    meta,
    doc_ref,
    q_ref,
    o_ref,
    lse_ref,
    k_ref,
    kt_ref,
    v_ref,
    *refs,
):
    g_refs = refs[:-7]
    dq_ref, mine_ref, other_ref, acc_ref, pair_ref, delta_ref, g_ref = refs[-7:]
    step = pl.program_id(0)
    steps = len(g_refs)
    for index, grad_ref in enumerate(g_refs):

        @pl.when(step == index)
        def _(grad_ref=grad_ref):
            g_ref[...] = grad_ref[...]

    query_start = meta[step]
    doc_first, doc_last = meta[steps + key_blocks + step], meta[2 * steps + key_blocks + step]
    doc_line = doc_ref[...]
    size = g_ref.shape[0] // heads
    lanes = q_ref.shape[0] // heads
    share = g_ref.shape[0]

    @pl.when(step == 0)
    def _():
        pair_ref[...] = jnp.zeros_like(pair_ref)

    acc_ref[...] = jnp.zeros_like(acc_ref)
    for head in range(heads):
        rows = slice(head * size, (head + 1) * size)
        delta_ref[head] = jnp.sum(
            g_ref[rows, :].astype(jnp.float32) * o_ref[rows, :], axis=0, keepdims=True
        )

    def fold(slot, allowed):
        span = pl.ds(pl.multiple_of(slot * block, block), block)
        probs, grad_scores = [], []
        for head in range(heads):
            wide_rows = slice(head * lanes, (head + 1) * lanes)
            rows = slice(head * size, (head + 1) * size)
            probs.append(nn_dot(k_ref[span, wide_rows], q_ref[wide_rows, :]))
            grad_scores.append(
                nn_dot(v_ref[span, head * lanes : head * lanes + size], g_ref[rows, :])
            )
        for head in range(heads):
            part = jnp.exp(probs[head] - lse_ref[head])
            if allowed is not None:
                part = jnp.where(allowed, part, 0.0)
            grad_scores[head] = (part * (grad_scores[head] - delta_ref[head])).astype(jnp.bfloat16)
            probs[head] = part.astype(jnp.bfloat16)
        for head in range(heads):
            rows = slice(head * size, (head + 1) * size)
            value_rows = slice(share + head * size, share + (head + 1) * size)
            query_rows = slice(head * lanes, head * lanes + size)
            pair_ref[value_rows, span] += nt_dot(g_ref[rows, :], probs[head])
            pair_ref[rows, span] += nt_dot(q_ref[query_rows, :], grad_scores[head])
            acc_ref[rows, :] += nn_dot(kt_ref[rows, span], grad_scores[head])

    def body(slot, carry):
        key_start = meta[steps + slot]
        live = (key_start <= query_start) & (key_start + block > doc_first)
        full = (key_start < query_start) & (key_start >= doc_last)

        @pl.when(full)
        def _():
            fold(slot, None)

        @pl.when(live & jnp.logical_not(full))
        def _():
            fold(slot, pair_mask(query_start, key_start, doc_line, block))

        return carry

    lax.fori_loop(0, key_blocks, body, 0)
    dq_ref[...] = (acc_ref[...] * scale).astype(dq_ref.dtype)

    @pl.when(step == steps - 1)
    def _():
        half = mine_ref.shape[1]
        mine_ref[...] = pair_ref[:, :half]
        other_ref[...] = pair_ref[:, half:].astype(jnp.bfloat16)


def whole(shape):
    return pl.BlockSpec(shape, lambda *index: (0,) * len(shape))


def attend(meta, doc_line, q_ext, k_ext, v_t, heads, block):
    wide, queries = q_ext.shape
    share, keys = v_t.shape
    steps, key_blocks = queries // block, keys // block
    return pl.pallas_call(
        partial(attend_kernel, heads, block, key_blocks),
        grid_spec=pltpu.PrefetchScalarGridSpec(
            num_scalar_prefetch=1,
            grid=(steps,),
            in_specs=[
                pl.BlockSpec((1, block), lambda i, meta: (0, i)),
                pl.BlockSpec((wide, block), lambda i, meta: (0, i)),
                pl.BlockSpec(memory_space=pltpu.VMEM),
                pl.BlockSpec(memory_space=pltpu.VMEM),
            ],
            out_specs=[
                pl.BlockSpec((share, block), lambda i, meta: (0, i)),
                pl.BlockSpec((heads, 1, block), lambda i, meta: (0, 0, i)),
            ]
            + [whole((share, block))] * steps,
            scratch_shapes=[
                pltpu.VMEM((heads, 1, block), jnp.float32),
                pltpu.VMEM((heads, 1, block), jnp.float32),
            ],
        ),
        out_shape=[
            jax.ShapeDtypeStruct((share, queries), jnp.float32),
            jax.ShapeDtypeStruct((heads, 1, queries), jnp.float32),
        ]
        + [jax.ShapeDtypeStruct((share, block), jnp.bfloat16)] * steps,
        compiler_params=pltpu.CompilerParams(vmem_limit_bytes=12 << 20),
        cost_estimate=NO_COST,
        name="attend",
    )(meta, doc_line, q_ext, k_ext, v_t)


def attend_back(meta, doc_line, q_ext, grad_t, mixed, lse, k_ext, k_t, v_ext, heads, block, scale):
    wide, queries = q_ext.shape
    share, keys = k_t.shape
    steps, key_blocks = queries // block, keys // block
    return pl.pallas_call(
        partial(attend_back_kernel, heads, block, key_blocks, scale),
        grid_spec=pltpu.PrefetchScalarGridSpec(
            num_scalar_prefetch=1,
            grid=(steps,),
            in_specs=[
                pl.BlockSpec((1, block), lambda i, meta: (0, i)),
                pl.BlockSpec((wide, block), lambda i, meta: (0, i)),
                pl.BlockSpec((share, block), lambda i, meta: (0, i)),
                pl.BlockSpec((heads, 1, block), lambda i, meta: (0, 0, i)),
                pl.BlockSpec(memory_space=pltpu.VMEM),
                pl.BlockSpec(memory_space=pltpu.VMEM),
                pl.BlockSpec(memory_space=pltpu.VMEM),
            ]
            + [whole((share, block))] * steps,
            out_specs=[
                pl.BlockSpec((share, block), lambda i, meta: (0, i)),
                whole((2 * share, keys // 2)),
                whole((2 * share, keys // 2)),
            ],
            scratch_shapes=[
                pltpu.VMEM((share, block), jnp.float32),
                pltpu.VMEM((2 * share, keys), jnp.float32),
                pltpu.VMEM((heads, 1, block), jnp.float32),
                pltpu.VMEM((share, block), jnp.bfloat16),
            ],
        ),
        out_shape=[
            jax.ShapeDtypeStruct((share, queries), jnp.bfloat16),
            jax.ShapeDtypeStruct((2 * share, keys // 2), jnp.float32),
            jax.ShapeDtypeStruct((2 * share, keys // 2), jnp.bfloat16),
        ],
        compiler_params=pltpu.CompilerParams(vmem_limit_bytes=20 << 20),
        cost_estimate=NO_COST,
        name="attend_back",
    )(meta, doc_line, q_ext, mixed, lse, k_ext, k_t, v_ext, *grad_t)


def join_kernel(chips, unused, dq_ref, mine_ref, other_ref, *out_refs):
    share = dq_ref.shape[0]
    block = dq_ref.shape[1] // chips
    for step in range(chips):
        span = slice(step * block, (step + 1) * block)
        pair = (mine_ref[:, span] + other_ref[:, span].astype(jnp.float32)).astype(jnp.bfloat16)
        out_refs[step][:share, :] = dq_ref[:, span]
        out_refs[step][share:, :] = pair


def join_parts(scalars, dq, mine, other, chips):
    rows, block = dq.shape[0] + mine.shape[0], dq.shape[1] // chips
    return call_whole(
        partial(join_kernel, chips),
        [jax.ShapeDtypeStruct((rows, block), jnp.bfloat16)] * chips,
        "join",
        scalars,
        dq,
        mine,
        other,
    )


def head_grads_kernel(chips, per, unused, *refs):
    normed, grads = refs[:chips], refs[chips : 2 * chips]
    wq_ref, wk_ref, wv_ref, gain_ref, inner_ref, feed_ref, hidden_ref = refs[2 * chips : 2 * chips + 7]
    perm_ref, row_ref, lane_ref, keep_ref, send_ref = refs[2 * chips + 7 :]
    share, model_width = wq_ref.shape
    own = nn_dot(grads[0][...], normed[0][...])
    for step in range(1, chips):
        own = own + nn_dot(grads[step][...], normed[step][...])
    attend = jnp.zeros((1, model_width), jnp.float32)
    for index, weight in enumerate((wq_ref, wk_ref, wv_ref)):
        part = own[index * share : (index + 1) * share] * weight[...].astype(jnp.float32)
        attend = attend + jnp.sum(part, axis=0, keepdims=True)
    gains = jnp.concatenate(
        [attend / gain_ref[...], inner_ref[...], feed_ref[...], hidden_ref[...]], axis=1
    )
    gains = (row_ref[...].astype(jnp.float32) * gains).astype(jnp.bfloat16)
    gains = nn_dot(gains, lane_ref[...]).astype(jnp.bfloat16)
    own = nt_dot(perm_ref[...], own.astype(jnp.bfloat16))
    chunks, _, width = keep_ref.shape
    columns = own.shape[1]
    gain_rows = gains.shape[0] // (2 * chunks)
    for which, target in enumerate((keep_ref, send_ref)):
        target[:, :, columns:] = jnp.zeros((chunks, per, width - columns), jnp.bfloat16)
        for chunk in range(chunks):
            place = which * chunks + chunk
            rows = slice(place * per, (place + 1) * per)
            target[chunk, :, :columns] = own[rows].astype(jnp.bfloat16)
            target[chunk, :gain_rows, width - 128 :] = gains[
                place * gain_rows : (place + 1) * gain_rows
            ]


def head_grads(scalars, normed, grads, weights, gain, late_gains, perm, where_row, where_lane, per):
    width = perm.shape[0]
    out = jax.ShapeDtypeStruct((width // (2 * per), per, width), jnp.bfloat16)
    return call_whole(
        partial(head_grads_kernel, len(grads), per),
        [out, out],
        "head_grads",
        scalars,
        *normed,
        *grads,
        *weights,
        gain,
        *late_gains,
        perm,
        where_row,
        where_lane,
        limit=24,
    )


def norm_parts(values):
    shifted = values - jnp.mean(values, axis=-1, keepdims=True)
    rate = lax.rsqrt(jnp.mean(shifted * shifted, axis=-1, keepdims=True) + 1e-05)
    return shifted * rate, rate


def norm_back(grad, hat, rate, gain):
    scaled = grad * gain
    mean_scaled = jnp.mean(scaled, axis=-1, keepdims=True)
    mean_product = jnp.mean(scaled * hat, axis=-1, keepdims=True)
    return (
        rate * (scaled - mean_scaled - hat * mean_product),
        jnp.sum(grad * hat, axis=0, keepdims=True),
    )


def middle_kernel(chips, tiles, position, *refs):
    mixed = refs[:chips]
    tokens_ref, cot_ref, wout_ref, wup_ref, wdown_ref, ginner_ref, gfeed_ref, ghidden_ref = refs[
        chips : chips + 8
    ]
    result_ref, gmid_ref, gmid_b_ref = refs[chips + 8 : chips + 11]
    go_refs = refs[chips + 11 : 2 * chips + 11]
    (
        z_ref,
        h2_ref,
        bent_out,
        pre_out,
        dinner_ref,
        dfeed_ref,
        dhidden_ref,
        swap_ref,
        work_ref,
        column_ref,
        zhat_ref,
        hat_ref,
        act_ref,
        slope_ref,
        dact_ref,
        acc_ref,
        stat_ref,
    ) = refs[2 * chips + 11 :]
    step = pl.program_id(0)
    chip = position[0]
    block, model_width = tokens_ref.shape
    share = model_width // chips
    tile = wdown_ref.shape[0]
    hidden = tile * tiles
    root = math.sqrt(2.0 / math.pi)
    phase, index = step // tiles, step % tiles
    lanes = stat_ref.shape[2]
    groups = tile // lanes

    def by_rows(body):
        body(slice(None))

    def spread(stat):
        return jnp.concatenate([stat] * groups, axis=1)

    def gathered_lanes(values):
        total = values[:, :lanes]
        for group in range(1, groups):
            total = total + values[:, group * lanes : (group + 1) * lanes]
        return total

    def lane_sum(values):
        return jnp.broadcast_to(jnp.sum(values, axis=-1, keepdims=True), values.shape)

    def column_sums(values):
        total = values[:8]
        for first in range(8, values.shape[0], 8):
            total = total + values[first : first + 8]
        return total

    def norm_rows(values):
        shifted = values - spread(lane_sum(gathered_lanes(values)) / tile)
        rate = lax.rsqrt(lane_sum(gathered_lanes(shifted * shifted)) / tile + 1e-05)
        return shifted * spread(rate), rate

    def norm_rows_back(grad, hat, rate, gain):
        scaled = grad * gain
        mean_scaled = lane_sum(gathered_lanes(scaled)) / tile
        mean_product = lane_sum(gathered_lanes(scaled * hat)) / tile
        return spread(rate) * (scaled - spread(mean_scaled) - hat * spread(mean_product))

    @pl.when(step == 0)
    def _():
        for near in range(chips):
            start = pl.multiple_of(share * lax.rem(chip + near, chips), share)
            swap_ref[pl.ds(start, share), :] = mixed[near][...].astype(jnp.float32)
        work_ref[...] = swap_ref[...].T

        def first_norm(rows):
            zhat, zrate = norm_rows(work_ref[rows, :])
            zhat_ref[rows, :] = zhat
            stat_ref[0, rows, :] = zrate
            z_ref[rows, :] = (zhat * ginner_ref[...]).astype(jnp.bfloat16)

        by_rows(first_norm)
        work_ref[...] = nn_dot(z_ref[...], wout_ref[...])

        def second_norm(rows):
            mid = tokens_ref[rows, :].astype(jnp.float32) + work_ref[rows, :]
            acc_ref[rows, :] = mid
            hat, rate = norm_rows(mid)
            hat_ref[rows, :] = hat
            stat_ref[1, rows, :] = rate
            h2_ref[rows, :] = (hat * gfeed_ref[...]).astype(jnp.bfloat16)

        by_rows(second_norm)
        for stat in range(3, 7):
            stat_ref[stat] = jnp.zeros_like(stat_ref[stat])

    @pl.when(phase == 0)
    def _():
        work_ref[...] = nn_dot(h2_ref[...], wup_ref[...])

        def bend_rows(rows):
            u = work_ref[rows, :]
            squared = u * u
            bend = jnp.tanh(root * (u + 0.044715 * u * squared))
            act_ref[index, rows, :] = 0.5 * u * (1.0 + bend)
            slope_ref[index, rows, :] = 0.5 * (1.0 + bend) + 0.5 * u * (1.0 - bend * bend) * root * (
                1.0 + 3.0 * 0.044715 * squared
            )

        by_rows(bend_rows)

        @pl.when(index == 0)
        def _():
            def pivot(rows):
                stat_ref[2, rows, :] = lane_sum(gathered_lanes(act_ref[0, rows, :])) / tile

            by_rows(pivot)

        def sums(rows):
            off = act_ref[index, rows, :] - spread(stat_ref[2, rows, :])
            stat_ref[3, rows, :] += gathered_lanes(off)
            stat_ref[4, rows, :] += gathered_lanes(off * off)

        by_rows(sums)

    @pl.when(step == tiles)
    def _():
        drift = lane_sum(stat_ref[3]) / hidden
        stat_ref[2] = stat_ref[2] + drift
        stat_ref[4] = lax.rsqrt(
            jnp.maximum(lane_sum(stat_ref[4]) / hidden - drift * drift, 0.0) + 1e-05
        )

    @pl.when(phase == 1)
    def _():
        def hidden_rows(rows):
            hat = (act_ref[index, rows, :] - spread(stat_ref[2, rows, :])) * spread(
                stat_ref[4, rows, :]
            )
            act_ref[index, rows, :] = hat
            bent_out[rows, :] = (hat * ghidden_ref[...]).astype(jnp.bfloat16)

        by_rows(hidden_rows)
        work_ref[...] = nt_dot(cot_ref[...], wdown_ref[...])
        acc_ref[...] += nn_dot(bent_out[...], wdown_ref[...])
        column_ref[...] = jnp.zeros_like(column_ref)

        def grad_rows(rows):
            hat, grad = act_ref[index, rows, :], work_ref[rows, :]
            column_ref[...] += column_sums(grad * hat)
            scaled = grad * ghidden_ref[...]
            dact_ref[index, rows, :] = scaled
            stat_ref[5, rows, :] += gathered_lanes(scaled)
            stat_ref[6, rows, :] += gathered_lanes(scaled * hat)

        by_rows(grad_rows)
        dhidden_ref[...] = jnp.sum(column_ref[...], axis=0, keepdims=True)

    @pl.when(step == 2 * tiles)
    def _():
        result_ref[...] = acc_ref[...].astype(jnp.bfloat16)
        acc_ref[...] = jnp.zeros_like(acc_ref)
        stat_ref[5] = lane_sum(stat_ref[5]) / hidden
        stat_ref[6] = lane_sum(stat_ref[6]) / hidden

    @pl.when(phase == 2)
    def _():
        def pre_rows(rows):
            inner = (
                dact_ref[index, rows, :]
                - spread(stat_ref[5, rows, :])
                - act_ref[index, rows, :] * spread(stat_ref[6, rows, :])
            )
            pre_out[rows, :] = (
                spread(stat_ref[4, rows, :]) * inner * slope_ref[index, rows, :]
            ).astype(jnp.bfloat16)

        by_rows(pre_rows)
        acc_ref[...] += nt_dot(pre_out[...], wup_ref[...])

    @pl.when(step == 3 * tiles - 1)
    def _():
        column_ref[...] = jnp.zeros_like(column_ref)

        def middle_rows(rows):
            grad, hat = acc_ref[rows, :], hat_ref[rows, :]
            column_ref[...] += column_sums(grad * hat)
            gmid = cot_ref[rows, :].astype(jnp.float32) + norm_rows_back(
                grad, hat, stat_ref[1, rows, :], gfeed_ref[...]
            )
            gmid_ref[rows, :] = gmid
            gmid_b_ref[rows, :] = gmid.astype(jnp.bfloat16)

        by_rows(middle_rows)
        dfeed_ref[...] = jnp.sum(column_ref[...], axis=0, keepdims=True)
        work_ref[...] = nt_dot(gmid_b_ref[...], wout_ref[...])
        column_ref[...] = jnp.zeros_like(column_ref)

        def inner_rows(rows):
            grad, hat = work_ref[rows, :], zhat_ref[rows, :]
            column_ref[...] += column_sums(grad * hat)
            work_ref[rows, :] = norm_rows_back(grad, hat, stat_ref[0, rows, :], ginner_ref[...])

        by_rows(inner_rows)
        dinner_ref[...] = jnp.sum(column_ref[...], axis=0, keepdims=True)
        swap_ref[...] = work_ref[...].T
        for near in range(chips):
            start = pl.multiple_of(share * lax.rem(chip + near, chips), share)
            go_refs[near][...] = swap_ref[pl.ds(start, share), :].astype(jnp.bfloat16)


def middle(position, mixed, tokens, cotangent, w_out, w_up, w_down, gains):
    chips = len(mixed)
    block, model_width = tokens.shape
    hidden = w_up.shape[1]
    tile = model_width
    tiles = hidden // tile
    share = model_width // chips
    last = tiles - 1

    def up_index(i, pos):
        return (0, jnp.where(i < tiles, i, jnp.where(i < 2 * tiles, last, i - 2 * tiles)))

    def down_index(i, pos):
        return (jnp.clip(i - tiles, 0, last), 0)

    def hidden_index(i, pos):
        return (0, jnp.clip(i - tiles, 0, last))

    def pre_index(i, pos):
        return (0, jnp.clip(i - 2 * tiles, 0, last))

    def f32(*shape):
        return pltpu.VMEM(shape, jnp.float32)

    row, rows = (1, model_width), (block, model_width)
    narrow = jax.ShapeDtypeStruct(rows, jnp.bfloat16)
    return pl.pallas_call(
        partial(middle_kernel, chips, tiles),
        grid_spec=pltpu.PrefetchScalarGridSpec(
            num_scalar_prefetch=1,
            grid=(3 * tiles,),
            in_specs=[whole((share, block))] * chips
            + [
                whole(rows),
                whole(rows),
                whole((model_width, model_width)),
                pl.BlockSpec((model_width, tile), up_index),
                pl.BlockSpec((tile, model_width), down_index),
                whole(row),
                whole(row),
                pl.BlockSpec((1, tile), hidden_index),
            ],
            out_specs=[whole(rows)] * 3
            + [whole((share, block))] * chips
            + [
                whole(rows),
                whole(rows),
                pl.BlockSpec((block, tile), hidden_index),
                pl.BlockSpec((block, tile), pre_index),
                whole(row),
                whole(row),
                pl.BlockSpec((1, tile), hidden_index),
            ],
            scratch_shapes=[
                f32(model_width, block),
                f32(block, tile),
                f32(8, tile),
                f32(block, model_width),
                f32(block, model_width),
                f32(tiles, block, tile),
                f32(tiles, block, tile),
                f32(tiles, block, tile),
                f32(block, model_width),
                f32(7, block, 128),
            ],
        ),
        out_shape=[narrow, jax.ShapeDtypeStruct(rows, jnp.float32), narrow]
        + [jax.ShapeDtypeStruct((share, block), jnp.bfloat16)] * chips
        + [
            narrow,
            narrow,
            jax.ShapeDtypeStruct((block, hidden), jnp.bfloat16),
            jax.ShapeDtypeStruct((block, hidden), jnp.bfloat16),
            jax.ShapeDtypeStruct(row, jnp.float32),
            jax.ShapeDtypeStruct(row, jnp.float32),
            jax.ShapeDtypeStruct((1, hidden), jnp.float32),
        ],
        compiler_params=pltpu.CompilerParams(vmem_limit_bytes=36 << 20),
        cost_estimate=NO_COST,
        name="middle",
    )(position, *mixed, tokens, cotangent, w_out, w_up, w_down, *gains)


def down_kernel(per, position, bent_ref, cot_ref, keep_ref, send_ref):
    first_core = position[1] == 0
    grad = lax.dot_general(
        bent_ref[...], cot_ref[...], (((0,), (0,)), ((), ())), preferred_element_type=jnp.float32
    ).astype(jnp.bfloat16)
    for part in range(keep_ref.shape[0]):
        even = grad[2 * per * part : 2 * per * part + per]
        odd = grad[2 * per * part + per : 2 * per * (part + 1)]
        keep_ref[part] = jnp.where(first_core, even, odd)
        send_ref[part] = jnp.where(first_core, odd, even)


def down_grad(position, bent, cotangent, per):
    (block, hidden), model_width = bent.shape, cotangent.shape[1]
    tiles, chunks = hidden // model_width, hidden // (2 * per)
    out = jax.ShapeDtypeStruct((chunks, per, model_width), jnp.bfloat16)
    out_spec = pl.BlockSpec((chunks // tiles, per, model_width), lambda i, pos: (i, 0, 0))
    return pl.pallas_call(
        partial(down_kernel, per),
        grid_spec=pltpu.PrefetchScalarGridSpec(
            num_scalar_prefetch=1,
            grid=(tiles,),
            in_specs=[
                pl.BlockSpec((block, model_width), lambda i, pos: (0, i)),
                whole(cotangent.shape),
            ],
            out_specs=[out_spec, out_spec],
        ),
        out_shape=[out, out],
        compiler_params=pltpu.CompilerParams(vmem_limit_bytes=20 << 20),
        cost_estimate=NO_COST,
        name="down_grad",
    )(position, bent, cotangent)


def up_out_kernel(tiles, position, h2_ref, pre_ref, z_ref, gmid_ref, perm_ref, keep_ref, send_ref, left_ref):
    step = pl.program_id(0)
    chunks, per = keep_ref.shape[:2]

    @pl.when(step == 0)
    def _():
        left_ref[...] = nt_dot(perm_ref[...], h2_ref[...]).astype(jnp.bfloat16)

    def store(right):
        grad = nn_dot(left_ref[...], right)
        for chunk in range(chunks):
            keep_ref[chunk] = grad[chunk * per : (chunk + 1) * per].astype(jnp.bfloat16)
            first = (chunks + chunk) * per
            send_ref[chunk] = grad[first : first + per].astype(jnp.bfloat16)

    @pl.when(step < tiles)
    def _():
        store(pre_ref[...])

    @pl.when(step == tiles)
    def _():
        left_ref[...] = nt_dot(perm_ref[...], z_ref[...]).astype(jnp.bfloat16)
        store(gmid_ref[...])


def up_out_grad(position, h2, pre, z, gmid, perm, per):
    (block, hidden), model_width = pre.shape, h2.shape[1]
    tiles, chunks = hidden // model_width, model_width // (2 * per)
    out = jax.ShapeDtypeStruct((chunks, per * (tiles + 1), model_width), jnp.bfloat16)
    out_spec = pl.BlockSpec((chunks, per, model_width), lambda i, pos: (0, i, 0))
    return pl.pallas_call(
        partial(up_out_kernel, tiles),
        grid_spec=pltpu.PrefetchScalarGridSpec(
            num_scalar_prefetch=1,
            grid=(tiles + 1,),
            in_specs=[
                whole(h2.shape),
                pl.BlockSpec((block, model_width), lambda i, pos: (0, jnp.minimum(i, tiles - 1))),
                whole(z.shape),
                whole(gmid.shape),
                whole(perm.shape),
            ],
            out_specs=[out_spec, out_spec],
            scratch_shapes=[pltpu.VMEM((model_width, block), jnp.bfloat16)],
        ),
        out_shape=[out, out],
        compiler_params=pltpu.CompilerParams(vmem_limit_bytes=20 << 20),
        cost_estimate=NO_COST,
        name="up_out_grad",
    )(position, h2, pre, z, gmid, perm)


def final_kernel(chips, position, *refs):
    homes = refs[:chips]
    (
        tokens_ref,
        gmid_ref,
        wq_ref,
        wk_ref,
        wv_ref,
        gain_ref,
        out_ref,
        swap_ref,
    ) = refs[chips:]
    chip = position[0]
    block, model_width = tokens_ref.shape
    share = model_width // chips
    total = jnp.zeros((block, model_width), jnp.float32)
    for index, weight in enumerate((wq_ref, wk_ref, wv_ref)):
        for near in range(chips):
            start = pl.multiple_of(share * lax.rem(chip + near, chips), share)
            swap_ref[pl.ds(start, share), :] = homes[near][
                index * share : (index + 1) * share, :
            ].astype(jnp.float32)
        total = total + nt_dot(swap_ref[...].T.astype(jnp.bfloat16), weight[...])
    hat, rate = norm_parts(tokens_ref[...].astype(jnp.float32))
    back = norm_back(total, hat, rate, gain_ref[...])[0]
    out_ref[...] = (gmid_ref[...] + back).astype(jnp.bfloat16)


def final(position, homes, tokens, gmid, w_query, w_key, w_value, gain):
    block, model_width = tokens.shape
    return call_whole(
        partial(final_kernel, len(homes)),
        [jax.ShapeDtypeStruct((block, model_width), jnp.bfloat16)],
        "final",
        position,
        *homes,
        tokens,
        gmid,
        w_query,
        w_key,
        w_value,
        gain,
        scratch=[pltpu.VMEM((model_width, block), jnp.float32)],
    )[0]


def chip_shift(value, steps):
    count = lax.axis_size("seq")
    return lax.ppermute(value, "seq", [(i, (i + 2 * steps) % count) for i in range(count)])


def seq_swap(value, bit):
    return lax.ppermute(value, "seq", [(i, i ^ bit) for i in range(lax.axis_size("seq"))])


def row_swap(value, bit):
    return lax.ppermute(value, "row", [(i, i ^ bit) for i in range(lax.axis_size("row"))])


def sent(array):
    return array.astype(jnp.bfloat16)


def wide(array):
    return array.astype(jnp.float32)


def low_part(shape, keep):
    def index(i, bits):
        return (0, bits[2] if keep else 1 - bits[2], 0, 0, 0)

    return pl.BlockSpec((2, 1, shape[2] // 2) + shape[3:], index)


def high_part(shape, keep):
    def index(i, bits):
        return (bits[3] if keep else 1 - bits[3], 0, 1, 0, 0)

    return pl.BlockSpec((1, 2, shape[2] // 2) + shape[3:], index)


def outgoing_kernel(scalars, low_a, low_b, high_a, high_b, low_ref, high_ref):
    low_ref[...] = sent(wide(low_a[:, 0]) + wide(low_b[:, 0]))
    high_ref[...] = sent(wide(high_a[0]) + wide(high_b[0]))


def outgoing(scalars, keep, other, kept=False):
    shape = keep.shape
    out = jax.ShapeDtypeStruct((2, shape[2] // 2) + shape[3:], jnp.bfloat16)
    low, high = low_part(shape, kept), high_part(shape, kept)
    return call_whole(
        outgoing_kernel,
        [out, out],
        "kept" if kept else "outgoing",
        scalars,
        keep,
        other,
        keep,
        other,
        in_specs=[low, low, high, high],
    )


def halfway_kernel(groups, scalars, *refs):
    ins, outs = refs[: 4 * groups], refs[4 * groups :]
    low_bit, high_bit = scalars[2], scalars[3]
    low_keep, low_send, high_keep, high_send = outs
    first = 0
    for group in range(groups):
        low, high, low_in, high_in = ins[4 * group : 4 * group + 4]
        rows = slice(first, first + low.shape[2])
        for target, side in ((low_keep, high_bit), (low_send, 1 - high_bit)):
            target[:, rows] = sent(wide(low[side]) + wide(low_in[side]))
        for target, side in ((high_keep, low_bit), (high_send, 1 - low_bit)):
            target[:, rows] = sent(wide(high[side]) + wide(high_in[side]))
        first += low.shape[2]


def halfway(scalars, groups):
    arrays = [array for group in groups for array in group]
    rows = sum(group[0].shape[2] for group in groups)
    out = jax.ShapeDtypeStruct((arrays[0].shape[1], rows, arrays[0].shape[3]), jnp.bfloat16)
    return call_whole(
        partial(halfway_kernel, len(groups)), [out] * 4, "halfway", scalars, *arrays, limit=24
    )


def split_kernel(chips, groups, scalars, *refs):
    ins, outs = refs[: 4 * groups], refs[4 * groups : 4 * groups + chips]
    all_ref = refs[-1]
    half = chips // 2
    first = 0
    for group in range(groups):
        low_keep, low_in, high_keep, high_in = ins[4 * group : 4 * group + 4]
        rows = slice(first, first + low_in.shape[1])
        all_ref[:half, rows] = sent(wide(low_keep[...]) + wide(low_in[...]))
        all_ref[half:, rows] = sent(wide(high_keep[...]) + wide(high_in[...]))
        first += low_in.shape[1]
    for step in range(chips):
        outs[step][...] = all_ref[lax.rem(scalars[0] + step, chips)]


def split(scalars, groups, chips):
    arrays = [array for group in groups for array in group]
    rows = sum(group[0].shape[1] for group in groups)
    width = arrays[0].shape[2]
    return call_whole(
        partial(split_kernel, chips, len(groups)),
        [jax.ShapeDtypeStruct((rows, width), jnp.bfloat16)] * chips,
        "split",
        scalars,
        *arrays,
        scratch=[pltpu.VMEM((chips, rows, width), jnp.bfloat16)],
    )


def lay_flat(target, values, first, step):
    for piece in range(values.shape[1] // 128):
        target[pl.ds(first + piece, values.shape[0], step), :] = values[
            :, 128 * piece : 128 * (piece + 1)
        ]


def finish_kernel(chips, per, share, factor, scalars, *refs):
    arrived, heads_in, refs = refs[:chips], refs[chips : 2 * chips], refs[chips:]
    down_ref, up_ref, out_ref, query_ref, key_ref, value_ref, gains_ref, heads_ref = refs[chips:]
    width = arrived[0].shape[1]
    chip, pieces = scalars[0], width // 128
    tiles = up_ref.shape[0] * 128 // (per * width)
    down_rows = down_ref.shape[0] * 128 // width

    def total(first, rows):
        result = wide(arrived[0][first : first + rows, :])
        for part in arrived[1:]:
            result = result + wide(part[first : first + rows, :])
        return result * factor

    lay_flat(down_ref, total(0, down_rows), 0, pieces)
    for tile in range(tiles):
        lay_flat(up_ref, total(down_rows + tile * per, per), tile * pieces, tiles * pieces)
    lay_flat(out_ref, total(down_rows + tiles * per, per), 0, pieces)
    gains = wide(heads_in[0][:8, -128:])
    for part in heads_in[1:]:
        gains = gains + wide(part[:8, -128:])
    gains_ref[...] = gains * factor
    for step in range(chips):
        heads_ref[lax.rem(chip - step + chips, chips)] = wide(heads_in[step][:, : 3 * share])
    for index, target in enumerate((query_ref, key_ref, value_ref)):
        values = jnp.concatenate(
            [heads_ref[near][:, index * share : (index + 1) * share] for near in range(chips)], axis=1
        )
        lay_flat(target, values * factor, 0, pieces)


def finish(scalars, arrived, hidden, parts, per, share, factor):
    chips, width = len(arrived) // 2, arrived[0].shape[1]
    square = jax.ShapeDtypeStruct((per * width // 128, 128), jnp.float32)
    large = jax.ShapeDtypeStruct((per * hidden // 128, 128), jnp.float32)
    return call_whole(
        partial(finish_kernel, chips, per, share, factor),
        [large, large, square, square, square, square, jax.ShapeDtypeStruct((8, 128), jnp.float32)],
        "finish",
        scalars,
        *arrived,
        scratch=[pltpu.VMEM((chips, per, 3 * share), jnp.float32)],
    )


def gathered(rows, chips, chip):
    if chips != 4:
        return [rows] + [chip_shift(rows, step) for step in range(1, chips)]
    behind, ahead = chip_shift(rows, 1), chip_shift(rows, -1)
    up = [(2 * i + core, 2 * i + 2 + core) for i in (1, 2) for core in (0, 1)]
    down = [(2 * i + core, 2 * i - 2 + core) for i in (1, 2) for core in (0, 1)]
    across = jnp.where(
        chip < 2, lax.ppermute(ahead, "seq", down), lax.ppermute(behind, "seq", up)
    )
    return [rows, behind, across, ahead]


def fast_local(
    tokens,
    lengths,
    w_query,
    w_key,
    w_value,
    w_out,
    w_up,
    w_down,
    gain_attend,
    gain_inner,
    gain_feed,
    gain_hidden,
    cotangent,
):
    block, model_width = tokens.shape
    hidden = w_up.shape[1]
    size = model_width // HEADS
    lanes = 2 * size
    scale = size ** (-0.5)
    seq_devices, row_devices = lax.axis_size("seq"), lax.axis_size("row")
    chips = seq_devices // 2
    heads = HEADS // chips
    share = heads * size
    spread = heads * lanes
    parts = row_devices * seq_devices
    position, row = lax.axis_index("seq"), lax.axis_index("row")
    chip, core = position // 2, position % 2
    place = jnp.stack([chip, core, row % 2, row // 2]).astype(jnp.int32)
    bounds = jnp.cumsum(lengths[0])[:-1]
    factor = 1.0 / math.sqrt(block * parts)

    normed_b = call_whole(
        norm_kernel,
        [jax.ShapeDtypeStruct(tokens.shape, jnp.bfloat16)],
        "norm",
        jnp.zeros((1,), jnp.int32),
        tokens,
        gain_attend[None, :],
    )[0]
    own = gathered(normed_b, chips, chip)

    chip_ids = (chip - jnp.arange(chips, dtype=jnp.int32)) % chips
    query_starts = block * (2 * chip_ids + core)
    key_starts = jnp.concatenate([query_starts, block * (2 * chip_ids + 1 - core)])
    in_block = jnp.arange(block, dtype=jnp.int32)[None, :]
    query_places = (query_starts[:, None] + in_block).reshape(-1)
    doc_line = jnp.max(jnp.where(bounds[:, None] <= query_places[None, :], bounds[:, None], 0), axis=0)
    meta = jnp.concatenate(
        [query_starts, key_starts, doc_line.reshape(chips, block)[:, 0], doc_line.reshape(chips, block)[:, -1]]
    )
    doc_line = doc_line[None, :]

    feature = jnp.arange(model_width, dtype=jnp.int32)
    wide_lane = jnp.arange(spread, dtype=jnp.int32)
    source = chip * share + wide_lane // lanes * size + wide_lane % lanes
    pick_wide = ((feature[:, None] == source[None, :]) & (wide_lane % lanes < size)[None, :]).astype(
        jnp.bfloat16
    )
    narrow = chip * share + jnp.arange(share, dtype=jnp.int32)
    pick_narrow = (feature[:, None] == narrow[None, :]).astype(jnp.bfloat16)

    def picked(weight, choice):
        return sent(nn_dot(weight, choice))

    def picked_rows(weight, choice):
        return sent(
            lax.dot_general(
                choice, weight, (((0,), (1,)), ((), ())), preferred_element_type=jnp.float32
            )
        )

    per = model_width // parts
    order = jnp.arange(model_width, dtype=jnp.int32)
    chunk, inside = order // per, order % per
    chunks = parts // 2
    parity = jnp.where(chunk < chunks, core, 1 - core)
    wanted = (2 * (chunk % chunks) + parity) * per + inside
    perm = (wanted[:, None] == feature[None, :]).astype(jnp.bfloat16)

    gains_share = (3 * model_width + hidden) // parts
    gains_rows = -(-gains_share // 128)
    line = jnp.arange(parts * gains_rows, dtype=jnp.int32)
    half_lines = parts // 2 * gains_rows
    line_parity = jnp.where(line < half_lines, core, 1 - core)
    owner = 2 * (line % half_lines // gains_rows) + line_parity
    first_gain = owner * gains_share + 128 * (line % gains_rows)
    end_gain = jnp.minimum(first_gain + 128, (owner + 1) * gains_share)
    gain_index = jnp.arange(gains_share * parts, dtype=jnp.int32)
    where_row = (
        (gain_index[None, :] >= first_gain[:, None]) & (gain_index[None, :] < end_gain[:, None])
    ).astype(jnp.bfloat16)
    where_lane = (
        (gain_index % gains_share % 128)[:, None] == jnp.arange(128, dtype=jnp.int32)[None, :]
    ).astype(jnp.bfloat16)
    early = (
        jnp.concatenate([query_starts, 2 * block * chip_ids + block * (1 - core), heads * chip[None]]),
        meta,
        doc_line,
        perm,
        picked_rows(w_query, pick_wide),
        picked(w_key, pick_wide),
        picked_rows(w_value, pick_narrow),
        picked_rows(w_key, pick_narrow),
        picked(w_value, pick_wide),
        picked_rows(w_query, pick_narrow),
        gain_attend[None, :],
        gain_inner[None, :],
        gain_feed[None, :],
        gain_hidden[None, :],
        place,
        where_row,
        where_lane,
    )
    own[1], early = lax.optimization_barrier((own[1], early))
    starts, meta, doc_line, perm, wq_wide, wk_wide, wv_rows, wk_rows, wv_wide, wq_rows = early[:10]
    gain_first, gain_inner, gain_feed, gain_hidden, place = early[10:15]
    where_row, where_lane = early[15:]
    sibling = [seq_swap(rows, 1) for rows in own]
    q_ext, k_ext, v_t = project(
        starts,
        own + sibling,
        wq_wide,
        wk_wide,
        wv_rows,
        chips,
        heads,
        scale,
    )
    mixed, lse, *mixed_b = attend(meta, doc_line, q_ext, k_ext, v_t, heads, block)
    mixed_b, wk_rows = lax.optimization_barrier((mixed_b, wk_rows))
    k_t, v_ext = project_back(place, own + sibling, wk_rows, wv_wide)
    back = [mixed_b[0]] + [chip_shift(mixed_b[step], -step) for step in range(1, chips)]
    back, k_t, v_ext = lax.optimization_barrier((back, k_t, v_ext))
    outs = middle(
        place, back, tokens, cotangent, w_out, w_up, w_down, (gain_inner, gain_feed, gain_hidden)
    )
    result, grad_middle, gmid_b = outs[:3]
    go = outs[3 : 3 + chips]
    z, h2, bent, pre, dinner, dfeed, dhidden = outs[3 + chips :]
    go = [go[0]] + [chip_shift(go[step], step) for step in range(1, chips)]
    keep_a, send_a = down_grad(place, bent, cotangent, hidden // parts)
    keep_b, send_b = up_out_grad(place, h2, pre, z, gmid_b, perm, per)


    def gridded(array):
        return array.reshape((2, 2, chips) + array.shape[1:])

    keep_a, other_a = gridded(keep_a), gridded(seq_swap(send_a, 1))
    other_b = seq_swap(send_b, 1)
    arrived_place = after(place, [*go, keep_b], HIGH_COST)
    out_a = outgoing(arrived_place, keep_a, other_a)
    kept_a = outgoing(arrived_place, keep_a, other_a, True)
    go, out_a, kept_a, keep_b, send_b = lax.optimization_barrier(
        (go, out_a, kept_a, keep_b, send_b)
    )
    in_a = [row_swap(out_a[0], 1), row_swap(out_a[1], 2)]
    dq, pair, other = attend_back(
        meta, doc_line, q_ext, go, mixed, lse, k_ext, k_t, v_ext, heads, block, scale
    )
    dq, pair, other, in_a, keep_b, other_b = lax.optimization_barrier(
        (dq, pair, other, in_a, keep_b, other_b)
    )
    keep_b, other_b = gridded(keep_b), gridded(other_b)
    out_b = outgoing(place, keep_b, other_b)
    in_b = [row_swap(out_b[0], 1), row_swap(out_b[1], 2)]
    grads = join_parts(place, dq, pair, seq_swap(other, 1), chips)
    home = [grads[0]] + [chip_shift(grads[step], -step) for step in range(1, chips)]
    grads, keep_b, other_b = lax.optimization_barrier((grads, keep_b, other_b))
    kept_b = outgoing(place, keep_b, other_b, True)
    mine_grad, send_grad = head_grads(
        place,
        own,
        grads,
        (wq_rows, wk_rows, wv_rows),
        gain_first,
        (dinner, dfeed, dhidden),
        perm,
        where_row,
        where_lane,
        per,
    )
    in_a, in_b, kept_a, kept_b, mine_grad, send_grad = lax.optimization_barrier(
        (in_a, in_b, kept_a, kept_b, mine_grad, send_grad)
    )
    low_keep, low_send, high_keep, high_send = halfway(place, [(*kept_a, *in_a), (*kept_b, *in_b)])
    low_in, high_in = row_swap(low_send, 2), row_swap(high_send, 1)
    home, mine_grad, send_grad = lax.optimization_barrier((home, mine_grad, send_grad))
    mine_grad, other_grad = gridded(mine_grad), gridded(seq_swap(send_grad, 1))
    stage = split(after(place, home, SOME_COST), [(low_keep, low_in, high_keep, high_in)], chips)
    arrived = [stage[0]] + [chip_shift(stage[step], step) for step in range(1, chips)]
    grad_input = final(
        place, home, tokens, grad_middle, w_query, w_key, w_value, gain_first
    )
    low, high = outgoing(place, mine_grad, other_grad)
    low_keep, low_send, high_keep, high_send = halfway(
        place,
        [(*outgoing(place, mine_grad, other_grad, True), row_swap(low, 1), row_swap(high, 2))],
    )
    stage = split(
        place, [(low_keep, row_swap(low_send, 2), high_keep, row_swap(high_send, 1))], chips
    )
    arrived += [stage[0]] + [chip_shift(stage[step], step) for step in range(1, chips)]
    down, up, out, query, key, value, gains_part = finish(
        place, arrived, hidden, parts, per, share, factor
    )
    return (
        result,
        grad_input,
        query.reshape(-1),
        key.reshape(-1),
        value.reshape(-1),
        out.reshape(-1),
        up.reshape(-1),
        down.reshape(-1),
        gains_part.reshape(-1)[:gains_share],
    )


def local(*arrays):
    seq_devices, row_devices = lax.axis_size("seq"), lax.axis_size("row")
    block = arrays[0].shape[0]
    one_segment = block * seq_devices <= SEGMENT and block % 2 ** (PATTERNS - 1) == 0
    if one_segment and seq_devices in (2, 4, 8) and row_devices == 4:
        return fast_local(*arrays)
    return ring_local(*arrays)


def solution(mesh):
    return jax.shard_map(
        local,
        mesh=mesh,
        in_specs=(
            P(("row", "seq"), None),
            P("row", None),
            P(),
            P(),
            P(),
            P(),
            P(),
            P(),
            P(),
            P(),
            P(),
            P(),
            P(("row", "seq"), None),
        ),
        out_specs=(
            P(("row", "seq"), None),
            P(("row", "seq"), None),
            P(("row", "seq")),
            P(("row", "seq")),
            P(("row", "seq")),
            P(("row", "seq")),
            P(("row", "seq")),
            P(("row", "seq")),
            P(("row", "seq")),
        ),
        check_vma=False,
    )
```

```python
from functools import partial
from functools import reduce
import math

import jax
import jax.numpy as jnp
import numpy as np
from jax import lax
from jax.experimental import pallas as pl
from jax.experimental.pallas import tpu as pltpu
from jax.sharding import PartitionSpec as P

HEADS = 12
SEGMENT = 2048
PATTERNS = 5


big_negative = -1e30


def shifted_2(shard, axis, by):
    length = lax.axis_size(axis)
    pairs = [(i, i + by) for i in range(length) if 0 <= i + by < length]
    return lax.ppermute(shard, axis, pairs)


def shifted_3(value, axis, steps):
    count = lax.axis_size(axis)
    pairs = [(source, (source + steps) % count) for source in range(count)]
    return lax.ppermute(value, axis, pairs)


def layer_norm(values, gain_vector):
    centre = jnp.mean(values, axis=-1, keepdims=True)
    shifted = values - centre
    variance = jnp.mean(shifted * shifted, axis=-1, keepdims=True)
    return shifted * lax.rsqrt(variance + 1e-05) * gain_vector


def hidden_norm(hidden_pre, gain_vector):
    return layer_norm(jax.nn.gelu(hidden_pre, approximate=True), gain_vector)


def selector(stride, head_count):
    return jnp.arange(stride)[:, None] == (jnp.arange(head_count) % stride)[None, :]


def compact(full_array, stride):
    length_in, head_count, inner_size = full_array.shape
    shaped = full_array.reshape(length_in // stride, stride, head_count, inner_size)
    picked = jnp.where(
        selector(stride, head_count)[None, :, :, None], shaped, jnp.zeros((), full_array.dtype)
    )
    return jnp.sum(picked, axis=1)


def expand(part_array, stride, fill_value):
    part_rows, head_count, inner_size = part_array.shape
    widened = jnp.where(
        selector(stride, head_count)[None, :, :, None],
        part_array[:, None],
        jnp.asarray(fill_value, part_array.dtype),
    )
    return widened.reshape(part_rows * stride, head_count, inner_size)


def positions(start_pos, part_rows, stride, head_count):
    row_ids = jnp.arange(part_rows, dtype=jnp.int32)[:, None] * stride
    head_ids = (jnp.arange(head_count, dtype=jnp.int32) % stride)[None, :]
    return start_pos + row_ids + head_ids


def doc_index(places, doc_bounds):
    return jnp.sum((places[..., None] >= doc_bounds).astype(jnp.int32), axis=-1)


def block_mask(doc_query, doc_key, local_block):
    allowed = doc_query.T[:, :, None] == doc_key.T[:, None, :]
    if local_block:
        rank_ids = jnp.arange(doc_query.shape[0])
        allowed = allowed & (rank_ids[:, None] >= rank_ids[None, :])[None]
    return allowed


def forward_block(query_part, key_part, value_part, allowed, score_scale):
    scores = (
        jnp.einsum("qhd,khd->hqk", query_part, key_part, preferred_element_type=jnp.float32)
        * score_scale
    )
    scores = jnp.where(allowed, scores, big_negative)
    row_peak = jnp.max(scores, axis=-1)
    weights = jnp.where(allowed, jnp.exp(scores - row_peak[..., None]), 0.0)
    row_total = jnp.sum(weights, axis=-1)
    mixed = jnp.einsum(
        "hqk,khd->qhd", weights.astype(jnp.bfloat16), value_part, preferred_element_type=jnp.float32
    )
    return (row_peak.T, row_total.T, mixed)


def merge(carried, new_block):
    best_peak = jnp.maximum(carried[0], new_block[0])
    keep_factor = jnp.exp(carried[0] - best_peak)
    take_factor = jnp.exp(new_block[0] - best_peak)
    new_total = carried[1] * keep_factor + new_block[1] * take_factor
    new_mixed = carried[2] * keep_factor[..., None] + new_block[2] * take_factor[..., None]
    return (best_peak, new_total, new_mixed)


def backward_block(
    query_part, grad_part, lse_part, delta_part, key_part, value_part, allowed, score_scale
):
    scores = (
        jnp.einsum("qhd,khd->hqk", query_part, key_part, preferred_element_type=jnp.float32)
        * score_scale
    )
    probs = jnp.where(allowed, jnp.exp(scores - lse_part.T[:, :, None]), 0.0)
    dots = jnp.einsum("qhd,khd->hqk", grad_part, value_part, preferred_element_type=jnp.float32)
    grad_scores = (probs * (dots - delta_part.T[:, :, None])).astype(jnp.bfloat16)
    query_grad = (
        jnp.einsum("hqk,khd->qhd", grad_scores, key_part, preferred_element_type=jnp.float32)
        * score_scale
    )
    key_grad = (
        jnp.einsum("hqk,qhd->khd", grad_scores, query_part, preferred_element_type=jnp.float32)
        * score_scale
    )
    value_grad = jnp.einsum(
        "hqk,qhd->khd", probs.astype(jnp.bfloat16), grad_part, preferred_element_type=jnp.float32
    )
    return (query_grad, key_grad, value_grad)


def keep_state(carried):
    return carried


def ring_local(
    tokens,
    lengths,
    w_query,
    w_key,
    w_value,
    w_out,
    w_up,
    w_down,
    gain_attend,
    gain_inner,
    gain_feed,
    gain_hidden,
    cotangent,
):
    block_rows, model_width = tokens.shape
    head_count = HEADS
    head_size = model_width // head_count
    score_scale = head_size ** (-0.5)
    seq_devices = lax.axis_size("seq")
    all_devices = seq_devices * lax.axis_size("row")
    my_index = lax.axis_index("seq")
    seq_total = block_rows * seq_devices
    doc_bounds = jnp.cumsum(lengths[0])[:-1]
    patterns = [
        (2**pattern, min(SEGMENT * 2**pattern, seq_total) // block_rows)
        for pattern in range(PATTERNS)
    ]
    near_ids = [0, 1]
    far_ids = list(range(2, PATTERNS))
    reach = patterns[1][1]
    far_rows = [block_rows // patterns[pattern][0] for pattern in far_ids]
    far_starts = [sum(far_rows[:slot_id]) for slot_id in range(len(far_ids))]
    far_total = sum(far_rows)

    def key_docs(pattern, source):
        stride = patterns[pattern][0]
        return doc_index(
            positions(source * block_rows, block_rows // stride, stride, head_count), doc_bounds
        )

    def is_live(pattern, cycle_step):
        group_size = patterns[pattern][1]
        return (cycle_step < group_size) & (my_index % group_size >= cycle_step)

    source_x = tokens.astype(jnp.float32)
    normed, attend_back = jax.vjp(layer_norm, source_x, gain_attend)
    normed_b = normed.astype(jnp.bfloat16)
    query_b = jnp.dot(normed_b, w_query, preferred_element_type=jnp.float32).astype(jnp.bfloat16)
    key_b = jnp.dot(normed_b, w_key, preferred_element_type=jnp.float32).astype(jnp.bfloat16)
    value_b = jnp.dot(normed_b, w_value, preferred_element_type=jnp.float32).astype(jnp.bfloat16)
    query_heads = query_b.reshape(block_rows, head_count, head_size)
    key_heads = key_b.reshape(block_rows, head_count, head_size)
    value_heads = value_b.reshape(block_rows, head_count, head_size)
    query_parts = [compact(query_heads, stride) for stride, group_size in patterns]
    key_parts = [compact(key_heads, stride) for stride, group_size in patterns]
    value_parts = [compact(value_heads, stride) for stride, group_size in patterns]
    own_docs = [key_docs(pattern, my_index) for pattern in range(PATTERNS)]
    states = [
        forward_block(
            query_parts[pattern],
            key_parts[pattern],
            value_parts[pattern],
            block_mask(own_docs[pattern], own_docs[pattern], True),
            score_scale,
        )
        for pattern in range(PATTERNS)
    ]

    def unpack_near(key_block):
        key_full = key_block[:, :model_width].reshape(block_rows, head_count, head_size)
        value_full = key_block[:, model_width:].reshape(block_rows, head_count, head_size)
        return (key_full, value_full)

    def near_fold_parts(pattern, key_part, value_part, source, carried):
        new_block = forward_block(
            query_parts[pattern],
            key_part,
            value_part,
            block_mask(own_docs[pattern], key_docs(pattern, source), False),
            score_scale,
        )
        return merge(carried, new_block)

    def near_fold(pattern, key_full, value_full, source, carried):
        stride = patterns[pattern][0]
        return near_fold_parts(
            pattern, compact(key_full, stride), compact(value_full, stride), source, carried
        )

    pair_block = jnp.concatenate([key_b, value_b], axis=1)
    kept_blocks = jnp.zeros((max(reach - 1, 1), block_rows, 2 * model_width), jnp.bfloat16)

    def near_forward(cycle_step, loop_state):
        key_block, near_now, kept_store = loop_state
        key_block = shifted_2(key_block, "seq", 1)
        key_full, value_full = unpack_near(key_block)
        new_states = []
        for pattern in near_ids:
            new_states.append(
                lax.cond(
                    is_live(pattern, cycle_step),
                    partial(near_fold, pattern, key_full, value_full, my_index - cycle_step),
                    keep_state,
                    near_now[pattern],
                )
            )
        return (key_block, tuple(new_states), kept_store)

    _, near_states, kept_blocks = lax.fori_loop(
        1, reach, near_forward, (pair_block, (states[0], states[1]), kept_blocks)
    )
    far_block = jnp.concatenate(
        [
            jnp.concatenate(
                [
                    key_parts[pattern].reshape(rows_here, model_width),
                    value_parts[pattern].reshape(rows_here, model_width),
                ],
                axis=1,
            )
            for pattern, rows_here in zip(far_ids, far_rows)
        ],
        axis=0,
    )

    def unpack_far(key_block, slot_id):
        rows_here = far_rows[slot_id]
        row_begin = far_starts[slot_id]
        piece_rows = key_block[row_begin : row_begin + rows_here]
        key_part = piece_rows[:, :model_width].reshape(rows_here, head_count, head_size)
        value_part = piece_rows[:, model_width:].reshape(rows_here, head_count, head_size)
        return (key_part, value_part)

    def far_fold(pattern, key_part, value_part, source, carried):
        new_block = forward_block(
            query_parts[pattern],
            key_part,
            value_part,
            block_mask(own_docs[pattern], key_docs(pattern, source), False),
            score_scale,
        )
        return merge(carried, new_block)

    def far_update(far_now, key_block, cycle_step):
        new_states = []
        for slot_id, pattern in enumerate(far_ids):
            key_part, value_part = unpack_far(key_block, slot_id)
            new_states.append(
                lax.cond(
                    is_live(pattern, cycle_step),
                    partial(far_fold, pattern, key_part, value_part, my_index - cycle_step),
                    keep_state,
                    far_now[slot_id],
                )
            )
        return tuple(new_states)

    far_states = tuple((states[pattern] for pattern in far_ids))

    def far_forward(cycle_step, loop_state):
        key_block, far_now = loop_state
        key_block = shifted_2(key_block, "seq", 1)
        return (key_block, far_update(far_now, key_block, cycle_step))

    _, far_states = lax.fori_loop(1, seq_devices, far_forward, (far_block, far_states))
    ordered = list(near_states) + list(far_states)
    peaks = [
        expand(ordered[pattern][0][..., None], patterns[pattern][0], big_negative)[..., 0]
        for pattern in range(PATTERNS)
    ]
    best_peak = reduce(jnp.maximum, peaks)
    weight_sum = jnp.zeros((block_rows, head_count), jnp.float32)
    mixed_sum = jnp.zeros((block_rows, head_count, head_size), jnp.float32)
    for pattern in range(PATTERNS):
        stride = patterns[pattern][0]
        factor = jnp.exp(peaks[pattern] - best_peak)
        weight_sum = (
            weight_sum + expand(ordered[pattern][1][..., None], stride, 0.0)[..., 0] * factor
        )
        mixed_sum = mixed_sum + expand(ordered[pattern][2], stride, 0.0) * factor[..., None]
    attended = mixed_sum / weight_sum[..., None]
    log_total = best_peak + jnp.log(weight_sum)
    inner_out, inner_back = jax.vjp(
        layer_norm, attended.reshape(block_rows, model_width), gain_inner
    )
    inner_b = inner_out.astype(jnp.bfloat16)
    middle = source_x + jnp.dot(inner_b, w_out, preferred_element_type=jnp.float32)
    normed_two, feed_back = jax.vjp(layer_norm, middle, gain_feed)
    normed_two_b = normed_two.astype(jnp.bfloat16)
    hidden_pre = jnp.dot(normed_two_b, w_up, preferred_element_type=jnp.float32)
    hidden, hidden_back = jax.vjp(hidden_norm, hidden_pre, gain_hidden)
    hidden_b = hidden.astype(jnp.bfloat16)
    result = (middle + jnp.dot(hidden_b, w_down, preferred_element_type=jnp.float32)).astype(
        jnp.bfloat16
    )
    grad_down = jnp.einsum("tf,tg->fg", hidden_b, cotangent, preferred_element_type=jnp.float32)
    grad_hidden = jnp.einsum("tg,fg->tf", cotangent, w_down, preferred_element_type=jnp.float32)
    grad_pre, grad_gain_hidden = hidden_back(grad_hidden)
    grad_pre_b = grad_pre.astype(jnp.bfloat16)
    grad_up = jnp.einsum("tf,tg->fg", normed_two_b, grad_pre_b, preferred_element_type=jnp.float32)
    grad_normed_two = jnp.einsum("tg,fg->tf", grad_pre_b, w_up, preferred_element_type=jnp.float32)
    grad_middle_part, grad_gain_feed = feed_back(grad_normed_two)
    grad_middle = cotangent.astype(jnp.float32) + grad_middle_part
    grad_middle_b = grad_middle.astype(jnp.bfloat16)
    grad_out = jnp.einsum("tf,tg->fg", inner_b, grad_middle_b, preferred_element_type=jnp.float32)
    grad_inner = jnp.einsum("tg,fg->tf", grad_middle_b, w_out, preferred_element_type=jnp.float32)
    grad_attended, grad_gain_inner = inner_back(grad_inner)
    grad_heads = grad_attended.astype(jnp.bfloat16).reshape(block_rows, head_count, head_size)
    delta_rows = jnp.sum(grad_heads.astype(jnp.float32) * attended, axis=-1)
    grad_parts = [compact(grad_heads, stride) for stride, group_size in patterns]
    lse_parts = [compact(log_total[..., None], stride)[..., 0] for stride, group_size in patterns]
    delta_parts = [
        compact(delta_rows[..., None], stride)[..., 0] for stride, group_size in patterns
    ]
    query_grads = []
    home_keys = []
    home_values = []
    for pattern in range(PATTERNS):
        part_query, part_key, part_value = backward_block(
            query_parts[pattern],
            grad_parts[pattern],
            lse_parts[pattern],
            delta_parts[pattern],
            key_parts[pattern],
            value_parts[pattern],
            block_mask(own_docs[pattern], own_docs[pattern], True),
            score_scale,
        )
        query_grads.append(part_query)
        home_keys.append(part_key)
        home_values.append(part_value)

    def fetch_full(key_block):
        return shifted_2(key_block, "seq", 1)

    def near_grad(pattern, key_full, value_full, source, operands):
        query_grad, travel = operands
        stride = patterns[pattern][0]
        part_query, part_key, part_value = backward_block(
            query_parts[pattern],
            grad_parts[pattern],
            lse_parts[pattern],
            delta_parts[pattern],
            compact(key_full, stride),
            compact(value_full, stride),
            block_mask(own_docs[pattern], key_docs(pattern, source), False),
            score_scale,
        )
        spread_rows = jnp.concatenate(
            [
                expand(part_key, stride, 0.0).reshape(block_rows, model_width),
                expand(part_value, stride, 0.0).reshape(block_rows, model_width),
            ],
            axis=1,
        )
        return (query_grad + part_query, travel + spread_rows)

    def near_backward(cycle_step, loop_state):
        key_block, grads_now, travel = loop_state
        key_block = fetch_full(key_block)
        travel = shifted_3(travel.astype(jnp.bfloat16), "seq", 1).astype(travel.dtype)
        key_full, value_full = unpack_near(key_block)
        new_grads = list(grads_now)
        for pattern in near_ids:
            new_grads[pattern], travel = lax.cond(
                is_live(pattern, cycle_step),
                partial(near_grad, pattern, key_full, value_full, my_index - cycle_step),
                keep_state,
                (new_grads[pattern], travel),
            )
        return (key_block, tuple(new_grads), travel)

    own_key_near = expand(home_keys[0], 1, 0.0) + expand(home_keys[1], 2, 0.0)
    own_value_near = expand(home_values[0], 1, 0.0) + expand(home_values[1], 2, 0.0)
    near_start = jnp.concatenate(
        [
            own_key_near.reshape(block_rows, model_width),
            own_value_near.reshape(block_rows, model_width),
        ],
        axis=1,
    )
    _, near_query, travel_near = lax.fori_loop(
        1, reach, near_backward, (pair_block, (query_grads[0], query_grads[1]), near_start)
    )
    near_home = shifted_3(travel_near.astype(jnp.bfloat16), "seq", 1 - reach).astype(
        travel_near.dtype
    )
    near_key_add = near_home[:, :model_width].reshape(block_rows, head_count, head_size)
    near_value_add = near_home[:, model_width:].reshape(block_rows, head_count, head_size)

    def far_grad(slot_id, key_part, value_part, source, operands):
        query_grad, travel = operands
        pattern = far_ids[slot_id]
        rows_here = far_rows[slot_id]
        row_begin = far_starts[slot_id]
        part_query, part_key, part_value = backward_block(
            query_parts[pattern],
            grad_parts[pattern],
            lse_parts[pattern],
            delta_parts[pattern],
            key_part,
            value_part,
            block_mask(own_docs[pattern], key_docs(pattern, source), False),
            score_scale,
        )
        spread_rows = jnp.concatenate(
            [part_key.reshape(rows_here, model_width), part_value.reshape(rows_here, model_width)],
            axis=1,
        )
        return (
            query_grad + part_query,
            travel.at[row_begin : row_begin + rows_here].add(spread_rows),
        )

    def far_back_update(grads_now, travel, key_block, cycle_step):
        new_grads = list(grads_now)
        for slot_id, pattern in enumerate(far_ids):
            key_part, value_part = unpack_far(key_block, slot_id)
            new_grads[slot_id], travel = lax.cond(
                is_live(pattern, cycle_step),
                partial(far_grad, slot_id, key_part, value_part, my_index - cycle_step),
                keep_state,
                (new_grads[slot_id], travel),
            )
        return (tuple(new_grads), travel)

    far_query = tuple((query_grads[pattern] for pattern in far_ids))
    far_empty = jnp.zeros((far_total, 2 * model_width), jnp.float32)

    def far_send(travel):
        return shifted_3(travel.astype(jnp.bfloat16), "seq", 1).astype(travel.dtype)

    def far_backward(cycle_step, loop_state):
        key_block, grads_now, travel = loop_state
        key_block = shifted_2(key_block, "seq", 1)
        travel = far_send(travel)
        grads_now, travel = far_back_update(grads_now, travel, key_block, cycle_step)
        return (key_block, grads_now, travel)

    _, far_query, travel_far = lax.fori_loop(
        1, seq_devices, far_backward, (far_block, far_query, far_empty)
    )
    far_home = far_send(travel_far)
    all_query = list(near_query) + list(far_query)
    query_grad = jnp.zeros((block_rows, head_count, head_size), jnp.float32)
    key_grad = near_key_add
    value_grad = near_value_add
    for pattern in range(PATTERNS):
        stride = patterns[pattern][0]
        query_grad = query_grad + expand(all_query[pattern], stride, 0.0)
    for pattern in far_ids:
        stride = patterns[pattern][0]
        key_grad = key_grad + expand(home_keys[pattern], stride, 0.0)
        value_grad = value_grad + expand(home_values[pattern], stride, 0.0)
    for slot_id, pattern in enumerate(far_ids):
        stride = patterns[pattern][0]
        rows_here = far_rows[slot_id]
        row_begin = far_starts[slot_id]
        piece_rows = far_home[row_begin : row_begin + rows_here]
        key_grad = key_grad + expand(
            piece_rows[:, :model_width].reshape(rows_here, head_count, head_size), stride, 0.0
        )
        value_grad = value_grad + expand(
            piece_rows[:, model_width:].reshape(rows_here, head_count, head_size), stride, 0.0
        )
    grad_query_b = query_grad.reshape(block_rows, model_width).astype(jnp.bfloat16)
    grad_key_b = key_grad.reshape(block_rows, model_width).astype(jnp.bfloat16)
    grad_value_b = value_grad.reshape(block_rows, model_width).astype(jnp.bfloat16)
    grad_w_query = jnp.einsum(
        "tf,tg->fg", normed_b, grad_query_b, preferred_element_type=jnp.float32
    )
    grad_w_key = jnp.einsum("tf,tg->fg", normed_b, grad_key_b, preferred_element_type=jnp.float32)
    grad_w_value = jnp.einsum(
        "tf,tg->fg", normed_b, grad_value_b, preferred_element_type=jnp.float32
    )
    grad_normed = jnp.einsum("tg,fg->tf", grad_query_b, w_query, preferred_element_type=jnp.float32)
    grad_normed = grad_normed + jnp.einsum(
        "tg,fg->tf", grad_key_b, w_key, preferred_element_type=jnp.float32
    )
    grad_normed = grad_normed + jnp.einsum(
        "tg,fg->tf", grad_value_b, w_value, preferred_element_type=jnp.float32
    )
    grad_x_part, grad_gain_attend = attend_back(grad_normed)
    grad_input = (grad_middle + grad_x_part).astype(jnp.bfloat16)
    gains_all = jnp.concatenate(
        [grad_gain_attend, grad_gain_inner, grad_gain_feed, grad_gain_hidden]
    )
    summed = (
        lax.psum_scatter(grad_w_query.reshape(-1), ("row", "seq"), scatter_dimension=0, tiled=True),
        lax.psum_scatter(grad_w_key.reshape(-1), ("row", "seq"), scatter_dimension=0, tiled=True),
        lax.psum_scatter(grad_w_value.reshape(-1), ("row", "seq"), scatter_dimension=0, tiled=True),
        lax.psum_scatter(grad_out.reshape(-1), ("row", "seq"), scatter_dimension=0, tiled=True),
        lax.psum_scatter(grad_up.reshape(-1), ("row", "seq"), scatter_dimension=0, tiled=True),
        lax.psum_scatter(grad_down.reshape(-1), ("row", "seq"), scatter_dimension=0, tiled=True),
        lax.psum_scatter(gains_all, ("row", "seq"), scatter_dimension=0, tiled=True),
    )
    factor = 1.0 / math.sqrt(block_rows * all_devices)
    return (result, grad_input) + tuple((summed_part * factor for summed_part in summed))


NO_COST = pl.CostEstimate(flops=1000, bytes_accessed=1000, transcendentals=0)
SOME_COST = pl.CostEstimate(flops=4 * 10**9, bytes_accessed=1000, transcendentals=0)
HIGH_COST = pl.CostEstimate(flops=5 * 10**10, bytes_accessed=1000, transcendentals=0)


def split_log(level):
    remaining = math.log((level + 1) / level)
    pieces = []
    for _ in range(3):
        piece = float(jnp.bfloat16.dtype.type(remaining))
        pieces.append(piece)
        remaining -= piece
    return pieces


def extra_values(places, features, head, size, per_piece):
    masks, values = jnp.zeros_like(features), jnp.zeros(features.shape, jnp.float32)
    for level in range(1, PATTERNS):
        for piece, value in enumerate(split_log(level)):
            here = features == size + 3 * (level - 1) + piece
            masks = jnp.where(here, 2**level - 1, masks)
            values = jnp.where(here, value if per_piece else 1.0, values)
    return jnp.where(((places - head) & masks) == 0, values, 0.0)


def nt_dot(left, right):
    return lax.dot_general(
        left, right, (((1,), (1,)), ((), ())), preferred_element_type=jnp.float32
    )


def nn_dot(left, right):
    return jnp.dot(left, right, preferred_element_type=jnp.float32)


def call_whole(kernel, out_shape, name, scalars, *arrays, in_specs=None, scratch=(), limit=12, cost=None):
    return pl.pallas_call(
        kernel,
        grid_spec=pltpu.PrefetchScalarGridSpec(
            num_scalar_prefetch=1,
            grid=(1,),
            in_specs=in_specs or [whole(array.shape) for array in arrays],
            out_specs=[whole(out.shape) for out in out_shape],
            scratch_shapes=list(scratch),
        ),
        out_shape=list(out_shape),
        compiler_params=pltpu.CompilerParams(vmem_limit_bytes=limit << 20),
        cost_estimate=cost or NO_COST,
        name=name,
    )(scalars, *arrays)


def after_kernel(scalars, *refs):
    for index in range(scalars.shape[0]):
        refs[-1][index] = scalars[index]


def after(scalars, arrays, cost):
    return pl.pallas_call(
        after_kernel,
        in_specs=[pl.BlockSpec(memory_space=pltpu.SMEM)]
        + [pl.BlockSpec(memory_space=pl.ANY)] * len(arrays),
        out_specs=pl.BlockSpec(memory_space=pltpu.SMEM),
        out_shape=jax.ShapeDtypeStruct(scalars.shape, scalars.dtype),
        compiler_params=pltpu.CompilerParams(vmem_limit_bytes=1 << 20),
        cost_estimate=cost,
        name="after",
    )(scalars, *arrays)


def norm_kernel(unused, rows_ref, gain_ref, out_ref):
    out_ref[...] = (norm_parts(rows_ref[...].astype(jnp.float32))[0] * gain_ref[...]).astype(
        jnp.bfloat16
    )


def project_kernel(blocks, own, heads, scale, meta, *refs):
    normed = refs[:blocks]
    wq_ref, wk_ref, wv_ref, q_ref, k_ref, vt_ref = refs[blocks:]
    length = normed[0].shape[0]
    lanes = wk_ref.shape[1] // heads
    size = lanes // 2
    first_head = meta[blocks]
    for index in range(blocks):
        rows = normed[index][...]
        start = meta[index]
        span = slice(index * length, (index + 1) * length)
        keys = nn_dot(rows, wk_ref[...])
        vt_ref[:, span] = nt_dot(wv_ref[...], rows).astype(jnp.bfloat16)
        places = start + lax.broadcasted_iota(jnp.int32, (length, 1), 0)
        features = lax.broadcasted_iota(jnp.int32, (1, lanes), 1)
        for head in range(heads):
            wide_rows = slice(head * lanes, (head + 1) * lanes)
            extra = extra_values(places, features, first_head + head, size, False)
            k_ref[span, wide_rows] = (keys[:, wide_rows] + extra).astype(jnp.bfloat16)
        if index < own:
            queries = nt_dot(wq_ref[...], rows).astype(jnp.bfloat16).astype(jnp.float32) * scale
            places = start + lax.broadcasted_iota(jnp.int32, (1, length), 1)
            features = lax.broadcasted_iota(jnp.int32, (lanes, 1), 0)
            for head in range(heads):
                wide_rows = slice(head * lanes, (head + 1) * lanes)
                extra = extra_values(places, features, first_head + head, size, True)
                q_ref[wide_rows, span] = (queries[wide_rows] + extra).astype(jnp.bfloat16)


def project(meta, normed, wq, wk, wv, own, heads, scale):
    blocks, length = len(normed), normed[0].shape[0]
    wide, share = wk.shape[1], wv.shape[0]
    return call_whole(
        partial(project_kernel, blocks, own, heads, scale),
        [
            jax.ShapeDtypeStruct((wide, own * length), jnp.bfloat16),
            jax.ShapeDtypeStruct((blocks * length, wide), jnp.bfloat16),
            jax.ShapeDtypeStruct((share, blocks * length), jnp.bfloat16),
        ],
        "project",
        meta,
        *normed,
        wq,
        wk,
        wv,
        limit=20,
    )


def project_back_kernel(blocks, unused, *refs):
    normed = refs[:blocks]
    wk_ref, wv_ref, kt_ref, v_ref = refs[blocks:]
    length = normed[0].shape[0]
    for index in range(blocks):
        rows = normed[index][...]
        span = slice(index * length, (index + 1) * length)
        kt_ref[:, span] = nt_dot(wk_ref[...], rows).astype(jnp.bfloat16)
        v_ref[span, :] = nn_dot(rows, wv_ref[...]).astype(jnp.bfloat16)


def project_back(scalars, normed, wk, wv):
    blocks, length = len(normed), normed[0].shape[0]
    return call_whole(
        partial(project_back_kernel, blocks),
        [
            jax.ShapeDtypeStruct((wk.shape[0], blocks * length), jnp.bfloat16),
            jax.ShapeDtypeStruct((blocks * length, wv.shape[1]), jnp.bfloat16),
        ],
        "project_back",
        scalars,
        *normed,
        wk,
        wv,
    )


def pair_mask(query_start, key_start, doc_line, block):
    query_place = query_start + lax.broadcasted_iota(jnp.int32, (1, block), 1)
    key_place = key_start + lax.broadcasted_iota(jnp.int32, (block, 1), 0)
    return (key_place <= query_place) & (key_place >= doc_line)


def attend_kernel(
    heads, block, key_blocks, meta, doc_ref, q_ref, k_ref, vt_ref, o_ref, lse_ref, *refs
):
    ob_refs, (m_ref, l_ref) = refs[:-2], refs[-2:]
    step = pl.program_id(0)
    steps = len(ob_refs)
    query_start = meta[step]
    doc_first, doc_last = meta[steps + key_blocks + step], meta[2 * steps + key_blocks + step]
    doc_line = doc_ref[...]
    size = o_ref.shape[0] // heads
    lanes = q_ref.shape[0] // heads
    m_ref[...] = jnp.full_like(m_ref, big_negative)
    l_ref[...] = jnp.zeros_like(l_ref)
    o_ref[...] = jnp.zeros_like(o_ref)

    def fold(slot, allowed):
        span = pl.ds(pl.multiple_of(slot * block, block), block)
        scores = [
            nn_dot(
                k_ref[span, head * lanes : (head + 1) * lanes],
                q_ref[head * lanes : (head + 1) * lanes, :],
            )
            for head in range(heads)
        ]
        if allowed is not None:
            scores = [jnp.where(allowed, part, big_negative) for part in scores]
        for head in range(heads):
            rows = slice(head * size, (head + 1) * size)
            old_peak = m_ref[head]
            new_peak = jnp.maximum(old_peak, jnp.max(scores[head], axis=0, keepdims=True))
            weights = jnp.exp(scores[head] - new_peak)
            fade = jnp.exp(old_peak - new_peak)
            m_ref[head] = new_peak
            l_ref[head] = l_ref[head] * fade + jnp.sum(weights, axis=0, keepdims=True)
            o_ref[rows, :] = o_ref[rows, :] * fade + nn_dot(
                vt_ref[rows, span], weights.astype(jnp.bfloat16)
            )

    def body(slot, carry):
        key_start = meta[steps + slot]
        live = (key_start <= query_start) & (key_start + block > doc_first)
        full = (key_start < query_start) & (key_start >= doc_last)

        @pl.when(full)
        def _():
            fold(slot, None)

        @pl.when(live & jnp.logical_not(full))
        def _():
            fold(slot, pair_mask(query_start, key_start, doc_line, block))

        return carry

    lax.fori_loop(0, key_blocks, body, 0)
    for head in range(heads):
        rows = slice(head * size, (head + 1) * size)
        total = l_ref[head]
        mixed = o_ref[rows, :] / total
        o_ref[rows, :] = mixed
        lse_ref[head] = m_ref[head] + jnp.log(total)
    for index, ob_ref in enumerate(ob_refs):

        @pl.when(step == index)
        def _(ob_ref=ob_ref):
            ob_ref[...] = o_ref[...].astype(jnp.bfloat16)


def attend_back_kernel(
    heads,
    block,
    key_blocks,
    scale,
    meta,
    doc_ref,
    q_ref,
    o_ref,
    lse_ref,
    k_ref,
    kt_ref,
    v_ref,
    *refs,
):
    g_refs = refs[:-7]
    dq_ref, mine_ref, other_ref, acc_ref, pair_ref, delta_ref, g_ref = refs[-7:]
    step = pl.program_id(0)
    steps = len(g_refs)
    for index, grad_ref in enumerate(g_refs):

        @pl.when(step == index)
        def _(grad_ref=grad_ref):
            g_ref[...] = grad_ref[...]

    query_start = meta[step]
    doc_first, doc_last = meta[steps + key_blocks + step], meta[2 * steps + key_blocks + step]
    doc_line = doc_ref[...]
    size = g_ref.shape[0] // heads
    lanes = q_ref.shape[0] // heads
    share = g_ref.shape[0]

    @pl.when(step == 0)
    def _():
        pair_ref[...] = jnp.zeros_like(pair_ref)

    acc_ref[...] = jnp.zeros_like(acc_ref)
    for head in range(heads):
        rows = slice(head * size, (head + 1) * size)
        delta_ref[head] = jnp.sum(
            g_ref[rows, :].astype(jnp.float32) * o_ref[rows, :], axis=0, keepdims=True
        )

    def fold(slot, allowed):
        span = pl.ds(pl.multiple_of(slot * block, block), block)
        probs, grad_scores = [], []
        for head in range(heads):
            wide_rows = slice(head * lanes, (head + 1) * lanes)
            rows = slice(head * size, (head + 1) * size)
            probs.append(nn_dot(k_ref[span, wide_rows], q_ref[wide_rows, :]))
            grad_scores.append(
                nn_dot(v_ref[span, head * lanes : head * lanes + size], g_ref[rows, :])
            )
        for head in range(heads):
            part = jnp.exp(probs[head] - lse_ref[head])
            if allowed is not None:
                part = jnp.where(allowed, part, 0.0)
            grad_scores[head] = (part * (grad_scores[head] - delta_ref[head])).astype(jnp.bfloat16)
            probs[head] = part.astype(jnp.bfloat16)
        for head in range(heads):
            rows = slice(head * size, (head + 1) * size)
            value_rows = slice(share + head * size, share + (head + 1) * size)
            query_rows = slice(head * lanes, head * lanes + size)
            pair_ref[value_rows, span] += nt_dot(g_ref[rows, :], probs[head])
            pair_ref[rows, span] += nt_dot(q_ref[query_rows, :], grad_scores[head])
            acc_ref[rows, :] += nn_dot(kt_ref[rows, span], grad_scores[head])

    def body(slot, carry):
        key_start = meta[steps + slot]
        live = (key_start <= query_start) & (key_start + block > doc_first)
        full = (key_start < query_start) & (key_start >= doc_last)

        @pl.when(full)
        def _():
            fold(slot, None)

        @pl.when(live & jnp.logical_not(full))
        def _():
            fold(slot, pair_mask(query_start, key_start, doc_line, block))

        return carry

    lax.fori_loop(0, key_blocks, body, 0)
    dq_ref[...] = (acc_ref[...] * scale).astype(dq_ref.dtype)

    @pl.when(step == steps - 1)
    def _():
        half = mine_ref.shape[1]
        mine_ref[...] = pair_ref[:, :half]
        other_ref[...] = pair_ref[:, half:].astype(jnp.bfloat16)


def whole(shape):
    return pl.BlockSpec(shape, lambda *index: (0,) * len(shape))


def attend(meta, doc_line, q_ext, k_ext, v_t, heads, block):
    wide, queries = q_ext.shape
    share, keys = v_t.shape
    steps, key_blocks = queries // block, keys // block
    return pl.pallas_call(
        partial(attend_kernel, heads, block, key_blocks),
        grid_spec=pltpu.PrefetchScalarGridSpec(
            num_scalar_prefetch=1,
            grid=(steps,),
            in_specs=[
                pl.BlockSpec((1, block), lambda i, meta: (0, i)),
                pl.BlockSpec((wide, block), lambda i, meta: (0, i)),
                pl.BlockSpec(memory_space=pltpu.VMEM),
                pl.BlockSpec(memory_space=pltpu.VMEM),
            ],
            out_specs=[
                pl.BlockSpec((share, block), lambda i, meta: (0, i)),
                pl.BlockSpec((heads, 1, block), lambda i, meta: (0, 0, i)),
            ]
            + [whole((share, block))] * steps,
            scratch_shapes=[
                pltpu.VMEM((heads, 1, block), jnp.float32),
                pltpu.VMEM((heads, 1, block), jnp.float32),
            ],
        ),
        out_shape=[
            jax.ShapeDtypeStruct((share, queries), jnp.float32),
            jax.ShapeDtypeStruct((heads, 1, queries), jnp.float32),
        ]
        + [jax.ShapeDtypeStruct((share, block), jnp.bfloat16)] * steps,
        compiler_params=pltpu.CompilerParams(vmem_limit_bytes=12 << 20),
        cost_estimate=NO_COST,
        name="attend",
    )(meta, doc_line, q_ext, k_ext, v_t)


def attend_back(meta, doc_line, q_ext, grad_t, mixed, lse, k_ext, k_t, v_ext, heads, block, scale):
    wide, queries = q_ext.shape
    share, keys = k_t.shape
    steps, key_blocks = queries // block, keys // block
    return pl.pallas_call(
        partial(attend_back_kernel, heads, block, key_blocks, scale),
        grid_spec=pltpu.PrefetchScalarGridSpec(
            num_scalar_prefetch=1,
            grid=(steps,),
            in_specs=[
                pl.BlockSpec((1, block), lambda i, meta: (0, i)),
                pl.BlockSpec((wide, block), lambda i, meta: (0, i)),
                pl.BlockSpec((share, block), lambda i, meta: (0, i)),
                pl.BlockSpec((heads, 1, block), lambda i, meta: (0, 0, i)),
                pl.BlockSpec(memory_space=pltpu.VMEM),
                pl.BlockSpec(memory_space=pltpu.VMEM),
                pl.BlockSpec(memory_space=pltpu.VMEM),
            ]
            + [whole((share, block))] * steps,
            out_specs=[
                pl.BlockSpec((share, block), lambda i, meta: (0, i)),
                whole((2 * share, keys // 2)),
                whole((2 * share, keys // 2)),
            ],
            scratch_shapes=[
                pltpu.VMEM((share, block), jnp.float32),
                pltpu.VMEM((2 * share, keys), jnp.float32),
                pltpu.VMEM((heads, 1, block), jnp.float32),
                pltpu.VMEM((share, block), jnp.bfloat16),
            ],
        ),
        out_shape=[
            jax.ShapeDtypeStruct((share, queries), jnp.bfloat16),
            jax.ShapeDtypeStruct((2 * share, keys // 2), jnp.float32),
            jax.ShapeDtypeStruct((2 * share, keys // 2), jnp.bfloat16),
        ],
        compiler_params=pltpu.CompilerParams(vmem_limit_bytes=20 << 20),
        cost_estimate=HIGH_COST,
        name="attend_back",
    )(meta, doc_line, q_ext, mixed, lse, k_ext, k_t, v_ext, *grad_t)


def join_kernel(chips, unused, dq_ref, mine_ref, other_ref, *out_refs):
    share = dq_ref.shape[0]
    block = dq_ref.shape[1] // chips
    for step in range(chips):
        span = slice(step * block, (step + 1) * block)
        pair = (mine_ref[:, span] + other_ref[:, span].astype(jnp.float32)).astype(jnp.bfloat16)
        out_refs[step][:share, :] = dq_ref[:, span]
        out_refs[step][share:, :] = pair


def join_parts(scalars, dq, mine, other, chips):
    rows, block = dq.shape[0] + mine.shape[0], dq.shape[1] // chips
    return call_whole(
        partial(join_kernel, chips),
        [jax.ShapeDtypeStruct((rows, block), jnp.bfloat16)] * chips,
        "join",
        scalars,
        dq,
        mine,
        other,
    )


def head_grads_kernel(chips, per, unused, *refs):
    normed, grads = refs[:chips], refs[chips : 2 * chips]
    wq_ref, wk_ref, wv_ref, gain_ref, inner_ref, feed_ref, hidden_ref = refs[2 * chips : 2 * chips + 7]
    perm_ref, row_ref, lane_ref, keep_ref, send_ref = refs[2 * chips + 7 :]
    share, model_width = wq_ref.shape
    own = nn_dot(grads[0][...], normed[0][...])
    for step in range(1, chips):
        own = own + nn_dot(grads[step][...], normed[step][...])
    attend = jnp.zeros((1, model_width), jnp.float32)
    for index, weight in enumerate((wq_ref, wk_ref, wv_ref)):
        part = own[index * share : (index + 1) * share] * weight[...].astype(jnp.float32)
        attend = attend + jnp.sum(part, axis=0, keepdims=True)
    gains = jnp.concatenate(
        [attend / gain_ref[...], inner_ref[...], feed_ref[...], hidden_ref[...]], axis=1
    )
    gains = (row_ref[...].astype(jnp.float32) * gains).astype(jnp.bfloat16)
    gains = nn_dot(gains, lane_ref[...]).astype(jnp.bfloat16)
    own = nt_dot(perm_ref[...], own.astype(jnp.bfloat16))
    chunks, _, width = keep_ref.shape
    columns = own.shape[1]
    gain_rows = gains.shape[0] // (2 * chunks)
    for which, target in enumerate((keep_ref, send_ref)):
        target[:, :, columns:] = jnp.zeros((chunks, per, width - columns), jnp.bfloat16)
        for chunk in range(chunks):
            place = which * chunks + chunk
            rows = slice(place * per, (place + 1) * per)
            target[chunk, :, :columns] = own[rows].astype(jnp.bfloat16)
            target[chunk, :gain_rows, width - 128 :] = gains[
                place * gain_rows : (place + 1) * gain_rows
            ]


def head_grads(scalars, normed, grads, weights, gain, late_gains, perm, where_row, where_lane, per):
    width = perm.shape[0]
    out = jax.ShapeDtypeStruct((width // (2 * per), per, width), jnp.bfloat16)
    return call_whole(
        partial(head_grads_kernel, len(grads), per),
        [out, out],
        "head_grads",
        scalars,
        *normed,
        *grads,
        *weights,
        gain,
        *late_gains,
        perm,
        where_row,
        where_lane,
        limit=24,
    )


def norm_parts(values):
    shifted = values - jnp.mean(values, axis=-1, keepdims=True)
    rate = lax.rsqrt(jnp.mean(shifted * shifted, axis=-1, keepdims=True) + 1e-05)
    return shifted * rate, rate


def norm_back(grad, hat, rate, gain):
    scaled = grad * gain
    mean_scaled = jnp.mean(scaled, axis=-1, keepdims=True)
    mean_product = jnp.mean(scaled * hat, axis=-1, keepdims=True)
    return (
        rate * (scaled - mean_scaled - hat * mean_product),
        jnp.sum(grad * hat, axis=0, keepdims=True),
    )


def middle_kernel(chips, tiles, position, *refs):
    mixed = refs[:chips]
    tokens_ref, cot_ref, wout_ref, wup_ref, wdown_ref, ginner_ref, gfeed_ref, ghidden_ref = refs[
        chips : chips + 8
    ]
    result_ref, gmid_ref, gmid_b_ref = refs[chips + 8 : chips + 11]
    go_refs = refs[chips + 11 : 2 * chips + 11]
    (
        z_ref,
        h2_ref,
        bent_out,
        pre_out,
        dinner_ref,
        dfeed_ref,
        dhidden_ref,
        swap_ref,
        work_ref,
        column_ref,
        zhat_ref,
        hat_ref,
        act_ref,
        slope_ref,
        dact_ref,
        acc_ref,
        stat_ref,
    ) = refs[2 * chips + 11 :]
    step = pl.program_id(0)
    chip = position[0]
    block, model_width = tokens_ref.shape
    share = model_width // chips
    tile = wdown_ref.shape[0]
    hidden = tile * tiles
    root = math.sqrt(2.0 / math.pi)
    phase, index = step // tiles, step % tiles
    lanes = stat_ref.shape[2]
    groups = tile // lanes

    def by_rows(body):
        body(slice(None))

    def spread(stat):
        return jnp.concatenate([stat] * groups, axis=1)

    def gathered_lanes(values):
        total = values[:, :lanes]
        for group in range(1, groups):
            total = total + values[:, group * lanes : (group + 1) * lanes]
        return total

    def lane_sum(values):
        return jnp.broadcast_to(jnp.sum(values, axis=-1, keepdims=True), values.shape)

    def column_sums(values):
        total = values[:8]
        for first in range(8, values.shape[0], 8):
            total = total + values[first : first + 8]
        return total

    def norm_rows(values):
        shifted = values - spread(lane_sum(gathered_lanes(values)) / tile)
        rate = lax.rsqrt(lane_sum(gathered_lanes(shifted * shifted)) / tile + 1e-05)
        return shifted * spread(rate), rate

    def norm_rows_back(grad, hat, rate, gain):
        scaled = grad * gain
        mean_scaled = lane_sum(gathered_lanes(scaled)) / tile
        mean_product = lane_sum(gathered_lanes(scaled * hat)) / tile
        return spread(rate) * (scaled - spread(mean_scaled) - hat * spread(mean_product))

    @pl.when(step == 0)
    def _():
        for near in range(chips):
            start = pl.multiple_of(share * lax.rem(chip + near, chips), share)
            swap_ref[pl.ds(start, share), :] = mixed[near][...].astype(jnp.float32)
        work_ref[...] = swap_ref[...].T

        def first_norm(rows):
            zhat, zrate = norm_rows(work_ref[rows, :])
            zhat_ref[rows, :] = zhat
            stat_ref[0, rows, :] = zrate
            z_ref[rows, :] = (zhat * ginner_ref[...]).astype(jnp.bfloat16)

        by_rows(first_norm)
        work_ref[...] = nn_dot(z_ref[...], wout_ref[...])

        def second_norm(rows):
            mid = tokens_ref[rows, :].astype(jnp.float32) + work_ref[rows, :]
            acc_ref[rows, :] = mid
            hat, rate = norm_rows(mid)
            hat_ref[rows, :] = hat
            stat_ref[1, rows, :] = rate
            h2_ref[rows, :] = (hat * gfeed_ref[...]).astype(jnp.bfloat16)

        by_rows(second_norm)
        for stat in range(3, 7):
            stat_ref[stat] = jnp.zeros_like(stat_ref[stat])

    @pl.when(phase == 0)
    def _():
        work_ref[...] = nn_dot(h2_ref[...], wup_ref[...])

        def bend_rows(rows):
            u = work_ref[rows, :]
            squared = u * u
            bend = jnp.tanh(root * (u + 0.044715 * u * squared))
            act_ref[index, rows, :] = 0.5 * u * (1.0 + bend)
            slope_ref[index, rows, :] = 0.5 * (1.0 + bend) + 0.5 * u * (1.0 - bend * bend) * root * (
                1.0 + 3.0 * 0.044715 * squared
            )

        by_rows(bend_rows)

        @pl.when(index == 0)
        def _():
            def pivot(rows):
                stat_ref[2, rows, :] = lane_sum(gathered_lanes(act_ref[0, rows, :])) / tile

            by_rows(pivot)

        def sums(rows):
            off = act_ref[index, rows, :] - spread(stat_ref[2, rows, :])
            stat_ref[3, rows, :] += gathered_lanes(off)
            stat_ref[4, rows, :] += gathered_lanes(off * off)

        by_rows(sums)

    @pl.when(step == tiles)
    def _():
        drift = lane_sum(stat_ref[3]) / hidden
        stat_ref[2] = stat_ref[2] + drift
        stat_ref[4] = lax.rsqrt(
            jnp.maximum(lane_sum(stat_ref[4]) / hidden - drift * drift, 0.0) + 1e-05
        )

    @pl.when(phase == 1)
    def _():
        def hidden_rows(rows):
            hat = (act_ref[index, rows, :] - spread(stat_ref[2, rows, :])) * spread(
                stat_ref[4, rows, :]
            )
            act_ref[index, rows, :] = hat
            bent_out[rows, :] = (hat * ghidden_ref[...]).astype(jnp.bfloat16)

        by_rows(hidden_rows)
        work_ref[...] = nt_dot(cot_ref[...], wdown_ref[...])
        acc_ref[...] += nn_dot(bent_out[...], wdown_ref[...])
        column_ref[...] = jnp.zeros_like(column_ref)

        def grad_rows(rows):
            hat, grad = act_ref[index, rows, :], work_ref[rows, :]
            column_ref[...] += column_sums(grad * hat)
            scaled = grad * ghidden_ref[...]
            dact_ref[index, rows, :] = scaled
            stat_ref[5, rows, :] += gathered_lanes(scaled)
            stat_ref[6, rows, :] += gathered_lanes(scaled * hat)

        by_rows(grad_rows)
        dhidden_ref[...] = jnp.sum(column_ref[...], axis=0, keepdims=True)

    @pl.when(step == 2 * tiles)
    def _():
        result_ref[...] = acc_ref[...].astype(jnp.bfloat16)
        acc_ref[...] = jnp.zeros_like(acc_ref)
        stat_ref[5] = lane_sum(stat_ref[5]) / hidden
        stat_ref[6] = lane_sum(stat_ref[6]) / hidden

    @pl.when(phase == 2)
    def _():
        def pre_rows(rows):
            inner = (
                dact_ref[index, rows, :]
                - spread(stat_ref[5, rows, :])
                - act_ref[index, rows, :] * spread(stat_ref[6, rows, :])
            )
            pre_out[rows, :] = (
                spread(stat_ref[4, rows, :]) * inner * slope_ref[index, rows, :]
            ).astype(jnp.bfloat16)

        by_rows(pre_rows)
        acc_ref[...] += nt_dot(pre_out[...], wup_ref[...])

    @pl.when(step == 3 * tiles - 1)
    def _():
        column_ref[...] = jnp.zeros_like(column_ref)

        def middle_rows(rows):
            grad, hat = acc_ref[rows, :], hat_ref[rows, :]
            column_ref[...] += column_sums(grad * hat)
            gmid = cot_ref[rows, :].astype(jnp.float32) + norm_rows_back(
                grad, hat, stat_ref[1, rows, :], gfeed_ref[...]
            )
            gmid_ref[rows, :] = gmid
            gmid_b_ref[rows, :] = gmid.astype(jnp.bfloat16)

        by_rows(middle_rows)
        dfeed_ref[...] = jnp.sum(column_ref[...], axis=0, keepdims=True)
        work_ref[...] = nt_dot(gmid_b_ref[...], wout_ref[...])
        column_ref[...] = jnp.zeros_like(column_ref)

        def inner_rows(rows):
            grad, hat = work_ref[rows, :], zhat_ref[rows, :]
            column_ref[...] += column_sums(grad * hat)
            work_ref[rows, :] = norm_rows_back(grad, hat, stat_ref[0, rows, :], ginner_ref[...])

        by_rows(inner_rows)
        dinner_ref[...] = jnp.sum(column_ref[...], axis=0, keepdims=True)
        swap_ref[...] = work_ref[...].T
        for near in range(chips):
            start = pl.multiple_of(share * lax.rem(chip + near, chips), share)
            go_refs[near][...] = swap_ref[pl.ds(start, share), :].astype(jnp.bfloat16)


def middle(position, mixed, tokens, cotangent, w_out, w_up, w_down, gains):
    chips = len(mixed)
    block, model_width = tokens.shape
    hidden = w_up.shape[1]
    tile = model_width
    tiles = hidden // tile
    share = model_width // chips
    last = tiles - 1

    def up_index(i, pos):
        return (0, jnp.where(i < tiles, i, jnp.where(i < 2 * tiles, last, i - 2 * tiles)))

    def down_index(i, pos):
        return (jnp.clip(i - tiles, 0, last), 0)

    def hidden_index(i, pos):
        return (0, jnp.clip(i - tiles, 0, last))

    def pre_index(i, pos):
        return (0, jnp.clip(i - 2 * tiles, 0, last))

    def f32(*shape):
        return pltpu.VMEM(shape, jnp.float32)

    row, rows = (1, model_width), (block, model_width)
    narrow = jax.ShapeDtypeStruct(rows, jnp.bfloat16)
    return pl.pallas_call(
        partial(middle_kernel, chips, tiles),
        grid_spec=pltpu.PrefetchScalarGridSpec(
            num_scalar_prefetch=1,
            grid=(3 * tiles,),
            in_specs=[whole((share, block))] * chips
            + [
                whole(rows),
                whole(rows),
                whole((model_width, model_width)),
                pl.BlockSpec((model_width, tile), up_index),
                pl.BlockSpec((tile, model_width), down_index),
                whole(row),
                whole(row),
                pl.BlockSpec((1, tile), hidden_index),
            ],
            out_specs=[whole(rows)] * 3
            + [whole((share, block))] * chips
            + [
                whole(rows),
                whole(rows),
                pl.BlockSpec((block, tile), hidden_index),
                pl.BlockSpec((block, tile), pre_index),
                whole(row),
                whole(row),
                pl.BlockSpec((1, tile), hidden_index),
            ],
            scratch_shapes=[
                f32(model_width, block),
                f32(block, tile),
                f32(8, tile),
                f32(block, model_width),
                f32(block, model_width),
                f32(tiles, block, tile),
                f32(tiles, block, tile),
                f32(tiles, block, tile),
                f32(block, model_width),
                f32(7, block, 128),
            ],
        ),
        out_shape=[narrow, jax.ShapeDtypeStruct(rows, jnp.float32), narrow]
        + [jax.ShapeDtypeStruct((share, block), jnp.bfloat16)] * chips
        + [
            narrow,
            narrow,
            jax.ShapeDtypeStruct((block, hidden), jnp.bfloat16),
            jax.ShapeDtypeStruct((block, hidden), jnp.bfloat16),
            jax.ShapeDtypeStruct(row, jnp.float32),
            jax.ShapeDtypeStruct(row, jnp.float32),
            jax.ShapeDtypeStruct((1, hidden), jnp.float32),
        ],
        compiler_params=pltpu.CompilerParams(vmem_limit_bytes=36 << 20),
        cost_estimate=NO_COST,
        name="middle",
    )(position, *mixed, tokens, cotangent, w_out, w_up, w_down, *gains)


def down_kernel(per, position, bent_ref, cot_ref, keep_ref, send_ref):
    first_core = position[1] == 0
    grad = lax.dot_general(
        bent_ref[...], cot_ref[...], (((0,), (0,)), ((), ())), preferred_element_type=jnp.float32
    ).astype(jnp.bfloat16)
    for part in range(keep_ref.shape[0]):
        even = grad[2 * per * part : 2 * per * part + per]
        odd = grad[2 * per * part + per : 2 * per * (part + 1)]
        keep_ref[part] = jnp.where(first_core, even, odd)
        send_ref[part] = jnp.where(first_core, odd, even)


def down_grad(position, bent, cotangent, per):
    (block, hidden), model_width = bent.shape, cotangent.shape[1]
    tiles, chunks = hidden // model_width, hidden // (2 * per)
    out = jax.ShapeDtypeStruct((chunks, per, model_width), jnp.bfloat16)
    out_spec = pl.BlockSpec((chunks // tiles, per, model_width), lambda i, pos: (i, 0, 0))
    return pl.pallas_call(
        partial(down_kernel, per),
        grid_spec=pltpu.PrefetchScalarGridSpec(
            num_scalar_prefetch=1,
            grid=(tiles,),
            in_specs=[
                pl.BlockSpec((block, model_width), lambda i, pos: (0, i)),
                whole(cotangent.shape),
            ],
            out_specs=[out_spec, out_spec],
        ),
        out_shape=[out, out],
        compiler_params=pltpu.CompilerParams(vmem_limit_bytes=20 << 20),
        cost_estimate=NO_COST,
        name="down_grad",
    )(position, bent, cotangent)


def up_out_kernel(tiles, position, h2_ref, pre_ref, z_ref, gmid_ref, perm_ref, keep_ref, send_ref, left_ref):
    step = pl.program_id(0)
    chunks, per = keep_ref.shape[:2]

    @pl.when(step == 0)
    def _():
        left_ref[...] = nt_dot(perm_ref[...], h2_ref[...]).astype(jnp.bfloat16)

    def store(right):
        grad = nn_dot(left_ref[...], right)
        for chunk in range(chunks):
            keep_ref[chunk] = grad[chunk * per : (chunk + 1) * per].astype(jnp.bfloat16)
            first = (chunks + chunk) * per
            send_ref[chunk] = grad[first : first + per].astype(jnp.bfloat16)

    @pl.when(step < tiles)
    def _():
        store(pre_ref[...])

    @pl.when(step == tiles)
    def _():
        left_ref[...] = nt_dot(perm_ref[...], z_ref[...]).astype(jnp.bfloat16)
        store(gmid_ref[...])


def up_out_grad(position, h2, pre, z, gmid, perm, per):
    (block, hidden), model_width = pre.shape, h2.shape[1]
    tiles, chunks = hidden // model_width, model_width // (2 * per)
    out = jax.ShapeDtypeStruct((chunks, per * (tiles + 1), model_width), jnp.bfloat16)
    out_spec = pl.BlockSpec((chunks, per, model_width), lambda i, pos: (0, i, 0))
    return pl.pallas_call(
        partial(up_out_kernel, tiles),
        grid_spec=pltpu.PrefetchScalarGridSpec(
            num_scalar_prefetch=1,
            grid=(tiles + 1,),
            in_specs=[
                whole(h2.shape),
                pl.BlockSpec((block, model_width), lambda i, pos: (0, jnp.minimum(i, tiles - 1))),
                whole(z.shape),
                whole(gmid.shape),
                whole(perm.shape),
            ],
            out_specs=[out_spec, out_spec],
            scratch_shapes=[pltpu.VMEM((model_width, block), jnp.bfloat16)],
        ),
        out_shape=[out, out],
        compiler_params=pltpu.CompilerParams(vmem_limit_bytes=20 << 20),
        cost_estimate=NO_COST,
        name="up_out_grad",
    )(position, h2, pre, z, gmid, perm)


def final_kernel(chips, position, *refs):
    homes = refs[:chips]
    (
        tokens_ref,
        gmid_ref,
        wq_ref,
        wk_ref,
        wv_ref,
        gain_ref,
        out_ref,
        swap_ref,
    ) = refs[chips:]
    chip = position[0]
    block, model_width = tokens_ref.shape
    share = model_width // chips
    total = jnp.zeros((block, model_width), jnp.float32)
    for index, weight in enumerate((wq_ref, wk_ref, wv_ref)):
        for near in range(chips):
            start = pl.multiple_of(share * lax.rem(chip + near, chips), share)
            swap_ref[pl.ds(start, share), :] = homes[near][
                index * share : (index + 1) * share, :
            ].astype(jnp.float32)
        total = total + nt_dot(swap_ref[...].T.astype(jnp.bfloat16), weight[...])
    hat, rate = norm_parts(tokens_ref[...].astype(jnp.float32))
    back = norm_back(total, hat, rate, gain_ref[...])[0]
    out_ref[...] = (gmid_ref[...] + back).astype(jnp.bfloat16)


def final(position, homes, tokens, gmid, w_query, w_key, w_value, gain):
    block, model_width = tokens.shape
    return call_whole(
        partial(final_kernel, len(homes)),
        [jax.ShapeDtypeStruct((block, model_width), jnp.bfloat16)],
        "final",
        position,
        *homes,
        tokens,
        gmid,
        w_query,
        w_key,
        w_value,
        gain,
        scratch=[pltpu.VMEM((model_width, block), jnp.float32)],
    )[0]


def chip_shift(value, steps):
    count = lax.axis_size("seq")
    return lax.ppermute(value, "seq", [(i, (i + 2 * steps) % count) for i in range(count)])


def seq_swap(value, bit):
    return lax.ppermute(value, "seq", [(i, i ^ bit) for i in range(lax.axis_size("seq"))])


def row_swap(value, bit):
    return lax.ppermute(value, "row", [(i, i ^ bit) for i in range(lax.axis_size("row"))])


def sent(array):
    return array.astype(jnp.bfloat16)


def wide(array):
    return array.astype(jnp.float32)


def low_part(shape, keep):
    def index(i, bits):
        return (0, bits[2] if keep else 1 - bits[2], 0, 0, 0)

    return pl.BlockSpec((2, 1, shape[2] // 2) + shape[3:], index)


def high_part(shape, keep):
    def index(i, bits):
        return (bits[3] if keep else 1 - bits[3], 0, 1, 0, 0)

    return pl.BlockSpec((1, 2, shape[2] // 2) + shape[3:], index)


def outgoing_kernel(scalars, *refs):
    low_ref, high_ref = refs[-2:]
    first = 0
    for group in range(len(refs) // 4):
        low_a, low_b, high_a, high_b = refs[4 * group : 4 * group + 4]
        rows = slice(first, first + low_a.shape[3])
        low_ref[:, :, rows] = sent(wide(low_a[:, 0]) + wide(low_b[:, 0]))
        high_ref[:, :, rows] = sent(wide(high_a[0]) + wide(high_b[0]))
        first += low_a.shape[3]


def outgoing(scalars, groups, kept=False):
    arrays, specs = [], []
    for keep, other in groups:
        low, high = low_part(keep.shape, kept), high_part(keep.shape, kept)
        arrays += [keep, other, keep, other]
        specs += [low, low, high, high]
    shape = groups[0][0].shape
    rows = sum(keep.shape[3] for keep, _ in groups)
    out = jax.ShapeDtypeStruct((2, shape[2] // 2, rows, shape[4]), jnp.bfloat16)
    return call_whole(
        outgoing_kernel,
        [out, out],
        "kept" if kept else "outgoing",
        scalars,
        *arrays,
        in_specs=specs,
        limit=20,
    )


def halfway_kernel(groups, scalars, *refs):
    ins, outs = refs[: 4 * groups], refs[4 * groups :]
    low_bit, high_bit = scalars[2], scalars[3]
    low_keep, low_send, high_keep, high_send = outs
    first = 0
    for group in range(groups):
        low, high, low_in, high_in = ins[4 * group : 4 * group + 4]
        rows = slice(first, first + low.shape[2])
        for target, side in ((low_keep, high_bit), (low_send, 1 - high_bit)):
            target[:, rows] = sent(wide(low[side]) + wide(low_in[side]))
        for target, side in ((high_keep, low_bit), (high_send, 1 - low_bit)):
            target[:, rows] = sent(wide(high[side]) + wide(high_in[side]))
        first += low.shape[2]


def halfway(scalars, groups):
    arrays = [array for group in groups for array in group]
    rows = sum(group[0].shape[2] for group in groups)
    out = jax.ShapeDtypeStruct((arrays[0].shape[1], rows, arrays[0].shape[3]), jnp.bfloat16)
    return call_whole(
        partial(halfway_kernel, len(groups)), [out] * 4, "halfway", scalars, *arrays, limit=24
    )


def split_kernel(chips, groups, scalars, *refs):
    ins, outs = refs[: 4 * groups], refs[4 * groups : 4 * groups + chips]
    all_ref = refs[-1]
    half = chips // 2
    first = 0
    for group in range(groups):
        low_keep, low_in, high_keep, high_in = ins[4 * group : 4 * group + 4]
        rows = slice(first, first + low_in.shape[1])
        all_ref[:half, rows] = sent(wide(low_keep[...]) + wide(low_in[...]))
        all_ref[half:, rows] = sent(wide(high_keep[...]) + wide(high_in[...]))
        first += low_in.shape[1]
    for step in range(chips):
        outs[step][...] = all_ref[lax.rem(scalars[0] + step, chips)]


def split(scalars, groups, chips):
    arrays = [array for group in groups for array in group]
    rows = sum(group[0].shape[1] for group in groups)
    width = arrays[0].shape[2]
    return call_whole(
        partial(split_kernel, chips, len(groups)),
        [jax.ShapeDtypeStruct((rows, width), jnp.bfloat16)] * chips,
        "split",
        scalars,
        *arrays,
        scratch=[pltpu.VMEM((chips, rows, width), jnp.bfloat16)],
    )


def lay_flat(target, values, first, step):
    for piece in range(values.shape[1] // 128):
        target[pl.ds(first + piece, values.shape[0], step), :] = values[
            :, 128 * piece : 128 * (piece + 1)
        ]


def finish_kernel(chips, per, share, factor, scalars, *refs):
    arrived, heads_in, refs = refs[:chips], refs[chips : 2 * chips], refs[chips:]
    down_ref, up_ref, out_ref, query_ref, key_ref, value_ref, gains_ref, heads_ref = refs[chips:]
    width = arrived[0].shape[1]
    chip, pieces = scalars[0], width // 128
    tiles = up_ref.shape[0] * 128 // (per * width)
    down_rows = down_ref.shape[0] * 128 // width

    def total(first, rows):
        result = wide(arrived[0][first : first + rows, :])
        for part in arrived[1:]:
            result = result + wide(part[first : first + rows, :])
        return result * factor

    lay_flat(down_ref, total(0, down_rows), 0, pieces)
    for tile in range(tiles):
        lay_flat(up_ref, total(down_rows + tile * per, per), tile * pieces, tiles * pieces)
    lay_flat(out_ref, total(down_rows + tiles * per, per), 0, pieces)
    gains = wide(heads_in[0][:8, -128:])
    for part in heads_in[1:]:
        gains = gains + wide(part[:8, -128:])
    gains_ref[...] = gains * factor
    for step in range(chips):
        heads_ref[lax.rem(chip - step + chips, chips)] = wide(heads_in[step][:, : 3 * share])
    for index, target in enumerate((query_ref, key_ref, value_ref)):
        values = jnp.concatenate(
            [heads_ref[near][:, index * share : (index + 1) * share] for near in range(chips)], axis=1
        )
        lay_flat(target, values * factor, 0, pieces)


def finish(scalars, arrived, hidden, parts, per, share, factor):
    chips, width = len(arrived) // 2, arrived[0].shape[1]
    square = jax.ShapeDtypeStruct((per * width // 128, 128), jnp.float32)
    large = jax.ShapeDtypeStruct((per * hidden // 128, 128), jnp.float32)
    return call_whole(
        partial(finish_kernel, chips, per, share, factor),
        [large, large, square, square, square, square, jax.ShapeDtypeStruct((8, 128), jnp.float32)],
        "finish",
        scalars,
        *arrived,
        scratch=[pltpu.VMEM((chips, per, 3 * share), jnp.float32)],
    )


def gathered(rows, chips, chip):
    if chips != 4:
        return [rows] + [chip_shift(rows, step) for step in range(1, chips)]
    behind, ahead = chip_shift(rows, 1), chip_shift(rows, -1)
    up = [(2 * i + core, 2 * i + 2 + core) for i in (1, 2) for core in (0, 1)]
    down = [(2 * i + core, 2 * i - 2 + core) for i in (1, 2) for core in (0, 1)]
    across = jnp.where(
        chip < 2, lax.ppermute(ahead, "seq", down), lax.ppermute(behind, "seq", up)
    )
    return [rows, behind, across, ahead]


def fast_local(
    tokens,
    lengths,
    w_query,
    w_key,
    w_value,
    w_out,
    w_up,
    w_down,
    gain_attend,
    gain_inner,
    gain_feed,
    gain_hidden,
    cotangent,
):
    block, model_width = tokens.shape
    hidden = w_up.shape[1]
    size = model_width // HEADS
    lanes = 2 * size
    scale = size ** (-0.5)
    seq_devices, row_devices = lax.axis_size("seq"), lax.axis_size("row")
    chips = seq_devices // 2
    heads = HEADS // chips
    share = heads * size
    spread = heads * lanes
    parts = row_devices * seq_devices
    position, row = lax.axis_index("seq"), lax.axis_index("row")
    chip, core = position // 2, position % 2
    place = jnp.stack([chip, core, row % 2, row // 2]).astype(jnp.int32)
    bounds = jnp.cumsum(lengths[0])[:-1]
    factor = 1.0 / math.sqrt(block * parts)

    normed_b = call_whole(
        norm_kernel,
        [jax.ShapeDtypeStruct(tokens.shape, jnp.bfloat16)],
        "norm",
        jnp.zeros((1,), jnp.int32),
        tokens,
        gain_attend[None, :],
    )[0]
    own = gathered(normed_b, chips, chip)

    chip_ids = (chip - jnp.arange(chips, dtype=jnp.int32)) % chips
    query_starts = block * (2 * chip_ids + core)
    key_starts = jnp.concatenate([query_starts, block * (2 * chip_ids + 1 - core)])
    in_block = jnp.arange(block, dtype=jnp.int32)[None, :]
    query_places = (query_starts[:, None] + in_block).reshape(-1)
    doc_line = jnp.max(jnp.where(bounds[:, None] <= query_places[None, :], bounds[:, None], 0), axis=0)
    meta = jnp.concatenate(
        [query_starts, key_starts, doc_line.reshape(chips, block)[:, 0], doc_line.reshape(chips, block)[:, -1]]
    )
    doc_line = doc_line[None, :]

    feature = jnp.arange(model_width, dtype=jnp.int32)
    wide_lane = jnp.arange(spread, dtype=jnp.int32)
    source = chip * share + wide_lane // lanes * size + wide_lane % lanes
    pick_wide = ((feature[:, None] == source[None, :]) & (wide_lane % lanes < size)[None, :]).astype(
        jnp.bfloat16
    )
    narrow = chip * share + jnp.arange(share, dtype=jnp.int32)
    pick_narrow = (feature[:, None] == narrow[None, :]).astype(jnp.bfloat16)

    def picked(weight, choice):
        return sent(nn_dot(weight, choice))

    def picked_rows(weight, choice):
        return sent(
            lax.dot_general(
                choice, weight, (((0,), (1,)), ((), ())), preferred_element_type=jnp.float32
            )
        )

    per = model_width // parts
    order = jnp.arange(model_width, dtype=jnp.int32)
    chunk, inside = order // per, order % per
    chunks = parts // 2
    parity = jnp.where(chunk < chunks, core, 1 - core)
    wanted = (2 * (chunk % chunks) + parity) * per + inside
    perm = (wanted[:, None] == feature[None, :]).astype(jnp.bfloat16)

    gains_share = (3 * model_width + hidden) // parts
    gains_rows = -(-gains_share // 128)
    line = jnp.arange(parts * gains_rows, dtype=jnp.int32)
    half_lines = parts // 2 * gains_rows
    line_parity = jnp.where(line < half_lines, core, 1 - core)
    owner = 2 * (line % half_lines // gains_rows) + line_parity
    first_gain = owner * gains_share + 128 * (line % gains_rows)
    end_gain = jnp.minimum(first_gain + 128, (owner + 1) * gains_share)
    gain_index = jnp.arange(gains_share * parts, dtype=jnp.int32)
    where_row = (
        (gain_index[None, :] >= first_gain[:, None]) & (gain_index[None, :] < end_gain[:, None])
    ).astype(jnp.bfloat16)
    where_lane = (
        (gain_index % gains_share % 128)[:, None] == jnp.arange(128, dtype=jnp.int32)[None, :]
    ).astype(jnp.bfloat16)
    early = (
        jnp.concatenate([query_starts, 2 * block * chip_ids + block * (1 - core), heads * chip[None]]),
        meta,
        doc_line,
        perm,
        picked_rows(w_query, pick_wide),
        picked(w_key, pick_wide),
        picked_rows(w_value, pick_narrow),
        picked_rows(w_key, pick_narrow),
        picked(w_value, pick_wide),
        picked_rows(w_query, pick_narrow),
        gain_attend[None, :],
        gain_inner[None, :],
        gain_feed[None, :],
        gain_hidden[None, :],
        place,
        where_row,
        where_lane,
    )
    own[1], early = lax.optimization_barrier((own[1], early))
    starts, meta, doc_line, perm, wq_wide, wk_wide, wv_rows, wk_rows, wv_wide, wq_rows = early[:10]
    gain_first, gain_inner, gain_feed, gain_hidden, place = early[10:15]
    where_row, where_lane = early[15:]
    sibling = [seq_swap(rows, 1) for rows in own]
    q_ext, k_ext, v_t = project(
        starts,
        own + sibling,
        wq_wide,
        wk_wide,
        wv_rows,
        chips,
        heads,
        scale,
    )
    mixed, lse, *mixed_b = attend(meta, doc_line, q_ext, k_ext, v_t, heads, block)
    mixed_b, wk_rows = lax.optimization_barrier((mixed_b, wk_rows))
    k_t, v_ext = project_back(place, own + sibling, wk_rows, wv_wide)
    back = [mixed_b[0]] + [chip_shift(mixed_b[step], -step) for step in range(1, chips)]
    back, k_t, v_ext = lax.optimization_barrier((back, k_t, v_ext))
    outs = middle(
        place, back, tokens, cotangent, w_out, w_up, w_down, (gain_inner, gain_feed, gain_hidden)
    )
    result, grad_middle, gmid_b = outs[:3]
    go = outs[3 : 3 + chips]
    z, h2, bent, pre, dinner, dfeed, dhidden = outs[3 + chips :]
    keep_a, send_a = down_grad(place, bent, cotangent, hidden // parts)
    keep_b, send_b = up_out_grad(place, h2, pre, z, gmid_b, perm, per)
    go, keep_b, send_b = lax.optimization_barrier((go, keep_b, send_b))
    go = [go[0]] + [chip_shift(go[step], step) for step in range(1, chips)]

    def gridded(array):
        return array.reshape((2, 2, chips) + array.shape[1:])

    sums = [
        (gridded(keep), gridded(seq_swap(send, 1)))
        for keep, send in ((keep_a, send_a), (keep_b, send_b))
    ]
    low, high = outgoing(place, sums)
    arrived_sums = [row_swap(low, 1), row_swap(high, 2)]
    dq, pair, other = attend_back(
        meta, doc_line, q_ext, go, mixed, lse, k_ext, k_t, v_ext, heads, block, scale
    )
    grads = join_parts(place, dq, pair, seq_swap(other, 1), chips)
    home = [grads[0]] + [chip_shift(grads[step], -step) for step in range(1, chips)]
    grads, sums = lax.optimization_barrier((grads, sums))
    kept = outgoing(place, sums, True)
    mine_grad, send_grad = head_grads(
        place,
        own,
        grads,
        (wq_rows, wk_rows, wv_rows),
        gain_first,
        (dinner, dfeed, dhidden),
        perm,
        where_row,
        where_lane,
        per,
    )
    arrived_sums, kept, mine_grad, send_grad = lax.optimization_barrier(
        (arrived_sums, kept, mine_grad, send_grad)
    )
    low_keep, low_send, high_keep, high_send = halfway(place, [(*kept, *arrived_sums)])
    low_in, high_in = row_swap(low_send, 2), row_swap(high_send, 1)
    home, mine_grad, send_grad = lax.optimization_barrier((home, mine_grad, send_grad))
    mine_grad, other_grad = gridded(mine_grad), gridded(seq_swap(send_grad, 1))
    stage = split(after(place, home, SOME_COST), [(low_keep, low_in, high_keep, high_in)], chips)
    arrived = [stage[0]] + [chip_shift(stage[step], step) for step in range(1, chips)]
    grad_input = final(
        place, home, tokens, grad_middle, w_query, w_key, w_value, gain_first
    )
    low, high = outgoing(place, [(mine_grad, other_grad)])
    low_keep, low_send, high_keep, high_send = halfway(
        place,
        [(*outgoing(place, [(mine_grad, other_grad)], True), row_swap(low, 1), row_swap(high, 2))],
    )
    stage = split(
        place, [(low_keep, row_swap(low_send, 2), high_keep, row_swap(high_send, 1))], chips
    )
    arrived += [stage[0]] + [chip_shift(stage[step], step) for step in range(1, chips)]
    down, up, out, query, key, value, gains_part = finish(
        place, arrived, hidden, parts, per, share, factor
    )
    return (
        result,
        grad_input,
        query.reshape(-1),
        key.reshape(-1),
        value.reshape(-1),
        out.reshape(-1),
        up.reshape(-1),
        down.reshape(-1),
        gains_part.reshape(-1)[:gains_share],
    )


def local(*arrays):
    seq_devices, row_devices = lax.axis_size("seq"), lax.axis_size("row")
    block = arrays[0].shape[0]
    one_segment = block * seq_devices <= SEGMENT and block % 2 ** (PATTERNS - 1) == 0
    if one_segment and seq_devices in (2, 4, 8) and row_devices == 4:
        return fast_local(*arrays)
    return ring_local(*arrays)


def solution(mesh):
    return jax.shard_map(
        local,
        mesh=mesh,
        in_specs=(
            P(("row", "seq"), None),
            P("row", None),
            P(),
            P(),
            P(),
            P(),
            P(),
            P(),
            P(),
            P(),
            P(),
            P(),
            P(("row", "seq"), None),
        ),
        out_specs=(
            P(("row", "seq"), None),
            P(("row", "seq"), None),
            P(("row", "seq")),
            P(("row", "seq")),
            P(("row", "seq")),
            P(("row", "seq")),
            P(("row", "seq")),
            P(("row", "seq")),
            P(("row", "seq")),
        ),
        check_vma=False,
    )
```

```python
from functools import partial
from functools import reduce
import math

import jax
import jax.numpy as jnp
import numpy as np
from jax import lax
from jax.experimental import pallas as pl
from jax.experimental.pallas import tpu as pltpu
from jax.sharding import PartitionSpec as P

HEADS = 12
SEGMENT = 2048
PATTERNS = 5


big_negative = -1e30


def shifted_2(shard, axis, by):
    length = lax.axis_size(axis)
    pairs = [(i, i + by) for i in range(length) if 0 <= i + by < length]
    return lax.ppermute(shard, axis, pairs)


def shifted_3(value, axis, steps):
    count = lax.axis_size(axis)
    pairs = [(source, (source + steps) % count) for source in range(count)]
    return lax.ppermute(value, axis, pairs)


def layer_norm(values, gain_vector):
    centre = jnp.mean(values, axis=-1, keepdims=True)
    shifted = values - centre
    variance = jnp.mean(shifted * shifted, axis=-1, keepdims=True)
    return shifted * lax.rsqrt(variance + 1e-05) * gain_vector


def hidden_norm(hidden_pre, gain_vector):
    return layer_norm(jax.nn.gelu(hidden_pre, approximate=True), gain_vector)


def selector(stride, head_count):
    return jnp.arange(stride)[:, None] == (jnp.arange(head_count) % stride)[None, :]


def compact(full_array, stride):
    length_in, head_count, inner_size = full_array.shape
    shaped = full_array.reshape(length_in // stride, stride, head_count, inner_size)
    picked = jnp.where(
        selector(stride, head_count)[None, :, :, None], shaped, jnp.zeros((), full_array.dtype)
    )
    return jnp.sum(picked, axis=1)


def expand(part_array, stride, fill_value):
    part_rows, head_count, inner_size = part_array.shape
    widened = jnp.where(
        selector(stride, head_count)[None, :, :, None],
        part_array[:, None],
        jnp.asarray(fill_value, part_array.dtype),
    )
    return widened.reshape(part_rows * stride, head_count, inner_size)


def positions(start_pos, part_rows, stride, head_count):
    row_ids = jnp.arange(part_rows, dtype=jnp.int32)[:, None] * stride
    head_ids = (jnp.arange(head_count, dtype=jnp.int32) % stride)[None, :]
    return start_pos + row_ids + head_ids


def doc_index(places, doc_bounds):
    return jnp.sum((places[..., None] >= doc_bounds).astype(jnp.int32), axis=-1)


def block_mask(doc_query, doc_key, local_block):
    allowed = doc_query.T[:, :, None] == doc_key.T[:, None, :]
    if local_block:
        rank_ids = jnp.arange(doc_query.shape[0])
        allowed = allowed & (rank_ids[:, None] >= rank_ids[None, :])[None]
    return allowed


def forward_block(query_part, key_part, value_part, allowed, score_scale):
    scores = (
        jnp.einsum("qhd,khd->hqk", query_part, key_part, preferred_element_type=jnp.float32)
        * score_scale
    )
    scores = jnp.where(allowed, scores, big_negative)
    row_peak = jnp.max(scores, axis=-1)
    weights = jnp.where(allowed, jnp.exp(scores - row_peak[..., None]), 0.0)
    row_total = jnp.sum(weights, axis=-1)
    mixed = jnp.einsum(
        "hqk,khd->qhd", weights.astype(jnp.bfloat16), value_part, preferred_element_type=jnp.float32
    )
    return (row_peak.T, row_total.T, mixed)


def merge(carried, new_block):
    best_peak = jnp.maximum(carried[0], new_block[0])
    keep_factor = jnp.exp(carried[0] - best_peak)
    take_factor = jnp.exp(new_block[0] - best_peak)
    new_total = carried[1] * keep_factor + new_block[1] * take_factor
    new_mixed = carried[2] * keep_factor[..., None] + new_block[2] * take_factor[..., None]
    return (best_peak, new_total, new_mixed)


def backward_block(
    query_part, grad_part, lse_part, delta_part, key_part, value_part, allowed, score_scale
):
    scores = (
        jnp.einsum("qhd,khd->hqk", query_part, key_part, preferred_element_type=jnp.float32)
        * score_scale
    )
    probs = jnp.where(allowed, jnp.exp(scores - lse_part.T[:, :, None]), 0.0)
    dots = jnp.einsum("qhd,khd->hqk", grad_part, value_part, preferred_element_type=jnp.float32)
    grad_scores = (probs * (dots - delta_part.T[:, :, None])).astype(jnp.bfloat16)
    query_grad = (
        jnp.einsum("hqk,khd->qhd", grad_scores, key_part, preferred_element_type=jnp.float32)
        * score_scale
    )
    key_grad = (
        jnp.einsum("hqk,qhd->khd", grad_scores, query_part, preferred_element_type=jnp.float32)
        * score_scale
    )
    value_grad = jnp.einsum(
        "hqk,qhd->khd", probs.astype(jnp.bfloat16), grad_part, preferred_element_type=jnp.float32
    )
    return (query_grad, key_grad, value_grad)


def keep_state(carried):
    return carried


def ring_local(
    tokens,
    lengths,
    w_query,
    w_key,
    w_value,
    w_out,
    w_up,
    w_down,
    gain_attend,
    gain_inner,
    gain_feed,
    gain_hidden,
    cotangent,
):
    block_rows, model_width = tokens.shape
    head_count = HEADS
    head_size = model_width // head_count
    score_scale = head_size ** (-0.5)
    seq_devices = lax.axis_size("seq")
    all_devices = seq_devices * lax.axis_size("row")
    my_index = lax.axis_index("seq")
    seq_total = block_rows * seq_devices
    doc_bounds = jnp.cumsum(lengths[0])[:-1]
    patterns = [
        (2**pattern, min(SEGMENT * 2**pattern, seq_total) // block_rows)
        for pattern in range(PATTERNS)
    ]
    near_ids = [0, 1]
    far_ids = list(range(2, PATTERNS))
    reach = patterns[1][1]
    far_rows = [block_rows // patterns[pattern][0] for pattern in far_ids]
    far_starts = [sum(far_rows[:slot_id]) for slot_id in range(len(far_ids))]
    far_total = sum(far_rows)

    def key_docs(pattern, source):
        stride = patterns[pattern][0]
        return doc_index(
            positions(source * block_rows, block_rows // stride, stride, head_count), doc_bounds
        )

    def is_live(pattern, cycle_step):
        group_size = patterns[pattern][1]
        return (cycle_step < group_size) & (my_index % group_size >= cycle_step)

    source_x = tokens.astype(jnp.float32)
    normed, attend_back = jax.vjp(layer_norm, source_x, gain_attend)
    normed_b = normed.astype(jnp.bfloat16)
    query_b = jnp.dot(normed_b, w_query, preferred_element_type=jnp.float32).astype(jnp.bfloat16)
    key_b = jnp.dot(normed_b, w_key, preferred_element_type=jnp.float32).astype(jnp.bfloat16)
    value_b = jnp.dot(normed_b, w_value, preferred_element_type=jnp.float32).astype(jnp.bfloat16)
    query_heads = query_b.reshape(block_rows, head_count, head_size)
    key_heads = key_b.reshape(block_rows, head_count, head_size)
    value_heads = value_b.reshape(block_rows, head_count, head_size)
    query_parts = [compact(query_heads, stride) for stride, group_size in patterns]
    key_parts = [compact(key_heads, stride) for stride, group_size in patterns]
    value_parts = [compact(value_heads, stride) for stride, group_size in patterns]
    own_docs = [key_docs(pattern, my_index) for pattern in range(PATTERNS)]
    states = [
        forward_block(
            query_parts[pattern],
            key_parts[pattern],
            value_parts[pattern],
            block_mask(own_docs[pattern], own_docs[pattern], True),
            score_scale,
        )
        for pattern in range(PATTERNS)
    ]

    def unpack_near(key_block):
        key_full = key_block[:, :model_width].reshape(block_rows, head_count, head_size)
        value_full = key_block[:, model_width:].reshape(block_rows, head_count, head_size)
        return (key_full, value_full)

    def near_fold_parts(pattern, key_part, value_part, source, carried):
        new_block = forward_block(
            query_parts[pattern],
            key_part,
            value_part,
            block_mask(own_docs[pattern], key_docs(pattern, source), False),
            score_scale,
        )
        return merge(carried, new_block)

    def near_fold(pattern, key_full, value_full, source, carried):
        stride = patterns[pattern][0]
        return near_fold_parts(
            pattern, compact(key_full, stride), compact(value_full, stride), source, carried
        )

    pair_block = jnp.concatenate([key_b, value_b], axis=1)
    kept_blocks = jnp.zeros((max(reach - 1, 1), block_rows, 2 * model_width), jnp.bfloat16)

    def near_forward(cycle_step, loop_state):
        key_block, near_now, kept_store = loop_state
        key_block = shifted_2(key_block, "seq", 1)
        key_full, value_full = unpack_near(key_block)
        new_states = []
        for pattern in near_ids:
            new_states.append(
                lax.cond(
                    is_live(pattern, cycle_step),
                    partial(near_fold, pattern, key_full, value_full, my_index - cycle_step),
                    keep_state,
                    near_now[pattern],
                )
            )
        return (key_block, tuple(new_states), kept_store)

    _, near_states, kept_blocks = lax.fori_loop(
        1, reach, near_forward, (pair_block, (states[0], states[1]), kept_blocks)
    )
    far_block = jnp.concatenate(
        [
            jnp.concatenate(
                [
                    key_parts[pattern].reshape(rows_here, model_width),
                    value_parts[pattern].reshape(rows_here, model_width),
                ],
                axis=1,
            )
            for pattern, rows_here in zip(far_ids, far_rows)
        ],
        axis=0,
    )

    def unpack_far(key_block, slot_id):
        rows_here = far_rows[slot_id]
        row_begin = far_starts[slot_id]
        piece_rows = key_block[row_begin : row_begin + rows_here]
        key_part = piece_rows[:, :model_width].reshape(rows_here, head_count, head_size)
        value_part = piece_rows[:, model_width:].reshape(rows_here, head_count, head_size)
        return (key_part, value_part)

    def far_fold(pattern, key_part, value_part, source, carried):
        new_block = forward_block(
            query_parts[pattern],
            key_part,
            value_part,
            block_mask(own_docs[pattern], key_docs(pattern, source), False),
            score_scale,
        )
        return merge(carried, new_block)

    def far_update(far_now, key_block, cycle_step):
        new_states = []
        for slot_id, pattern in enumerate(far_ids):
            key_part, value_part = unpack_far(key_block, slot_id)
            new_states.append(
                lax.cond(
                    is_live(pattern, cycle_step),
                    partial(far_fold, pattern, key_part, value_part, my_index - cycle_step),
                    keep_state,
                    far_now[slot_id],
                )
            )
        return tuple(new_states)

    far_states = tuple((states[pattern] for pattern in far_ids))

    def far_forward(cycle_step, loop_state):
        key_block, far_now = loop_state
        key_block = shifted_2(key_block, "seq", 1)
        return (key_block, far_update(far_now, key_block, cycle_step))

    _, far_states = lax.fori_loop(1, seq_devices, far_forward, (far_block, far_states))
    ordered = list(near_states) + list(far_states)
    peaks = [
        expand(ordered[pattern][0][..., None], patterns[pattern][0], big_negative)[..., 0]
        for pattern in range(PATTERNS)
    ]
    best_peak = reduce(jnp.maximum, peaks)
    weight_sum = jnp.zeros((block_rows, head_count), jnp.float32)
    mixed_sum = jnp.zeros((block_rows, head_count, head_size), jnp.float32)
    for pattern in range(PATTERNS):
        stride = patterns[pattern][0]
        factor = jnp.exp(peaks[pattern] - best_peak)
        weight_sum = (
            weight_sum + expand(ordered[pattern][1][..., None], stride, 0.0)[..., 0] * factor
        )
        mixed_sum = mixed_sum + expand(ordered[pattern][2], stride, 0.0) * factor[..., None]
    attended = mixed_sum / weight_sum[..., None]
    log_total = best_peak + jnp.log(weight_sum)
    inner_out, inner_back = jax.vjp(
        layer_norm, attended.reshape(block_rows, model_width), gain_inner
    )
    inner_b = inner_out.astype(jnp.bfloat16)
    middle = source_x + jnp.dot(inner_b, w_out, preferred_element_type=jnp.float32)
    normed_two, feed_back = jax.vjp(layer_norm, middle, gain_feed)
    normed_two_b = normed_two.astype(jnp.bfloat16)
    hidden_pre = jnp.dot(normed_two_b, w_up, preferred_element_type=jnp.float32)
    hidden, hidden_back = jax.vjp(hidden_norm, hidden_pre, gain_hidden)
    hidden_b = hidden.astype(jnp.bfloat16)
    result = (middle + jnp.dot(hidden_b, w_down, preferred_element_type=jnp.float32)).astype(
        jnp.bfloat16
    )
    grad_down = jnp.einsum("tf,tg->fg", hidden_b, cotangent, preferred_element_type=jnp.float32)
    grad_hidden = jnp.einsum("tg,fg->tf", cotangent, w_down, preferred_element_type=jnp.float32)
    grad_pre, grad_gain_hidden = hidden_back(grad_hidden)
    grad_pre_b = grad_pre.astype(jnp.bfloat16)
    grad_up = jnp.einsum("tf,tg->fg", normed_two_b, grad_pre_b, preferred_element_type=jnp.float32)
    grad_normed_two = jnp.einsum("tg,fg->tf", grad_pre_b, w_up, preferred_element_type=jnp.float32)
    grad_middle_part, grad_gain_feed = feed_back(grad_normed_two)
    grad_middle = cotangent.astype(jnp.float32) + grad_middle_part
    grad_middle_b = grad_middle.astype(jnp.bfloat16)
    grad_out = jnp.einsum("tf,tg->fg", inner_b, grad_middle_b, preferred_element_type=jnp.float32)
    grad_inner = jnp.einsum("tg,fg->tf", grad_middle_b, w_out, preferred_element_type=jnp.float32)
    grad_attended, grad_gain_inner = inner_back(grad_inner)
    grad_heads = grad_attended.astype(jnp.bfloat16).reshape(block_rows, head_count, head_size)
    delta_rows = jnp.sum(grad_heads.astype(jnp.float32) * attended, axis=-1)
    grad_parts = [compact(grad_heads, stride) for stride, group_size in patterns]
    lse_parts = [compact(log_total[..., None], stride)[..., 0] for stride, group_size in patterns]
    delta_parts = [
        compact(delta_rows[..., None], stride)[..., 0] for stride, group_size in patterns
    ]
    query_grads = []
    home_keys = []
    home_values = []
    for pattern in range(PATTERNS):
        part_query, part_key, part_value = backward_block(
            query_parts[pattern],
            grad_parts[pattern],
            lse_parts[pattern],
            delta_parts[pattern],
            key_parts[pattern],
            value_parts[pattern],
            block_mask(own_docs[pattern], own_docs[pattern], True),
            score_scale,
        )
        query_grads.append(part_query)
        home_keys.append(part_key)
        home_values.append(part_value)

    def fetch_full(key_block):
        return shifted_2(key_block, "seq", 1)

    def near_grad(pattern, key_full, value_full, source, operands):
        query_grad, travel = operands
        stride = patterns[pattern][0]
        part_query, part_key, part_value = backward_block(
            query_parts[pattern],
            grad_parts[pattern],
            lse_parts[pattern],
            delta_parts[pattern],
            compact(key_full, stride),
            compact(value_full, stride),
            block_mask(own_docs[pattern], key_docs(pattern, source), False),
            score_scale,
        )
        spread_rows = jnp.concatenate(
            [
                expand(part_key, stride, 0.0).reshape(block_rows, model_width),
                expand(part_value, stride, 0.0).reshape(block_rows, model_width),
            ],
            axis=1,
        )
        return (query_grad + part_query, travel + spread_rows)

    def near_backward(cycle_step, loop_state):
        key_block, grads_now, travel = loop_state
        key_block = fetch_full(key_block)
        travel = shifted_3(travel.astype(jnp.bfloat16), "seq", 1).astype(travel.dtype)
        key_full, value_full = unpack_near(key_block)
        new_grads = list(grads_now)
        for pattern in near_ids:
            new_grads[pattern], travel = lax.cond(
                is_live(pattern, cycle_step),
                partial(near_grad, pattern, key_full, value_full, my_index - cycle_step),
                keep_state,
                (new_grads[pattern], travel),
            )
        return (key_block, tuple(new_grads), travel)

    own_key_near = expand(home_keys[0], 1, 0.0) + expand(home_keys[1], 2, 0.0)
    own_value_near = expand(home_values[0], 1, 0.0) + expand(home_values[1], 2, 0.0)
    near_start = jnp.concatenate(
        [
            own_key_near.reshape(block_rows, model_width),
            own_value_near.reshape(block_rows, model_width),
        ],
        axis=1,
    )
    _, near_query, travel_near = lax.fori_loop(
        1, reach, near_backward, (pair_block, (query_grads[0], query_grads[1]), near_start)
    )
    near_home = shifted_3(travel_near.astype(jnp.bfloat16), "seq", 1 - reach).astype(
        travel_near.dtype
    )
    near_key_add = near_home[:, :model_width].reshape(block_rows, head_count, head_size)
    near_value_add = near_home[:, model_width:].reshape(block_rows, head_count, head_size)

    def far_grad(slot_id, key_part, value_part, source, operands):
        query_grad, travel = operands
        pattern = far_ids[slot_id]
        rows_here = far_rows[slot_id]
        row_begin = far_starts[slot_id]
        part_query, part_key, part_value = backward_block(
            query_parts[pattern],
            grad_parts[pattern],
            lse_parts[pattern],
            delta_parts[pattern],
            key_part,
            value_part,
            block_mask(own_docs[pattern], key_docs(pattern, source), False),
            score_scale,
        )
        spread_rows = jnp.concatenate(
            [part_key.reshape(rows_here, model_width), part_value.reshape(rows_here, model_width)],
            axis=1,
        )
        return (
            query_grad + part_query,
            travel.at[row_begin : row_begin + rows_here].add(spread_rows),
        )

    def far_back_update(grads_now, travel, key_block, cycle_step):
        new_grads = list(grads_now)
        for slot_id, pattern in enumerate(far_ids):
            key_part, value_part = unpack_far(key_block, slot_id)
            new_grads[slot_id], travel = lax.cond(
                is_live(pattern, cycle_step),
                partial(far_grad, slot_id, key_part, value_part, my_index - cycle_step),
                keep_state,
                (new_grads[slot_id], travel),
            )
        return (tuple(new_grads), travel)

    far_query = tuple((query_grads[pattern] for pattern in far_ids))
    far_empty = jnp.zeros((far_total, 2 * model_width), jnp.float32)

    def far_send(travel):
        return shifted_3(travel.astype(jnp.bfloat16), "seq", 1).astype(travel.dtype)

    def far_backward(cycle_step, loop_state):
        key_block, grads_now, travel = loop_state
        key_block = shifted_2(key_block, "seq", 1)
        travel = far_send(travel)
        grads_now, travel = far_back_update(grads_now, travel, key_block, cycle_step)
        return (key_block, grads_now, travel)

    _, far_query, travel_far = lax.fori_loop(
        1, seq_devices, far_backward, (far_block, far_query, far_empty)
    )
    far_home = far_send(travel_far)
    all_query = list(near_query) + list(far_query)
    query_grad = jnp.zeros((block_rows, head_count, head_size), jnp.float32)
    key_grad = near_key_add
    value_grad = near_value_add
    for pattern in range(PATTERNS):
        stride = patterns[pattern][0]
        query_grad = query_grad + expand(all_query[pattern], stride, 0.0)
    for pattern in far_ids:
        stride = patterns[pattern][0]
        key_grad = key_grad + expand(home_keys[pattern], stride, 0.0)
        value_grad = value_grad + expand(home_values[pattern], stride, 0.0)
    for slot_id, pattern in enumerate(far_ids):
        stride = patterns[pattern][0]
        rows_here = far_rows[slot_id]
        row_begin = far_starts[slot_id]
        piece_rows = far_home[row_begin : row_begin + rows_here]
        key_grad = key_grad + expand(
            piece_rows[:, :model_width].reshape(rows_here, head_count, head_size), stride, 0.0
        )
        value_grad = value_grad + expand(
            piece_rows[:, model_width:].reshape(rows_here, head_count, head_size), stride, 0.0
        )
    grad_query_b = query_grad.reshape(block_rows, model_width).astype(jnp.bfloat16)
    grad_key_b = key_grad.reshape(block_rows, model_width).astype(jnp.bfloat16)
    grad_value_b = value_grad.reshape(block_rows, model_width).astype(jnp.bfloat16)
    grad_w_query = jnp.einsum(
        "tf,tg->fg", normed_b, grad_query_b, preferred_element_type=jnp.float32
    )
    grad_w_key = jnp.einsum("tf,tg->fg", normed_b, grad_key_b, preferred_element_type=jnp.float32)
    grad_w_value = jnp.einsum(
        "tf,tg->fg", normed_b, grad_value_b, preferred_element_type=jnp.float32
    )
    grad_normed = jnp.einsum("tg,fg->tf", grad_query_b, w_query, preferred_element_type=jnp.float32)
    grad_normed = grad_normed + jnp.einsum(
        "tg,fg->tf", grad_key_b, w_key, preferred_element_type=jnp.float32
    )
    grad_normed = grad_normed + jnp.einsum(
        "tg,fg->tf", grad_value_b, w_value, preferred_element_type=jnp.float32
    )
    grad_x_part, grad_gain_attend = attend_back(grad_normed)
    grad_input = (grad_middle + grad_x_part).astype(jnp.bfloat16)
    gains_all = jnp.concatenate(
        [grad_gain_attend, grad_gain_inner, grad_gain_feed, grad_gain_hidden]
    )
    summed = (
        lax.psum_scatter(grad_w_query.reshape(-1), ("row", "seq"), scatter_dimension=0, tiled=True),
        lax.psum_scatter(grad_w_key.reshape(-1), ("row", "seq"), scatter_dimension=0, tiled=True),
        lax.psum_scatter(grad_w_value.reshape(-1), ("row", "seq"), scatter_dimension=0, tiled=True),
        lax.psum_scatter(grad_out.reshape(-1), ("row", "seq"), scatter_dimension=0, tiled=True),
        lax.psum_scatter(grad_up.reshape(-1), ("row", "seq"), scatter_dimension=0, tiled=True),
        lax.psum_scatter(grad_down.reshape(-1), ("row", "seq"), scatter_dimension=0, tiled=True),
        lax.psum_scatter(gains_all, ("row", "seq"), scatter_dimension=0, tiled=True),
    )
    factor = 1.0 / math.sqrt(block_rows * all_devices)
    return (result, grad_input) + tuple((summed_part * factor for summed_part in summed))


NO_COST = pl.CostEstimate(flops=1000, bytes_accessed=1000, transcendentals=0)
SOME_COST = pl.CostEstimate(flops=4 * 10**9, bytes_accessed=1000, transcendentals=0)
HIGH_COST = pl.CostEstimate(flops=5 * 10**10, bytes_accessed=1000, transcendentals=0)


def split_log(level):
    remaining = math.log((level + 1) / level)
    pieces = []
    for _ in range(3):
        piece = float(jnp.bfloat16.dtype.type(remaining))
        pieces.append(piece)
        remaining -= piece
    return pieces


def extra_values(places, features, head, size, per_piece):
    masks, values = jnp.zeros_like(features), jnp.zeros(features.shape, jnp.float32)
    for level in range(1, PATTERNS):
        for piece, value in enumerate(split_log(level)):
            here = features == size + 3 * (level - 1) + piece
            masks = jnp.where(here, 2**level - 1, masks)
            values = jnp.where(here, value if per_piece else 1.0, values)
    return jnp.where(((places - head) & masks) == 0, values, 0.0)


def nt_dot(left, right):
    return lax.dot_general(
        left, right, (((1,), (1,)), ((), ())), preferred_element_type=jnp.float32
    )


def nn_dot(left, right):
    return jnp.dot(left, right, preferred_element_type=jnp.float32)


def call_whole(kernel, out_shape, name, scalars, *arrays, in_specs=None, scratch=(), limit=12, cost=None):
    return pl.pallas_call(
        kernel,
        grid_spec=pltpu.PrefetchScalarGridSpec(
            num_scalar_prefetch=1,
            grid=(1,),
            in_specs=in_specs or [whole(array.shape) for array in arrays],
            out_specs=[whole(out.shape) for out in out_shape],
            scratch_shapes=list(scratch),
        ),
        out_shape=list(out_shape),
        compiler_params=pltpu.CompilerParams(vmem_limit_bytes=limit << 20),
        cost_estimate=cost or NO_COST,
        name=name,
    )(scalars, *arrays)


def after_kernel(scalars, *refs):
    for index in range(scalars.shape[0]):
        refs[-1][index] = scalars[index]


def after(scalars, arrays, cost):
    return pl.pallas_call(
        after_kernel,
        in_specs=[pl.BlockSpec(memory_space=pltpu.SMEM)]
        + [pl.BlockSpec(memory_space=pl.ANY)] * len(arrays),
        out_specs=pl.BlockSpec(memory_space=pltpu.SMEM),
        out_shape=jax.ShapeDtypeStruct(scalars.shape, scalars.dtype),
        compiler_params=pltpu.CompilerParams(vmem_limit_bytes=1 << 20),
        cost_estimate=cost,
        name="after",
    )(scalars, *arrays)


def norm_kernel(unused, rows_ref, gain_ref, out_ref):
    out_ref[...] = (norm_parts(rows_ref[...].astype(jnp.float32))[0] * gain_ref[...]).astype(
        jnp.bfloat16
    )


def column_choice(chip, heads, size, lanes, width, transposed):
    shape, axis = ((lanes, width), 0) if transposed else ((width, lanes), 1)
    lane = lax.broadcasted_iota(jnp.int32, shape, axis)
    feature = lax.broadcasted_iota(jnp.int32, shape, 1 - axis)
    parts = []
    for head in range(heads):
        here = (feature == lane + (chip * heads + head) * size) & (lane < size)
        parts.append(jnp.where(here, 1.0, 0.0).astype(jnp.bfloat16))
    return jnp.concatenate(parts, axis=axis)


def choose_kernel(heads, size, scalars, wq_ref, wk_ref, wv_ref, *refs):
    query_rows, key_columns, value_rows, key_rows, value_columns, narrow_rows = refs
    width, chip = wq_ref.shape[0], scalars[0]
    tall = column_choice(chip, heads, size, 2 * size, width, True)
    flat = column_choice(chip, heads, size, 2 * size, width, False)
    narrow = column_choice(chip, heads, size, size, width, True)
    query_rows[...] = sent(nt_dot(tall, wq_ref[...]))
    key_columns[...] = sent(nn_dot(wk_ref[...], flat))
    value_columns[...] = sent(nn_dot(wv_ref[...], flat))
    for target, weight in ((value_rows, wv_ref), (key_rows, wk_ref), (narrow_rows, wq_ref)):
        target[...] = sent(nt_dot(narrow, weight[...]))


def choose(scalars, w_query, w_key, w_value, heads, size):
    width = w_query.shape[0]
    shapes = [
        (2 * heads * size, width),
        (width, 2 * heads * size),
        (heads * size, width),
        (heads * size, width),
        (width, 2 * heads * size),
        (heads * size, width),
    ]
    return call_whole(
        partial(choose_kernel, heads, size),
        [jax.ShapeDtypeStruct(shape, jnp.bfloat16) for shape in shapes],
        "choose",
        scalars,
        w_query,
        w_key,
        w_value,
        limit=24,
    )


def project_kernel(blocks, own, heads, scale, meta, *refs):
    normed = refs[:blocks]
    wq_ref, wk_ref, wv_ref = refs[blocks : blocks + 3]
    q_ref, k_ref, vt_ref = refs[-3:]
    length = normed[0].shape[0]
    lanes = wk_ref.shape[1] // heads
    size = lanes // 2
    first_head = meta[blocks]
    for index in range(blocks):
        rows = normed[index][...]
        start = meta[index]
        span = slice(index * length, (index + 1) * length)
        keys = nn_dot(rows, wk_ref[...])
        vt_ref[:, span] = nt_dot(wv_ref[...], rows).astype(jnp.bfloat16)
        places = start + lax.broadcasted_iota(jnp.int32, (length, 1), 0)
        features = lax.broadcasted_iota(jnp.int32, (1, lanes), 1)
        for head in range(heads):
            wide_rows = slice(head * lanes, (head + 1) * lanes)
            extra = extra_values(places, features, first_head + head, size, False)
            k_ref[span, wide_rows] = (keys[:, wide_rows] + extra).astype(jnp.bfloat16)
        if index < own:
            queries = nt_dot(wq_ref[...], rows).astype(jnp.bfloat16).astype(jnp.float32) * scale
            places = start + lax.broadcasted_iota(jnp.int32, (1, length), 1)
            features = lax.broadcasted_iota(jnp.int32, (lanes, 1), 0)
            for head in range(heads):
                wide_rows = slice(head * lanes, (head + 1) * lanes)
                extra = extra_values(places, features, first_head + head, size, True)
                q_ref[wide_rows, span] = (queries[wide_rows] + extra).astype(jnp.bfloat16)


def project(meta, normed, wq, wk, wv, own, heads, scale, chips, filled=None):
    blocks, length = len(normed), normed[0].shape[0]
    wide_columns, share = wk.shape[1], wv.shape[0]
    last = 0 if filled is None else 2 * chips // blocks - 1
    last_own = 0 if filled is None else chips // own - 1
    aliases = {} if filled is None else {blocks + 4 + index: index for index in range(3)}
    return pl.pallas_call(
        partial(project_kernel, blocks, own, heads, scale),
        grid_spec=pltpu.PrefetchScalarGridSpec(
            num_scalar_prefetch=1,
            grid=(1,),
            in_specs=[whole(array.shape) for array in (*normed, wq, wk, wv)]
            + [pl.BlockSpec(memory_space=pl.ANY)] * (0 if filled is None else 3),
            out_specs=[
                pl.BlockSpec((wide_columns, own * length), lambda i, meta: (0, last_own)),
                pl.BlockSpec((blocks * length, wide_columns), lambda i, meta: (last, 0)),
                pl.BlockSpec((share, blocks * length), lambda i, meta: (0, last)),
            ],
        ),
        out_shape=[
            jax.ShapeDtypeStruct((wide_columns, chips * length), jnp.bfloat16),
            jax.ShapeDtypeStruct((2 * chips * length, wide_columns), jnp.bfloat16),
            jax.ShapeDtypeStruct((share, 2 * chips * length), jnp.bfloat16),
        ],
        input_output_aliases=aliases,
        compiler_params=pltpu.CompilerParams(vmem_limit_bytes=16 << 20),
        cost_estimate=NO_COST,
        name="project",
    )(meta, *normed, wq, wk, wv, *(filled or ()))


def project_back_kernel(blocks, unused, *refs):
    normed = refs[:blocks]
    wk_ref, wv_ref, kt_ref, v_ref = refs[blocks:]
    length = normed[0].shape[0]
    for index in range(blocks):
        rows = normed[index][...]
        span = slice(index * length, (index + 1) * length)
        kt_ref[:, span] = nt_dot(wk_ref[...], rows).astype(jnp.bfloat16)
        v_ref[span, :] = nn_dot(rows, wv_ref[...]).astype(jnp.bfloat16)


def project_back(scalars, normed, wk, wv):
    blocks, length = len(normed), normed[0].shape[0]
    return call_whole(
        partial(project_back_kernel, blocks),
        [
            jax.ShapeDtypeStruct((wk.shape[0], blocks * length), jnp.bfloat16),
            jax.ShapeDtypeStruct((blocks * length, wv.shape[1]), jnp.bfloat16),
        ],
        "project_back",
        scalars,
        *normed,
        wk,
        wv,
    )


def pair_mask(query_start, key_start, doc_line, block):
    query_place = query_start + lax.broadcasted_iota(jnp.int32, (1, block), 1)
    key_place = key_start + lax.broadcasted_iota(jnp.int32, (block, 1), 0)
    return (key_place <= query_place) & (key_place >= doc_line)


def attend_kernel(
    heads, block, key_blocks, meta, doc_ref, q_ref, k_ref, vt_ref, o_ref, lse_ref, *refs
):
    ob_refs, (m_ref, l_ref) = refs[:-2], refs[-2:]
    step = pl.program_id(0)
    steps = len(ob_refs)
    query_start = meta[step]
    doc_first, doc_last = meta[steps + key_blocks + step], meta[2 * steps + key_blocks + step]
    doc_line = doc_ref[...]
    size = o_ref.shape[0] // heads
    lanes = q_ref.shape[0] // heads
    m_ref[...] = jnp.full_like(m_ref, big_negative)
    l_ref[...] = jnp.zeros_like(l_ref)
    o_ref[...] = jnp.zeros_like(o_ref)

    def fold(slot, allowed):
        span = pl.ds(pl.multiple_of(slot * block, block), block)
        scores = [
            nn_dot(
                k_ref[span, head * lanes : (head + 1) * lanes],
                q_ref[head * lanes : (head + 1) * lanes, :],
            )
            for head in range(heads)
        ]
        if allowed is not None:
            scores = [jnp.where(allowed, part, big_negative) for part in scores]
        for head in range(heads):
            rows = slice(head * size, (head + 1) * size)
            old_peak = m_ref[head]
            new_peak = jnp.maximum(old_peak, jnp.max(scores[head], axis=0, keepdims=True))
            weights = jnp.exp(scores[head] - new_peak)
            fade = jnp.exp(old_peak - new_peak)
            m_ref[head] = new_peak
            l_ref[head] = l_ref[head] * fade + jnp.sum(weights, axis=0, keepdims=True)
            o_ref[rows, :] = o_ref[rows, :] * fade + nn_dot(
                vt_ref[rows, span], weights.astype(jnp.bfloat16)
            )

    def body(slot, carry):
        key_start = meta[steps + slot]
        live = (key_start <= query_start) & (key_start + block > doc_first)
        full = (key_start < query_start) & (key_start >= doc_last)

        @pl.when(full)
        def _():
            fold(slot, None)

        @pl.when(live & jnp.logical_not(full))
        def _():
            fold(slot, pair_mask(query_start, key_start, doc_line, block))

        return carry

    lax.fori_loop(0, key_blocks, body, 0)
    for head in range(heads):
        rows = slice(head * size, (head + 1) * size)
        total = l_ref[head]
        mixed = o_ref[rows, :] / total
        o_ref[rows, :] = mixed
        lse_ref[head] = m_ref[head] + jnp.log(total)
    for index, ob_ref in enumerate(ob_refs):

        @pl.when(step == index)
        def _(ob_ref=ob_ref):
            ob_ref[...] = o_ref[...].astype(jnp.bfloat16)


def attend_back_kernel(
    heads,
    block,
    key_blocks,
    scale,
    meta,
    doc_ref,
    q_ref,
    o_ref,
    lse_ref,
    k_ref,
    kt_ref,
    v_ref,
    *refs,
):
    g_refs = refs[:-7]
    dq_ref, mine_ref, other_ref, acc_ref, pair_ref, delta_ref, g_ref = refs[-7:]
    step = pl.program_id(0)
    steps = len(g_refs)
    for index, grad_ref in enumerate(g_refs):

        @pl.when(step == index)
        def _(grad_ref=grad_ref):
            g_ref[...] = grad_ref[...]

    query_start = meta[step]
    doc_first, doc_last = meta[steps + key_blocks + step], meta[2 * steps + key_blocks + step]
    doc_line = doc_ref[...]
    size = g_ref.shape[0] // heads
    lanes = q_ref.shape[0] // heads
    share = g_ref.shape[0]

    @pl.when(step == 0)
    def _():
        pair_ref[...] = jnp.zeros_like(pair_ref)

    acc_ref[...] = jnp.zeros_like(acc_ref)
    for head in range(heads):
        rows = slice(head * size, (head + 1) * size)
        delta_ref[head] = jnp.sum(
            g_ref[rows, :].astype(jnp.float32) * o_ref[rows, :], axis=0, keepdims=True
        )

    def fold(slot, allowed):
        span = pl.ds(pl.multiple_of(slot * block, block), block)
        probs, grad_scores = [], []
        for head in range(heads):
            wide_rows = slice(head * lanes, (head + 1) * lanes)
            rows = slice(head * size, (head + 1) * size)
            probs.append(nn_dot(k_ref[span, wide_rows], q_ref[wide_rows, :]))
            grad_scores.append(
                nn_dot(v_ref[span, head * lanes : head * lanes + size], g_ref[rows, :])
            )
        for head in range(heads):
            part = jnp.exp(probs[head] - lse_ref[head])
            if allowed is not None:
                part = jnp.where(allowed, part, 0.0)
            grad_scores[head] = (part * (grad_scores[head] - delta_ref[head])).astype(jnp.bfloat16)
            probs[head] = part.astype(jnp.bfloat16)
        for head in range(heads):
            rows = slice(head * size, (head + 1) * size)
            value_rows = slice(share + head * size, share + (head + 1) * size)
            query_rows = slice(head * lanes, head * lanes + size)
            pair_ref[value_rows, span] += nt_dot(g_ref[rows, :], probs[head])
            pair_ref[rows, span] += nt_dot(q_ref[query_rows, :], grad_scores[head])
            acc_ref[rows, :] += nn_dot(kt_ref[rows, span], grad_scores[head])

    def body(slot, carry):
        key_start = meta[steps + slot]
        live = (key_start <= query_start) & (key_start + block > doc_first)
        full = (key_start < query_start) & (key_start >= doc_last)

        @pl.when(full)
        def _():
            fold(slot, None)

        @pl.when(live & jnp.logical_not(full))
        def _():
            fold(slot, pair_mask(query_start, key_start, doc_line, block))

        return carry

    lax.fori_loop(0, key_blocks, body, 0)
    dq_ref[...] = (acc_ref[...] * scale).astype(dq_ref.dtype)

    @pl.when(step == steps - 1)
    def _():
        for index in range(steps):
            late = index == steps - 1
            mine = 2 * index if late else index
            other = 2 * index + 1 if late else steps - 1 + index
            span = slice(index * block, (index + 1) * block)
            mine_ref[:, span] = pair_ref[:, mine * block : (mine + 1) * block]
            other_ref[:, span] = pair_ref[:, other * block : (other + 1) * block].astype(
                jnp.bfloat16
            )


def whole(shape):
    return pl.BlockSpec(shape, lambda *index: (0,) * len(shape))


def attend(meta, doc_line, q_ext, k_ext, v_t, heads, block):
    wide, queries = q_ext.shape
    share, keys = v_t.shape
    steps, key_blocks = queries // block, keys // block
    return pl.pallas_call(
        partial(attend_kernel, heads, block, key_blocks),
        grid_spec=pltpu.PrefetchScalarGridSpec(
            num_scalar_prefetch=1,
            grid=(steps,),
            in_specs=[
                pl.BlockSpec((1, block), lambda i, meta: (0, i)),
                pl.BlockSpec((wide, block), lambda i, meta: (0, i)),
                pl.BlockSpec(memory_space=pltpu.VMEM),
                pl.BlockSpec(memory_space=pltpu.VMEM),
            ],
            out_specs=[
                pl.BlockSpec((share, block), lambda i, meta: (0, i)),
                pl.BlockSpec((heads, 1, block), lambda i, meta: (0, 0, i)),
            ]
            + [whole((share, block))] * steps,
            scratch_shapes=[
                pltpu.VMEM((heads, 1, block), jnp.float32),
                pltpu.VMEM((heads, 1, block), jnp.float32),
            ],
        ),
        out_shape=[
            jax.ShapeDtypeStruct((share, queries), jnp.float32),
            jax.ShapeDtypeStruct((heads, 1, queries), jnp.float32),
        ]
        + [jax.ShapeDtypeStruct((share, block), jnp.bfloat16)] * steps,
        compiler_params=pltpu.CompilerParams(vmem_limit_bytes=12 << 20),
        cost_estimate=NO_COST,
        name="attend",
    )(meta, doc_line, q_ext, k_ext, v_t)


def attend_back(meta, doc_line, q_ext, grad_t, mixed, lse, k_ext, k_t, v_ext, heads, block, scale):
    wide, queries = q_ext.shape
    share, keys = k_t.shape
    steps, key_blocks = queries // block, keys // block
    return pl.pallas_call(
        partial(attend_back_kernel, heads, block, key_blocks, scale),
        grid_spec=pltpu.PrefetchScalarGridSpec(
            num_scalar_prefetch=1,
            grid=(steps,),
            in_specs=[
                pl.BlockSpec((1, block), lambda i, meta: (0, i)),
                pl.BlockSpec((wide, block), lambda i, meta: (0, i)),
                pl.BlockSpec((share, block), lambda i, meta: (0, i)),
                pl.BlockSpec((heads, 1, block), lambda i, meta: (0, 0, i)),
                pl.BlockSpec(memory_space=pltpu.VMEM),
                pl.BlockSpec(memory_space=pltpu.VMEM),
                pl.BlockSpec(memory_space=pltpu.VMEM),
            ]
            + [whole((share, block))] * steps,
            out_specs=[
                pl.BlockSpec((share, block), lambda i, meta: (0, i)),
                whole((2 * share, keys // 2)),
                whole((2 * share, keys // 2)),
            ],
            scratch_shapes=[
                pltpu.VMEM((share, block), jnp.float32),
                pltpu.VMEM((2 * share, keys), jnp.float32),
                pltpu.VMEM((heads, 1, block), jnp.float32),
                pltpu.VMEM((share, block), jnp.bfloat16),
            ],
        ),
        out_shape=[
            jax.ShapeDtypeStruct((share, queries), jnp.bfloat16),
            jax.ShapeDtypeStruct((2 * share, keys // 2), jnp.float32),
            jax.ShapeDtypeStruct((2 * share, keys // 2), jnp.bfloat16),
        ],
        compiler_params=pltpu.CompilerParams(vmem_limit_bytes=20 << 20),
        cost_estimate=HIGH_COST,
        name="attend_back",
    )(meta, doc_line, q_ext, mixed, lse, k_ext, k_t, v_ext, *grad_t)


def join_kernel(chips, unused, dq_ref, mine_ref, other_ref, *out_refs):
    share = dq_ref.shape[0]
    block = dq_ref.shape[1] // chips
    for step in range(chips):
        span = slice(step * block, (step + 1) * block)
        pair = (mine_ref[:, span] + other_ref[:, span].astype(jnp.float32)).astype(jnp.bfloat16)
        out_refs[step][:share, :] = dq_ref[:, span]
        out_refs[step][share:, :] = pair


def join_parts(scalars, dq, mine, other, chips):
    rows, block = dq.shape[0] + mine.shape[0], dq.shape[1] // chips
    return call_whole(
        partial(join_kernel, chips),
        [jax.ShapeDtypeStruct((rows, block), jnp.bfloat16)] * chips,
        "join",
        scalars,
        dq,
        mine,
        other,
    )


def head_grads_kernel(chips, per, scalars, *refs):
    normed, grads = refs[:chips], refs[chips : 2 * chips]
    wq_ref, wk_ref, wv_ref, gain_ref, inner_ref, feed_ref, hidden_ref = refs[2 * chips : 2 * chips + 7]
    perm_ref, keep_ref, send_ref = refs[2 * chips + 7 :]
    first_core = scalars[1] == 0
    share, model_width = wq_ref.shape
    own = nn_dot(grads[0][...], normed[0][...])
    for step in range(1, chips):
        own = own + nn_dot(grads[step][...], normed[step][...])
    attend = jnp.zeros((1, model_width), jnp.float32)
    for index, weight in enumerate((wq_ref, wk_ref, wv_ref)):
        part = own[index * share : (index + 1) * share] * weight[...].astype(jnp.float32)
        attend = attend + jnp.sum(part, axis=0, keepdims=True)
    gains = [attend / gain_ref[...], inner_ref[...], feed_ref[...], hidden_ref[...]]
    own = nt_dot(perm_ref[...], own.astype(jnp.bfloat16))
    chunks, _, width = keep_ref.shape
    columns = own.shape[1]
    part = sum(row.shape[1] for row in gains) // (2 * chunks)
    lines = -(-part // 128)
    gains = jnp.concatenate(gains + [jnp.zeros((1, 128), jnp.float32)], axis=1)

    def device_gains(device):
        starts = [device * part + 128 * line for line in range(lines)]
        rows = [gains[:, start : start + 128] for start in starts]
        return jnp.concatenate(rows, axis=0).astype(jnp.bfloat16)

    for target in (keep_ref, send_ref):
        target[:, :, columns:] = jnp.zeros((chunks, per, width - columns), jnp.bfloat16)
    for chunk in range(chunks):
        even, odd = device_gains(2 * chunk), device_gains(2 * chunk + 1)
        keep_ref[chunk, :lines, width - 128 :] = jnp.where(first_core, even, odd)
        send_ref[chunk, :lines, width - 128 :] = jnp.where(first_core, odd, even)
        for which, target in enumerate((keep_ref, send_ref)):
            first = (which * chunks + chunk) * per
            target[chunk, :, :columns] = own[first : first + per].astype(jnp.bfloat16)


def head_grads(scalars, normed, grads, weights, gain, late_gains, perm, per):
    width = perm.shape[0]
    out = jax.ShapeDtypeStruct((width // (2 * per), per, width), jnp.bfloat16)
    return call_whole(
        partial(head_grads_kernel, len(grads), per),
        [out, out],
        "head_grads",
        scalars,
        *normed,
        *grads,
        *weights,
        gain,
        *late_gains,
        perm,
        limit=24,
    )


def norm_parts(values):
    shifted = values - jnp.mean(values, axis=-1, keepdims=True)
    rate = lax.rsqrt(jnp.mean(shifted * shifted, axis=-1, keepdims=True) + 1e-05)
    return shifted * rate, rate


def norm_back(grad, hat, rate, gain):
    scaled = grad * gain
    mean_scaled = jnp.mean(scaled, axis=-1, keepdims=True)
    mean_product = jnp.mean(scaled * hat, axis=-1, keepdims=True)
    return (
        rate * (scaled - mean_scaled - hat * mean_product),
        jnp.sum(grad * hat, axis=0, keepdims=True),
    )


def middle_kernel(chips, tiles, position, *refs):
    mixed = refs[:chips]
    tokens_ref, cot_ref, wout_ref, wup_ref, wdown_ref, ginner_ref, gfeed_ref, ghidden_ref = refs[
        chips : chips + 8
    ]
    result_ref, gmid_ref, gmid_b_ref = refs[chips + 8 : chips + 11]
    go_refs = refs[chips + 11 : 2 * chips + 11]
    (
        z_ref,
        h2_ref,
        bent_out,
        pre_out,
        dinner_ref,
        dfeed_ref,
        dhidden_ref,
        swap_ref,
        work_ref,
        column_ref,
        zhat_ref,
        hat_ref,
        act_ref,
        slope_ref,
        dact_ref,
        acc_ref,
        stat_ref,
    ) = refs[2 * chips + 11 :]
    step = pl.program_id(0)
    chip = position[0]
    block, model_width = tokens_ref.shape
    share = model_width // chips
    tile = wdown_ref.shape[0]
    hidden = tile * tiles
    root = math.sqrt(2.0 / math.pi)
    phase, index = step // tiles, step % tiles
    lanes = stat_ref.shape[2]
    groups = tile // lanes

    def by_rows(body):
        body(slice(None))

    def spread(stat):
        return jnp.concatenate([stat] * groups, axis=1)

    def gathered_lanes(values):
        total = values[:, :lanes]
        for group in range(1, groups):
            total = total + values[:, group * lanes : (group + 1) * lanes]
        return total

    def lane_sum(values):
        return jnp.broadcast_to(jnp.sum(values, axis=-1, keepdims=True), values.shape)

    def column_sums(values):
        total = values[:8]
        for first in range(8, values.shape[0], 8):
            total = total + values[first : first + 8]
        return total

    def norm_rows(values):
        shifted = values - spread(lane_sum(gathered_lanes(values)) / tile)
        rate = lax.rsqrt(lane_sum(gathered_lanes(shifted * shifted)) / tile + 1e-05)
        return shifted * spread(rate), rate

    def norm_rows_back(grad, hat, rate, gain):
        scaled = grad * gain
        mean_scaled = lane_sum(gathered_lanes(scaled)) / tile
        mean_product = lane_sum(gathered_lanes(scaled * hat)) / tile
        return spread(rate) * (scaled - spread(mean_scaled) - hat * spread(mean_product))

    @pl.when(step == 0)
    def _():
        for near in range(chips):
            start = pl.multiple_of(share * lax.rem(chip + near, chips), share)
            swap_ref[pl.ds(start, share), :] = mixed[near][...].astype(jnp.float32)
        work_ref[...] = swap_ref[...].T

        def first_norm(rows):
            zhat, zrate = norm_rows(work_ref[rows, :])
            zhat_ref[rows, :] = zhat
            stat_ref[0, rows, :] = zrate
            z_ref[rows, :] = (zhat * ginner_ref[...]).astype(jnp.bfloat16)

        by_rows(first_norm)
        work_ref[...] = nn_dot(z_ref[...], wout_ref[...])

        def second_norm(rows):
            mid = tokens_ref[rows, :].astype(jnp.float32) + work_ref[rows, :]
            acc_ref[rows, :] = mid
            hat, rate = norm_rows(mid)
            hat_ref[rows, :] = hat
            stat_ref[1, rows, :] = rate
            h2_ref[rows, :] = (hat * gfeed_ref[...]).astype(jnp.bfloat16)

        by_rows(second_norm)
        for stat in range(3, 7):
            stat_ref[stat] = jnp.zeros_like(stat_ref[stat])

    @pl.when(phase == 0)
    def _():
        work_ref[...] = nn_dot(h2_ref[...], wup_ref[...])

        def bend_rows(rows):
            u = work_ref[rows, :]
            squared = u * u
            bend = jnp.tanh(root * (u + 0.044715 * u * squared))
            act_ref[index, rows, :] = 0.5 * u * (1.0 + bend)
            slope_ref[index, rows, :] = 0.5 * (1.0 + bend) + 0.5 * u * (1.0 - bend * bend) * root * (
                1.0 + 3.0 * 0.044715 * squared
            )

        by_rows(bend_rows)

        @pl.when(index == 0)
        def _():
            def pivot(rows):
                stat_ref[2, rows, :] = lane_sum(gathered_lanes(act_ref[0, rows, :])) / tile

            by_rows(pivot)

        def sums(rows):
            off = act_ref[index, rows, :] - spread(stat_ref[2, rows, :])
            stat_ref[3, rows, :] += gathered_lanes(off)
            stat_ref[4, rows, :] += gathered_lanes(off * off)

        by_rows(sums)

    @pl.when(step == tiles)
    def _():
        drift = lane_sum(stat_ref[3]) / hidden
        stat_ref[2] = stat_ref[2] + drift
        stat_ref[4] = lax.rsqrt(
            jnp.maximum(lane_sum(stat_ref[4]) / hidden - drift * drift, 0.0) + 1e-05
        )

    @pl.when(phase == 1)
    def _():
        def hidden_rows(rows):
            hat = (act_ref[index, rows, :] - spread(stat_ref[2, rows, :])) * spread(
                stat_ref[4, rows, :]
            )
            act_ref[index, rows, :] = hat
            bent_out[rows, :] = (hat * ghidden_ref[...]).astype(jnp.bfloat16)

        by_rows(hidden_rows)
        work_ref[...] = nt_dot(cot_ref[...], wdown_ref[...])
        acc_ref[...] += nn_dot(bent_out[...], wdown_ref[...])
        column_ref[...] = jnp.zeros_like(column_ref)

        def grad_rows(rows):
            hat, grad = act_ref[index, rows, :], work_ref[rows, :]
            column_ref[...] += column_sums(grad * hat)
            scaled = grad * ghidden_ref[...]
            dact_ref[index, rows, :] = scaled
            stat_ref[5, rows, :] += gathered_lanes(scaled)
            stat_ref[6, rows, :] += gathered_lanes(scaled * hat)

        by_rows(grad_rows)
        dhidden_ref[...] = jnp.sum(column_ref[...], axis=0, keepdims=True)

    @pl.when(step == 2 * tiles)
    def _():
        result_ref[...] = acc_ref[...].astype(jnp.bfloat16)
        acc_ref[...] = jnp.zeros_like(acc_ref)
        stat_ref[5] = lane_sum(stat_ref[5]) / hidden
        stat_ref[6] = lane_sum(stat_ref[6]) / hidden

    @pl.when(phase == 2)
    def _():
        def pre_rows(rows):
            inner = (
                dact_ref[index, rows, :]
                - spread(stat_ref[5, rows, :])
                - act_ref[index, rows, :] * spread(stat_ref[6, rows, :])
            )
            pre_out[rows, :] = (
                spread(stat_ref[4, rows, :]) * inner * slope_ref[index, rows, :]
            ).astype(jnp.bfloat16)

        by_rows(pre_rows)
        acc_ref[...] += nt_dot(pre_out[...], wup_ref[...])

    @pl.when(step == 3 * tiles - 1)
    def _():
        column_ref[...] = jnp.zeros_like(column_ref)

        def middle_rows(rows):
            grad, hat = acc_ref[rows, :], hat_ref[rows, :]
            column_ref[...] += column_sums(grad * hat)
            gmid = cot_ref[rows, :].astype(jnp.float32) + norm_rows_back(
                grad, hat, stat_ref[1, rows, :], gfeed_ref[...]
            )
            gmid_ref[rows, :] = gmid
            gmid_b_ref[rows, :] = gmid.astype(jnp.bfloat16)

        by_rows(middle_rows)
        dfeed_ref[...] = jnp.sum(column_ref[...], axis=0, keepdims=True)
        work_ref[...] = nt_dot(gmid_b_ref[...], wout_ref[...])
        column_ref[...] = jnp.zeros_like(column_ref)

        def inner_rows(rows):
            grad, hat = work_ref[rows, :], zhat_ref[rows, :]
            column_ref[...] += column_sums(grad * hat)
            work_ref[rows, :] = norm_rows_back(grad, hat, stat_ref[0, rows, :], ginner_ref[...])

        by_rows(inner_rows)
        dinner_ref[...] = jnp.sum(column_ref[...], axis=0, keepdims=True)
        swap_ref[...] = work_ref[...].T
        for near in range(chips):
            start = pl.multiple_of(share * lax.rem(chip + near, chips), share)
            go_refs[near][...] = swap_ref[pl.ds(start, share), :].astype(jnp.bfloat16)


def middle(position, mixed, tokens, cotangent, w_out, w_up, w_down, gains):
    chips = len(mixed)
    block, model_width = tokens.shape
    hidden = w_up.shape[1]
    tile = model_width
    tiles = hidden // tile
    share = model_width // chips
    last = tiles - 1

    def up_index(i, pos):
        return (0, jnp.where(i < tiles, i, jnp.where(i < 2 * tiles, last, i - 2 * tiles)))

    def down_index(i, pos):
        return (jnp.clip(i - tiles, 0, last), 0)

    def hidden_index(i, pos):
        return (0, jnp.clip(i - tiles, 0, last))

    def pre_index(i, pos):
        return (0, jnp.clip(i - 2 * tiles, 0, last))

    def f32(*shape):
        return pltpu.VMEM(shape, jnp.float32)

    row, rows = (1, model_width), (block, model_width)
    narrow = jax.ShapeDtypeStruct(rows, jnp.bfloat16)
    return pl.pallas_call(
        partial(middle_kernel, chips, tiles),
        grid_spec=pltpu.PrefetchScalarGridSpec(
            num_scalar_prefetch=1,
            grid=(3 * tiles,),
            in_specs=[whole((share, block))] * chips
            + [
                whole(rows),
                whole(rows),
                whole((model_width, model_width)),
                pl.BlockSpec((model_width, tile), up_index),
                pl.BlockSpec((tile, model_width), down_index),
                whole(row),
                whole(row),
                pl.BlockSpec((1, tile), hidden_index),
            ],
            out_specs=[whole(rows)] * 3
            + [whole((share, block))] * chips
            + [
                whole(rows),
                whole(rows),
                pl.BlockSpec((block, tile), hidden_index),
                pl.BlockSpec((block, tile), pre_index),
                whole(row),
                whole(row),
                pl.BlockSpec((1, tile), hidden_index),
            ],
            scratch_shapes=[
                f32(model_width, block),
                f32(block, tile),
                f32(8, tile),
                f32(block, model_width),
                f32(block, model_width),
                f32(tiles, block, tile),
                f32(tiles, block, tile),
                f32(tiles, block, tile),
                f32(block, model_width),
                f32(7, block, 128),
            ],
        ),
        out_shape=[narrow, jax.ShapeDtypeStruct(rows, jnp.float32), narrow]
        + [jax.ShapeDtypeStruct((share, block), jnp.bfloat16)] * chips
        + [
            narrow,
            narrow,
            jax.ShapeDtypeStruct((block, hidden), jnp.bfloat16),
            jax.ShapeDtypeStruct((block, hidden), jnp.bfloat16),
            jax.ShapeDtypeStruct(row, jnp.float32),
            jax.ShapeDtypeStruct(row, jnp.float32),
            jax.ShapeDtypeStruct((1, hidden), jnp.float32),
        ],
        compiler_params=pltpu.CompilerParams(vmem_limit_bytes=36 << 20),
        cost_estimate=NO_COST,
        name="middle",
    )(position, *mixed, tokens, cotangent, w_out, w_up, w_down, *gains)


def down_kernel(per, position, bent_ref, cot_ref, keep_ref, send_ref):
    first_core = position[1] == 0
    grad = lax.dot_general(
        bent_ref[...], cot_ref[...], (((0,), (0,)), ((), ())), preferred_element_type=jnp.float32
    ).astype(jnp.bfloat16)
    for part in range(keep_ref.shape[0]):
        even = grad[2 * per * part : 2 * per * part + per]
        odd = grad[2 * per * part + per : 2 * per * (part + 1)]
        keep_ref[part] = jnp.where(first_core, even, odd)
        send_ref[part] = jnp.where(first_core, odd, even)


def down_grad(position, bent, cotangent, per):
    (block, hidden), model_width = bent.shape, cotangent.shape[1]
    tiles, chunks = hidden // model_width, hidden // (2 * per)
    out = jax.ShapeDtypeStruct((chunks, per, model_width), jnp.bfloat16)
    out_spec = pl.BlockSpec((chunks // tiles, per, model_width), lambda i, pos: (i, 0, 0))
    return pl.pallas_call(
        partial(down_kernel, per),
        grid_spec=pltpu.PrefetchScalarGridSpec(
            num_scalar_prefetch=1,
            grid=(tiles,),
            in_specs=[
                pl.BlockSpec((block, model_width), lambda i, pos: (0, i)),
                whole(cotangent.shape),
            ],
            out_specs=[out_spec, out_spec],
        ),
        out_shape=[out, out],
        compiler_params=pltpu.CompilerParams(vmem_limit_bytes=20 << 20),
        cost_estimate=NO_COST,
        name="down_grad",
    )(position, bent, cotangent)


def up_out_kernel(tiles, position, h2_ref, pre_ref, z_ref, gmid_ref, perm_ref, keep_ref, send_ref, left_ref):
    step = pl.program_id(0)
    chunks, per = keep_ref.shape[:2]

    @pl.when(step == 0)
    def _():
        left_ref[...] = nt_dot(perm_ref[...], h2_ref[...]).astype(jnp.bfloat16)

    def store(right):
        grad = nn_dot(left_ref[...], right)
        for chunk in range(chunks):
            keep_ref[chunk] = grad[chunk * per : (chunk + 1) * per].astype(jnp.bfloat16)
            first = (chunks + chunk) * per
            send_ref[chunk] = grad[first : first + per].astype(jnp.bfloat16)

    @pl.when(step < tiles)
    def _():
        store(pre_ref[...])

    @pl.when(step == tiles)
    def _():
        left_ref[...] = nt_dot(perm_ref[...], z_ref[...]).astype(jnp.bfloat16)
        store(gmid_ref[...])


def up_out_grad(position, h2, pre, z, gmid, perm, per):
    (block, hidden), model_width = pre.shape, h2.shape[1]
    tiles, chunks = hidden // model_width, model_width // (2 * per)
    out = jax.ShapeDtypeStruct((chunks, per * (tiles + 1), model_width), jnp.bfloat16)
    out_spec = pl.BlockSpec((chunks, per, model_width), lambda i, pos: (0, i, 0))
    return pl.pallas_call(
        partial(up_out_kernel, tiles),
        grid_spec=pltpu.PrefetchScalarGridSpec(
            num_scalar_prefetch=1,
            grid=(tiles + 1,),
            in_specs=[
                whole(h2.shape),
                pl.BlockSpec((block, model_width), lambda i, pos: (0, jnp.minimum(i, tiles - 1))),
                whole(z.shape),
                whole(gmid.shape),
                whole(perm.shape),
            ],
            out_specs=[out_spec, out_spec],
            scratch_shapes=[pltpu.VMEM((model_width, block), jnp.bfloat16)],
        ),
        out_shape=[out, out],
        compiler_params=pltpu.CompilerParams(vmem_limit_bytes=20 << 20),
        cost_estimate=NO_COST,
        name="up_out_grad",
    )(position, h2, pre, z, gmid, perm)


def final_kernel(chips, position, *refs):
    homes = refs[:chips]
    (
        tokens_ref,
        gmid_ref,
        wq_ref,
        wk_ref,
        wv_ref,
        gain_ref,
        out_ref,
        swap_ref,
    ) = refs[chips:]
    chip = position[0]
    block, model_width = tokens_ref.shape
    share = model_width // chips
    total = jnp.zeros((block, model_width), jnp.float32)
    for index, weight in enumerate((wq_ref, wk_ref, wv_ref)):
        for near in range(chips):
            start = pl.multiple_of(share * lax.rem(chip + near, chips), share)
            swap_ref[pl.ds(start, share), :] = homes[near][
                index * share : (index + 1) * share, :
            ].astype(jnp.float32)
        total = total + nt_dot(swap_ref[...].T.astype(jnp.bfloat16), weight[...])
    hat, rate = norm_parts(tokens_ref[...].astype(jnp.float32))
    back = norm_back(total, hat, rate, gain_ref[...])[0]
    out_ref[...] = (gmid_ref[...] + back).astype(jnp.bfloat16)


def final(position, homes, tokens, gmid, w_query, w_key, w_value, gain):
    block, model_width = tokens.shape
    return call_whole(
        partial(final_kernel, len(homes)),
        [jax.ShapeDtypeStruct((block, model_width), jnp.bfloat16)],
        "final",
        position,
        *homes,
        tokens,
        gmid,
        w_query,
        w_key,
        w_value,
        gain,
        scratch=[pltpu.VMEM((model_width, block), jnp.float32)],
    )[0]


def chip_shift(value, steps):
    count = lax.axis_size("seq")
    return lax.ppermute(value, "seq", [(i, (i + 2 * steps) % count) for i in range(count)])


def seq_swap(value, bit):
    return lax.ppermute(value, "seq", [(i, i ^ bit) for i in range(lax.axis_size("seq"))])


def row_swap(value, bit):
    return lax.ppermute(value, "row", [(i, i ^ bit) for i in range(lax.axis_size("row"))])


def sent(array):
    return array.astype(jnp.bfloat16)


def wide(array):
    return array.astype(jnp.float32)


def low_part(shape, keep):
    def index(i, bits):
        return (0, bits[2] if keep else 1 - bits[2], 0, 0, 0)

    return pl.BlockSpec((2, 1, shape[2] // 2) + shape[3:], index)


def high_part(shape, keep):
    def index(i, bits):
        return (bits[3] if keep else 1 - bits[3], 0, 1, 0, 0)

    return pl.BlockSpec((1, 2, shape[2] // 2) + shape[3:], index)


def outgoing_kernel(scalars, *refs):
    low_ref, high_ref = refs[-2:]
    first = 0
    for group in range(len(refs) // 4):
        low_a, low_b, high_a, high_b = refs[4 * group : 4 * group + 4]
        rows = slice(first, first + low_a.shape[3])
        low_ref[:, :, rows] = sent(wide(low_a[:, 0]) + wide(low_b[:, 0]))
        high_ref[:, :, rows] = sent(wide(high_a[0]) + wide(high_b[0]))
        first += low_a.shape[3]


def outgoing(scalars, groups, kept=False):
    arrays, specs = [], []
    for keep, other in groups:
        low, high = low_part(keep.shape, kept), high_part(keep.shape, kept)
        arrays += [keep, other, keep, other]
        specs += [low, low, high, high]
    shape = groups[0][0].shape
    rows = sum(keep.shape[3] for keep, _ in groups)
    out = jax.ShapeDtypeStruct((2, shape[2] // 2, rows, shape[4]), jnp.bfloat16)
    return call_whole(
        outgoing_kernel,
        [out, out],
        "kept" if kept else "outgoing",
        scalars,
        *arrays,
        in_specs=specs,
        limit=20,
    )


def halfway_kernel(groups, scalars, *refs):
    ins, outs = refs[: 4 * groups], refs[4 * groups :]
    low_bit, high_bit = scalars[2], scalars[3]
    low_keep, low_send, high_keep, high_send = outs
    first = 0
    for group in range(groups):
        low, high, low_in, high_in = ins[4 * group : 4 * group + 4]
        rows = slice(first, first + low.shape[2])
        for target, side in ((low_keep, high_bit), (low_send, 1 - high_bit)):
            target[:, rows] = sent(wide(low[side]) + wide(low_in[side]))
        for target, side in ((high_keep, low_bit), (high_send, 1 - low_bit)):
            target[:, rows] = sent(wide(high[side]) + wide(high_in[side]))
        first += low.shape[2]


def halfway(scalars, groups):
    arrays = [array for group in groups for array in group]
    rows = sum(group[0].shape[2] for group in groups)
    out = jax.ShapeDtypeStruct((arrays[0].shape[1], rows, arrays[0].shape[3]), jnp.bfloat16)
    return call_whole(
        partial(halfway_kernel, len(groups)), [out] * 4, "halfway", scalars, *arrays, limit=24
    )


def split_kernel(chips, groups, scalars, *refs):
    ins, outs = refs[: 4 * groups], refs[4 * groups : 4 * groups + chips]
    all_ref = refs[-1]
    half = chips // 2
    first = 0
    for group in range(groups):
        low_keep, low_in, high_keep, high_in = ins[4 * group : 4 * group + 4]
        rows = slice(first, first + low_in.shape[1])
        all_ref[:half, rows] = sent(wide(low_keep[...]) + wide(low_in[...]))
        all_ref[half:, rows] = sent(wide(high_keep[...]) + wide(high_in[...]))
        first += low_in.shape[1]
    for step in range(chips):
        outs[step][...] = all_ref[lax.rem(scalars[0] + step, chips)]


def split(scalars, groups, chips):
    arrays = [array for group in groups for array in group]
    rows = sum(group[0].shape[1] for group in groups)
    width = arrays[0].shape[2]
    return call_whole(
        partial(split_kernel, chips, len(groups)),
        [jax.ShapeDtypeStruct((rows, width), jnp.bfloat16)] * chips,
        "split",
        scalars,
        *arrays,
        scratch=[pltpu.VMEM((chips, rows, width), jnp.bfloat16)],
    )


def lay_flat(target, values, first, step):
    for piece in range(values.shape[1] // 128):
        target[pl.ds(first + piece, values.shape[0], step), :] = values[
            :, 128 * piece : 128 * (piece + 1)
        ]


def finish_kernel(chips, per, share, factor, scalars, *refs):
    arrived, heads_in, refs = refs[:chips], refs[chips : 2 * chips], refs[chips:]
    down_ref, up_ref, out_ref, query_ref, key_ref, value_ref, gains_ref, heads_ref = refs[chips:]
    width = arrived[0].shape[1]
    chip, pieces = scalars[0], width // 128
    tiles = up_ref.shape[0] * 128 // (per * width)
    down_rows = down_ref.shape[0] * 128 // width

    def total(first, rows):
        result = wide(arrived[0][first : first + rows, :])
        for part in arrived[1:]:
            result = result + wide(part[first : first + rows, :])
        return result * factor

    lay_flat(down_ref, total(0, down_rows), 0, pieces)
    for tile in range(tiles):
        lay_flat(up_ref, total(down_rows + tile * per, per), tile * pieces, tiles * pieces)
    lay_flat(out_ref, total(down_rows + tiles * per, per), 0, pieces)
    gains = wide(heads_in[0][:8, -128:])
    for part in heads_in[1:]:
        gains = gains + wide(part[:8, -128:])
    gains_ref[...] = gains * factor
    for step in range(chips):
        heads_ref[lax.rem(chip - step + chips, chips)] = wide(heads_in[step][:, : 3 * share])
    for index, target in enumerate((query_ref, key_ref, value_ref)):
        values = jnp.concatenate(
            [heads_ref[near][:, index * share : (index + 1) * share] for near in range(chips)], axis=1
        )
        lay_flat(target, values * factor, 0, pieces)


def finish(scalars, arrived, hidden, parts, per, share, factor):
    chips, width = len(arrived) // 2, arrived[0].shape[1]
    square = jax.ShapeDtypeStruct((per * width // 128, 128), jnp.float32)
    large = jax.ShapeDtypeStruct((per * hidden // 128, 128), jnp.float32)
    return call_whole(
        partial(finish_kernel, chips, per, share, factor),
        [large, large, square, square, square, square, jax.ShapeDtypeStruct((8, 128), jnp.float32)],
        "finish",
        scalars,
        *arrived,
        scratch=[pltpu.VMEM((chips, per, 3 * share), jnp.float32)],
    )


def gathered(rows):
    behind, ahead = chip_shift(rows, 1), chip_shift(rows, -1)
    up = [(2 * i + core, 2 * i + 2 + core) for i in (1, 2) for core in (0, 1)]
    down = [(2 * i + core, 2 * i - 2 + core) for i in (1, 2) for core in (0, 1)]
    across = (lax.ppermute(ahead, "seq", down), lax.ppermute(behind, "seq", up))
    return behind, ahead, across


def fast_local(
    tokens,
    lengths,
    w_query,
    w_key,
    w_value,
    w_out,
    w_up,
    w_down,
    gain_attend,
    gain_inner,
    gain_feed,
    gain_hidden,
    cotangent,
):
    block, model_width = tokens.shape
    hidden = w_up.shape[1]
    size = model_width // HEADS
    lanes = 2 * size
    scale = size ** (-0.5)
    seq_devices, row_devices = lax.axis_size("seq"), lax.axis_size("row")
    chips = seq_devices // 2
    heads = HEADS // chips
    share = heads * size
    spread = heads * lanes
    parts = row_devices * seq_devices
    position, row = lax.axis_index("seq"), lax.axis_index("row")
    chip, core = position // 2, position % 2
    place = jnp.stack([chip, core, row % 2, row // 2]).astype(jnp.int32)
    bounds = jnp.cumsum(lengths[0])[:-1]
    factor = 1.0 / math.sqrt(block * parts)

    normed_b = call_whole(
        norm_kernel,
        [jax.ShapeDtypeStruct(tokens.shape, jnp.bfloat16)],
        "norm",
        jnp.zeros((1,), jnp.int32),
        tokens,
        gain_attend[None, :],
    )[0]
    behind, ahead, across = gathered(normed_b)

    order = [step for step in range(chips) if step != chips // 2] + [chips // 2]
    slots = [order.index(step) for step in range(chips)]
    chip_ids = (chip - jnp.asarray(order, jnp.int32)) % chips
    query_starts = block * (2 * chip_ids + core)
    other_starts = block * (2 * chip_ids + 1 - core)
    key_starts = jnp.concatenate(
        [query_starts[:-1], other_starts[:-1], query_starts[-1:], other_starts[-1:]]
    )
    in_block = jnp.arange(block, dtype=jnp.int32)[None, :]
    query_places = (query_starts[:, None] + in_block).reshape(-1)
    doc_line = jnp.max(jnp.where(bounds[:, None] <= query_places[None, :], bounds[:, None], 0), axis=0)
    meta = jnp.concatenate(
        [query_starts, key_starts, doc_line.reshape(chips, block)[:, 0], doc_line.reshape(chips, block)[:, -1]]
    )
    doc_line = doc_line[None, :]

    feature = jnp.arange(model_width, dtype=jnp.int32)
    per = model_width // parts
    chunk, inside = feature // per, feature % per
    chunks = parts // 2
    parity = jnp.where(chunk < chunks, core, 1 - core)
    wanted = (2 * (chunk % chunks) + parity) * per + inside
    perm = (wanted[:, None] == feature[None, :]).astype(jnp.bfloat16)

    gains_share = (3 * model_width + hidden) // parts
    gains_rows = -(-gains_share // 128)
    first_head = heads * chip[None]
    small = (
        jnp.concatenate([query_starts[:-1], other_starts[:-1], first_head]),
        jnp.concatenate([query_starts[-1:], other_starts[-1:], first_head]),
        meta,
        doc_line,
        gain_attend[None, :],
        gain_inner[None, :],
        gain_feed[None, :],
        gain_hidden[None, :],
        place,
        perm,
    )
    small = lax.optimization_barrier(small)
    starts, late_starts, meta, doc_line, gain_first, gain_inner, gain_feed, gain_hidden = small[:8]
    place, perm = small[8:]
    early = choose(place, w_query, w_key, w_value, heads, size)
    behind, early = lax.optimization_barrier((behind, early))
    wq_wide, wk_wide, wv_rows, wk_rows, wv_wide, wq_rows = early
    own = [normed_b, behind, ahead]
    early_blocks = own + [seq_swap(rows, 1) for rows in own]
    filled = project(
        starts, early_blocks, wq_wide, wk_wide, wv_rows, chips - 1, heads, scale, chips
    )
    filled, across = lax.optimization_barrier((filled, across))
    own.append(across[0] + across[1])
    late_blocks = [own[-1], seq_swap(own[-1], 1)]
    q_ext, k_ext, v_t = project(
        late_starts, late_blocks, wq_wide, wk_wide, wv_rows, 1, heads, scale, chips, filled
    )
    mixed, lse, *mixed_b = attend(meta, doc_line, q_ext, k_ext, v_t, heads, block)
    mixed_b, wk_rows = lax.optimization_barrier((mixed_b, wk_rows))
    k_t, v_ext = project_back(place, early_blocks + late_blocks, wk_rows, wv_wide)
    back = [mixed_b[slots[0]]] + [
        chip_shift(mixed_b[slots[step]], -step) for step in range(1, chips)
    ]
    back, k_t, v_ext = lax.optimization_barrier((back, k_t, v_ext))
    outs = middle(
        place, back, tokens, cotangent, w_out, w_up, w_down, (gain_inner, gain_feed, gain_hidden)
    )
    result, grad_middle, gmid_b = outs[:3]
    go = outs[3 : 3 + chips]
    z, h2, bent, pre, dinner, dfeed, dhidden = outs[3 + chips :]
    keep_a, send_a = down_grad(place, bent, cotangent, hidden // parts)
    keep_b, send_b = up_out_grad(place, h2, pre, z, gmid_b, perm, per)
    go, keep_b, send_b = lax.optimization_barrier((go, keep_b, send_b))
    go = [go[0]] + [chip_shift(go[step], step) for step in range(1, chips)]

    def gridded(array):
        return array.reshape((2, 2, chips) + array.shape[1:])

    sums = [
        (gridded(keep), gridded(seq_swap(send, 1)))
        for keep, send in ((keep_a, send_a), (keep_b, send_b))
    ]
    low, high = outgoing(place, sums)
    arrived_sums = [row_swap(low, 1), row_swap(high, 2)]
    dq, pair, other = attend_back(
        meta, doc_line, q_ext, [go[step] for step in order], mixed, lse, k_ext, k_t, v_ext, heads, block, scale
    )
    grads = join_parts(place, dq, pair, seq_swap(other, 1), chips)
    home = [grads[slots[0]]] + [chip_shift(grads[slots[step]], -step) for step in range(1, chips)]
    grads, sums = lax.optimization_barrier((grads, sums))
    kept = outgoing(place, sums, True)
    mine_grad, send_grad = head_grads(
        place,
        own,
        grads,
        (wq_rows, wk_rows, wv_rows),
        gain_first,
        (dinner, dfeed, dhidden),
        perm,
        per,
    )
    arrived_sums, kept, mine_grad, send_grad = lax.optimization_barrier(
        (arrived_sums, kept, mine_grad, send_grad)
    )
    low_keep, low_send, high_keep, high_send = halfway(place, [(*kept, *arrived_sums)])
    low_in, high_in = row_swap(low_send, 2), row_swap(high_send, 1)
    home, mine_grad, send_grad = lax.optimization_barrier((home, mine_grad, send_grad))
    mine_grad, other_grad = gridded(mine_grad), gridded(seq_swap(send_grad, 1))
    stage = split(after(place, home, SOME_COST), [(low_keep, low_in, high_keep, high_in)], chips)
    arrived = [stage[0]] + [chip_shift(stage[step], step) for step in range(1, chips)]
    grad_input = final(
        place, home, tokens, grad_middle, w_query, w_key, w_value, gain_first
    )
    low, high = outgoing(place, [(mine_grad, other_grad)])
    low_keep, low_send, high_keep, high_send = halfway(
        place,
        [(*outgoing(place, [(mine_grad, other_grad)], True), row_swap(low, 1), row_swap(high, 2))],
    )
    stage = split(
        place, [(low_keep, row_swap(low_send, 2), high_keep, row_swap(high_send, 1))], chips
    )
    arrived += [stage[0]] + [chip_shift(stage[step], step) for step in range(1, chips)]
    down, up, out, query, key, value, gains_part = finish(
        place, arrived, hidden, parts, per, share, factor
    )
    return (
        result,
        grad_input,
        query.reshape(-1),
        key.reshape(-1),
        value.reshape(-1),
        out.reshape(-1),
        up.reshape(-1),
        down.reshape(-1),
        gains_part.reshape(-1)[:gains_share],
    )


def local(*arrays):
    seq_devices, row_devices = lax.axis_size("seq"), lax.axis_size("row")
    block = arrays[0].shape[0]
    one_segment = block * seq_devices <= SEGMENT and block % 2 ** (PATTERNS - 1) == 0
    if one_segment and seq_devices == 8 and row_devices == 4:
        return fast_local(*arrays)
    return ring_local(*arrays)


def solution(mesh):
    return jax.shard_map(
        local,
        mesh=mesh,
        in_specs=(
            P(("row", "seq"), None),
            P("row", None),
            P(),
            P(),
            P(),
            P(),
            P(),
            P(),
            P(),
            P(),
            P(),
            P(),
            P(("row", "seq"), None),
        ),
        out_specs=(
            P(("row", "seq"), None),
            P(("row", "seq"), None),
            P(("row", "seq")),
            P(("row", "seq")),
            P(("row", "seq")),
            P(("row", "seq")),
            P(("row", "seq")),
            P(("row", "seq")),
            P(("row", "seq")),
        ),
        check_vma=False,
    )
```

```python
from functools import partial
from functools import reduce
import math

import jax
import jax.numpy as jnp
import numpy as np
from jax import lax
from jax.experimental import pallas as pl
from jax.experimental.pallas import tpu as pltpu
from jax.sharding import PartitionSpec as P

HEADS = 12
SEGMENT = 2048
PATTERNS = 5


big_negative = -1e30


def shifted_2(shard, axis, by):
    length = lax.axis_size(axis)
    pairs = [(i, i + by) for i in range(length) if 0 <= i + by < length]
    return lax.ppermute(shard, axis, pairs)


def shifted_3(value, axis, steps):
    count = lax.axis_size(axis)
    pairs = [(source, (source + steps) % count) for source in range(count)]
    return lax.ppermute(value, axis, pairs)


def layer_norm(values, gain_vector):
    centre = jnp.mean(values, axis=-1, keepdims=True)
    shifted = values - centre
    variance = jnp.mean(shifted * shifted, axis=-1, keepdims=True)
    return shifted * lax.rsqrt(variance + 1e-05) * gain_vector


def hidden_norm(hidden_pre, gain_vector):
    return layer_norm(jax.nn.gelu(hidden_pre, approximate=True), gain_vector)


def selector(stride, head_count):
    return jnp.arange(stride)[:, None] == (jnp.arange(head_count) % stride)[None, :]


def compact(full_array, stride):
    length_in, head_count, inner_size = full_array.shape
    shaped = full_array.reshape(length_in // stride, stride, head_count, inner_size)
    picked = jnp.where(
        selector(stride, head_count)[None, :, :, None], shaped, jnp.zeros((), full_array.dtype)
    )
    return jnp.sum(picked, axis=1)


def expand(part_array, stride, fill_value):
    part_rows, head_count, inner_size = part_array.shape
    widened = jnp.where(
        selector(stride, head_count)[None, :, :, None],
        part_array[:, None],
        jnp.asarray(fill_value, part_array.dtype),
    )
    return widened.reshape(part_rows * stride, head_count, inner_size)


def positions(start_pos, part_rows, stride, head_count):
    row_ids = jnp.arange(part_rows, dtype=jnp.int32)[:, None] * stride
    head_ids = (jnp.arange(head_count, dtype=jnp.int32) % stride)[None, :]
    return start_pos + row_ids + head_ids


def doc_index(places, doc_bounds):
    return jnp.sum((places[..., None] >= doc_bounds).astype(jnp.int32), axis=-1)


def block_mask(doc_query, doc_key, local_block):
    allowed = doc_query.T[:, :, None] == doc_key.T[:, None, :]
    if local_block:
        rank_ids = jnp.arange(doc_query.shape[0])
        allowed = allowed & (rank_ids[:, None] >= rank_ids[None, :])[None]
    return allowed


def forward_block(query_part, key_part, value_part, allowed, score_scale):
    scores = (
        jnp.einsum("qhd,khd->hqk", query_part, key_part, preferred_element_type=jnp.float32)
        * score_scale
    )
    scores = jnp.where(allowed, scores, big_negative)
    row_peak = jnp.max(scores, axis=-1)
    weights = jnp.where(allowed, jnp.exp(scores - row_peak[..., None]), 0.0)
    row_total = jnp.sum(weights, axis=-1)
    mixed = jnp.einsum(
        "hqk,khd->qhd", weights.astype(jnp.bfloat16), value_part, preferred_element_type=jnp.float32
    )
    return (row_peak.T, row_total.T, mixed)


def merge(carried, new_block):
    best_peak = jnp.maximum(carried[0], new_block[0])
    keep_factor = jnp.exp(carried[0] - best_peak)
    take_factor = jnp.exp(new_block[0] - best_peak)
    new_total = carried[1] * keep_factor + new_block[1] * take_factor
    new_mixed = carried[2] * keep_factor[..., None] + new_block[2] * take_factor[..., None]
    return (best_peak, new_total, new_mixed)


def backward_block(
    query_part, grad_part, lse_part, delta_part, key_part, value_part, allowed, score_scale
):
    scores = (
        jnp.einsum("qhd,khd->hqk", query_part, key_part, preferred_element_type=jnp.float32)
        * score_scale
    )
    probs = jnp.where(allowed, jnp.exp(scores - lse_part.T[:, :, None]), 0.0)
    dots = jnp.einsum("qhd,khd->hqk", grad_part, value_part, preferred_element_type=jnp.float32)
    grad_scores = (probs * (dots - delta_part.T[:, :, None])).astype(jnp.bfloat16)
    query_grad = (
        jnp.einsum("hqk,khd->qhd", grad_scores, key_part, preferred_element_type=jnp.float32)
        * score_scale
    )
    key_grad = (
        jnp.einsum("hqk,qhd->khd", grad_scores, query_part, preferred_element_type=jnp.float32)
        * score_scale
    )
    value_grad = jnp.einsum(
        "hqk,qhd->khd", probs.astype(jnp.bfloat16), grad_part, preferred_element_type=jnp.float32
    )
    return (query_grad, key_grad, value_grad)


def keep_state(carried):
    return carried


def ring_local(
    tokens,
    lengths,
    w_query,
    w_key,
    w_value,
    w_out,
    w_up,
    w_down,
    gain_attend,
    gain_inner,
    gain_feed,
    gain_hidden,
    cotangent,
):
    block_rows, model_width = tokens.shape
    head_count = HEADS
    head_size = model_width // head_count
    score_scale = head_size ** (-0.5)
    seq_devices = lax.axis_size("seq")
    all_devices = seq_devices * lax.axis_size("row")
    my_index = lax.axis_index("seq")
    seq_total = block_rows * seq_devices
    doc_bounds = jnp.cumsum(lengths[0])[:-1]
    patterns = [
        (2**pattern, min(SEGMENT * 2**pattern, seq_total) // block_rows)
        for pattern in range(PATTERNS)
    ]
    near_ids = [0, 1]
    far_ids = list(range(2, PATTERNS))
    reach = patterns[1][1]
    far_rows = [block_rows // patterns[pattern][0] for pattern in far_ids]
    far_starts = [sum(far_rows[:slot_id]) for slot_id in range(len(far_ids))]
    far_total = sum(far_rows)

    def key_docs(pattern, source):
        stride = patterns[pattern][0]
        return doc_index(
            positions(source * block_rows, block_rows // stride, stride, head_count), doc_bounds
        )

    def is_live(pattern, cycle_step):
        group_size = patterns[pattern][1]
        return (cycle_step < group_size) & (my_index % group_size >= cycle_step)

    source_x = tokens.astype(jnp.float32)
    normed, attend_back = jax.vjp(layer_norm, source_x, gain_attend)
    normed_b = normed.astype(jnp.bfloat16)
    query_b = jnp.dot(normed_b, w_query, preferred_element_type=jnp.float32).astype(jnp.bfloat16)
    key_b = jnp.dot(normed_b, w_key, preferred_element_type=jnp.float32).astype(jnp.bfloat16)
    value_b = jnp.dot(normed_b, w_value, preferred_element_type=jnp.float32).astype(jnp.bfloat16)
    query_heads = query_b.reshape(block_rows, head_count, head_size)
    key_heads = key_b.reshape(block_rows, head_count, head_size)
    value_heads = value_b.reshape(block_rows, head_count, head_size)
    query_parts = [compact(query_heads, stride) for stride, group_size in patterns]
    key_parts = [compact(key_heads, stride) for stride, group_size in patterns]
    value_parts = [compact(value_heads, stride) for stride, group_size in patterns]
    own_docs = [key_docs(pattern, my_index) for pattern in range(PATTERNS)]
    states = [
        forward_block(
            query_parts[pattern],
            key_parts[pattern],
            value_parts[pattern],
            block_mask(own_docs[pattern], own_docs[pattern], True),
            score_scale,
        )
        for pattern in range(PATTERNS)
    ]

    def unpack_near(key_block):
        key_full = key_block[:, :model_width].reshape(block_rows, head_count, head_size)
        value_full = key_block[:, model_width:].reshape(block_rows, head_count, head_size)
        return (key_full, value_full)

    def near_fold_parts(pattern, key_part, value_part, source, carried):
        new_block = forward_block(
            query_parts[pattern],
            key_part,
            value_part,
            block_mask(own_docs[pattern], key_docs(pattern, source), False),
            score_scale,
        )
        return merge(carried, new_block)

    def near_fold(pattern, key_full, value_full, source, carried):
        stride = patterns[pattern][0]
        return near_fold_parts(
            pattern, compact(key_full, stride), compact(value_full, stride), source, carried
        )

    pair_block = jnp.concatenate([key_b, value_b], axis=1)
    kept_blocks = jnp.zeros((max(reach - 1, 1), block_rows, 2 * model_width), jnp.bfloat16)

    def near_forward(cycle_step, loop_state):
        key_block, near_now, kept_store = loop_state
        key_block = shifted_2(key_block, "seq", 1)
        key_full, value_full = unpack_near(key_block)
        new_states = []
        for pattern in near_ids:
            new_states.append(
                lax.cond(
                    is_live(pattern, cycle_step),
                    partial(near_fold, pattern, key_full, value_full, my_index - cycle_step),
                    keep_state,
                    near_now[pattern],
                )
            )
        return (key_block, tuple(new_states), kept_store)

    _, near_states, kept_blocks = lax.fori_loop(
        1, reach, near_forward, (pair_block, (states[0], states[1]), kept_blocks)
    )
    far_block = jnp.concatenate(
        [
            jnp.concatenate(
                [
                    key_parts[pattern].reshape(rows_here, model_width),
                    value_parts[pattern].reshape(rows_here, model_width),
                ],
                axis=1,
            )
            for pattern, rows_here in zip(far_ids, far_rows)
        ],
        axis=0,
    )

    def unpack_far(key_block, slot_id):
        rows_here = far_rows[slot_id]
        row_begin = far_starts[slot_id]
        piece_rows = key_block[row_begin : row_begin + rows_here]
        key_part = piece_rows[:, :model_width].reshape(rows_here, head_count, head_size)
        value_part = piece_rows[:, model_width:].reshape(rows_here, head_count, head_size)
        return (key_part, value_part)

    def far_fold(pattern, key_part, value_part, source, carried):
        new_block = forward_block(
            query_parts[pattern],
            key_part,
            value_part,
            block_mask(own_docs[pattern], key_docs(pattern, source), False),
            score_scale,
        )
        return merge(carried, new_block)

    def far_update(far_now, key_block, cycle_step):
        new_states = []
        for slot_id, pattern in enumerate(far_ids):
            key_part, value_part = unpack_far(key_block, slot_id)
            new_states.append(
                lax.cond(
                    is_live(pattern, cycle_step),
                    partial(far_fold, pattern, key_part, value_part, my_index - cycle_step),
                    keep_state,
                    far_now[slot_id],
                )
            )
        return tuple(new_states)

    far_states = tuple((states[pattern] for pattern in far_ids))

    def far_forward(cycle_step, loop_state):
        key_block, far_now = loop_state
        key_block = shifted_2(key_block, "seq", 1)
        return (key_block, far_update(far_now, key_block, cycle_step))

    _, far_states = lax.fori_loop(1, seq_devices, far_forward, (far_block, far_states))
    ordered = list(near_states) + list(far_states)
    peaks = [
        expand(ordered[pattern][0][..., None], patterns[pattern][0], big_negative)[..., 0]
        for pattern in range(PATTERNS)
    ]
    best_peak = reduce(jnp.maximum, peaks)
    weight_sum = jnp.zeros((block_rows, head_count), jnp.float32)
    mixed_sum = jnp.zeros((block_rows, head_count, head_size), jnp.float32)
    for pattern in range(PATTERNS):
        stride = patterns[pattern][0]
        factor = jnp.exp(peaks[pattern] - best_peak)
        weight_sum = (
            weight_sum + expand(ordered[pattern][1][..., None], stride, 0.0)[..., 0] * factor
        )
        mixed_sum = mixed_sum + expand(ordered[pattern][2], stride, 0.0) * factor[..., None]
    attended = mixed_sum / weight_sum[..., None]
    log_total = best_peak + jnp.log(weight_sum)
    inner_out, inner_back = jax.vjp(
        layer_norm, attended.reshape(block_rows, model_width), gain_inner
    )
    inner_b = inner_out.astype(jnp.bfloat16)
    middle = source_x + jnp.dot(inner_b, w_out, preferred_element_type=jnp.float32)
    normed_two, feed_back = jax.vjp(layer_norm, middle, gain_feed)
    normed_two_b = normed_two.astype(jnp.bfloat16)
    hidden_pre = jnp.dot(normed_two_b, w_up, preferred_element_type=jnp.float32)
    hidden, hidden_back = jax.vjp(hidden_norm, hidden_pre, gain_hidden)
    hidden_b = hidden.astype(jnp.bfloat16)
    result = (middle + jnp.dot(hidden_b, w_down, preferred_element_type=jnp.float32)).astype(
        jnp.bfloat16
    )
    grad_down = jnp.einsum("tf,tg->fg", hidden_b, cotangent, preferred_element_type=jnp.float32)
    grad_hidden = jnp.einsum("tg,fg->tf", cotangent, w_down, preferred_element_type=jnp.float32)
    grad_pre, grad_gain_hidden = hidden_back(grad_hidden)
    grad_pre_b = grad_pre.astype(jnp.bfloat16)
    grad_up = jnp.einsum("tf,tg->fg", normed_two_b, grad_pre_b, preferred_element_type=jnp.float32)
    grad_normed_two = jnp.einsum("tg,fg->tf", grad_pre_b, w_up, preferred_element_type=jnp.float32)
    grad_middle_part, grad_gain_feed = feed_back(grad_normed_two)
    grad_middle = cotangent.astype(jnp.float32) + grad_middle_part
    grad_middle_b = grad_middle.astype(jnp.bfloat16)
    grad_out = jnp.einsum("tf,tg->fg", inner_b, grad_middle_b, preferred_element_type=jnp.float32)
    grad_inner = jnp.einsum("tg,fg->tf", grad_middle_b, w_out, preferred_element_type=jnp.float32)
    grad_attended, grad_gain_inner = inner_back(grad_inner)
    grad_heads = grad_attended.astype(jnp.bfloat16).reshape(block_rows, head_count, head_size)
    delta_rows = jnp.sum(grad_heads.astype(jnp.float32) * attended, axis=-1)
    grad_parts = [compact(grad_heads, stride) for stride, group_size in patterns]
    lse_parts = [compact(log_total[..., None], stride)[..., 0] for stride, group_size in patterns]
    delta_parts = [
        compact(delta_rows[..., None], stride)[..., 0] for stride, group_size in patterns
    ]
    query_grads = []
    home_keys = []
    home_values = []
    for pattern in range(PATTERNS):
        part_query, part_key, part_value = backward_block(
            query_parts[pattern],
            grad_parts[pattern],
            lse_parts[pattern],
            delta_parts[pattern],
            key_parts[pattern],
            value_parts[pattern],
            block_mask(own_docs[pattern], own_docs[pattern], True),
            score_scale,
        )
        query_grads.append(part_query)
        home_keys.append(part_key)
        home_values.append(part_value)

    def fetch_full(key_block):
        return shifted_2(key_block, "seq", 1)

    def near_grad(pattern, key_full, value_full, source, operands):
        query_grad, travel = operands
        stride = patterns[pattern][0]
        part_query, part_key, part_value = backward_block(
            query_parts[pattern],
            grad_parts[pattern],
            lse_parts[pattern],
            delta_parts[pattern],
            compact(key_full, stride),
            compact(value_full, stride),
            block_mask(own_docs[pattern], key_docs(pattern, source), False),
            score_scale,
        )
        spread_rows = jnp.concatenate(
            [
                expand(part_key, stride, 0.0).reshape(block_rows, model_width),
                expand(part_value, stride, 0.0).reshape(block_rows, model_width),
            ],
            axis=1,
        )
        return (query_grad + part_query, travel + spread_rows)

    def near_backward(cycle_step, loop_state):
        key_block, grads_now, travel = loop_state
        key_block = fetch_full(key_block)
        travel = shifted_3(travel.astype(jnp.bfloat16), "seq", 1).astype(travel.dtype)
        key_full, value_full = unpack_near(key_block)
        new_grads = list(grads_now)
        for pattern in near_ids:
            new_grads[pattern], travel = lax.cond(
                is_live(pattern, cycle_step),
                partial(near_grad, pattern, key_full, value_full, my_index - cycle_step),
                keep_state,
                (new_grads[pattern], travel),
            )
        return (key_block, tuple(new_grads), travel)

    own_key_near = expand(home_keys[0], 1, 0.0) + expand(home_keys[1], 2, 0.0)
    own_value_near = expand(home_values[0], 1, 0.0) + expand(home_values[1], 2, 0.0)
    near_start = jnp.concatenate(
        [
            own_key_near.reshape(block_rows, model_width),
            own_value_near.reshape(block_rows, model_width),
        ],
        axis=1,
    )
    _, near_query, travel_near = lax.fori_loop(
        1, reach, near_backward, (pair_block, (query_grads[0], query_grads[1]), near_start)
    )
    near_home = shifted_3(travel_near.astype(jnp.bfloat16), "seq", 1 - reach).astype(
        travel_near.dtype
    )
    near_key_add = near_home[:, :model_width].reshape(block_rows, head_count, head_size)
    near_value_add = near_home[:, model_width:].reshape(block_rows, head_count, head_size)

    def far_grad(slot_id, key_part, value_part, source, operands):
        query_grad, travel = operands
        pattern = far_ids[slot_id]
        rows_here = far_rows[slot_id]
        row_begin = far_starts[slot_id]
        part_query, part_key, part_value = backward_block(
            query_parts[pattern],
            grad_parts[pattern],
            lse_parts[pattern],
            delta_parts[pattern],
            key_part,
            value_part,
            block_mask(own_docs[pattern], key_docs(pattern, source), False),
            score_scale,
        )
        spread_rows = jnp.concatenate(
            [part_key.reshape(rows_here, model_width), part_value.reshape(rows_here, model_width)],
            axis=1,
        )
        return (
            query_grad + part_query,
            travel.at[row_begin : row_begin + rows_here].add(spread_rows),
        )

    def far_back_update(grads_now, travel, key_block, cycle_step):
        new_grads = list(grads_now)
        for slot_id, pattern in enumerate(far_ids):
            key_part, value_part = unpack_far(key_block, slot_id)
            new_grads[slot_id], travel = lax.cond(
                is_live(pattern, cycle_step),
                partial(far_grad, slot_id, key_part, value_part, my_index - cycle_step),
                keep_state,
                (new_grads[slot_id], travel),
            )
        return (tuple(new_grads), travel)

    far_query = tuple((query_grads[pattern] for pattern in far_ids))
    far_empty = jnp.zeros((far_total, 2 * model_width), jnp.float32)

    def far_send(travel):
        return shifted_3(travel.astype(jnp.bfloat16), "seq", 1).astype(travel.dtype)

    def far_backward(cycle_step, loop_state):
        key_block, grads_now, travel = loop_state
        key_block = shifted_2(key_block, "seq", 1)
        travel = far_send(travel)
        grads_now, travel = far_back_update(grads_now, travel, key_block, cycle_step)
        return (key_block, grads_now, travel)

    _, far_query, travel_far = lax.fori_loop(
        1, seq_devices, far_backward, (far_block, far_query, far_empty)
    )
    far_home = far_send(travel_far)
    all_query = list(near_query) + list(far_query)
    query_grad = jnp.zeros((block_rows, head_count, head_size), jnp.float32)
    key_grad = near_key_add
    value_grad = near_value_add
    for pattern in range(PATTERNS):
        stride = patterns[pattern][0]
        query_grad = query_grad + expand(all_query[pattern], stride, 0.0)
    for pattern in far_ids:
        stride = patterns[pattern][0]
        key_grad = key_grad + expand(home_keys[pattern], stride, 0.0)
        value_grad = value_grad + expand(home_values[pattern], stride, 0.0)
    for slot_id, pattern in enumerate(far_ids):
        stride = patterns[pattern][0]
        rows_here = far_rows[slot_id]
        row_begin = far_starts[slot_id]
        piece_rows = far_home[row_begin : row_begin + rows_here]
        key_grad = key_grad + expand(
            piece_rows[:, :model_width].reshape(rows_here, head_count, head_size), stride, 0.0
        )
        value_grad = value_grad + expand(
            piece_rows[:, model_width:].reshape(rows_here, head_count, head_size), stride, 0.0
        )
    grad_query_b = query_grad.reshape(block_rows, model_width).astype(jnp.bfloat16)
    grad_key_b = key_grad.reshape(block_rows, model_width).astype(jnp.bfloat16)
    grad_value_b = value_grad.reshape(block_rows, model_width).astype(jnp.bfloat16)
    grad_w_query = jnp.einsum(
        "tf,tg->fg", normed_b, grad_query_b, preferred_element_type=jnp.float32
    )
    grad_w_key = jnp.einsum("tf,tg->fg", normed_b, grad_key_b, preferred_element_type=jnp.float32)
    grad_w_value = jnp.einsum(
        "tf,tg->fg", normed_b, grad_value_b, preferred_element_type=jnp.float32
    )
    grad_normed = jnp.einsum("tg,fg->tf", grad_query_b, w_query, preferred_element_type=jnp.float32)
    grad_normed = grad_normed + jnp.einsum(
        "tg,fg->tf", grad_key_b, w_key, preferred_element_type=jnp.float32
    )
    grad_normed = grad_normed + jnp.einsum(
        "tg,fg->tf", grad_value_b, w_value, preferred_element_type=jnp.float32
    )
    grad_x_part, grad_gain_attend = attend_back(grad_normed)
    grad_input = (grad_middle + grad_x_part).astype(jnp.bfloat16)
    gains_all = jnp.concatenate(
        [grad_gain_attend, grad_gain_inner, grad_gain_feed, grad_gain_hidden]
    )
    summed = (
        lax.psum_scatter(grad_w_query.reshape(-1), ("row", "seq"), scatter_dimension=0, tiled=True),
        lax.psum_scatter(grad_w_key.reshape(-1), ("row", "seq"), scatter_dimension=0, tiled=True),
        lax.psum_scatter(grad_w_value.reshape(-1), ("row", "seq"), scatter_dimension=0, tiled=True),
        lax.psum_scatter(grad_out.reshape(-1), ("row", "seq"), scatter_dimension=0, tiled=True),
        lax.psum_scatter(grad_up.reshape(-1), ("row", "seq"), scatter_dimension=0, tiled=True),
        lax.psum_scatter(grad_down.reshape(-1), ("row", "seq"), scatter_dimension=0, tiled=True),
        lax.psum_scatter(gains_all, ("row", "seq"), scatter_dimension=0, tiled=True),
    )
    factor = 1.0 / math.sqrt(block_rows * all_devices)
    return (result, grad_input) + tuple((summed_part * factor for summed_part in summed))


NO_COST = pl.CostEstimate(flops=1000, bytes_accessed=1000, transcendentals=0)
SOME_COST = pl.CostEstimate(flops=4 * 10**9, bytes_accessed=1000, transcendentals=0)
HIGH_COST = pl.CostEstimate(flops=5 * 10**10, bytes_accessed=1000, transcendentals=0)


def split_log(level):
    remaining = math.log((level + 1) / level)
    pieces = []
    for _ in range(3):
        piece = float(jnp.bfloat16.dtype.type(remaining))
        pieces.append(piece)
        remaining -= piece
    return pieces


def extra_values(places, features, head, size, per_piece):
    masks, values = jnp.zeros_like(features), jnp.zeros(features.shape, jnp.float32)
    for level in range(1, PATTERNS):
        for piece, value in enumerate(split_log(level)):
            here = features == size + 3 * (level - 1) + piece
            masks = jnp.where(here, 2**level - 1, masks)
            values = jnp.where(here, value if per_piece else 1.0, values)
    return jnp.where(((places - head) & masks) == 0, values, 0.0)


def nt_dot(left, right):
    return lax.dot_general(
        left, right, (((1,), (1,)), ((), ())), preferred_element_type=jnp.float32
    )


def nn_dot(left, right):
    return jnp.dot(left, right, preferred_element_type=jnp.float32)


def call_whole(kernel, out_shape, name, scalars, *arrays, scratch=(), limit=12, ins=True, outs=True):
    direct = pl.BlockSpec(memory_space=pltpu.VMEM)
    return pl.pallas_call(
        kernel,
        grid_spec=pltpu.PrefetchScalarGridSpec(
            num_scalar_prefetch=1,
            grid=(1,),
            in_specs=[direct if ins else whole(array.shape) for array in arrays],
            out_specs=[direct if outs else whole(out.shape) for out in out_shape],
            scratch_shapes=list(scratch),
        ),
        out_shape=list(out_shape),
        compiler_params=pltpu.CompilerParams(vmem_limit_bytes=limit << 20),
        cost_estimate=NO_COST,
        name=name,
    )(scalars, *arrays)


def after_kernel(scalars, *refs):
    for index in range(scalars.shape[0]):
        refs[-1][index] = scalars[index]


def after(scalars, arrays, cost):
    return pl.pallas_call(
        after_kernel,
        in_specs=[pl.BlockSpec(memory_space=pltpu.SMEM)]
        + [pl.BlockSpec(memory_space=pl.ANY)] * len(arrays),
        out_specs=pl.BlockSpec(memory_space=pltpu.SMEM),
        out_shape=jax.ShapeDtypeStruct(scalars.shape, scalars.dtype),
        compiler_params=pltpu.CompilerParams(vmem_limit_bytes=1 << 20),
        cost_estimate=cost,
        name="after",
    )(scalars, *arrays)


def norm_kernel(unused, rows_ref, gain_ref, out_ref):
    out_ref[...] = (norm_parts(rows_ref[...].astype(jnp.float32))[0] * gain_ref[...]).astype(
        jnp.bfloat16
    )


def column_choice(chip, heads, size, lanes, width, transposed):
    shape, axis = ((lanes, width), 0) if transposed else ((width, lanes), 1)
    lane = lax.broadcasted_iota(jnp.int32, shape, axis)
    feature = lax.broadcasted_iota(jnp.int32, shape, 1 - axis)
    parts = []
    for head in range(heads):
        here = (feature == lane + (chip * heads + head) * size) & (lane < size)
        parts.append(jnp.where(here, 1.0, 0.0).astype(jnp.bfloat16))
    return jnp.concatenate(parts, axis=axis)


def choose_kernel(heads, size, scalars, wq_ref, wk_ref, wv_ref, *refs):
    query_rows, key_columns, value_rows, key_rows, value_columns, narrow_rows = refs
    width, chip = wq_ref.shape[0], scalars[0]
    tall = column_choice(chip, heads, size, 2 * size, width, True)
    flat = column_choice(chip, heads, size, 2 * size, width, False)
    narrow = column_choice(chip, heads, size, size, width, True)
    query_rows[...] = sent(nt_dot(tall, wq_ref[...]))
    key_columns[...] = sent(nn_dot(wk_ref[...], flat))
    value_columns[...] = sent(nn_dot(wv_ref[...], flat))
    for target, weight in ((value_rows, wv_ref), (key_rows, wk_ref), (narrow_rows, wq_ref)):
        target[...] = sent(nt_dot(narrow, weight[...]))


def choose(scalars, w_query, w_key, w_value, heads, size):
    width = w_query.shape[0]
    shapes = [
        (2 * heads * size, width),
        (width, 2 * heads * size),
        (heads * size, width),
        (heads * size, width),
        (width, 2 * heads * size),
        (heads * size, width),
    ]
    return call_whole(
        partial(choose_kernel, heads, size),
        [jax.ShapeDtypeStruct(shape, jnp.bfloat16) for shape in shapes],
        "choose",
        scalars,
        w_query,
        w_key,
        w_value,
        limit=24,
        ins=False,
    )


def project_kernel(blocks, own, heads, scale, meta, *refs):
    normed = refs[:blocks]
    wq_ref, wk_ref, wv_ref = refs[blocks : blocks + 3]
    q_ref, k_ref, vt_ref = refs[-3:]
    length = normed[0].shape[0]
    lanes = wk_ref.shape[1] // heads
    size = lanes // 2
    first_head = meta[blocks]
    for index in range(blocks):
        rows = normed[index][...]
        start = meta[index]
        span = slice(index * length, (index + 1) * length)
        keys = nn_dot(rows, wk_ref[...])
        vt_ref[:, span] = nt_dot(wv_ref[...], rows).astype(jnp.bfloat16)
        places = start + lax.broadcasted_iota(jnp.int32, (length, 1), 0)
        features = lax.broadcasted_iota(jnp.int32, (1, lanes), 1)
        for head in range(heads):
            wide_rows = slice(head * lanes, (head + 1) * lanes)
            extra = extra_values(places, features, first_head + head, size, False)
            k_ref[span, wide_rows] = (keys[:, wide_rows] + extra).astype(jnp.bfloat16)
        if index < own:
            queries = nt_dot(wq_ref[...], rows).astype(jnp.bfloat16).astype(jnp.float32) * scale
            places = start + lax.broadcasted_iota(jnp.int32, (1, length), 1)
            features = lax.broadcasted_iota(jnp.int32, (lanes, 1), 0)
            for head in range(heads):
                wide_rows = slice(head * lanes, (head + 1) * lanes)
                extra = extra_values(places, features, first_head + head, size, True)
                q_ref[wide_rows, span] = (queries[wide_rows] + extra).astype(jnp.bfloat16)


def project(meta, normed, wq, wk, wv, own, heads, scale, chips, filled=None):
    blocks, length = len(normed), normed[0].shape[0]
    wide_columns, share = wk.shape[1], wv.shape[0]
    last = 0 if filled is None else 2 * chips // blocks - 1
    last_own = 0 if filled is None else chips // own - 1
    aliases = {} if filled is None else {blocks + 4 + index: index for index in range(3)}
    return pl.pallas_call(
        partial(project_kernel, blocks, own, heads, scale),
        grid_spec=pltpu.PrefetchScalarGridSpec(
            num_scalar_prefetch=1,
            grid=(1,),
            in_specs=[whole(array.shape) for array in (*normed, wq, wk, wv)]
            + [pl.BlockSpec(memory_space=pl.ANY)] * (0 if filled is None else 3),
            out_specs=[
                pl.BlockSpec((wide_columns, own * length), lambda i, meta: (0, last_own)),
                pl.BlockSpec((blocks * length, wide_columns), lambda i, meta: (last, 0)),
                pl.BlockSpec((share, blocks * length), lambda i, meta: (0, last)),
            ],
        ),
        out_shape=[
            jax.ShapeDtypeStruct((wide_columns, chips * length), jnp.bfloat16),
            jax.ShapeDtypeStruct((2 * chips * length, wide_columns), jnp.bfloat16),
            jax.ShapeDtypeStruct((share, 2 * chips * length), jnp.bfloat16),
        ],
        input_output_aliases=aliases,
        compiler_params=pltpu.CompilerParams(vmem_limit_bytes=16 << 20),
        cost_estimate=NO_COST,
        name="project",
    )(meta, *normed, wq, wk, wv, *(filled or ()))


def project_back_kernel(blocks, unused, *refs):
    normed = refs[:blocks]
    wk_ref, wv_ref, kt_ref, v_ref = refs[blocks:]
    length = normed[0].shape[0]
    for index in range(blocks):
        rows = normed[index][...]
        span = slice(index * length, (index + 1) * length)
        kt_ref[:, span] = nt_dot(wk_ref[...], rows).astype(jnp.bfloat16)
        v_ref[span, :] = nn_dot(rows, wv_ref[...]).astype(jnp.bfloat16)


def project_back(scalars, normed, wk, wv):
    blocks, length = len(normed), normed[0].shape[0]
    return call_whole(
        partial(project_back_kernel, blocks),
        [
            jax.ShapeDtypeStruct((wk.shape[0], blocks * length), jnp.bfloat16),
            jax.ShapeDtypeStruct((blocks * length, wv.shape[1]), jnp.bfloat16),
        ],
        "project_back",
        scalars,
        *normed,
        wk,
        wv,
    )


def pair_mask(query_start, key_start, doc_line, block):
    query_place = query_start + lax.broadcasted_iota(jnp.int32, (1, block), 1)
    key_place = key_start + lax.broadcasted_iota(jnp.int32, (block, 1), 0)
    return (key_place <= query_place) & (key_place >= doc_line)


def attend_kernel(heads, block, first, steps, key_blocks, meta, doc_ref, q_ref, k_ref, vt_ref, *refs):
    o_ref, m_ref, l_ref = refs[-3:]
    count = (len(refs) - 3) // 3
    mixed_refs, lse_refs, ob_refs = (refs[count * part : count * (part + 1)] for part in range(3))
    step = first + pl.program_id(0)
    query_start = meta[step]
    doc_first, doc_last = meta[steps + key_blocks + step], meta[2 * steps + key_blocks + step]
    doc_line = doc_ref[...]
    size = o_ref.shape[0] // heads
    lanes = q_ref.shape[0] // heads
    m_ref[...] = jnp.full_like(m_ref, big_negative)
    l_ref[...] = jnp.zeros_like(l_ref)
    o_ref[...] = jnp.zeros_like(o_ref)

    def fold(slot, allowed):
        span = pl.ds(pl.multiple_of(slot * block, block), block)
        scores = [
            nn_dot(
                k_ref[span, head * lanes : (head + 1) * lanes],
                q_ref[head * lanes : (head + 1) * lanes, :],
            )
            for head in range(heads)
        ]
        if allowed is not None:
            scores = [jnp.where(allowed, part, big_negative) for part in scores]
        for head in range(heads):
            rows = slice(head * size, (head + 1) * size)
            old_peak = m_ref[head]
            new_peak = jnp.maximum(old_peak, jnp.max(scores[head], axis=0, keepdims=True))
            weights = jnp.exp(scores[head] - new_peak)
            fade = jnp.exp(old_peak - new_peak)
            m_ref[head] = new_peak
            l_ref[head] = l_ref[head] * fade + jnp.sum(weights, axis=0, keepdims=True)
            o_ref[rows, :] = o_ref[rows, :] * fade + nn_dot(
                vt_ref[rows, span], weights.astype(jnp.bfloat16)
            )

    def body(slot, carry):
        key_start = meta[steps + slot]
        live = (key_start <= query_start) & (key_start + block > doc_first)
        full = (key_start < query_start) & (key_start >= doc_last)

        @pl.when(full)
        def _():
            fold(slot, None)

        @pl.when(live & jnp.logical_not(full))
        def _():
            fold(slot, pair_mask(query_start, key_start, doc_line, block))

        return carry

    lax.fori_loop(0, key_blocks, body, 0)
    for index in range(count):

        @pl.when(step == first + index)
        def _(index=index):
            for head in range(heads):
                rows = slice(head * size, (head + 1) * size)
                total = l_ref[head]
                mixed = o_ref[rows, :] / total
                mixed_refs[index][rows, :] = mixed
                ob_refs[index][rows, :] = mixed.astype(jnp.bfloat16)
                lse_refs[index][head] = m_ref[head] + jnp.log(total)


def attend_back_kernel(heads, block, steps, key_blocks, scale, meta, doc_ref, q_ref, k_ref, kt_ref, v_ref, *refs):
    o_refs, lse_refs, g_refs = (refs[steps * part : steps * (part + 1)] for part in range(3))
    dq_ref, mine_ref, other_ref, acc_ref, pair_ref, delta_ref, g_ref, lse_ref = refs[3 * steps :]
    step = pl.program_id(0)
    query_start = meta[step]
    doc_first, doc_last = meta[steps + key_blocks + step], meta[2 * steps + key_blocks + step]
    doc_line = doc_ref[...]
    size = g_ref.shape[0] // heads
    lanes = q_ref.shape[0] // heads
    share = g_ref.shape[0]

    @pl.when(step == 0)
    def _():
        pair_ref[...] = jnp.zeros_like(pair_ref)

    acc_ref[...] = jnp.zeros_like(acc_ref)
    for index in range(steps):

        @pl.when(step == index)
        def _(index=index):
            g_ref[...] = g_refs[index][...]
            lse_ref[...] = lse_refs[index][...]
            for head in range(heads):
                rows = slice(head * size, (head + 1) * size)
                delta_ref[head] = jnp.sum(
                    g_refs[index][rows, :].astype(jnp.float32) * o_refs[index][rows, :],
                    axis=0,
                    keepdims=True,
                )

    def fold(slot, allowed):
        span = pl.ds(pl.multiple_of(slot * block, block), block)
        probs, grad_scores = [], []
        for head in range(heads):
            wide_rows = slice(head * lanes, (head + 1) * lanes)
            rows = slice(head * size, (head + 1) * size)
            probs.append(nn_dot(k_ref[span, wide_rows], q_ref[wide_rows, :]))
            grad_scores.append(
                nn_dot(v_ref[span, head * lanes : head * lanes + size], g_ref[rows, :])
            )
        for head in range(heads):
            part = jnp.exp(probs[head] - lse_ref[head])
            if allowed is not None:
                part = jnp.where(allowed, part, 0.0)
            grad_scores[head] = (part * (grad_scores[head] - delta_ref[head])).astype(jnp.bfloat16)
            probs[head] = part.astype(jnp.bfloat16)
        for head in range(heads):
            rows = slice(head * size, (head + 1) * size)
            value_rows = slice(share + head * size, share + (head + 1) * size)
            query_rows = slice(head * lanes, head * lanes + size)
            pair_ref[value_rows, span] += nt_dot(g_ref[rows, :], probs[head])
            pair_ref[rows, span] += nt_dot(q_ref[query_rows, :], grad_scores[head])
            acc_ref[rows, :] += nn_dot(kt_ref[rows, span], grad_scores[head])

    def body(slot, carry):
        key_start = meta[steps + slot]
        live = (key_start <= query_start) & (key_start + block > doc_first)
        full = (key_start < query_start) & (key_start >= doc_last)

        @pl.when(full)
        def _():
            fold(slot, None)

        @pl.when(live & jnp.logical_not(full))
        def _():
            fold(slot, pair_mask(query_start, key_start, doc_line, block))

        return carry

    lax.fori_loop(0, key_blocks, body, 0)
    dq_ref[...] = (acc_ref[...] * scale).astype(dq_ref.dtype)

    @pl.when(step == steps - 1)
    def _():
        for index in range(steps):
            late = index == steps - 1
            mine = 2 * index if late else index
            other = 2 * index + 1 if late else steps - 1 + index
            span = slice(index * block, (index + 1) * block)
            mine_ref[:, span] = pair_ref[:, mine * block : (mine + 1) * block]
            other_ref[:, span] = pair_ref[:, other * block : (other + 1) * block].astype(
                jnp.bfloat16
            )


def whole(shape):
    return pl.BlockSpec(shape, lambda *index: (0,) * len(shape))


def attend(meta, doc_line, q_ext, k_ext, v_t, heads, block, first, last):
    wide_rows, queries = q_ext.shape
    share, keys = v_t.shape
    steps, key_blocks, count = queries // block, keys // block, last - first
    direct = pl.BlockSpec(memory_space=pltpu.VMEM)
    outs = pl.pallas_call(
        partial(attend_kernel, heads, block, first, steps, key_blocks),
        grid_spec=pltpu.PrefetchScalarGridSpec(
            num_scalar_prefetch=1,
            grid=(count,),
            in_specs=[
                pl.BlockSpec((1, block), lambda i, meta: (0, first + i)),
                pl.BlockSpec((wide_rows, block), lambda i, meta: (0, first + i)),
                direct,
                direct,
            ],
            out_specs=[direct] * (3 * count),
            scratch_shapes=[
                pltpu.VMEM((share, block), jnp.float32),
                pltpu.VMEM((heads, 1, block), jnp.float32),
                pltpu.VMEM((heads, 1, block), jnp.float32),
            ],
        ),
        out_shape=[jax.ShapeDtypeStruct((share, block), jnp.float32)] * count
        + [jax.ShapeDtypeStruct((heads, 1, block), jnp.float32)] * count
        + [jax.ShapeDtypeStruct((share, block), jnp.bfloat16)] * count,
        compiler_params=pltpu.CompilerParams(vmem_limit_bytes=12 << 20),
        cost_estimate=NO_COST,
        name="attend",
    )(meta, doc_line, q_ext, k_ext, v_t)
    return outs[:count], outs[count : 2 * count], outs[2 * count :]


def attend_back(meta, doc_line, q_ext, grads, mixed, lse, k_ext, k_t, v_ext, heads, block, scale):
    wide_rows, queries = q_ext.shape
    share, keys = k_t.shape
    steps, key_blocks = queries // block, keys // block
    direct = pl.BlockSpec(memory_space=pltpu.VMEM)
    return pl.pallas_call(
        partial(attend_back_kernel, heads, block, steps, key_blocks, scale),
        grid_spec=pltpu.PrefetchScalarGridSpec(
            num_scalar_prefetch=1,
            grid=(steps,),
            in_specs=[
                pl.BlockSpec((1, block), lambda i, meta: (0, i)),
                pl.BlockSpec((wide_rows, block), lambda i, meta: (0, i)),
            ]
            + [direct] * (3 + 3 * steps),
            out_specs=[pl.BlockSpec((share, block), lambda i, meta: (0, i)), direct, direct],
            scratch_shapes=[
                pltpu.VMEM((share, block), jnp.float32),
                pltpu.VMEM((2 * share, keys), jnp.float32),
                pltpu.VMEM((heads, 1, block), jnp.float32),
                pltpu.VMEM((share, block), jnp.bfloat16),
                pltpu.VMEM((heads, 1, block), jnp.float32),
            ],
        ),
        out_shape=[
            jax.ShapeDtypeStruct((share, queries), jnp.bfloat16),
            jax.ShapeDtypeStruct((2 * share, keys // 2), jnp.float32),
            jax.ShapeDtypeStruct((2 * share, keys // 2), jnp.bfloat16),
        ],
        compiler_params=pltpu.CompilerParams(vmem_limit_bytes=20 << 20),
        cost_estimate=HIGH_COST,
        name="attend_back",
    )(meta, doc_line, q_ext, k_ext, k_t, v_ext, *mixed, *lse, *grads)


def join_kernel(chips, unused, dq_ref, mine_ref, other_ref, *out_refs):
    share = dq_ref.shape[0]
    block = dq_ref.shape[1] // chips
    for step in range(chips):
        span = slice(step * block, (step + 1) * block)
        pair = (mine_ref[:, span] + other_ref[:, span].astype(jnp.float32)).astype(jnp.bfloat16)
        out_refs[step][:share, :] = dq_ref[:, span]
        out_refs[step][share:, :] = pair


def join_parts(scalars, dq, mine, other, chips):
    rows, block = dq.shape[0] + mine.shape[0], dq.shape[1] // chips
    return call_whole(
        partial(join_kernel, chips),
        [jax.ShapeDtypeStruct((rows, block), jnp.bfloat16)] * chips,
        "join",
        scalars,
        dq,
        mine,
        other,
    )


def head_grads_kernel(chips, per, scalars, *refs):
    normed, grads = refs[:chips], refs[chips : 2 * chips]
    wq_ref, wk_ref, wv_ref, gain_ref, inner_ref, feed_ref, hidden_ref = refs[2 * chips : 2 * chips + 7]
    perm_ref, keep_ref, send_ref = refs[2 * chips + 7 :]
    first_core = scalars[1] == 0
    share, model_width = wq_ref.shape
    own = nn_dot(grads[0][...], normed[0][...])
    for step in range(1, chips):
        own = own + nn_dot(grads[step][...], normed[step][...])
    attend = jnp.zeros((1, model_width), jnp.float32)
    for index, weight in enumerate((wq_ref, wk_ref, wv_ref)):
        part = own[index * share : (index + 1) * share] * weight[...].astype(jnp.float32)
        attend = attend + jnp.sum(part, axis=0, keepdims=True)
    gains = [attend / gain_ref[...], inner_ref[...], feed_ref[...], hidden_ref[...]]
    own = nt_dot(perm_ref[...], own.astype(jnp.bfloat16))
    chunks, _, width = keep_ref.shape
    columns = own.shape[1]
    part = sum(row.shape[1] for row in gains) // (2 * chunks)
    lines = -(-part // 128)
    gains = jnp.concatenate(gains + [jnp.zeros((1, 128), jnp.float32)], axis=1)

    def device_gains(device):
        starts = [device * part + 128 * line for line in range(lines)]
        rows = [gains[:, start : start + 128] for start in starts]
        return jnp.concatenate(rows, axis=0).astype(jnp.bfloat16)

    for target in (keep_ref, send_ref):
        target[:, :, columns:] = jnp.zeros((chunks, per, width - columns), jnp.bfloat16)
    for chunk in range(chunks):
        even, odd = device_gains(2 * chunk), device_gains(2 * chunk + 1)
        keep_ref[chunk, :lines, width - 128 :] = jnp.where(first_core, even, odd)
        send_ref[chunk, :lines, width - 128 :] = jnp.where(first_core, odd, even)
        for which, target in enumerate((keep_ref, send_ref)):
            first = (which * chunks + chunk) * per
            target[chunk, :, :columns] = own[first : first + per].astype(jnp.bfloat16)


def head_grads(scalars, normed, grads, weights, gain, late_gains, perm, per):
    width = perm.shape[0]
    out = jax.ShapeDtypeStruct((width // (2 * per), per, width), jnp.bfloat16)
    return call_whole(
        partial(head_grads_kernel, len(grads), per),
        [out, out],
        "head_grads",
        scalars,
        *normed,
        *grads,
        *weights,
        gain,
        *late_gains,
        perm,
        limit=24,
    )


def norm_parts(values):
    shifted = values - jnp.mean(values, axis=-1, keepdims=True)
    rate = lax.rsqrt(jnp.mean(shifted * shifted, axis=-1, keepdims=True) + 1e-05)
    return shifted * rate, rate


def norm_back(grad, hat, rate, gain):
    scaled = grad * gain
    mean_scaled = jnp.mean(scaled, axis=-1, keepdims=True)
    mean_product = jnp.mean(scaled * hat, axis=-1, keepdims=True)
    return (
        rate * (scaled - mean_scaled - hat * mean_product),
        jnp.sum(grad * hat, axis=0, keepdims=True),
    )


def middle_kernel(chips, tiles, position, *refs):
    mixed = refs[:chips]
    tokens_ref, cot_ref, wout_ref, wup_ref, wdown_ref, ginner_ref, gfeed_ref, ghidden_ref = refs[
        chips : chips + 8
    ]
    result_ref, gmid_ref, gmid_b_ref = refs[chips + 8 : chips + 11]
    go_refs = refs[chips + 11 : 2 * chips + 11]
    (
        z_ref,
        h2_ref,
        bent_out,
        pre_out,
        dinner_ref,
        dfeed_ref,
        dhidden_ref,
        swap_ref,
        work_ref,
        column_ref,
        zhat_ref,
        hat_ref,
        act_ref,
        slope_ref,
        dact_ref,
        acc_ref,
        stat_ref,
    ) = refs[2 * chips + 11 :]
    step = pl.program_id(0)
    chip = position[0]
    block, model_width = tokens_ref.shape
    share = model_width // chips
    tile = wdown_ref.shape[0]
    hidden = tile * tiles
    root = math.sqrt(2.0 / math.pi)
    phase, index = step // tiles, step % tiles
    lanes = stat_ref.shape[2]
    groups = tile // lanes

    def by_rows(body):
        body(slice(None))

    def spread(stat):
        return jnp.concatenate([stat] * groups, axis=1)

    def gathered_lanes(values):
        total = values[:, :lanes]
        for group in range(1, groups):
            total = total + values[:, group * lanes : (group + 1) * lanes]
        return total

    def lane_sum(values):
        return jnp.broadcast_to(jnp.sum(values, axis=-1, keepdims=True), values.shape)

    def column_sums(values):
        total = values[:8]
        for first in range(8, values.shape[0], 8):
            total = total + values[first : first + 8]
        return total

    def norm_rows(values):
        shifted = values - spread(lane_sum(gathered_lanes(values)) / tile)
        rate = lax.rsqrt(lane_sum(gathered_lanes(shifted * shifted)) / tile + 1e-05)
        return shifted * spread(rate), rate

    def norm_rows_back(grad, hat, rate, gain):
        scaled = grad * gain
        mean_scaled = lane_sum(gathered_lanes(scaled)) / tile
        mean_product = lane_sum(gathered_lanes(scaled * hat)) / tile
        return spread(rate) * (scaled - spread(mean_scaled) - hat * spread(mean_product))

    @pl.when(step == 0)
    def _():
        for near in range(chips):
            start = pl.multiple_of(share * lax.rem(chip + near, chips), share)
            swap_ref[pl.ds(start, share), :] = mixed[near][...].astype(jnp.float32)
        work_ref[...] = swap_ref[...].T

        def first_norm(rows):
            zhat, zrate = norm_rows(work_ref[rows, :])
            zhat_ref[rows, :] = zhat
            stat_ref[0, rows, :] = zrate
            z_ref[rows, :] = (zhat * ginner_ref[...]).astype(jnp.bfloat16)

        by_rows(first_norm)
        work_ref[...] = nn_dot(z_ref[...], wout_ref[...])

        def second_norm(rows):
            mid = tokens_ref[rows, :].astype(jnp.float32) + work_ref[rows, :]
            acc_ref[rows, :] = mid
            hat, rate = norm_rows(mid)
            hat_ref[rows, :] = hat
            stat_ref[1, rows, :] = rate
            h2_ref[rows, :] = (hat * gfeed_ref[...]).astype(jnp.bfloat16)

        by_rows(second_norm)
        for stat in range(3, 7):
            stat_ref[stat] = jnp.zeros_like(stat_ref[stat])

    @pl.when(phase == 0)
    def _():
        work_ref[...] = nn_dot(h2_ref[...], wup_ref[...])

        def bend_rows(rows):
            u = work_ref[rows, :]
            squared = u * u
            bend = jnp.tanh(root * (u + 0.044715 * u * squared))
            act_ref[index, rows, :] = 0.5 * u * (1.0 + bend)
            slope_ref[index, rows, :] = 0.5 * (1.0 + bend) + 0.5 * u * (1.0 - bend * bend) * root * (
                1.0 + 3.0 * 0.044715 * squared
            )

        by_rows(bend_rows)

        @pl.when(index == 0)
        def _():
            def pivot(rows):
                stat_ref[2, rows, :] = lane_sum(gathered_lanes(act_ref[0, rows, :])) / tile

            by_rows(pivot)

        def sums(rows):
            off = act_ref[index, rows, :] - spread(stat_ref[2, rows, :])
            stat_ref[3, rows, :] += gathered_lanes(off)
            stat_ref[4, rows, :] += gathered_lanes(off * off)

        by_rows(sums)

    @pl.when(step == tiles)
    def _():
        drift = lane_sum(stat_ref[3]) / hidden
        stat_ref[2] = stat_ref[2] + drift
        stat_ref[4] = lax.rsqrt(
            jnp.maximum(lane_sum(stat_ref[4]) / hidden - drift * drift, 0.0) + 1e-05
        )

    @pl.when(phase == 1)
    def _():
        def hidden_rows(rows):
            hat = (act_ref[index, rows, :] - spread(stat_ref[2, rows, :])) * spread(
                stat_ref[4, rows, :]
            )
            act_ref[index, rows, :] = hat
            bent_out[rows, :] = (hat * ghidden_ref[...]).astype(jnp.bfloat16)

        by_rows(hidden_rows)
        work_ref[...] = nt_dot(cot_ref[...], wdown_ref[...])
        acc_ref[...] += nn_dot(bent_out[...], wdown_ref[...])
        column_ref[...] = jnp.zeros_like(column_ref)

        def grad_rows(rows):
            hat, grad = act_ref[index, rows, :], work_ref[rows, :]
            column_ref[...] += column_sums(grad * hat)
            scaled = grad * ghidden_ref[...]
            dact_ref[index, rows, :] = scaled
            stat_ref[5, rows, :] += gathered_lanes(scaled)
            stat_ref[6, rows, :] += gathered_lanes(scaled * hat)

        by_rows(grad_rows)
        dhidden_ref[...] = jnp.sum(column_ref[...], axis=0, keepdims=True)

    @pl.when(step == 2 * tiles)
    def _():
        result_ref[...] = acc_ref[...].astype(jnp.bfloat16)
        acc_ref[...] = jnp.zeros_like(acc_ref)
        stat_ref[5] = lane_sum(stat_ref[5]) / hidden
        stat_ref[6] = lane_sum(stat_ref[6]) / hidden

    @pl.when(phase == 2)
    def _():
        def pre_rows(rows):
            inner = (
                dact_ref[index, rows, :]
                - spread(stat_ref[5, rows, :])
                - act_ref[index, rows, :] * spread(stat_ref[6, rows, :])
            )
            pre_out[rows, :] = (
                spread(stat_ref[4, rows, :]) * inner * slope_ref[index, rows, :]
            ).astype(jnp.bfloat16)

        by_rows(pre_rows)
        acc_ref[...] += nt_dot(pre_out[...], wup_ref[...])

    @pl.when(step == 3 * tiles - 1)
    def _():
        column_ref[...] = jnp.zeros_like(column_ref)

        def middle_rows(rows):
            grad, hat = acc_ref[rows, :], hat_ref[rows, :]
            column_ref[...] += column_sums(grad * hat)
            gmid = cot_ref[rows, :].astype(jnp.float32) + norm_rows_back(
                grad, hat, stat_ref[1, rows, :], gfeed_ref[...]
            )
            gmid_ref[rows, :] = gmid
            gmid_b_ref[rows, :] = gmid.astype(jnp.bfloat16)

        by_rows(middle_rows)
        dfeed_ref[...] = jnp.sum(column_ref[...], axis=0, keepdims=True)
        work_ref[...] = nt_dot(gmid_b_ref[...], wout_ref[...])
        column_ref[...] = jnp.zeros_like(column_ref)

        def inner_rows(rows):
            grad, hat = work_ref[rows, :], zhat_ref[rows, :]
            column_ref[...] += column_sums(grad * hat)
            work_ref[rows, :] = norm_rows_back(grad, hat, stat_ref[0, rows, :], ginner_ref[...])

        by_rows(inner_rows)
        dinner_ref[...] = jnp.sum(column_ref[...], axis=0, keepdims=True)
        swap_ref[...] = work_ref[...].T
        for near in range(chips):
            start = pl.multiple_of(share * lax.rem(chip + near, chips), share)
            go_refs[near][...] = swap_ref[pl.ds(start, share), :].astype(jnp.bfloat16)


def middle(position, mixed, tokens, cotangent, w_out, w_up, w_down, gains):
    chips = len(mixed)
    block, model_width = tokens.shape
    hidden = w_up.shape[1]
    tile = model_width
    tiles = hidden // tile
    share = model_width // chips
    last = tiles - 1

    def up_index(i, pos):
        return (0, jnp.where(i < tiles, i, jnp.where(i < 2 * tiles, last, i - 2 * tiles)))

    def down_index(i, pos):
        return (jnp.clip(i - tiles, 0, last), 0)

    def hidden_index(i, pos):
        return (0, jnp.clip(i - tiles, 0, last))

    def pre_index(i, pos):
        return (0, jnp.clip(i - 2 * tiles, 0, last))

    def f32(*shape):
        return pltpu.VMEM(shape, jnp.float32)

    row, rows = (1, model_width), (block, model_width)
    narrow = jax.ShapeDtypeStruct(rows, jnp.bfloat16)
    return pl.pallas_call(
        partial(middle_kernel, chips, tiles),
        grid_spec=pltpu.PrefetchScalarGridSpec(
            num_scalar_prefetch=1,
            grid=(3 * tiles,),
            in_specs=[whole((share, block))] * chips
            + [
                whole(rows),
                whole(rows),
                whole((model_width, model_width)),
                pl.BlockSpec((model_width, tile), up_index),
                pl.BlockSpec((tile, model_width), down_index),
                whole(row),
                whole(row),
                pl.BlockSpec((1, tile), hidden_index),
            ],
            out_specs=[whole(rows)] * 3
            + [whole((share, block))] * chips
            + [
                whole(rows),
                whole(rows),
                pl.BlockSpec((block, tile), hidden_index),
                pl.BlockSpec((block, tile), pre_index),
                whole(row),
                whole(row),
                pl.BlockSpec((1, tile), hidden_index),
            ],
            scratch_shapes=[
                f32(model_width, block),
                f32(block, tile),
                f32(8, tile),
                f32(block, model_width),
                f32(block, model_width),
                f32(tiles, block, tile),
                f32(tiles, block, tile),
                f32(tiles, block, tile),
                f32(block, model_width),
                f32(7, block, 128),
            ],
        ),
        out_shape=[narrow, jax.ShapeDtypeStruct(rows, jnp.float32), narrow]
        + [jax.ShapeDtypeStruct((share, block), jnp.bfloat16)] * chips
        + [
            narrow,
            narrow,
            jax.ShapeDtypeStruct((block, hidden), jnp.bfloat16),
            jax.ShapeDtypeStruct((block, hidden), jnp.bfloat16),
            jax.ShapeDtypeStruct(row, jnp.float32),
            jax.ShapeDtypeStruct(row, jnp.float32),
            jax.ShapeDtypeStruct((1, hidden), jnp.float32),
        ],
        compiler_params=pltpu.CompilerParams(vmem_limit_bytes=26 << 20),
        cost_estimate=NO_COST,
        name="middle",
    )(position, *mixed, tokens, cotangent, w_out, w_up, w_down, *gains)


def down_kernel(per, position, bent_ref, cot_ref, keep_ref, send_ref):
    first_core = position[1] == 0
    parts = bent_ref.shape[1] // (2 * per)
    first = pl.program_id(0) * parts
    grad = lax.dot_general(
        bent_ref[...], cot_ref[...], (((0,), (0,)), ((), ())), preferred_element_type=jnp.float32
    ).astype(jnp.bfloat16)
    for part in range(parts):
        even = grad[2 * per * part : 2 * per * part + per]
        odd = grad[2 * per * part + per : 2 * per * (part + 1)]
        keep_ref[first + part] = jnp.where(first_core, even, odd)
        send_ref[first + part] = jnp.where(first_core, odd, even)


def down_grad(position, bent, cotangent, per):
    (block, hidden), model_width = bent.shape, cotangent.shape[1]
    tiles, chunks = hidden // model_width, hidden // (2 * per)
    out = jax.ShapeDtypeStruct((chunks, per, model_width), jnp.bfloat16)
    out_spec = pl.BlockSpec(memory_space=pltpu.VMEM)
    return pl.pallas_call(
        partial(down_kernel, per),
        grid_spec=pltpu.PrefetchScalarGridSpec(
            num_scalar_prefetch=1,
            grid=(tiles,),
            in_specs=[
                pl.BlockSpec((block, model_width), lambda i, pos: (0, i)),
                pl.BlockSpec(memory_space=pltpu.VMEM),
            ],
            out_specs=[out_spec, out_spec],
        ),
        out_shape=[out, out],
        compiler_params=pltpu.CompilerParams(vmem_limit_bytes=20 << 20),
        cost_estimate=NO_COST,
        name="down_grad",
    )(position, bent, cotangent)


def up_out_kernel(tiles, position, h2_ref, pre_ref, z_ref, gmid_ref, perm_ref, keep_ref, send_ref, left_ref):
    step = pl.program_id(0)
    chunks = keep_ref.shape[0]
    per = perm_ref.shape[0] // (2 * chunks)
    place = pl.ds(pl.multiple_of(step * per, per), per)

    @pl.when(step == 0)
    def _():
        left_ref[...] = nt_dot(perm_ref[...], h2_ref[...]).astype(jnp.bfloat16)

    def store(right):
        grad = nn_dot(left_ref[...], right)
        for chunk in range(chunks):
            keep_ref[chunk, place] = grad[chunk * per : (chunk + 1) * per].astype(jnp.bfloat16)
            first = (chunks + chunk) * per
            send_ref[chunk, place] = grad[first : first + per].astype(jnp.bfloat16)

    @pl.when(step < tiles)
    def _():
        store(pre_ref[...])

    @pl.when(step == tiles)
    def _():
        left_ref[...] = nt_dot(perm_ref[...], z_ref[...]).astype(jnp.bfloat16)
        store(gmid_ref[...])


def up_out_grad(position, h2, pre, z, gmid, perm, per):
    (block, hidden), model_width = pre.shape, h2.shape[1]
    tiles, chunks = hidden // model_width, model_width // (2 * per)
    out = jax.ShapeDtypeStruct((chunks, per * (tiles + 1), model_width), jnp.bfloat16)
    out_spec = pl.BlockSpec(memory_space=pltpu.VMEM)
    return pl.pallas_call(
        partial(up_out_kernel, tiles),
        grid_spec=pltpu.PrefetchScalarGridSpec(
            num_scalar_prefetch=1,
            grid=(tiles + 1,),
            in_specs=[
                pl.BlockSpec(memory_space=pltpu.VMEM),
                pl.BlockSpec((block, model_width), lambda i, pos: (0, jnp.minimum(i, tiles - 1))),
            ]
            + [pl.BlockSpec(memory_space=pltpu.VMEM)] * 3,
            out_specs=[out_spec, out_spec],
            scratch_shapes=[pltpu.VMEM((model_width, block), jnp.bfloat16)],
        ),
        out_shape=[out, out],
        compiler_params=pltpu.CompilerParams(vmem_limit_bytes=20 << 20),
        cost_estimate=NO_COST,
        name="up_out_grad",
    )(position, h2, pre, z, gmid, perm)


def final_kernel(chips, position, *refs):
    homes = refs[:chips]
    (
        tokens_ref,
        gmid_ref,
        wq_ref,
        wk_ref,
        wv_ref,
        gain_ref,
        out_ref,
        swap_ref,
    ) = refs[chips:]
    chip = position[0]
    block, model_width = tokens_ref.shape
    share = model_width // chips
    total = jnp.zeros((block, model_width), jnp.float32)
    for index, weight in enumerate((wq_ref, wk_ref, wv_ref)):
        for near in range(chips):
            start = pl.multiple_of(share * lax.rem(chip + near, chips), share)
            swap_ref[pl.ds(start, share), :] = homes[near][
                index * share : (index + 1) * share, :
            ].astype(jnp.float32)
        total = total + nt_dot(swap_ref[...].T.astype(jnp.bfloat16), weight[...])
    hat, rate = norm_parts(tokens_ref[...].astype(jnp.float32))
    back = norm_back(total, hat, rate, gain_ref[...])[0]
    out_ref[...] = (gmid_ref[...] + back).astype(jnp.bfloat16)


def final(position, homes, tokens, gmid, w_query, w_key, w_value, gain):
    block, model_width = tokens.shape
    return call_whole(
        partial(final_kernel, len(homes)),
        [jax.ShapeDtypeStruct((block, model_width), jnp.bfloat16)],
        "final",
        position,
        *homes,
        tokens,
        gmid,
        w_query,
        w_key,
        w_value,
        gain,
        scratch=[pltpu.VMEM((model_width, block), jnp.float32)],
        outs=False,
    )[0]


def chip_shift(value, steps):
    count = lax.axis_size("seq")
    return lax.ppermute(value, "seq", [(i, (i + 2 * steps) % count) for i in range(count)])


def seq_swap(value, bit):
    return lax.ppermute(value, "seq", [(i, i ^ bit) for i in range(lax.axis_size("seq"))])


def row_swap(value, bit):
    return lax.ppermute(value, "row", [(i, i ^ bit) for i in range(lax.axis_size("row"))])


def sent(array):
    return array.astype(jnp.bfloat16)


def wide(array):
    return array.astype(jnp.float32)


def outgoing_kernel(kept, scalars, *refs):
    low_ref, high_ref = refs[-2:]
    low_bit, high_bit = scalars[2], scalars[3]
    if not kept:
        low_bit, high_bit = 1 - low_bit, 1 - high_bit
    half = refs[0].shape[2] // 2
    first = 0
    for group in range(len(refs) // 2 - 1):
        keep, other = refs[2 * group : 2 * group + 2]
        rows = slice(first, first + keep.shape[3])
        for side in range(2):
            low_ref[side, :, rows] = sent(
                wide(keep[side, low_bit, :half]) + wide(other[side, low_bit, :half])
            )
            high_ref[side, :, rows] = sent(
                wide(keep[high_bit, side, half:]) + wide(other[high_bit, side, half:])
            )
        first += keep.shape[3]


def outgoing(scalars, groups, kept=False):
    arrays = [array for group in groups for array in group]
    shape = groups[0][0].shape
    rows = sum(keep.shape[3] for keep, _ in groups)
    out = jax.ShapeDtypeStruct((2, shape[2] // 2, rows, shape[4]), jnp.bfloat16)
    return call_whole(
        partial(outgoing_kernel, kept),
        [out, out],
        "kept" if kept else "outgoing",
        scalars,
        *arrays,
    )


def halfway_kernel(groups, scalars, *refs):
    ins, outs = refs[: 4 * groups], refs[4 * groups :]
    low_bit, high_bit = scalars[2], scalars[3]
    low_keep, low_send, high_keep, high_send = outs
    first = 0
    for group in range(groups):
        low, high, low_in, high_in = ins[4 * group : 4 * group + 4]
        rows = slice(first, first + low.shape[2])
        for target, side in ((low_keep, high_bit), (low_send, 1 - high_bit)):
            target[:, rows] = sent(wide(low[side]) + wide(low_in[side]))
        for target, side in ((high_keep, low_bit), (high_send, 1 - low_bit)):
            target[:, rows] = sent(wide(high[side]) + wide(high_in[side]))
        first += low.shape[2]


def halfway(scalars, groups):
    arrays = [array for group in groups for array in group]
    rows = sum(group[0].shape[2] for group in groups)
    out = jax.ShapeDtypeStruct((arrays[0].shape[1], rows, arrays[0].shape[3]), jnp.bfloat16)
    return call_whole(
        partial(halfway_kernel, len(groups)), [out] * 4, "halfway", scalars, *arrays, limit=12
    )


def split_kernel(chips, groups, scalars, *refs):
    ins, outs = refs[: 4 * groups], refs[4 * groups : 4 * groups + chips]
    all_ref = refs[-1]
    half = chips // 2
    first = 0
    for group in range(groups):
        low_keep, low_in, high_keep, high_in = ins[4 * group : 4 * group + 4]
        rows = slice(first, first + low_in.shape[1])
        all_ref[:half, rows] = sent(wide(low_keep[...]) + wide(low_in[...]))
        all_ref[half:, rows] = sent(wide(high_keep[...]) + wide(high_in[...]))
        first += low_in.shape[1]
    for step in range(chips):
        outs[step][...] = all_ref[lax.rem(scalars[0] + step, chips)]


def split(scalars, groups, chips):
    arrays = [array for group in groups for array in group]
    rows = sum(group[0].shape[1] for group in groups)
    width = arrays[0].shape[2]
    return call_whole(
        partial(split_kernel, chips, len(groups)),
        [jax.ShapeDtypeStruct((rows, width), jnp.bfloat16)] * chips,
        "split",
        scalars,
        *arrays,
        scratch=[pltpu.VMEM((chips, rows, width), jnp.bfloat16)],
    )


def lay_flat(target, values, first, step):
    for piece in range(values.shape[1] // 128):
        target[pl.ds(first + piece, values.shape[0], step), :] = values[
            :, 128 * piece : 128 * (piece + 1)
        ]


def finish_kernel(chips, per, share, factor, scalars, *refs):
    arrived, heads_in, refs = refs[:chips], refs[chips : 2 * chips], refs[chips:]
    down_ref, up_ref, out_ref, query_ref, key_ref, value_ref, gains_ref, heads_ref = refs[chips:]
    width = arrived[0].shape[1]
    chip, pieces = scalars[0], width // 128
    tiles = up_ref.shape[0] * 128 // (per * width)
    down_rows = down_ref.shape[0] * 128 // width

    def total(first, rows):
        result = wide(arrived[0][first : first + rows, :])
        for part in arrived[1:]:
            result = result + wide(part[first : first + rows, :])
        return result * factor

    lay_flat(down_ref, total(0, down_rows), 0, pieces)
    for tile in range(tiles):
        lay_flat(up_ref, total(down_rows + tile * per, per), tile * pieces, tiles * pieces)
    lay_flat(out_ref, total(down_rows + tiles * per, per), 0, pieces)
    gains = wide(heads_in[0][:8, -128:])
    for part in heads_in[1:]:
        gains = gains + wide(part[:8, -128:])
    gains_ref[...] = gains * factor
    for step in range(chips):
        heads_ref[lax.rem(chip - step + chips, chips)] = wide(heads_in[step][:, : 3 * share])
    for index, target in enumerate((query_ref, key_ref, value_ref)):
        values = jnp.concatenate(
            [heads_ref[near][:, index * share : (index + 1) * share] for near in range(chips)], axis=1
        )
        lay_flat(target, values * factor, 0, pieces)


def finish(scalars, arrived, hidden, parts, per, share, factor):
    chips, width = len(arrived) // 2, arrived[0].shape[1]
    square = jax.ShapeDtypeStruct((per * width // 128, 128), jnp.float32)
    large = jax.ShapeDtypeStruct((per * hidden // 128, 128), jnp.float32)
    return call_whole(
        partial(finish_kernel, chips, per, share, factor),
        [large, large, square, square, square, square, jax.ShapeDtypeStruct((8, 128), jnp.float32)],
        "finish",
        scalars,
        *arrived,
        scratch=[pltpu.VMEM((chips, per, 3 * share), jnp.float32)],
        outs=False,
    )


def gathered(rows):
    behind, ahead = chip_shift(rows, 1), chip_shift(rows, -1)
    up = [(2 * i + core, 2 * i + 2 + core) for i in (1, 2) for core in (0, 1)]
    down = [(2 * i + core, 2 * i - 2 + core) for i in (1, 2) for core in (0, 1)]
    across = (lax.ppermute(ahead, "seq", down), lax.ppermute(behind, "seq", up))
    return behind, ahead, across


def fast_local(
    tokens,
    lengths,
    w_query,
    w_key,
    w_value,
    w_out,
    w_up,
    w_down,
    gain_attend,
    gain_inner,
    gain_feed,
    gain_hidden,
    cotangent,
):
    block, model_width = tokens.shape
    hidden = w_up.shape[1]
    size = model_width // HEADS
    lanes = 2 * size
    scale = size ** (-0.5)
    seq_devices, row_devices = lax.axis_size("seq"), lax.axis_size("row")
    chips = seq_devices // 2
    heads = HEADS // chips
    share = heads * size
    spread = heads * lanes
    parts = row_devices * seq_devices
    position, row = lax.axis_index("seq"), lax.axis_index("row")
    chip, core = position // 2, position % 2
    place = jnp.stack([chip, core, row % 2, row // 2]).astype(jnp.int32)
    bounds = jnp.cumsum(lengths[0])[:-1]
    factor = 1.0 / math.sqrt(block * parts)

    normed_b = call_whole(
        norm_kernel,
        [jax.ShapeDtypeStruct(tokens.shape, jnp.bfloat16)],
        "norm",
        jnp.zeros((1,), jnp.int32),
        tokens,
        gain_attend[None, :],
        ins=False,
    )[0]
    behind, ahead, across = gathered(normed_b)

    order = [step for step in range(chips) if step != chips // 2] + [chips // 2]
    slots = [order.index(step) for step in range(chips)]
    chip_ids = (chip - jnp.asarray(order, jnp.int32)) % chips
    query_starts = block * (2 * chip_ids + core)
    other_starts = block * (2 * chip_ids + 1 - core)
    key_starts = jnp.concatenate(
        [query_starts[:-1], other_starts[:-1], query_starts[-1:], other_starts[-1:]]
    )
    in_block = jnp.arange(block, dtype=jnp.int32)[None, :]
    query_places = (query_starts[:, None] + in_block).reshape(-1)
    doc_line = jnp.max(jnp.where(bounds[:, None] <= query_places[None, :], bounds[:, None], 0), axis=0)
    meta = jnp.concatenate(
        [query_starts, key_starts, doc_line.reshape(chips, block)[:, 0], doc_line.reshape(chips, block)[:, -1]]
    )
    doc_line = doc_line[None, :]

    feature = jnp.arange(model_width, dtype=jnp.int32)
    per = model_width // parts
    chunk, inside = feature // per, feature % per
    chunks = parts // 2
    parity = jnp.where(chunk < chunks, core, 1 - core)
    wanted = (2 * (chunk % chunks) + parity) * per + inside
    perm = (wanted[:, None] == feature[None, :]).astype(jnp.bfloat16)

    gains_share = (3 * model_width + hidden) // parts
    gains_rows = -(-gains_share // 128)
    first_head = heads * chip[None]
    small = (
        jnp.concatenate([query_starts[:-1], other_starts[:-1], first_head]),
        jnp.concatenate([query_starts[-1:], other_starts[-1:], first_head]),
        meta,
        doc_line,
        gain_attend[None, :],
        gain_inner[None, :],
        gain_feed[None, :],
        gain_hidden[None, :],
        place,
        perm,
    )
    small = lax.optimization_barrier(small)
    starts, late_starts, meta, doc_line, gain_first, gain_inner, gain_feed, gain_hidden = small[:8]
    place, perm = small[8:]
    early = choose(place, w_query, w_key, w_value, heads, size)
    behind, early = lax.optimization_barrier((behind, early))
    wq_wide, wk_wide, wv_rows, wk_rows, wv_wide, wq_rows = early
    own = [normed_b, behind, ahead]
    early_blocks = own + [seq_swap(rows, 1) for rows in own]
    filled = project(
        starts, early_blocks, wq_wide, wk_wide, wv_rows, chips - 1, heads, scale, chips
    )
    filled, across = lax.optimization_barrier((filled, across))
    own.append(across[0] + across[1])
    late_blocks = [own[-1], seq_swap(own[-1], 1)]
    q_ext, k_ext, v_t = project(
        late_starts, late_blocks, wq_wide, wk_wide, wv_rows, 1, heads, scale, chips, filled
    )
    parts_of = [
        attend(meta, doc_line, q_ext, k_ext, v_t, heads, block, *span) for span in ((0, 1), (1, chips))
    ]
    mixed, lse, mixed_b = (
        list(parts_of[0][item]) + list(parts_of[1][item]) for item in range(3)
    )
    mixed_b[1:], wk_rows = lax.optimization_barrier((mixed_b[1:], wk_rows))
    k_t, v_ext = project_back(place, early_blocks + late_blocks, wk_rows, wv_wide)
    back = [mixed_b[slots[0]]] + [
        chip_shift(mixed_b[slots[step]], -step) for step in range(1, chips)
    ]
    back, k_t, v_ext = lax.optimization_barrier((back, k_t, v_ext))
    outs = middle(
        place, back, tokens, cotangent, w_out, w_up, w_down, (gain_inner, gain_feed, gain_hidden)
    )
    result, grad_middle, gmid_b = outs[:3]
    go = outs[3 : 3 + chips]
    z, h2, bent, pre, dinner, dfeed, dhidden = outs[3 + chips :]
    keep_a, send_a = down_grad(place, bent, cotangent, hidden // parts)
    keep_b, send_b = up_out_grad(place, h2, pre, z, gmid_b, perm, per)
    go, keep_b, send_b = lax.optimization_barrier((go, keep_b, send_b))
    go = [go[0]] + [chip_shift(go[step], step) for step in range(1, chips)]

    def gridded(array):
        return array.reshape((2, 2, chips) + array.shape[1:])

    sums = [
        (gridded(keep), gridded(seq_swap(send, 1)))
        for keep, send in ((keep_a, send_a), (keep_b, send_b))
    ]
    low, high = outgoing(place, sums)
    arrived_sums = [row_swap(low, 1), row_swap(high, 2)]
    dq, pair, other = attend_back(
        meta, doc_line, q_ext, [go[step] for step in order], mixed, lse, k_ext, k_t, v_ext, heads, block, scale
    )
    grads = join_parts(place, dq, pair, seq_swap(other, 1), chips)
    home = [grads[slots[0]]] + [chip_shift(grads[slots[step]], -step) for step in range(1, chips)]
    grads, sums = lax.optimization_barrier((grads, sums))
    kept = outgoing(place, sums, True)
    mine_grad, send_grad = head_grads(
        place,
        own,
        grads,
        (wq_rows, wk_rows, wv_rows),
        gain_first,
        (dinner, dfeed, dhidden),
        perm,
        per,
    )
    arrived_sums, kept, mine_grad, send_grad = lax.optimization_barrier(
        (arrived_sums, kept, mine_grad, send_grad)
    )
    low_keep, low_send, high_keep, high_send = halfway(place, [(*kept, *arrived_sums)])
    low_in, high_in = row_swap(low_send, 2), row_swap(high_send, 1)
    home, mine_grad, send_grad = lax.optimization_barrier((home, mine_grad, send_grad))
    mine_grad, other_grad = gridded(mine_grad), gridded(seq_swap(send_grad, 1))
    stage = split(after(place, home, SOME_COST), [(low_keep, low_in, high_keep, high_in)], chips)
    arrived = [stage[0]] + [chip_shift(stage[step], step) for step in range(1, chips)]
    grad_input = final(
        place, home, tokens, grad_middle, w_query, w_key, w_value, gain_first
    )
    low, high = outgoing(place, [(mine_grad, other_grad)])
    low_keep, low_send, high_keep, high_send = halfway(
        place,
        [(*outgoing(place, [(mine_grad, other_grad)], True), row_swap(low, 1), row_swap(high, 2))],
    )
    stage = split(
        place, [(low_keep, row_swap(low_send, 2), high_keep, row_swap(high_send, 1))], chips
    )
    arrived += [stage[0]] + [chip_shift(stage[step], step) for step in range(1, chips)]
    down, up, out, query, key, value, gains_part = finish(
        place, arrived, hidden, parts, per, share, factor
    )
    return (
        result,
        grad_input,
        query.reshape(-1),
        key.reshape(-1),
        value.reshape(-1),
        out.reshape(-1),
        up.reshape(-1),
        down.reshape(-1),
        gains_part.reshape(-1)[:gains_share],
    )


def local(*arrays):
    seq_devices, row_devices = lax.axis_size("seq"), lax.axis_size("row")
    block = arrays[0].shape[0]
    one_segment = block * seq_devices <= SEGMENT and block % 2 ** (PATTERNS - 1) == 0
    if one_segment and seq_devices == 8 and row_devices == 4:
        return fast_local(*arrays)
    return ring_local(*arrays)


def solution(mesh):
    return jax.shard_map(
        local,
        mesh=mesh,
        in_specs=(
            P(("row", "seq"), None),
            P("row", None),
            P(),
            P(),
            P(),
            P(),
            P(),
            P(),
            P(),
            P(),
            P(),
            P(),
            P(("row", "seq"), None),
        ),
        out_specs=(
            P(("row", "seq"), None),
            P(("row", "seq"), None),
            P(("row", "seq")),
            P(("row", "seq")),
            P(("row", "seq")),
            P(("row", "seq")),
            P(("row", "seq")),
            P(("row", "seq")),
            P(("row", "seq")),
        ),
        check_vma=False,
    )
```

```python
from functools import partial
from functools import reduce
import math

import jax
import jax.numpy as jnp
import numpy as np
from jax import lax
from jax.experimental import pallas as pl
from jax.experimental.pallas import tpu as pltpu
from jax.sharding import PartitionSpec as P

HEADS = 12
SEGMENT = 2048
PATTERNS = 5


big_negative = -1e30


def shifted_2(shard, axis, by):
    length = lax.axis_size(axis)
    pairs = [(i, i + by) for i in range(length) if 0 <= i + by < length]
    return lax.ppermute(shard, axis, pairs)


def shifted_3(value, axis, steps):
    count = lax.axis_size(axis)
    pairs = [(source, (source + steps) % count) for source in range(count)]
    return lax.ppermute(value, axis, pairs)


def layer_norm(values, gain_vector):
    centre = jnp.mean(values, axis=-1, keepdims=True)
    shifted = values - centre
    variance = jnp.mean(shifted * shifted, axis=-1, keepdims=True)
    return shifted * lax.rsqrt(variance + 1e-05) * gain_vector


def hidden_norm(hidden_pre, gain_vector):
    return layer_norm(jax.nn.gelu(hidden_pre, approximate=True), gain_vector)


def selector(stride, head_count):
    return jnp.arange(stride)[:, None] == (jnp.arange(head_count) % stride)[None, :]


def compact(full_array, stride):
    length_in, head_count, inner_size = full_array.shape
    shaped = full_array.reshape(length_in // stride, stride, head_count, inner_size)
    picked = jnp.where(
        selector(stride, head_count)[None, :, :, None], shaped, jnp.zeros((), full_array.dtype)
    )
    return jnp.sum(picked, axis=1)


def expand(part_array, stride, fill_value):
    part_rows, head_count, inner_size = part_array.shape
    widened = jnp.where(
        selector(stride, head_count)[None, :, :, None],
        part_array[:, None],
        jnp.asarray(fill_value, part_array.dtype),
    )
    return widened.reshape(part_rows * stride, head_count, inner_size)


def positions(start_pos, part_rows, stride, head_count):
    row_ids = jnp.arange(part_rows, dtype=jnp.int32)[:, None] * stride
    head_ids = (jnp.arange(head_count, dtype=jnp.int32) % stride)[None, :]
    return start_pos + row_ids + head_ids


def doc_index(places, doc_bounds):
    return jnp.sum((places[..., None] >= doc_bounds).astype(jnp.int32), axis=-1)


def block_mask(doc_query, doc_key, local_block):
    allowed = doc_query.T[:, :, None] == doc_key.T[:, None, :]
    if local_block:
        rank_ids = jnp.arange(doc_query.shape[0])
        allowed = allowed & (rank_ids[:, None] >= rank_ids[None, :])[None]
    return allowed


def forward_block(query_part, key_part, value_part, allowed, score_scale):
    scores = (
        jnp.einsum("qhd,khd->hqk", query_part, key_part, preferred_element_type=jnp.float32)
        * score_scale
    )
    scores = jnp.where(allowed, scores, big_negative)
    row_peak = jnp.max(scores, axis=-1)
    weights = jnp.where(allowed, jnp.exp(scores - row_peak[..., None]), 0.0)
    row_total = jnp.sum(weights, axis=-1)
    mixed = jnp.einsum(
        "hqk,khd->qhd", weights.astype(jnp.bfloat16), value_part, preferred_element_type=jnp.float32
    )
    return (row_peak.T, row_total.T, mixed)


def merge(carried, new_block):
    best_peak = jnp.maximum(carried[0], new_block[0])
    keep_factor = jnp.exp(carried[0] - best_peak)
    take_factor = jnp.exp(new_block[0] - best_peak)
    new_total = carried[1] * keep_factor + new_block[1] * take_factor
    new_mixed = carried[2] * keep_factor[..., None] + new_block[2] * take_factor[..., None]
    return (best_peak, new_total, new_mixed)


def backward_block(
    query_part, grad_part, lse_part, delta_part, key_part, value_part, allowed, score_scale
):
    scores = (
        jnp.einsum("qhd,khd->hqk", query_part, key_part, preferred_element_type=jnp.float32)
        * score_scale
    )
    probs = jnp.where(allowed, jnp.exp(scores - lse_part.T[:, :, None]), 0.0)
    dots = jnp.einsum("qhd,khd->hqk", grad_part, value_part, preferred_element_type=jnp.float32)
    grad_scores = (probs * (dots - delta_part.T[:, :, None])).astype(jnp.bfloat16)
    query_grad = (
        jnp.einsum("hqk,khd->qhd", grad_scores, key_part, preferred_element_type=jnp.float32)
        * score_scale
    )
    key_grad = (
        jnp.einsum("hqk,qhd->khd", grad_scores, query_part, preferred_element_type=jnp.float32)
        * score_scale
    )
    value_grad = jnp.einsum(
        "hqk,qhd->khd", probs.astype(jnp.bfloat16), grad_part, preferred_element_type=jnp.float32
    )
    return (query_grad, key_grad, value_grad)


def keep_state(carried):
    return carried


def ring_local(
    tokens,
    lengths,
    w_query,
    w_key,
    w_value,
    w_out,
    w_up,
    w_down,
    gain_attend,
    gain_inner,
    gain_feed,
    gain_hidden,
    cotangent,
):
    block_rows, model_width = tokens.shape
    head_count = HEADS
    head_size = model_width // head_count
    score_scale = head_size ** (-0.5)
    seq_devices = lax.axis_size("seq")
    all_devices = seq_devices * lax.axis_size("row")
    my_index = lax.axis_index("seq")
    seq_total = block_rows * seq_devices
    doc_bounds = jnp.cumsum(lengths[0])[:-1]
    patterns = [
        (2**pattern, min(SEGMENT * 2**pattern, seq_total) // block_rows)
        for pattern in range(PATTERNS)
    ]
    near_ids = [0, 1]
    far_ids = list(range(2, PATTERNS))
    reach = patterns[1][1]
    far_rows = [block_rows // patterns[pattern][0] for pattern in far_ids]
    far_starts = [sum(far_rows[:slot_id]) for slot_id in range(len(far_ids))]
    far_total = sum(far_rows)

    def key_docs(pattern, source):
        stride = patterns[pattern][0]
        return doc_index(
            positions(source * block_rows, block_rows // stride, stride, head_count), doc_bounds
        )

    def is_live(pattern, cycle_step):
        group_size = patterns[pattern][1]
        return (cycle_step < group_size) & (my_index % group_size >= cycle_step)

    source_x = tokens.astype(jnp.float32)
    normed, attend_back = jax.vjp(layer_norm, source_x, gain_attend)
    normed_b = normed.astype(jnp.bfloat16)
    query_b = jnp.dot(normed_b, w_query, preferred_element_type=jnp.float32).astype(jnp.bfloat16)
    key_b = jnp.dot(normed_b, w_key, preferred_element_type=jnp.float32).astype(jnp.bfloat16)
    value_b = jnp.dot(normed_b, w_value, preferred_element_type=jnp.float32).astype(jnp.bfloat16)
    query_heads = query_b.reshape(block_rows, head_count, head_size)
    key_heads = key_b.reshape(block_rows, head_count, head_size)
    value_heads = value_b.reshape(block_rows, head_count, head_size)
    query_parts = [compact(query_heads, stride) for stride, group_size in patterns]
    key_parts = [compact(key_heads, stride) for stride, group_size in patterns]
    value_parts = [compact(value_heads, stride) for stride, group_size in patterns]
    own_docs = [key_docs(pattern, my_index) for pattern in range(PATTERNS)]
    states = [
        forward_block(
            query_parts[pattern],
            key_parts[pattern],
            value_parts[pattern],
            block_mask(own_docs[pattern], own_docs[pattern], True),
            score_scale,
        )
        for pattern in range(PATTERNS)
    ]

    def unpack_near(key_block):
        key_full = key_block[:, :model_width].reshape(block_rows, head_count, head_size)
        value_full = key_block[:, model_width:].reshape(block_rows, head_count, head_size)
        return (key_full, value_full)

    def near_fold_parts(pattern, key_part, value_part, source, carried):
        new_block = forward_block(
            query_parts[pattern],
            key_part,
            value_part,
            block_mask(own_docs[pattern], key_docs(pattern, source), False),
            score_scale,
        )
        return merge(carried, new_block)

    def near_fold(pattern, key_full, value_full, source, carried):
        stride = patterns[pattern][0]
        return near_fold_parts(
            pattern, compact(key_full, stride), compact(value_full, stride), source, carried
        )

    pair_block = jnp.concatenate([key_b, value_b], axis=1)
    kept_blocks = jnp.zeros((max(reach - 1, 1), block_rows, 2 * model_width), jnp.bfloat16)

    def near_forward(cycle_step, loop_state):
        key_block, near_now, kept_store = loop_state
        key_block = shifted_2(key_block, "seq", 1)
        key_full, value_full = unpack_near(key_block)
        new_states = []
        for pattern in near_ids:
            new_states.append(
                lax.cond(
                    is_live(pattern, cycle_step),
                    partial(near_fold, pattern, key_full, value_full, my_index - cycle_step),
                    keep_state,
                    near_now[pattern],
                )
            )
        return (key_block, tuple(new_states), kept_store)

    _, near_states, kept_blocks = lax.fori_loop(
        1, reach, near_forward, (pair_block, (states[0], states[1]), kept_blocks)
    )
    far_block = jnp.concatenate(
        [
            jnp.concatenate(
                [
                    key_parts[pattern].reshape(rows_here, model_width),
                    value_parts[pattern].reshape(rows_here, model_width),
                ],
                axis=1,
            )
            for pattern, rows_here in zip(far_ids, far_rows)
        ],
        axis=0,
    )

    def unpack_far(key_block, slot_id):
        rows_here = far_rows[slot_id]
        row_begin = far_starts[slot_id]
        piece_rows = key_block[row_begin : row_begin + rows_here]
        key_part = piece_rows[:, :model_width].reshape(rows_here, head_count, head_size)
        value_part = piece_rows[:, model_width:].reshape(rows_here, head_count, head_size)
        return (key_part, value_part)

    def far_fold(pattern, key_part, value_part, source, carried):
        new_block = forward_block(
            query_parts[pattern],
            key_part,
            value_part,
            block_mask(own_docs[pattern], key_docs(pattern, source), False),
            score_scale,
        )
        return merge(carried, new_block)

    def far_update(far_now, key_block, cycle_step):
        new_states = []
        for slot_id, pattern in enumerate(far_ids):
            key_part, value_part = unpack_far(key_block, slot_id)
            new_states.append(
                lax.cond(
                    is_live(pattern, cycle_step),
                    partial(far_fold, pattern, key_part, value_part, my_index - cycle_step),
                    keep_state,
                    far_now[slot_id],
                )
            )
        return tuple(new_states)

    far_states = tuple((states[pattern] for pattern in far_ids))

    def far_forward(cycle_step, loop_state):
        key_block, far_now = loop_state
        key_block = shifted_2(key_block, "seq", 1)
        return (key_block, far_update(far_now, key_block, cycle_step))

    _, far_states = lax.fori_loop(1, seq_devices, far_forward, (far_block, far_states))
    ordered = list(near_states) + list(far_states)
    peaks = [
        expand(ordered[pattern][0][..., None], patterns[pattern][0], big_negative)[..., 0]
        for pattern in range(PATTERNS)
    ]
    best_peak = reduce(jnp.maximum, peaks)
    weight_sum = jnp.zeros((block_rows, head_count), jnp.float32)
    mixed_sum = jnp.zeros((block_rows, head_count, head_size), jnp.float32)
    for pattern in range(PATTERNS):
        stride = patterns[pattern][0]
        factor = jnp.exp(peaks[pattern] - best_peak)
        weight_sum = (
            weight_sum + expand(ordered[pattern][1][..., None], stride, 0.0)[..., 0] * factor
        )
        mixed_sum = mixed_sum + expand(ordered[pattern][2], stride, 0.0) * factor[..., None]
    attended = mixed_sum / weight_sum[..., None]
    log_total = best_peak + jnp.log(weight_sum)
    inner_out, inner_back = jax.vjp(
        layer_norm, attended.reshape(block_rows, model_width), gain_inner
    )
    inner_b = inner_out.astype(jnp.bfloat16)
    middle = source_x + jnp.dot(inner_b, w_out, preferred_element_type=jnp.float32)
    normed_two, feed_back = jax.vjp(layer_norm, middle, gain_feed)
    normed_two_b = normed_two.astype(jnp.bfloat16)
    hidden_pre = jnp.dot(normed_two_b, w_up, preferred_element_type=jnp.float32)
    hidden, hidden_back = jax.vjp(hidden_norm, hidden_pre, gain_hidden)
    hidden_b = hidden.astype(jnp.bfloat16)
    result = (middle + jnp.dot(hidden_b, w_down, preferred_element_type=jnp.float32)).astype(
        jnp.bfloat16
    )
    grad_down = jnp.einsum("tf,tg->fg", hidden_b, cotangent, preferred_element_type=jnp.float32)
    grad_hidden = jnp.einsum("tg,fg->tf", cotangent, w_down, preferred_element_type=jnp.float32)
    grad_pre, grad_gain_hidden = hidden_back(grad_hidden)
    grad_pre_b = grad_pre.astype(jnp.bfloat16)
    grad_up = jnp.einsum("tf,tg->fg", normed_two_b, grad_pre_b, preferred_element_type=jnp.float32)
    grad_normed_two = jnp.einsum("tg,fg->tf", grad_pre_b, w_up, preferred_element_type=jnp.float32)
    grad_middle_part, grad_gain_feed = feed_back(grad_normed_two)
    grad_middle = cotangent.astype(jnp.float32) + grad_middle_part
    grad_middle_b = grad_middle.astype(jnp.bfloat16)
    grad_out = jnp.einsum("tf,tg->fg", inner_b, grad_middle_b, preferred_element_type=jnp.float32)
    grad_inner = jnp.einsum("tg,fg->tf", grad_middle_b, w_out, preferred_element_type=jnp.float32)
    grad_attended, grad_gain_inner = inner_back(grad_inner)
    grad_heads = grad_attended.astype(jnp.bfloat16).reshape(block_rows, head_count, head_size)
    delta_rows = jnp.sum(grad_heads.astype(jnp.float32) * attended, axis=-1)
    grad_parts = [compact(grad_heads, stride) for stride, group_size in patterns]
    lse_parts = [compact(log_total[..., None], stride)[..., 0] for stride, group_size in patterns]
    delta_parts = [
        compact(delta_rows[..., None], stride)[..., 0] for stride, group_size in patterns
    ]
    query_grads = []
    home_keys = []
    home_values = []
    for pattern in range(PATTERNS):
        part_query, part_key, part_value = backward_block(
            query_parts[pattern],
            grad_parts[pattern],
            lse_parts[pattern],
            delta_parts[pattern],
            key_parts[pattern],
            value_parts[pattern],
            block_mask(own_docs[pattern], own_docs[pattern], True),
            score_scale,
        )
        query_grads.append(part_query)
        home_keys.append(part_key)
        home_values.append(part_value)

    def fetch_full(key_block):
        return shifted_2(key_block, "seq", 1)

    def near_grad(pattern, key_full, value_full, source, operands):
        query_grad, travel = operands
        stride = patterns[pattern][0]
        part_query, part_key, part_value = backward_block(
            query_parts[pattern],
            grad_parts[pattern],
            lse_parts[pattern],
            delta_parts[pattern],
            compact(key_full, stride),
            compact(value_full, stride),
            block_mask(own_docs[pattern], key_docs(pattern, source), False),
            score_scale,
        )
        spread_rows = jnp.concatenate(
            [
                expand(part_key, stride, 0.0).reshape(block_rows, model_width),
                expand(part_value, stride, 0.0).reshape(block_rows, model_width),
            ],
            axis=1,
        )
        return (query_grad + part_query, travel + spread_rows)

    def near_backward(cycle_step, loop_state):
        key_block, grads_now, travel = loop_state
        key_block = fetch_full(key_block)
        travel = shifted_3(travel.astype(jnp.bfloat16), "seq", 1).astype(travel.dtype)
        key_full, value_full = unpack_near(key_block)
        new_grads = list(grads_now)
        for pattern in near_ids:
            new_grads[pattern], travel = lax.cond(
                is_live(pattern, cycle_step),
                partial(near_grad, pattern, key_full, value_full, my_index - cycle_step),
                keep_state,
                (new_grads[pattern], travel),
            )
        return (key_block, tuple(new_grads), travel)

    own_key_near = expand(home_keys[0], 1, 0.0) + expand(home_keys[1], 2, 0.0)
    own_value_near = expand(home_values[0], 1, 0.0) + expand(home_values[1], 2, 0.0)
    near_start = jnp.concatenate(
        [
            own_key_near.reshape(block_rows, model_width),
            own_value_near.reshape(block_rows, model_width),
        ],
        axis=1,
    )
    _, near_query, travel_near = lax.fori_loop(
        1, reach, near_backward, (pair_block, (query_grads[0], query_grads[1]), near_start)
    )
    near_home = shifted_3(travel_near.astype(jnp.bfloat16), "seq", 1 - reach).astype(
        travel_near.dtype
    )
    near_key_add = near_home[:, :model_width].reshape(block_rows, head_count, head_size)
    near_value_add = near_home[:, model_width:].reshape(block_rows, head_count, head_size)

    def far_grad(slot_id, key_part, value_part, source, operands):
        query_grad, travel = operands
        pattern = far_ids[slot_id]
        rows_here = far_rows[slot_id]
        row_begin = far_starts[slot_id]
        part_query, part_key, part_value = backward_block(
            query_parts[pattern],
            grad_parts[pattern],
            lse_parts[pattern],
            delta_parts[pattern],
            key_part,
            value_part,
            block_mask(own_docs[pattern], key_docs(pattern, source), False),
            score_scale,
        )
        spread_rows = jnp.concatenate(
            [part_key.reshape(rows_here, model_width), part_value.reshape(rows_here, model_width)],
            axis=1,
        )
        return (
            query_grad + part_query,
            travel.at[row_begin : row_begin + rows_here].add(spread_rows),
        )

    def far_back_update(grads_now, travel, key_block, cycle_step):
        new_grads = list(grads_now)
        for slot_id, pattern in enumerate(far_ids):
            key_part, value_part = unpack_far(key_block, slot_id)
            new_grads[slot_id], travel = lax.cond(
                is_live(pattern, cycle_step),
                partial(far_grad, slot_id, key_part, value_part, my_index - cycle_step),
                keep_state,
                (new_grads[slot_id], travel),
            )
        return (tuple(new_grads), travel)

    far_query = tuple((query_grads[pattern] for pattern in far_ids))
    far_empty = jnp.zeros((far_total, 2 * model_width), jnp.float32)

    def far_send(travel):
        return shifted_3(travel.astype(jnp.bfloat16), "seq", 1).astype(travel.dtype)

    def far_backward(cycle_step, loop_state):
        key_block, grads_now, travel = loop_state
        key_block = shifted_2(key_block, "seq", 1)
        travel = far_send(travel)
        grads_now, travel = far_back_update(grads_now, travel, key_block, cycle_step)
        return (key_block, grads_now, travel)

    _, far_query, travel_far = lax.fori_loop(
        1, seq_devices, far_backward, (far_block, far_query, far_empty)
    )
    far_home = far_send(travel_far)
    all_query = list(near_query) + list(far_query)
    query_grad = jnp.zeros((block_rows, head_count, head_size), jnp.float32)
    key_grad = near_key_add
    value_grad = near_value_add
    for pattern in range(PATTERNS):
        stride = patterns[pattern][0]
        query_grad = query_grad + expand(all_query[pattern], stride, 0.0)
    for pattern in far_ids:
        stride = patterns[pattern][0]
        key_grad = key_grad + expand(home_keys[pattern], stride, 0.0)
        value_grad = value_grad + expand(home_values[pattern], stride, 0.0)
    for slot_id, pattern in enumerate(far_ids):
        stride = patterns[pattern][0]
        rows_here = far_rows[slot_id]
        row_begin = far_starts[slot_id]
        piece_rows = far_home[row_begin : row_begin + rows_here]
        key_grad = key_grad + expand(
            piece_rows[:, :model_width].reshape(rows_here, head_count, head_size), stride, 0.0
        )
        value_grad = value_grad + expand(
            piece_rows[:, model_width:].reshape(rows_here, head_count, head_size), stride, 0.0
        )
    grad_query_b = query_grad.reshape(block_rows, model_width).astype(jnp.bfloat16)
    grad_key_b = key_grad.reshape(block_rows, model_width).astype(jnp.bfloat16)
    grad_value_b = value_grad.reshape(block_rows, model_width).astype(jnp.bfloat16)
    grad_w_query = jnp.einsum(
        "tf,tg->fg", normed_b, grad_query_b, preferred_element_type=jnp.float32
    )
    grad_w_key = jnp.einsum("tf,tg->fg", normed_b, grad_key_b, preferred_element_type=jnp.float32)
    grad_w_value = jnp.einsum(
        "tf,tg->fg", normed_b, grad_value_b, preferred_element_type=jnp.float32
    )
    grad_normed = jnp.einsum("tg,fg->tf", grad_query_b, w_query, preferred_element_type=jnp.float32)
    grad_normed = grad_normed + jnp.einsum(
        "tg,fg->tf", grad_key_b, w_key, preferred_element_type=jnp.float32
    )
    grad_normed = grad_normed + jnp.einsum(
        "tg,fg->tf", grad_value_b, w_value, preferred_element_type=jnp.float32
    )
    grad_x_part, grad_gain_attend = attend_back(grad_normed)
    grad_input = (grad_middle + grad_x_part).astype(jnp.bfloat16)
    gains_all = jnp.concatenate(
        [grad_gain_attend, grad_gain_inner, grad_gain_feed, grad_gain_hidden]
    )
    summed = (
        lax.psum_scatter(grad_w_query.reshape(-1), ("row", "seq"), scatter_dimension=0, tiled=True),
        lax.psum_scatter(grad_w_key.reshape(-1), ("row", "seq"), scatter_dimension=0, tiled=True),
        lax.psum_scatter(grad_w_value.reshape(-1), ("row", "seq"), scatter_dimension=0, tiled=True),
        lax.psum_scatter(grad_out.reshape(-1), ("row", "seq"), scatter_dimension=0, tiled=True),
        lax.psum_scatter(grad_up.reshape(-1), ("row", "seq"), scatter_dimension=0, tiled=True),
        lax.psum_scatter(grad_down.reshape(-1), ("row", "seq"), scatter_dimension=0, tiled=True),
        lax.psum_scatter(gains_all, ("row", "seq"), scatter_dimension=0, tiled=True),
    )
    factor = 1.0 / math.sqrt(block_rows * all_devices)
    return (result, grad_input) + tuple((summed_part * factor for summed_part in summed))


NO_COST = pl.CostEstimate(flops=1000, bytes_accessed=1000, transcendentals=0)
SOME_COST = pl.CostEstimate(flops=4 * 10**9, bytes_accessed=1000, transcendentals=0)
HIGH_COST = pl.CostEstimate(flops=5 * 10**10, bytes_accessed=1000, transcendentals=0)


def split_log(level):
    remaining = math.log((level + 1) / level)
    pieces = []
    for _ in range(3):
        piece = float(jnp.bfloat16.dtype.type(remaining))
        pieces.append(piece)
        remaining -= piece
    return pieces


def extra_values(places, features, head, size, per_piece):
    masks, values = jnp.zeros_like(features), jnp.zeros(features.shape, jnp.float32)
    for level in range(1, PATTERNS):
        for piece, value in enumerate(split_log(level)):
            here = features == size + 3 * (level - 1) + piece
            masks = jnp.where(here, 2**level - 1, masks)
            values = jnp.where(here, value if per_piece else 1.0, values)
    return jnp.where(((places - head) & masks) == 0, values, 0.0)


def nt_dot(left, right):
    return lax.dot_general(
        left, right, (((1,), (1,)), ((), ())), preferred_element_type=jnp.float32
    )


def nn_dot(left, right):
    return jnp.dot(left, right, preferred_element_type=jnp.float32)


def call_whole(kernel, out_shape, name, scalars, *arrays, scratch=(), limit=12, ins=True, outs=True):
    direct = pl.BlockSpec(memory_space=pltpu.VMEM)
    return pl.pallas_call(
        kernel,
        grid_spec=pltpu.PrefetchScalarGridSpec(
            num_scalar_prefetch=1,
            grid=(1,),
            in_specs=[direct if ins else whole(array.shape) for array in arrays],
            out_specs=[direct if outs else whole(out.shape) for out in out_shape],
            scratch_shapes=list(scratch),
        ),
        out_shape=list(out_shape),
        compiler_params=pltpu.CompilerParams(vmem_limit_bytes=limit << 20),
        cost_estimate=NO_COST,
        name=name,
    )(scalars, *arrays)


def after_kernel(scalars, *refs):
    for index in range(scalars.shape[0]):
        refs[-1][index] = scalars[index]


def after(scalars, arrays, cost):
    return pl.pallas_call(
        after_kernel,
        in_specs=[pl.BlockSpec(memory_space=pltpu.SMEM)]
        + [pl.BlockSpec(memory_space=pl.ANY)] * len(arrays),
        out_specs=pl.BlockSpec(memory_space=pltpu.SMEM),
        out_shape=jax.ShapeDtypeStruct(scalars.shape, scalars.dtype),
        compiler_params=pltpu.CompilerParams(vmem_limit_bytes=1 << 20),
        cost_estimate=cost,
        name="after",
    )(scalars, *arrays)


def norm_kernel(unused, rows_ref, gain_ref, out_ref):
    hat = norm_parts(rows_ref[...].astype(jnp.float32))[0]
    out_ref[...] = (hat * gain_ref[...].reshape(1, -1)).astype(jnp.bfloat16)


def column_choice(chip, heads, size, lanes, width, transposed):
    shape, axis = ((lanes, width), 0) if transposed else ((width, lanes), 1)
    lane = lax.broadcasted_iota(jnp.int32, shape, axis)
    feature = lax.broadcasted_iota(jnp.int32, shape, 1 - axis)
    parts = []
    for head in range(heads):
        here = (feature == lane + (chip * heads + head) * size) & (lane < size)
        parts.append(jnp.where(here, 1.0, 0.0).astype(jnp.bfloat16))
    return jnp.concatenate(parts, axis=axis)


def choose_kernel(heads, size, scalars, wq_ref, wk_ref, wv_ref, *refs):
    query_rows, key_columns, value_rows, key_rows, value_columns, narrow_rows = refs
    width, chip = wq_ref.shape[0], scalars[0]
    tall = column_choice(chip, heads, size, 2 * size, width, True)
    flat = column_choice(chip, heads, size, 2 * size, width, False)
    narrow = column_choice(chip, heads, size, size, width, True)
    query_rows[...] = sent(nt_dot(tall, wq_ref[...]))
    key_columns[...] = sent(nn_dot(wk_ref[...], flat))
    value_columns[...] = sent(nn_dot(wv_ref[...], flat))
    for target, weight in ((value_rows, wv_ref), (key_rows, wk_ref), (narrow_rows, wq_ref)):
        target[...] = sent(nt_dot(narrow, weight[...]))


def choose(scalars, w_query, w_key, w_value, heads, size):
    width = w_query.shape[0]
    shapes = [
        (2 * heads * size, width),
        (width, 2 * heads * size),
        (heads * size, width),
        (heads * size, width),
        (width, 2 * heads * size),
        (heads * size, width),
    ]
    return call_whole(
        partial(choose_kernel, heads, size),
        [jax.ShapeDtypeStruct(shape, jnp.bfloat16) for shape in shapes],
        "choose",
        scalars,
        w_query,
        w_key,
        w_value,
        limit=24,
        ins=False,
    )


def project_kernel(blocks, own, heads, scale, meta, *refs):
    normed = refs[:blocks]
    wq_ref, wk_ref, wv_ref = refs[blocks : blocks + 3]
    q_ref, k_ref, vt_ref = refs[-3:]
    length = normed[0].shape[0]
    lanes = wk_ref.shape[1] // heads
    size = lanes // 2
    first_head = meta[blocks]
    for index in range(blocks):
        rows = normed[index][...]
        start = meta[index]
        span = slice(index * length, (index + 1) * length)
        keys = nn_dot(rows, wk_ref[...])
        vt_ref[:, span] = nt_dot(wv_ref[...], rows).astype(jnp.bfloat16)
        places = start + lax.broadcasted_iota(jnp.int32, (length, 1), 0)
        features = lax.broadcasted_iota(jnp.int32, (1, lanes), 1)
        for head in range(heads):
            wide_rows = slice(head * lanes, (head + 1) * lanes)
            extra = extra_values(places, features, first_head + head, size, False)
            k_ref[span, wide_rows] = (keys[:, wide_rows] + extra).astype(jnp.bfloat16)
        if index < own:
            queries = nt_dot(wq_ref[...], rows).astype(jnp.bfloat16).astype(jnp.float32) * scale
            places = start + lax.broadcasted_iota(jnp.int32, (1, length), 1)
            features = lax.broadcasted_iota(jnp.int32, (lanes, 1), 0)
            for head in range(heads):
                wide_rows = slice(head * lanes, (head + 1) * lanes)
                extra = extra_values(places, features, first_head + head, size, True)
                q_ref[wide_rows, span] = (queries[wide_rows] + extra).astype(jnp.bfloat16)


def project(meta, normed, wq, wk, wv, own, heads, scale, chips, filled=None):
    blocks, length = len(normed), normed[0].shape[0]
    wide_columns, share = wk.shape[1], wv.shape[0]
    last = 0 if filled is None else 2 * chips // blocks - 1
    last_own = 0 if filled is None else chips // own - 1
    aliases = {} if filled is None else {blocks + 4 + index: index for index in range(3)}
    return pl.pallas_call(
        partial(project_kernel, blocks, own, heads, scale),
        grid_spec=pltpu.PrefetchScalarGridSpec(
            num_scalar_prefetch=1,
            grid=(1,),
            in_specs=[whole(array.shape) for array in (*normed, wq, wk, wv)]
            + [pl.BlockSpec(memory_space=pl.ANY)] * (0 if filled is None else 3),
            out_specs=[
                pl.BlockSpec((wide_columns, own * length), lambda i, meta: (0, last_own)),
                pl.BlockSpec((blocks * length, wide_columns), lambda i, meta: (last, 0)),
                pl.BlockSpec((share, blocks * length), lambda i, meta: (0, last)),
            ],
        ),
        out_shape=[
            jax.ShapeDtypeStruct((wide_columns, chips * length), jnp.bfloat16),
            jax.ShapeDtypeStruct((2 * chips * length, wide_columns), jnp.bfloat16),
            jax.ShapeDtypeStruct((share, 2 * chips * length), jnp.bfloat16),
        ],
        input_output_aliases=aliases,
        compiler_params=pltpu.CompilerParams(vmem_limit_bytes=16 << 20),
        cost_estimate=NO_COST,
        name="project",
    )(meta, *normed, wq, wk, wv, *(filled or ()))


def project_back_kernel(blocks, unused, *refs):
    normed = refs[:blocks]
    wk_ref, wv_ref, kt_ref, v_ref = refs[blocks:]
    length = normed[0].shape[0]
    for index in range(blocks):
        rows = normed[index][...]
        span = slice(index * length, (index + 1) * length)
        kt_ref[:, span] = nt_dot(wk_ref[...], rows).astype(jnp.bfloat16)
        v_ref[span, :] = nn_dot(rows, wv_ref[...]).astype(jnp.bfloat16)


def project_back(scalars, normed, wk, wv):
    blocks, length = len(normed), normed[0].shape[0]
    return call_whole(
        partial(project_back_kernel, blocks),
        [
            jax.ShapeDtypeStruct((wk.shape[0], blocks * length), jnp.bfloat16),
            jax.ShapeDtypeStruct((blocks * length, wv.shape[1]), jnp.bfloat16),
        ],
        "project_back",
        scalars,
        *normed,
        wk,
        wv,
    )


def pair_mask(query_start, key_start, doc_line, block):
    query_place = query_start + lax.broadcasted_iota(jnp.int32, (1, block), 1)
    key_place = key_start + lax.broadcasted_iota(jnp.int32, (block, 1), 0)
    return (key_place <= query_place) & (key_place >= doc_line)


def attend_kernel(heads, block, first, steps, key_blocks, meta, doc_ref, q_ref, k_ref, vt_ref, *refs):
    o_ref, m_ref, l_ref = refs[-3:]
    count = (len(refs) - 3) // 3
    mixed_refs, lse_refs, ob_refs = (refs[count * part : count * (part + 1)] for part in range(3))
    step = first + pl.program_id(0)
    query_start = meta[step]
    doc_first, doc_last = meta[steps + key_blocks + step], meta[2 * steps + key_blocks + step]
    doc_line = doc_ref[...]
    size = o_ref.shape[0] // heads
    lanes = q_ref.shape[0] // heads
    m_ref[...] = jnp.full_like(m_ref, big_negative)
    l_ref[...] = jnp.zeros_like(l_ref)
    o_ref[...] = jnp.zeros_like(o_ref)

    def fold(slot, allowed):
        span = pl.ds(pl.multiple_of(slot * block, block), block)
        scores = [
            nn_dot(
                k_ref[span, head * lanes : (head + 1) * lanes],
                q_ref[head * lanes : (head + 1) * lanes, :],
            )
            for head in range(heads)
        ]
        if allowed is not None:
            scores = [jnp.where(allowed, part, big_negative) for part in scores]
        for head in range(heads):
            rows = slice(head * size, (head + 1) * size)
            old_peak = m_ref[head]
            new_peak = jnp.maximum(old_peak, jnp.max(scores[head], axis=0, keepdims=True))
            weights = jnp.exp(scores[head] - new_peak)
            fade = jnp.exp(old_peak - new_peak)
            m_ref[head] = new_peak
            l_ref[head] = l_ref[head] * fade + jnp.sum(weights, axis=0, keepdims=True)
            o_ref[rows, :] = o_ref[rows, :] * fade + nn_dot(
                vt_ref[rows, span], weights.astype(jnp.bfloat16)
            )

    def body(slot, carry):
        key_start = meta[steps + slot]
        live = (key_start <= query_start) & (key_start + block > doc_first)
        full = (key_start < query_start) & (key_start >= doc_last)

        @pl.when(full)
        def _():
            fold(slot, None)

        @pl.when(live & jnp.logical_not(full))
        def _():
            fold(slot, pair_mask(query_start, key_start, doc_line, block))

        return carry

    lax.fori_loop(0, key_blocks, body, 0)
    for index in range(count):

        @pl.when(step == first + index)
        def _(index=index):
            for head in range(heads):
                rows = slice(head * size, (head + 1) * size)
                total = l_ref[head]
                mixed = o_ref[rows, :] / total
                mixed_refs[index][rows, :] = mixed
                ob_refs[index][rows, :] = mixed.astype(jnp.bfloat16)
                lse_refs[index][head] = m_ref[head] + jnp.log(total)


def attend_back_kernel(heads, block, steps, key_blocks, scale, meta, doc_ref, q_ref, k_ref, kt_ref, v_ref, *refs):
    o_refs, lse_refs, g_refs = (refs[steps * part : steps * (part + 1)] for part in range(3))
    dq_ref, mine_ref, other_ref, acc_ref, pair_ref, delta_ref, g_ref, lse_ref = refs[3 * steps :]
    step = pl.program_id(0)
    query_start = meta[step]
    doc_first, doc_last = meta[steps + key_blocks + step], meta[2 * steps + key_blocks + step]
    doc_line = doc_ref[...]
    size = g_ref.shape[0] // heads
    lanes = q_ref.shape[0] // heads
    share = g_ref.shape[0]

    @pl.when(step == 0)
    def _():
        pair_ref[...] = jnp.zeros_like(pair_ref)

    acc_ref[...] = jnp.zeros_like(acc_ref)
    for index in range(steps):

        @pl.when(step == index)
        def _(index=index):
            g_ref[...] = g_refs[index][...]
            lse_ref[...] = lse_refs[index][...]
            for head in range(heads):
                rows = slice(head * size, (head + 1) * size)
                delta_ref[head] = jnp.sum(
                    g_refs[index][rows, :].astype(jnp.float32) * o_refs[index][rows, :],
                    axis=0,
                    keepdims=True,
                )

    def fold(slot, allowed):
        span = pl.ds(pl.multiple_of(slot * block, block), block)
        probs, grad_scores = [], []
        for head in range(heads):
            wide_rows = slice(head * lanes, (head + 1) * lanes)
            rows = slice(head * size, (head + 1) * size)
            probs.append(nn_dot(k_ref[span, wide_rows], q_ref[wide_rows, :]))
            grad_scores.append(
                nn_dot(v_ref[span, head * lanes : head * lanes + size], g_ref[rows, :])
            )
        for head in range(heads):
            part = jnp.exp(probs[head] - lse_ref[head])
            if allowed is not None:
                part = jnp.where(allowed, part, 0.0)
            grad_scores[head] = (part * (grad_scores[head] - delta_ref[head])).astype(jnp.bfloat16)
            probs[head] = part.astype(jnp.bfloat16)
        for head in range(heads):
            rows = slice(head * size, (head + 1) * size)
            value_rows = slice(share + head * size, share + (head + 1) * size)
            query_rows = slice(head * lanes, head * lanes + size)
            pair_ref[value_rows, span] += nt_dot(g_ref[rows, :], probs[head])
            pair_ref[rows, span] += nt_dot(q_ref[query_rows, :], grad_scores[head])
            acc_ref[rows, :] += nn_dot(kt_ref[rows, span], grad_scores[head])

    def body(slot, carry):
        key_start = meta[steps + slot]
        live = (key_start <= query_start) & (key_start + block > doc_first)
        full = (key_start < query_start) & (key_start >= doc_last)

        @pl.when(full)
        def _():
            fold(slot, None)

        @pl.when(live & jnp.logical_not(full))
        def _():
            fold(slot, pair_mask(query_start, key_start, doc_line, block))

        return carry

    lax.fori_loop(0, key_blocks, body, 0)
    dq_ref[...] = (acc_ref[...] * scale).astype(dq_ref.dtype)

    @pl.when(step == steps - 1)
    def _():
        for index in range(steps):
            late = index == steps - 1
            mine = 2 * index if late else index
            other = 2 * index + 1 if late else steps - 1 + index
            span = slice(index * block, (index + 1) * block)
            mine_ref[:, span] = pair_ref[:, mine * block : (mine + 1) * block]
            other_ref[:, span] = pair_ref[:, other * block : (other + 1) * block].astype(
                jnp.bfloat16
            )


def whole(shape):
    return pl.BlockSpec(shape, lambda *index: (0,) * len(shape))


def attend(meta, doc_line, q_ext, k_ext, v_t, heads, block, first, last):
    wide_rows, queries = q_ext.shape
    share, keys = v_t.shape
    steps, key_blocks, count = queries // block, keys // block, last - first
    direct = pl.BlockSpec(memory_space=pltpu.VMEM)
    outs = pl.pallas_call(
        partial(attend_kernel, heads, block, first, steps, key_blocks),
        grid_spec=pltpu.PrefetchScalarGridSpec(
            num_scalar_prefetch=1,
            grid=(count,),
            in_specs=[
                pl.BlockSpec((1, block), lambda i, meta: (0, first + i)),
                pl.BlockSpec((wide_rows, block), lambda i, meta: (0, first + i)),
                direct,
                direct,
            ],
            out_specs=[direct] * (3 * count),
            scratch_shapes=[
                pltpu.VMEM((share, block), jnp.float32),
                pltpu.VMEM((heads, 1, block), jnp.float32),
                pltpu.VMEM((heads, 1, block), jnp.float32),
            ],
        ),
        out_shape=[jax.ShapeDtypeStruct((share, block), jnp.float32)] * count
        + [jax.ShapeDtypeStruct((heads, 1, block), jnp.float32)] * count
        + [jax.ShapeDtypeStruct((share, block), jnp.bfloat16)] * count,
        compiler_params=pltpu.CompilerParams(vmem_limit_bytes=12 << 20),
        cost_estimate=NO_COST,
        name="attend",
    )(meta, doc_line, q_ext, k_ext, v_t)
    return outs[:count], outs[count : 2 * count], outs[2 * count :]


def attend_back(meta, doc_line, q_ext, grads, mixed, lse, k_ext, k_t, v_ext, heads, block, scale):
    wide_rows, queries = q_ext.shape
    share, keys = k_t.shape
    steps, key_blocks = queries // block, keys // block
    direct = pl.BlockSpec(memory_space=pltpu.VMEM)
    return pl.pallas_call(
        partial(attend_back_kernel, heads, block, steps, key_blocks, scale),
        grid_spec=pltpu.PrefetchScalarGridSpec(
            num_scalar_prefetch=1,
            grid=(steps,),
            in_specs=[
                pl.BlockSpec((1, block), lambda i, meta: (0, i)),
                pl.BlockSpec((wide_rows, block), lambda i, meta: (0, i)),
            ]
            + [direct] * (3 + 3 * steps),
            out_specs=[pl.BlockSpec((share, block), lambda i, meta: (0, i)), direct, direct],
            scratch_shapes=[
                pltpu.VMEM((share, block), jnp.float32),
                pltpu.VMEM((2 * share, keys), jnp.float32),
                pltpu.VMEM((heads, 1, block), jnp.float32),
                pltpu.VMEM((share, block), jnp.bfloat16),
                pltpu.VMEM((heads, 1, block), jnp.float32),
            ],
        ),
        out_shape=[
            jax.ShapeDtypeStruct((share, queries), jnp.bfloat16),
            jax.ShapeDtypeStruct((2 * share, keys // 2), jnp.float32),
            jax.ShapeDtypeStruct((2 * share, keys // 2), jnp.bfloat16),
        ],
        compiler_params=pltpu.CompilerParams(vmem_limit_bytes=20 << 20),
        cost_estimate=HIGH_COST,
        name="attend_back",
    )(meta, doc_line, q_ext, k_ext, k_t, v_ext, *mixed, *lse, *grads)


def join_kernel(chips, unused, dq_ref, mine_ref, other_ref, *out_refs):
    share = dq_ref.shape[0]
    block = dq_ref.shape[1] // chips
    for step in range(chips):
        span = slice(step * block, (step + 1) * block)
        pair = (mine_ref[:, span] + other_ref[:, span].astype(jnp.float32)).astype(jnp.bfloat16)
        out_refs[step][:share, :] = dq_ref[:, span]
        out_refs[step][share:, :] = pair


def join_parts(scalars, dq, mine, other, chips):
    rows, block = dq.shape[0] + mine.shape[0], dq.shape[1] // chips
    return call_whole(
        partial(join_kernel, chips),
        [jax.ShapeDtypeStruct((rows, block), jnp.bfloat16)] * chips,
        "join",
        scalars,
        dq,
        mine,
        other,
    )


def head_grads_kernel(chips, per, scalars, *refs):
    normed, grads = refs[:chips], refs[chips : 2 * chips]
    wq_ref, wk_ref, wv_ref, gain_ref, inner_ref, feed_ref, hidden_ref = refs[2 * chips : 2 * chips + 7]
    perm_ref, keep_ref, send_ref = refs[2 * chips + 7 :]
    first_core = scalars[1] == 0
    share, model_width = wq_ref.shape
    own = nn_dot(grads[0][...], normed[0][...])
    for step in range(1, chips):
        own = own + nn_dot(grads[step][...], normed[step][...])
    attend = jnp.zeros((1, model_width), jnp.float32)
    for index, weight in enumerate((wq_ref, wk_ref, wv_ref)):
        part = own[index * share : (index + 1) * share] * weight[...].astype(jnp.float32)
        attend = attend + jnp.sum(part, axis=0, keepdims=True)
    gains = [attend / gain_ref[...], inner_ref[...], feed_ref[...], hidden_ref[...]]
    own = nt_dot(perm_ref[...], own.astype(jnp.bfloat16))
    chunks, _, width = keep_ref.shape
    columns = own.shape[1]
    part = sum(row.shape[1] for row in gains) // (2 * chunks)
    lines = -(-part // 128)
    gains = jnp.concatenate(gains + [jnp.zeros((1, 128), jnp.float32)], axis=1)

    def device_gains(device):
        starts = [device * part + 128 * line for line in range(lines)]
        rows = [gains[:, start : start + 128] for start in starts]
        return jnp.concatenate(rows, axis=0).astype(jnp.bfloat16)

    for target in (keep_ref, send_ref):
        target[:, :, columns:] = jnp.zeros((chunks, per, width - columns), jnp.bfloat16)
    for chunk in range(chunks):
        even, odd = device_gains(2 * chunk), device_gains(2 * chunk + 1)
        keep_ref[chunk, :lines, width - 128 :] = jnp.where(first_core, even, odd)
        send_ref[chunk, :lines, width - 128 :] = jnp.where(first_core, odd, even)
        for which, target in enumerate((keep_ref, send_ref)):
            first = (which * chunks + chunk) * per
            target[chunk, :, :columns] = own[first : first + per].astype(jnp.bfloat16)


def head_grads(scalars, normed, grads, weights, gain, late_gains, perm, per):
    width = perm.shape[0]
    out = jax.ShapeDtypeStruct((width // (2 * per), per, width), jnp.bfloat16)
    return call_whole(
        partial(head_grads_kernel, len(grads), per),
        [out, out],
        "head_grads",
        scalars,
        *normed,
        *grads,
        *weights,
        gain,
        *late_gains,
        perm,
        limit=24,
    )


def norm_parts(values):
    shifted = values - jnp.mean(values, axis=-1, keepdims=True)
    rate = lax.rsqrt(jnp.mean(shifted * shifted, axis=-1, keepdims=True) + 1e-05)
    return shifted * rate, rate


def norm_back(grad, hat, rate, gain):
    scaled = grad * gain
    mean_scaled = jnp.mean(scaled, axis=-1, keepdims=True)
    mean_product = jnp.mean(scaled * hat, axis=-1, keepdims=True)
    return (
        rate * (scaled - mean_scaled - hat * mean_product),
        jnp.sum(grad * hat, axis=0, keepdims=True),
    )


def middle_kernel(chips, tiles, position, *refs):
    mixed = refs[:chips]
    tokens_ref, cot_ref, wout_ref, wup_ref, wdown_ref, ginner_ref, gfeed_ref, ghidden_ref = refs[
        chips : chips + 8
    ]
    result_ref, gmid_ref, gmid_b_ref = refs[chips + 8 : chips + 11]
    go_refs = refs[chips + 11 : 2 * chips + 11]
    (
        z_ref,
        h2_ref,
        bent_out,
        pre_out,
        dinner_ref,
        dfeed_ref,
        dhidden_ref,
        swap_ref,
        work_ref,
        column_ref,
        zhat_ref,
        hat_ref,
        act_ref,
        slope_ref,
        dact_ref,
        acc_ref,
        stat_ref,
    ) = refs[2 * chips + 11 :]
    step = pl.program_id(0)
    chip = position[0]
    block, model_width = tokens_ref.shape
    share = model_width // chips
    tile = wdown_ref.shape[0]
    hidden = tile * tiles
    root = math.sqrt(2.0 / math.pi)
    phase, index = step // tiles, step % tiles
    lanes = stat_ref.shape[2]
    groups = tile // lanes

    def by_rows(body):
        body(slice(None))

    def spread(stat):
        return jnp.concatenate([stat] * groups, axis=1)

    def gathered_lanes(values):
        total = values[:, :lanes]
        for group in range(1, groups):
            total = total + values[:, group * lanes : (group + 1) * lanes]
        return total

    def lane_sum(values):
        return jnp.broadcast_to(jnp.sum(values, axis=-1, keepdims=True), values.shape)

    def column_sums(values):
        total = values[:8]
        for first in range(8, values.shape[0], 8):
            total = total + values[first : first + 8]
        return total

    def norm_rows(values):
        shifted = values - spread(lane_sum(gathered_lanes(values)) / tile)
        rate = lax.rsqrt(lane_sum(gathered_lanes(shifted * shifted)) / tile + 1e-05)
        return shifted * spread(rate), rate

    def norm_rows_back(grad, hat, rate, gain):
        scaled = grad * gain
        mean_scaled = lane_sum(gathered_lanes(scaled)) / tile
        mean_product = lane_sum(gathered_lanes(scaled * hat)) / tile
        return spread(rate) * (scaled - spread(mean_scaled) - hat * spread(mean_product))

    @pl.when(step == 0)
    def _():
        for near in range(chips):
            start = pl.multiple_of(share * lax.rem(chip + near, chips), share)
            swap_ref[pl.ds(start, share), :] = mixed[near][...].astype(jnp.float32)
        work_ref[...] = swap_ref[...].T

        def first_norm(rows):
            zhat, zrate = norm_rows(work_ref[rows, :])
            zhat_ref[rows, :] = zhat
            stat_ref[0, rows, :] = zrate
            z_ref[rows, :] = (zhat * ginner_ref[...]).astype(jnp.bfloat16)

        by_rows(first_norm)
        work_ref[...] = nn_dot(z_ref[...], wout_ref[...])

        def second_norm(rows):
            mid = tokens_ref[rows, :].astype(jnp.float32) + work_ref[rows, :]
            acc_ref[rows, :] = mid
            hat, rate = norm_rows(mid)
            hat_ref[rows, :] = hat
            stat_ref[1, rows, :] = rate
            h2_ref[rows, :] = (hat * gfeed_ref[...]).astype(jnp.bfloat16)

        by_rows(second_norm)
        for stat in range(3, 7):
            stat_ref[stat] = jnp.zeros_like(stat_ref[stat])

    @pl.when(phase == 0)
    def _():
        work_ref[...] = nn_dot(h2_ref[...], wup_ref[...])

        def bend_rows(rows):
            u = work_ref[rows, :]
            squared = u * u
            bend = jnp.tanh(root * (u + 0.044715 * u * squared))
            act_ref[index, rows, :] = 0.5 * u * (1.0 + bend)
            slope_ref[index, rows, :] = 0.5 * (1.0 + bend) + 0.5 * u * (1.0 - bend * bend) * root * (
                1.0 + 3.0 * 0.044715 * squared
            )

        by_rows(bend_rows)

        @pl.when(index == 0)
        def _():
            def pivot(rows):
                stat_ref[2, rows, :] = lane_sum(gathered_lanes(act_ref[0, rows, :])) / tile

            by_rows(pivot)

        def sums(rows):
            off = act_ref[index, rows, :] - spread(stat_ref[2, rows, :])
            stat_ref[3, rows, :] += gathered_lanes(off)
            stat_ref[4, rows, :] += gathered_lanes(off * off)

        by_rows(sums)

    @pl.when(step == tiles)
    def _():
        drift = lane_sum(stat_ref[3]) / hidden
        stat_ref[2] = stat_ref[2] + drift
        stat_ref[4] = lax.rsqrt(
            jnp.maximum(lane_sum(stat_ref[4]) / hidden - drift * drift, 0.0) + 1e-05
        )

    @pl.when(phase == 1)
    def _():
        def hidden_rows(rows):
            hat = (act_ref[index, rows, :] - spread(stat_ref[2, rows, :])) * spread(
                stat_ref[4, rows, :]
            )
            act_ref[index, rows, :] = hat
            bent_out[rows, :] = (hat * ghidden_ref[...]).astype(jnp.bfloat16)

        by_rows(hidden_rows)
        work_ref[...] = nt_dot(cot_ref[...], wdown_ref[...])
        acc_ref[...] += nn_dot(bent_out[...], wdown_ref[...])
        column_ref[...] = jnp.zeros_like(column_ref)

        def grad_rows(rows):
            hat, grad = act_ref[index, rows, :], work_ref[rows, :]
            column_ref[...] += column_sums(grad * hat)
            scaled = grad * ghidden_ref[...]
            dact_ref[index, rows, :] = scaled
            stat_ref[5, rows, :] += gathered_lanes(scaled)
            stat_ref[6, rows, :] += gathered_lanes(scaled * hat)

        by_rows(grad_rows)
        dhidden_ref[...] = jnp.sum(column_ref[...], axis=0, keepdims=True)

    @pl.when(step == 2 * tiles)
    def _():
        result_ref[...] = acc_ref[...].astype(jnp.bfloat16)
        acc_ref[...] = jnp.zeros_like(acc_ref)
        stat_ref[5] = lane_sum(stat_ref[5]) / hidden
        stat_ref[6] = lane_sum(stat_ref[6]) / hidden

    @pl.when(phase == 2)
    def _():
        def pre_rows(rows):
            inner = (
                dact_ref[index, rows, :]
                - spread(stat_ref[5, rows, :])
                - act_ref[index, rows, :] * spread(stat_ref[6, rows, :])
            )
            pre_out[rows, :] = (
                spread(stat_ref[4, rows, :]) * inner * slope_ref[index, rows, :]
            ).astype(jnp.bfloat16)

        by_rows(pre_rows)
        acc_ref[...] += nt_dot(pre_out[...], wup_ref[...])

    @pl.when(step == 3 * tiles - 1)
    def _():
        column_ref[...] = jnp.zeros_like(column_ref)

        def middle_rows(rows):
            grad, hat = acc_ref[rows, :], hat_ref[rows, :]
            column_ref[...] += column_sums(grad * hat)
            gmid = cot_ref[rows, :].astype(jnp.float32) + norm_rows_back(
                grad, hat, stat_ref[1, rows, :], gfeed_ref[...]
            )
            gmid_ref[rows, :] = gmid
            gmid_b_ref[rows, :] = gmid.astype(jnp.bfloat16)

        by_rows(middle_rows)
        dfeed_ref[...] = jnp.sum(column_ref[...], axis=0, keepdims=True)
        work_ref[...] = nt_dot(gmid_b_ref[...], wout_ref[...])
        column_ref[...] = jnp.zeros_like(column_ref)

        def inner_rows(rows):
            grad, hat = work_ref[rows, :], zhat_ref[rows, :]
            column_ref[...] += column_sums(grad * hat)
            work_ref[rows, :] = norm_rows_back(grad, hat, stat_ref[0, rows, :], ginner_ref[...])

        by_rows(inner_rows)
        dinner_ref[...] = jnp.sum(column_ref[...], axis=0, keepdims=True)
        swap_ref[...] = work_ref[...].T
        for near in range(chips):
            start = pl.multiple_of(share * lax.rem(chip + near, chips), share)
            go_refs[near][...] = swap_ref[pl.ds(start, share), :].astype(jnp.bfloat16)


def middle(position, mixed, tokens, cotangent, w_out, w_up, w_down, gains):
    chips = len(mixed)
    block, model_width = tokens.shape
    hidden = w_up.shape[1]
    tile = model_width
    tiles = hidden // tile
    share = model_width // chips
    last = tiles - 1

    def up_index(i, pos):
        return (0, jnp.where(i < tiles, i, jnp.where(i < 2 * tiles, last, i - 2 * tiles)))

    def down_index(i, pos):
        return (jnp.clip(i - tiles, 0, last), 0)

    def hidden_index(i, pos):
        return (0, jnp.clip(i - tiles, 0, last))

    def pre_index(i, pos):
        return (0, jnp.clip(i - 2 * tiles, 0, last))

    def f32(*shape):
        return pltpu.VMEM(shape, jnp.float32)

    row, rows = (1, model_width), (block, model_width)
    narrow = jax.ShapeDtypeStruct(rows, jnp.bfloat16)
    return pl.pallas_call(
        partial(middle_kernel, chips, tiles),
        grid_spec=pltpu.PrefetchScalarGridSpec(
            num_scalar_prefetch=1,
            grid=(3 * tiles,),
            in_specs=[whole((share, block))] * chips
            + [
                whole(rows),
                whole(rows),
                whole((model_width, model_width)),
                pl.BlockSpec((model_width, tile), up_index),
                pl.BlockSpec((tile, model_width), down_index),
                whole(row),
                whole(row),
                pl.BlockSpec((1, tile), hidden_index),
            ],
            out_specs=[whole(rows)] * 3
            + [whole((share, block))] * chips
            + [
                whole(rows),
                whole(rows),
                pl.BlockSpec((block, tile), hidden_index),
                pl.BlockSpec((block, tile), pre_index),
                whole(row),
                whole(row),
                pl.BlockSpec((1, tile), hidden_index),
            ],
            scratch_shapes=[
                f32(model_width, block),
                f32(block, tile),
                f32(8, tile),
                f32(block, model_width),
                f32(block, model_width),
                f32(tiles, block, tile),
                f32(tiles, block, tile),
                f32(tiles, block, tile),
                f32(block, model_width),
                f32(7, block, 128),
            ],
        ),
        out_shape=[narrow, jax.ShapeDtypeStruct(rows, jnp.float32), narrow]
        + [jax.ShapeDtypeStruct((share, block), jnp.bfloat16)] * chips
        + [
            narrow,
            narrow,
            jax.ShapeDtypeStruct((block, hidden), jnp.bfloat16),
            jax.ShapeDtypeStruct((block, hidden), jnp.bfloat16),
            jax.ShapeDtypeStruct(row, jnp.float32),
            jax.ShapeDtypeStruct(row, jnp.float32),
            jax.ShapeDtypeStruct((1, hidden), jnp.float32),
        ],
        compiler_params=pltpu.CompilerParams(vmem_limit_bytes=26 << 20),
        cost_estimate=NO_COST,
        name="middle",
    )(position, *mixed, tokens, cotangent, w_out, w_up, w_down, *gains)


def down_kernel(per, position, bent_ref, cot_ref, keep_ref, send_ref):
    first_core = position[1] == 0
    parts = bent_ref.shape[1] // (2 * per)
    first = pl.program_id(0) * parts
    grad = lax.dot_general(
        bent_ref[...], cot_ref[...], (((0,), (0,)), ((), ())), preferred_element_type=jnp.float32
    ).astype(jnp.bfloat16)
    for part in range(parts):
        even = grad[2 * per * part : 2 * per * part + per]
        odd = grad[2 * per * part + per : 2 * per * (part + 1)]
        keep_ref[first + part] = jnp.where(first_core, even, odd)
        send_ref[first + part] = jnp.where(first_core, odd, even)


def down_grad(position, bent, cotangent, per):
    (block, hidden), model_width = bent.shape, cotangent.shape[1]
    tiles, chunks = hidden // model_width, hidden // (2 * per)
    out = jax.ShapeDtypeStruct((chunks, per, model_width), jnp.bfloat16)
    out_spec = pl.BlockSpec(memory_space=pltpu.VMEM)
    return pl.pallas_call(
        partial(down_kernel, per),
        grid_spec=pltpu.PrefetchScalarGridSpec(
            num_scalar_prefetch=1,
            grid=(tiles,),
            in_specs=[
                pl.BlockSpec((block, model_width), lambda i, pos: (0, i)),
                pl.BlockSpec(memory_space=pltpu.VMEM),
            ],
            out_specs=[out_spec, out_spec],
        ),
        out_shape=[out, out],
        compiler_params=pltpu.CompilerParams(vmem_limit_bytes=20 << 20),
        cost_estimate=NO_COST,
        name="down_grad",
    )(position, bent, cotangent)


def up_out_kernel(tiles, position, h2_ref, pre_ref, z_ref, gmid_ref, perm_ref, keep_ref, send_ref, left_ref):
    step = pl.program_id(0)
    chunks = keep_ref.shape[0]
    per = perm_ref.shape[0] // (2 * chunks)
    place = pl.ds(pl.multiple_of(step * per, per), per)

    @pl.when(step == 0)
    def _():
        left_ref[...] = nt_dot(perm_ref[...], h2_ref[...]).astype(jnp.bfloat16)

    def store(right):
        grad = nn_dot(left_ref[...], right)
        for chunk in range(chunks):
            keep_ref[chunk, place] = grad[chunk * per : (chunk + 1) * per].astype(jnp.bfloat16)
            first = (chunks + chunk) * per
            send_ref[chunk, place] = grad[first : first + per].astype(jnp.bfloat16)

    @pl.when(step < tiles)
    def _():
        store(pre_ref[...])

    @pl.when(step == tiles)
    def _():
        left_ref[...] = nt_dot(perm_ref[...], z_ref[...]).astype(jnp.bfloat16)
        store(gmid_ref[...])


def up_out_grad(position, h2, pre, z, gmid, perm, per):
    (block, hidden), model_width = pre.shape, h2.shape[1]
    tiles, chunks = hidden // model_width, model_width // (2 * per)
    out = jax.ShapeDtypeStruct((chunks, per * (tiles + 1), model_width), jnp.bfloat16)
    out_spec = pl.BlockSpec(memory_space=pltpu.VMEM)
    return pl.pallas_call(
        partial(up_out_kernel, tiles),
        grid_spec=pltpu.PrefetchScalarGridSpec(
            num_scalar_prefetch=1,
            grid=(tiles + 1,),
            in_specs=[
                pl.BlockSpec(memory_space=pltpu.VMEM),
                pl.BlockSpec((block, model_width), lambda i, pos: (0, jnp.minimum(i, tiles - 1))),
            ]
            + [pl.BlockSpec(memory_space=pltpu.VMEM)] * 3,
            out_specs=[out_spec, out_spec],
            scratch_shapes=[pltpu.VMEM((model_width, block), jnp.bfloat16)],
        ),
        out_shape=[out, out],
        compiler_params=pltpu.CompilerParams(vmem_limit_bytes=20 << 20),
        cost_estimate=NO_COST,
        name="up_out_grad",
    )(position, h2, pre, z, gmid, perm)


def final_kernel(chips, position, *refs):
    homes = refs[:chips]
    (
        tokens_ref,
        gmid_ref,
        wq_ref,
        wk_ref,
        wv_ref,
        gain_ref,
        out_ref,
        swap_ref,
    ) = refs[chips:]
    chip = position[0]
    block, model_width = tokens_ref.shape
    share = model_width // chips
    total = jnp.zeros((block, model_width), jnp.float32)
    for index, weight in enumerate((wq_ref, wk_ref, wv_ref)):
        for near in range(chips):
            start = pl.multiple_of(share * lax.rem(chip + near, chips), share)
            swap_ref[pl.ds(start, share), :] = homes[near][
                index * share : (index + 1) * share, :
            ].astype(jnp.float32)
        total = total + nt_dot(swap_ref[...].T.astype(jnp.bfloat16), weight[...])
    hat, rate = norm_parts(tokens_ref[...].astype(jnp.float32))
    back = norm_back(total, hat, rate, gain_ref[...])[0]
    out_ref[...] = (gmid_ref[...] + back).astype(jnp.bfloat16)


def final(position, homes, tokens, gmid, w_query, w_key, w_value, gain):
    block, model_width = tokens.shape
    return call_whole(
        partial(final_kernel, len(homes)),
        [jax.ShapeDtypeStruct((block, model_width), jnp.bfloat16)],
        "final",
        position,
        *homes,
        tokens,
        gmid,
        w_query,
        w_key,
        w_value,
        gain,
        scratch=[pltpu.VMEM((model_width, block), jnp.float32)],
        outs=False,
    )[0]


def chip_shift(value, steps):
    count = lax.axis_size("seq")
    return lax.ppermute(value, "seq", [(i, (i + 2 * steps) % count) for i in range(count)])


def seq_swap(value, bit):
    return lax.ppermute(value, "seq", [(i, i ^ bit) for i in range(lax.axis_size("seq"))])


def row_swap(value, bit):
    return lax.ppermute(value, "row", [(i, i ^ bit) for i in range(lax.axis_size("row"))])


def sent(array):
    return array.astype(jnp.bfloat16)


def wide(array):
    return array.astype(jnp.float32)


def outgoing_kernel(kept, scalars, *refs):
    low_ref, high_ref = refs[-2:]
    low_bit, high_bit = scalars[2], scalars[3]
    if not kept:
        low_bit, high_bit = 1 - low_bit, 1 - high_bit
    half = refs[0].shape[2] // 2
    first = 0
    for group in range(len(refs) // 2 - 1):
        keep, other = refs[2 * group : 2 * group + 2]
        rows = slice(first, first + keep.shape[3])
        for side in range(2):
            low_ref[side, :, rows] = sent(
                wide(keep[side, low_bit, :half]) + wide(other[side, low_bit, :half])
            )
            high_ref[side, :, rows] = sent(
                wide(keep[high_bit, side, half:]) + wide(other[high_bit, side, half:])
            )
        first += keep.shape[3]


def outgoing(scalars, groups, kept=False):
    arrays = [array for group in groups for array in group]
    shape = groups[0][0].shape
    rows = sum(keep.shape[3] for keep, _ in groups)
    out = jax.ShapeDtypeStruct((2, shape[2] // 2, rows, shape[4]), jnp.bfloat16)
    return call_whole(
        partial(outgoing_kernel, kept),
        [out, out],
        "kept" if kept else "outgoing",
        scalars,
        *arrays,
    )


def halfway_kernel(groups, scalars, *refs):
    ins, outs = refs[: 4 * groups], refs[4 * groups :]
    low_bit, high_bit = scalars[2], scalars[3]
    low_keep, low_send, high_keep, high_send = outs
    first = 0
    for group in range(groups):
        low, high, low_in, high_in = ins[4 * group : 4 * group + 4]
        rows = slice(first, first + low.shape[2])
        for target, side in ((low_keep, high_bit), (low_send, 1 - high_bit)):
            target[:, rows] = sent(wide(low[side]) + wide(low_in[side]))
        for target, side in ((high_keep, low_bit), (high_send, 1 - low_bit)):
            target[:, rows] = sent(wide(high[side]) + wide(high_in[side]))
        first += low.shape[2]


def halfway(scalars, groups):
    arrays = [array for group in groups for array in group]
    rows = sum(group[0].shape[2] for group in groups)
    out = jax.ShapeDtypeStruct((arrays[0].shape[1], rows, arrays[0].shape[3]), jnp.bfloat16)
    return call_whole(
        partial(halfway_kernel, len(groups)), [out] * 4, "halfway", scalars, *arrays, limit=12
    )


def split_kernel(chips, groups, scalars, *refs):
    ins, outs = refs[: 4 * groups], refs[4 * groups : 4 * groups + chips]
    all_ref = refs[-1]
    half = chips // 2
    first = 0
    for group in range(groups):
        low_keep, low_in, high_keep, high_in = ins[4 * group : 4 * group + 4]
        rows = slice(first, first + low_in.shape[1])
        all_ref[:half, rows] = sent(wide(low_keep[...]) + wide(low_in[...]))
        all_ref[half:, rows] = sent(wide(high_keep[...]) + wide(high_in[...]))
        first += low_in.shape[1]
    for step in range(chips):
        outs[step][...] = all_ref[lax.rem(scalars[0] + step, chips)]


def split(scalars, groups, chips):
    arrays = [array for group in groups for array in group]
    rows = sum(group[0].shape[1] for group in groups)
    width = arrays[0].shape[2]
    return call_whole(
        partial(split_kernel, chips, len(groups)),
        [jax.ShapeDtypeStruct((rows, width), jnp.bfloat16)] * chips,
        "split",
        scalars,
        *arrays,
        scratch=[pltpu.VMEM((chips, rows, width), jnp.bfloat16)],
    )


def lay_flat(target, values, first, step):
    for piece in range(values.shape[1] // 128):
        target[pl.ds(first + piece, values.shape[0], step), :] = values[
            :, 128 * piece : 128 * (piece + 1)
        ]


def finish_kernel(chips, per, share, factor, scalars, *refs):
    arrived, heads_in, refs = refs[:chips], refs[chips : 2 * chips], refs[chips:]
    down_ref, up_ref, out_ref, query_ref, key_ref, value_ref, gains_ref, heads_ref = refs[chips:]
    width = arrived[0].shape[1]
    chip, pieces = scalars[0], width // 128
    tiles = up_ref.shape[0] * 128 // (per * width)
    down_rows = down_ref.shape[0] * 128 // width

    def total(first, rows):
        result = wide(arrived[0][first : first + rows, :])
        for part in arrived[1:]:
            result = result + wide(part[first : first + rows, :])
        return result * factor

    lay_flat(down_ref, total(0, down_rows), 0, pieces)
    for tile in range(tiles):
        lay_flat(up_ref, total(down_rows + tile * per, per), tile * pieces, tiles * pieces)
    lay_flat(out_ref, total(down_rows + tiles * per, per), 0, pieces)
    gains = wide(heads_in[0][:8, -128:])
    for part in heads_in[1:]:
        gains = gains + wide(part[:8, -128:])
    gains = gains * factor
    part = gains_ref.shape[0]
    for line in range(-(-part // 128)):
        stop = min(part, 128 * (line + 1))
        gains_ref[128 * line : stop] = gains[line, : stop - 128 * line]
    for step in range(chips):
        heads_ref[lax.rem(chip - step + chips, chips)] = wide(heads_in[step][:, : 3 * share])
    for index, target in enumerate((query_ref, key_ref, value_ref)):
        values = jnp.concatenate(
            [heads_ref[near][:, index * share : (index + 1) * share] for near in range(chips)], axis=1
        )
        lay_flat(target, values * factor, 0, pieces)


def finish(scalars, arrived, hidden, gains_part, per, share, factor):
    chips, width = len(arrived) // 2, arrived[0].shape[1]
    square = jax.ShapeDtypeStruct((per * width // 128, 128), jnp.float32)
    large = jax.ShapeDtypeStruct((per * hidden // 128, 128), jnp.float32)
    return call_whole(
        partial(finish_kernel, chips, per, share, factor),
        [large, large, square, square, square, square, jax.ShapeDtypeStruct((gains_part,), jnp.float32)],
        "finish",
        scalars,
        *arrived,
        scratch=[pltpu.VMEM((chips, per, 3 * share), jnp.float32)],
        outs=False,
    )


def gathered(rows):
    behind, ahead = chip_shift(rows, 1), chip_shift(rows, -1)
    up = [(2 * i + core, 2 * i + 2 + core) for i in (1, 2) for core in (0, 1)]
    down = [(2 * i + core, 2 * i - 2 + core) for i in (1, 2) for core in (0, 1)]
    across = (lax.ppermute(ahead, "seq", down), lax.ppermute(behind, "seq", up))
    return behind, ahead, across


def fast_local(
    tokens,
    lengths,
    w_query,
    w_key,
    w_value,
    w_out,
    w_up,
    w_down,
    gain_attend,
    gain_inner,
    gain_feed,
    gain_hidden,
    cotangent,
):
    block, model_width = tokens.shape
    hidden = w_up.shape[1]
    size = model_width // HEADS
    lanes = 2 * size
    scale = size ** (-0.5)
    seq_devices, row_devices = lax.axis_size("seq"), lax.axis_size("row")
    chips = seq_devices // 2
    heads = HEADS // chips
    share = heads * size
    spread = heads * lanes
    parts = row_devices * seq_devices
    position, row = lax.axis_index("seq"), lax.axis_index("row")
    chip, core = position // 2, position % 2
    place = jnp.stack([chip, core, row % 2, row // 2]).astype(jnp.int32)
    bounds = jnp.cumsum(lengths[0])[:-1]
    factor = 1.0 / math.sqrt(block * parts)

    normed_b = call_whole(
        norm_kernel,
        [jax.ShapeDtypeStruct(tokens.shape, jnp.bfloat16)],
        "norm",
        jnp.zeros((1,), jnp.int32),
        tokens,
        gain_attend,
        ins=False,
    )[0]
    behind, ahead, across = gathered(normed_b)

    order = [step for step in range(chips) if step != chips // 2] + [chips // 2]
    slots = [order.index(step) for step in range(chips)]
    chip_ids = (chip - jnp.asarray(order, jnp.int32)) % chips
    query_starts = block * (2 * chip_ids + core)
    other_starts = block * (2 * chip_ids + 1 - core)
    key_starts = jnp.concatenate(
        [query_starts[:-1], other_starts[:-1], query_starts[-1:], other_starts[-1:]]
    )
    in_block = jnp.arange(block, dtype=jnp.int32)[None, :]
    query_places = (query_starts[:, None] + in_block).reshape(-1)
    doc_line = jnp.max(jnp.where(bounds[:, None] <= query_places[None, :], bounds[:, None], 0), axis=0)
    meta = jnp.concatenate(
        [query_starts, key_starts, doc_line.reshape(chips, block)[:, 0], doc_line.reshape(chips, block)[:, -1]]
    )
    doc_line = doc_line[None, :]

    feature = jnp.arange(model_width, dtype=jnp.int32)
    per = model_width // parts
    chunk, inside = feature // per, feature % per
    chunks = parts // 2
    parity = jnp.where(chunk < chunks, core, 1 - core)
    wanted = (2 * (chunk % chunks) + parity) * per + inside
    perm = (wanted[:, None] == feature[None, :]).astype(jnp.bfloat16)

    gains_share = (3 * model_width + hidden) // parts
    gains_rows = -(-gains_share // 128)
    first_head = heads * chip[None]
    small = (
        jnp.concatenate([query_starts[:-1], other_starts[:-1], first_head]),
        jnp.concatenate([query_starts[-1:], other_starts[-1:], first_head]),
        meta,
        doc_line,
        gain_attend[None, :],
        gain_inner[None, :],
        gain_feed[None, :],
        gain_hidden[None, :],
        place,
        perm,
    )
    small = lax.optimization_barrier(small)
    starts, late_starts, meta, doc_line, gain_first, gain_inner, gain_feed, gain_hidden = small[:8]
    place, perm = small[8:]
    early = choose(place, w_query, w_key, w_value, heads, size)
    behind, early = lax.optimization_barrier((behind, early))
    wq_wide, wk_wide, wv_rows, wk_rows, wv_wide, wq_rows = early
    own = [normed_b, behind, ahead]
    early_blocks = own + [seq_swap(rows, 1) for rows in own]
    filled = project(
        starts, early_blocks, wq_wide, wk_wide, wv_rows, chips - 1, heads, scale, chips
    )
    filled, across = lax.optimization_barrier((filled, across))
    own.append(across[0] + across[1])
    late_blocks = [own[-1], seq_swap(own[-1], 1)]
    q_ext, k_ext, v_t = project(
        late_starts, late_blocks, wq_wide, wk_wide, wv_rows, 1, heads, scale, chips, filled
    )
    parts_of = [
        attend(meta, doc_line, q_ext, k_ext, v_t, heads, block, *span) for span in ((0, 1), (1, chips))
    ]
    mixed, lse, mixed_b = (
        list(parts_of[0][item]) + list(parts_of[1][item]) for item in range(3)
    )
    mixed_b[1:], wk_rows = lax.optimization_barrier((mixed_b[1:], wk_rows))
    k_t, v_ext = project_back(place, early_blocks + late_blocks, wk_rows, wv_wide)
    back = [mixed_b[slots[0]]] + [
        chip_shift(mixed_b[slots[step]], -step) for step in range(1, chips)
    ]
    back, k_t, v_ext = lax.optimization_barrier((back, k_t, v_ext))
    outs = middle(
        place, back, tokens, cotangent, w_out, w_up, w_down, (gain_inner, gain_feed, gain_hidden)
    )
    result, grad_middle, gmid_b = outs[:3]
    go = outs[3 : 3 + chips]
    z, h2, bent, pre, dinner, dfeed, dhidden = outs[3 + chips :]
    keep_a, send_a = down_grad(place, bent, cotangent, hidden // parts)
    keep_b, send_b = up_out_grad(place, h2, pre, z, gmid_b, perm, per)
    go, keep_b, send_b = lax.optimization_barrier((go, keep_b, send_b))
    go = [go[0]] + [chip_shift(go[step], step) for step in range(1, chips)]

    def gridded(array):
        return array.reshape((2, 2, chips) + array.shape[1:])

    sums = [
        (gridded(keep), gridded(seq_swap(send, 1)))
        for keep, send in ((keep_a, send_a), (keep_b, send_b))
    ]
    low, high = outgoing(place, sums)
    arrived_sums = [row_swap(low, 1), row_swap(high, 2)]
    dq, pair, other = attend_back(
        meta, doc_line, q_ext, [go[step] for step in order], mixed, lse, k_ext, k_t, v_ext, heads, block, scale
    )
    grads = join_parts(place, dq, pair, seq_swap(other, 1), chips)
    home = [grads[slots[0]]] + [chip_shift(grads[slots[step]], -step) for step in range(1, chips)]
    grads, sums = lax.optimization_barrier((grads, sums))
    kept = outgoing(place, sums, True)
    mine_grad, send_grad = head_grads(
        place,
        own,
        grads,
        (wq_rows, wk_rows, wv_rows),
        gain_first,
        (dinner, dfeed, dhidden),
        perm,
        per,
    )
    arrived_sums, kept, mine_grad, send_grad = lax.optimization_barrier(
        (arrived_sums, kept, mine_grad, send_grad)
    )
    low_keep, low_send, high_keep, high_send = halfway(place, [(*kept, *arrived_sums)])
    low_in, high_in = row_swap(low_send, 2), row_swap(high_send, 1)
    home, mine_grad, send_grad = lax.optimization_barrier((home, mine_grad, send_grad))
    mine_grad, other_grad = gridded(mine_grad), gridded(seq_swap(send_grad, 1))
    stage = split(after(place, home, SOME_COST), [(low_keep, low_in, high_keep, high_in)], chips)
    arrived = [stage[0]] + [chip_shift(stage[step], step) for step in range(1, chips)]
    grad_input = final(
        place, home, tokens, grad_middle, w_query, w_key, w_value, gain_first
    )
    low, high = outgoing(place, [(mine_grad, other_grad)])
    low_keep, low_send, high_keep, high_send = halfway(
        place,
        [(*outgoing(place, [(mine_grad, other_grad)], True), row_swap(low, 1), row_swap(high, 2))],
    )
    stage = split(
        place, [(low_keep, row_swap(low_send, 2), high_keep, row_swap(high_send, 1))], chips
    )
    arrived += [stage[0]] + [chip_shift(stage[step], step) for step in range(1, chips)]
    down, up, out, query, key, value, gains_part = finish(
        place, arrived, hidden, gains_share, per, share, factor
    )
    return (
        result,
        grad_input,
        query.reshape(-1),
        key.reshape(-1),
        value.reshape(-1),
        out.reshape(-1),
        up.reshape(-1),
        down.reshape(-1),
        gains_part,
    )


def local(*arrays):
    seq_devices, row_devices = lax.axis_size("seq"), lax.axis_size("row")
    block = arrays[0].shape[0]
    one_segment = block * seq_devices <= SEGMENT and block % 2 ** (PATTERNS - 1) == 0
    if one_segment and seq_devices == 8 and row_devices == 4:
        return fast_local(*arrays)
    return ring_local(*arrays)


def solution(mesh):
    return jax.shard_map(
        local,
        mesh=mesh,
        in_specs=(
            P(("row", "seq"), None),
            P("row", None),
            P(),
            P(),
            P(),
            P(),
            P(),
            P(),
            P(),
            P(),
            P(),
            P(),
            P(("row", "seq"), None),
        ),
        out_specs=(
            P(("row", "seq"), None),
            P(("row", "seq"), None),
            P(("row", "seq")),
            P(("row", "seq")),
            P(("row", "seq")),
            P(("row", "seq")),
            P(("row", "seq")),
            P(("row", "seq")),
            P(("row", "seq")),
        ),
        check_vma=False,
    )
```

```python
from functools import partial
from functools import reduce
import math

import jax
import jax.numpy as jnp
import numpy as np
from jax import lax
from jax.experimental import pallas as pl
from jax.experimental.pallas import tpu as pltpu
from jax.sharding import PartitionSpec as P

HEADS = 12
SEGMENT = 2048
PATTERNS = 5


big_negative = -1e30


def shifted_2(shard, axis, by):
    length = lax.axis_size(axis)
    pairs = [(i, i + by) for i in range(length) if 0 <= i + by < length]
    return lax.ppermute(shard, axis, pairs)


def shifted_3(value, axis, steps):
    count = lax.axis_size(axis)
    pairs = [(source, (source + steps) % count) for source in range(count)]
    return lax.ppermute(value, axis, pairs)


def layer_norm(values, gain_vector):
    centre = jnp.mean(values, axis=-1, keepdims=True)
    shifted = values - centre
    variance = jnp.mean(shifted * shifted, axis=-1, keepdims=True)
    return shifted * lax.rsqrt(variance + 1e-05) * gain_vector


def hidden_norm(hidden_pre, gain_vector):
    return layer_norm(jax.nn.gelu(hidden_pre, approximate=True), gain_vector)


def selector(stride, head_count):
    return jnp.arange(stride)[:, None] == (jnp.arange(head_count) % stride)[None, :]


def compact(full_array, stride):
    length_in, head_count, inner_size = full_array.shape
    shaped = full_array.reshape(length_in // stride, stride, head_count, inner_size)
    picked = jnp.where(
        selector(stride, head_count)[None, :, :, None], shaped, jnp.zeros((), full_array.dtype)
    )
    return jnp.sum(picked, axis=1)


def expand(part_array, stride, fill_value):
    part_rows, head_count, inner_size = part_array.shape
    widened = jnp.where(
        selector(stride, head_count)[None, :, :, None],
        part_array[:, None],
        jnp.asarray(fill_value, part_array.dtype),
    )
    return widened.reshape(part_rows * stride, head_count, inner_size)


def positions(start_pos, part_rows, stride, head_count):
    row_ids = jnp.arange(part_rows, dtype=jnp.int32)[:, None] * stride
    head_ids = (jnp.arange(head_count, dtype=jnp.int32) % stride)[None, :]
    return start_pos + row_ids + head_ids


def doc_index(places, doc_bounds):
    return jnp.sum((places[..., None] >= doc_bounds).astype(jnp.int32), axis=-1)


def block_mask(doc_query, doc_key, local_block):
    allowed = doc_query.T[:, :, None] == doc_key.T[:, None, :]
    if local_block:
        rank_ids = jnp.arange(doc_query.shape[0])
        allowed = allowed & (rank_ids[:, None] >= rank_ids[None, :])[None]
    return allowed


def forward_block(query_part, key_part, value_part, allowed, score_scale):
    scores = (
        jnp.einsum("qhd,khd->hqk", query_part, key_part, preferred_element_type=jnp.float32)
        * score_scale
    )
    scores = jnp.where(allowed, scores, big_negative)
    row_peak = jnp.max(scores, axis=-1)
    weights = jnp.where(allowed, jnp.exp(scores - row_peak[..., None]), 0.0)
    row_total = jnp.sum(weights, axis=-1)
    mixed = jnp.einsum(
        "hqk,khd->qhd", weights.astype(jnp.bfloat16), value_part, preferred_element_type=jnp.float32
    )
    return (row_peak.T, row_total.T, mixed)


def merge(carried, new_block):
    best_peak = jnp.maximum(carried[0], new_block[0])
    keep_factor = jnp.exp(carried[0] - best_peak)
    take_factor = jnp.exp(new_block[0] - best_peak)
    new_total = carried[1] * keep_factor + new_block[1] * take_factor
    new_mixed = carried[2] * keep_factor[..., None] + new_block[2] * take_factor[..., None]
    return (best_peak, new_total, new_mixed)


def backward_block(
    query_part, grad_part, lse_part, delta_part, key_part, value_part, allowed, score_scale
):
    scores = (
        jnp.einsum("qhd,khd->hqk", query_part, key_part, preferred_element_type=jnp.float32)
        * score_scale
    )
    probs = jnp.where(allowed, jnp.exp(scores - lse_part.T[:, :, None]), 0.0)
    dots = jnp.einsum("qhd,khd->hqk", grad_part, value_part, preferred_element_type=jnp.float32)
    grad_scores = (probs * (dots - delta_part.T[:, :, None])).astype(jnp.bfloat16)
    query_grad = (
        jnp.einsum("hqk,khd->qhd", grad_scores, key_part, preferred_element_type=jnp.float32)
        * score_scale
    )
    key_grad = (
        jnp.einsum("hqk,qhd->khd", grad_scores, query_part, preferred_element_type=jnp.float32)
        * score_scale
    )
    value_grad = jnp.einsum(
        "hqk,qhd->khd", probs.astype(jnp.bfloat16), grad_part, preferred_element_type=jnp.float32
    )
    return (query_grad, key_grad, value_grad)


def keep_state(carried):
    return carried


def ring_local(
    tokens,
    lengths,
    w_query,
    w_key,
    w_value,
    w_out,
    w_up,
    w_down,
    gain_attend,
    gain_inner,
    gain_feed,
    gain_hidden,
    cotangent,
):
    block_rows, model_width = tokens.shape
    head_count = HEADS
    head_size = model_width // head_count
    score_scale = head_size ** (-0.5)
    seq_devices = lax.axis_size("seq")
    all_devices = seq_devices * lax.axis_size("row")
    my_index = lax.axis_index("seq")
    seq_total = block_rows * seq_devices
    doc_bounds = jnp.cumsum(lengths[0])[:-1]
    patterns = [
        (2**pattern, min(SEGMENT * 2**pattern, seq_total) // block_rows)
        for pattern in range(PATTERNS)
    ]
    near_ids = [0, 1]
    far_ids = list(range(2, PATTERNS))
    reach = patterns[1][1]
    far_rows = [block_rows // patterns[pattern][0] for pattern in far_ids]
    far_starts = [sum(far_rows[:slot_id]) for slot_id in range(len(far_ids))]
    far_total = sum(far_rows)

    def key_docs(pattern, source):
        stride = patterns[pattern][0]
        return doc_index(
            positions(source * block_rows, block_rows // stride, stride, head_count), doc_bounds
        )

    def is_live(pattern, cycle_step):
        group_size = patterns[pattern][1]
        return (cycle_step < group_size) & (my_index % group_size >= cycle_step)

    source_x = tokens.astype(jnp.float32)
    normed, attend_back = jax.vjp(layer_norm, source_x, gain_attend)
    normed_b = normed.astype(jnp.bfloat16)
    query_b = jnp.dot(normed_b, w_query, preferred_element_type=jnp.float32).astype(jnp.bfloat16)
    key_b = jnp.dot(normed_b, w_key, preferred_element_type=jnp.float32).astype(jnp.bfloat16)
    value_b = jnp.dot(normed_b, w_value, preferred_element_type=jnp.float32).astype(jnp.bfloat16)
    query_heads = query_b.reshape(block_rows, head_count, head_size)
    key_heads = key_b.reshape(block_rows, head_count, head_size)
    value_heads = value_b.reshape(block_rows, head_count, head_size)
    query_parts = [compact(query_heads, stride) for stride, group_size in patterns]
    key_parts = [compact(key_heads, stride) for stride, group_size in patterns]
    value_parts = [compact(value_heads, stride) for stride, group_size in patterns]
    own_docs = [key_docs(pattern, my_index) for pattern in range(PATTERNS)]
    states = [
        forward_block(
            query_parts[pattern],
            key_parts[pattern],
            value_parts[pattern],
            block_mask(own_docs[pattern], own_docs[pattern], True),
            score_scale,
        )
        for pattern in range(PATTERNS)
    ]

    def unpack_near(key_block):
        key_full = key_block[:, :model_width].reshape(block_rows, head_count, head_size)
        value_full = key_block[:, model_width:].reshape(block_rows, head_count, head_size)
        return (key_full, value_full)

    def near_fold_parts(pattern, key_part, value_part, source, carried):
        new_block = forward_block(
            query_parts[pattern],
            key_part,
            value_part,
            block_mask(own_docs[pattern], key_docs(pattern, source), False),
            score_scale,
        )
        return merge(carried, new_block)

    def near_fold(pattern, key_full, value_full, source, carried):
        stride = patterns[pattern][0]
        return near_fold_parts(
            pattern, compact(key_full, stride), compact(value_full, stride), source, carried
        )

    pair_block = jnp.concatenate([key_b, value_b], axis=1)
    kept_blocks = jnp.zeros((max(reach - 1, 1), block_rows, 2 * model_width), jnp.bfloat16)

    def near_forward(cycle_step, loop_state):
        key_block, near_now, kept_store = loop_state
        key_block = shifted_2(key_block, "seq", 1)
        key_full, value_full = unpack_near(key_block)
        new_states = []
        for pattern in near_ids:
            new_states.append(
                lax.cond(
                    is_live(pattern, cycle_step),
                    partial(near_fold, pattern, key_full, value_full, my_index - cycle_step),
                    keep_state,
                    near_now[pattern],
                )
            )
        return (key_block, tuple(new_states), kept_store)

    _, near_states, kept_blocks = lax.fori_loop(
        1, reach, near_forward, (pair_block, (states[0], states[1]), kept_blocks)
    )
    far_block = jnp.concatenate(
        [
            jnp.concatenate(
                [
                    key_parts[pattern].reshape(rows_here, model_width),
                    value_parts[pattern].reshape(rows_here, model_width),
                ],
                axis=1,
            )
            for pattern, rows_here in zip(far_ids, far_rows)
        ],
        axis=0,
    )

    def unpack_far(key_block, slot_id):
        rows_here = far_rows[slot_id]
        row_begin = far_starts[slot_id]
        piece_rows = key_block[row_begin : row_begin + rows_here]
        key_part = piece_rows[:, :model_width].reshape(rows_here, head_count, head_size)
        value_part = piece_rows[:, model_width:].reshape(rows_here, head_count, head_size)
        return (key_part, value_part)

    def far_fold(pattern, key_part, value_part, source, carried):
        new_block = forward_block(
            query_parts[pattern],
            key_part,
            value_part,
            block_mask(own_docs[pattern], key_docs(pattern, source), False),
            score_scale,
        )
        return merge(carried, new_block)

    def far_update(far_now, key_block, cycle_step):
        new_states = []
        for slot_id, pattern in enumerate(far_ids):
            key_part, value_part = unpack_far(key_block, slot_id)
            new_states.append(
                lax.cond(
                    is_live(pattern, cycle_step),
                    partial(far_fold, pattern, key_part, value_part, my_index - cycle_step),
                    keep_state,
                    far_now[slot_id],
                )
            )
        return tuple(new_states)

    far_states = tuple((states[pattern] for pattern in far_ids))

    def far_forward(cycle_step, loop_state):
        key_block, far_now = loop_state
        key_block = shifted_2(key_block, "seq", 1)
        return (key_block, far_update(far_now, key_block, cycle_step))

    _, far_states = lax.fori_loop(1, seq_devices, far_forward, (far_block, far_states))
    ordered = list(near_states) + list(far_states)
    peaks = [
        expand(ordered[pattern][0][..., None], patterns[pattern][0], big_negative)[..., 0]
        for pattern in range(PATTERNS)
    ]
    best_peak = reduce(jnp.maximum, peaks)
    weight_sum = jnp.zeros((block_rows, head_count), jnp.float32)
    mixed_sum = jnp.zeros((block_rows, head_count, head_size), jnp.float32)
    for pattern in range(PATTERNS):
        stride = patterns[pattern][0]
        factor = jnp.exp(peaks[pattern] - best_peak)
        weight_sum = (
            weight_sum + expand(ordered[pattern][1][..., None], stride, 0.0)[..., 0] * factor
        )
        mixed_sum = mixed_sum + expand(ordered[pattern][2], stride, 0.0) * factor[..., None]
    attended = mixed_sum / weight_sum[..., None]
    log_total = best_peak + jnp.log(weight_sum)
    inner_out, inner_back = jax.vjp(
        layer_norm, attended.reshape(block_rows, model_width), gain_inner
    )
    inner_b = inner_out.astype(jnp.bfloat16)
    middle = source_x + jnp.dot(inner_b, w_out, preferred_element_type=jnp.float32)
    normed_two, feed_back = jax.vjp(layer_norm, middle, gain_feed)
    normed_two_b = normed_two.astype(jnp.bfloat16)
    hidden_pre = jnp.dot(normed_two_b, w_up, preferred_element_type=jnp.float32)
    hidden, hidden_back = jax.vjp(hidden_norm, hidden_pre, gain_hidden)
    hidden_b = hidden.astype(jnp.bfloat16)
    result = (middle + jnp.dot(hidden_b, w_down, preferred_element_type=jnp.float32)).astype(
        jnp.bfloat16
    )
    grad_down = jnp.einsum("tf,tg->fg", hidden_b, cotangent, preferred_element_type=jnp.float32)
    grad_hidden = jnp.einsum("tg,fg->tf", cotangent, w_down, preferred_element_type=jnp.float32)
    grad_pre, grad_gain_hidden = hidden_back(grad_hidden)
    grad_pre_b = grad_pre.astype(jnp.bfloat16)
    grad_up = jnp.einsum("tf,tg->fg", normed_two_b, grad_pre_b, preferred_element_type=jnp.float32)
    grad_normed_two = jnp.einsum("tg,fg->tf", grad_pre_b, w_up, preferred_element_type=jnp.float32)
    grad_middle_part, grad_gain_feed = feed_back(grad_normed_two)
    grad_middle = cotangent.astype(jnp.float32) + grad_middle_part
    grad_middle_b = grad_middle.astype(jnp.bfloat16)
    grad_out = jnp.einsum("tf,tg->fg", inner_b, grad_middle_b, preferred_element_type=jnp.float32)
    grad_inner = jnp.einsum("tg,fg->tf", grad_middle_b, w_out, preferred_element_type=jnp.float32)
    grad_attended, grad_gain_inner = inner_back(grad_inner)
    grad_heads = grad_attended.astype(jnp.bfloat16).reshape(block_rows, head_count, head_size)
    delta_rows = jnp.sum(grad_heads.astype(jnp.float32) * attended, axis=-1)
    grad_parts = [compact(grad_heads, stride) for stride, group_size in patterns]
    lse_parts = [compact(log_total[..., None], stride)[..., 0] for stride, group_size in patterns]
    delta_parts = [
        compact(delta_rows[..., None], stride)[..., 0] for stride, group_size in patterns
    ]
    query_grads = []
    home_keys = []
    home_values = []
    for pattern in range(PATTERNS):
        part_query, part_key, part_value = backward_block(
            query_parts[pattern],
            grad_parts[pattern],
            lse_parts[pattern],
            delta_parts[pattern],
            key_parts[pattern],
            value_parts[pattern],
            block_mask(own_docs[pattern], own_docs[pattern], True),
            score_scale,
        )
        query_grads.append(part_query)
        home_keys.append(part_key)
        home_values.append(part_value)

    def fetch_full(key_block):
        return shifted_2(key_block, "seq", 1)

    def near_grad(pattern, key_full, value_full, source, operands):
        query_grad, travel = operands
        stride = patterns[pattern][0]
        part_query, part_key, part_value = backward_block(
            query_parts[pattern],
            grad_parts[pattern],
            lse_parts[pattern],
            delta_parts[pattern],
            compact(key_full, stride),
            compact(value_full, stride),
            block_mask(own_docs[pattern], key_docs(pattern, source), False),
            score_scale,
        )
        spread_rows = jnp.concatenate(
            [
                expand(part_key, stride, 0.0).reshape(block_rows, model_width),
                expand(part_value, stride, 0.0).reshape(block_rows, model_width),
            ],
            axis=1,
        )
        return (query_grad + part_query, travel + spread_rows)

    def near_backward(cycle_step, loop_state):
        key_block, grads_now, travel = loop_state
        key_block = fetch_full(key_block)
        travel = shifted_3(travel.astype(jnp.bfloat16), "seq", 1).astype(travel.dtype)
        key_full, value_full = unpack_near(key_block)
        new_grads = list(grads_now)
        for pattern in near_ids:
            new_grads[pattern], travel = lax.cond(
                is_live(pattern, cycle_step),
                partial(near_grad, pattern, key_full, value_full, my_index - cycle_step),
                keep_state,
                (new_grads[pattern], travel),
            )
        return (key_block, tuple(new_grads), travel)

    own_key_near = expand(home_keys[0], 1, 0.0) + expand(home_keys[1], 2, 0.0)
    own_value_near = expand(home_values[0], 1, 0.0) + expand(home_values[1], 2, 0.0)
    near_start = jnp.concatenate(
        [
            own_key_near.reshape(block_rows, model_width),
            own_value_near.reshape(block_rows, model_width),
        ],
        axis=1,
    )
    _, near_query, travel_near = lax.fori_loop(
        1, reach, near_backward, (pair_block, (query_grads[0], query_grads[1]), near_start)
    )
    near_home = shifted_3(travel_near.astype(jnp.bfloat16), "seq", 1 - reach).astype(
        travel_near.dtype
    )
    near_key_add = near_home[:, :model_width].reshape(block_rows, head_count, head_size)
    near_value_add = near_home[:, model_width:].reshape(block_rows, head_count, head_size)

    def far_grad(slot_id, key_part, value_part, source, operands):
        query_grad, travel = operands
        pattern = far_ids[slot_id]
        rows_here = far_rows[slot_id]
        row_begin = far_starts[slot_id]
        part_query, part_key, part_value = backward_block(
            query_parts[pattern],
            grad_parts[pattern],
            lse_parts[pattern],
            delta_parts[pattern],
            key_part,
            value_part,
            block_mask(own_docs[pattern], key_docs(pattern, source), False),
            score_scale,
        )
        spread_rows = jnp.concatenate(
            [part_key.reshape(rows_here, model_width), part_value.reshape(rows_here, model_width)],
            axis=1,
        )
        return (
            query_grad + part_query,
            travel.at[row_begin : row_begin + rows_here].add(spread_rows),
        )

    def far_back_update(grads_now, travel, key_block, cycle_step):
        new_grads = list(grads_now)
        for slot_id, pattern in enumerate(far_ids):
            key_part, value_part = unpack_far(key_block, slot_id)
            new_grads[slot_id], travel = lax.cond(
                is_live(pattern, cycle_step),
                partial(far_grad, slot_id, key_part, value_part, my_index - cycle_step),
                keep_state,
                (new_grads[slot_id], travel),
            )
        return (tuple(new_grads), travel)

    far_query = tuple((query_grads[pattern] for pattern in far_ids))
    far_empty = jnp.zeros((far_total, 2 * model_width), jnp.float32)

    def far_send(travel):
        return shifted_3(travel.astype(jnp.bfloat16), "seq", 1).astype(travel.dtype)

    def far_backward(cycle_step, loop_state):
        key_block, grads_now, travel = loop_state
        key_block = shifted_2(key_block, "seq", 1)
        travel = far_send(travel)
        grads_now, travel = far_back_update(grads_now, travel, key_block, cycle_step)
        return (key_block, grads_now, travel)

    _, far_query, travel_far = lax.fori_loop(
        1, seq_devices, far_backward, (far_block, far_query, far_empty)
    )
    far_home = far_send(travel_far)
    all_query = list(near_query) + list(far_query)
    query_grad = jnp.zeros((block_rows, head_count, head_size), jnp.float32)
    key_grad = near_key_add
    value_grad = near_value_add
    for pattern in range(PATTERNS):
        stride = patterns[pattern][0]
        query_grad = query_grad + expand(all_query[pattern], stride, 0.0)
    for pattern in far_ids:
        stride = patterns[pattern][0]
        key_grad = key_grad + expand(home_keys[pattern], stride, 0.0)
        value_grad = value_grad + expand(home_values[pattern], stride, 0.0)
    for slot_id, pattern in enumerate(far_ids):
        stride = patterns[pattern][0]
        rows_here = far_rows[slot_id]
        row_begin = far_starts[slot_id]
        piece_rows = far_home[row_begin : row_begin + rows_here]
        key_grad = key_grad + expand(
            piece_rows[:, :model_width].reshape(rows_here, head_count, head_size), stride, 0.0
        )
        value_grad = value_grad + expand(
            piece_rows[:, model_width:].reshape(rows_here, head_count, head_size), stride, 0.0
        )
    grad_query_b = query_grad.reshape(block_rows, model_width).astype(jnp.bfloat16)
    grad_key_b = key_grad.reshape(block_rows, model_width).astype(jnp.bfloat16)
    grad_value_b = value_grad.reshape(block_rows, model_width).astype(jnp.bfloat16)
    grad_w_query = jnp.einsum(
        "tf,tg->fg", normed_b, grad_query_b, preferred_element_type=jnp.float32
    )
    grad_w_key = jnp.einsum("tf,tg->fg", normed_b, grad_key_b, preferred_element_type=jnp.float32)
    grad_w_value = jnp.einsum(
        "tf,tg->fg", normed_b, grad_value_b, preferred_element_type=jnp.float32
    )
    grad_normed = jnp.einsum("tg,fg->tf", grad_query_b, w_query, preferred_element_type=jnp.float32)
    grad_normed = grad_normed + jnp.einsum(
        "tg,fg->tf", grad_key_b, w_key, preferred_element_type=jnp.float32
    )
    grad_normed = grad_normed + jnp.einsum(
        "tg,fg->tf", grad_value_b, w_value, preferred_element_type=jnp.float32
    )
    grad_x_part, grad_gain_attend = attend_back(grad_normed)
    grad_input = (grad_middle + grad_x_part).astype(jnp.bfloat16)
    gains_all = jnp.concatenate(
        [grad_gain_attend, grad_gain_inner, grad_gain_feed, grad_gain_hidden]
    )
    summed = (
        lax.psum_scatter(grad_w_query.reshape(-1), ("row", "seq"), scatter_dimension=0, tiled=True),
        lax.psum_scatter(grad_w_key.reshape(-1), ("row", "seq"), scatter_dimension=0, tiled=True),
        lax.psum_scatter(grad_w_value.reshape(-1), ("row", "seq"), scatter_dimension=0, tiled=True),
        lax.psum_scatter(grad_out.reshape(-1), ("row", "seq"), scatter_dimension=0, tiled=True),
        lax.psum_scatter(grad_up.reshape(-1), ("row", "seq"), scatter_dimension=0, tiled=True),
        lax.psum_scatter(grad_down.reshape(-1), ("row", "seq"), scatter_dimension=0, tiled=True),
        lax.psum_scatter(gains_all, ("row", "seq"), scatter_dimension=0, tiled=True),
    )
    factor = 1.0 / math.sqrt(block_rows * all_devices)
    return (result, grad_input) + tuple((summed_part * factor for summed_part in summed))


NO_COST = pl.CostEstimate(flops=1000, bytes_accessed=1000, transcendentals=0)
SOME_COST = pl.CostEstimate(flops=4 * 10**9, bytes_accessed=1000, transcendentals=0)
HIGH_COST = pl.CostEstimate(flops=5 * 10**10, bytes_accessed=1000, transcendentals=0)


def split_log(level):
    remaining = math.log((level + 1) / level)
    pieces = []
    for _ in range(3):
        piece = float(jnp.bfloat16.dtype.type(remaining))
        pieces.append(piece)
        remaining -= piece
    return pieces


def extra_values(places, features, head, size, per_piece):
    masks, values = jnp.zeros_like(features), jnp.zeros(features.shape, jnp.float32)
    for level in range(1, PATTERNS):
        for piece, value in enumerate(split_log(level)):
            here = features == size + 3 * (level - 1) + piece
            masks = jnp.where(here, 2**level - 1, masks)
            values = jnp.where(here, value if per_piece else 1.0, values)
    return jnp.where(((places - head) & masks) == 0, values, 0.0)


def nt_dot(left, right):
    return lax.dot_general(
        left, right, (((1,), (1,)), ((), ())), preferred_element_type=jnp.float32
    )


def nn_dot(left, right):
    return jnp.dot(left, right, preferred_element_type=jnp.float32)


def call_whole(kernel, out_shape, name, scalars, *arrays, scratch=(), limit=12, ins=True, outs=True):
    direct = pl.BlockSpec(memory_space=pltpu.VMEM)
    return pl.pallas_call(
        kernel,
        grid_spec=pltpu.PrefetchScalarGridSpec(
            num_scalar_prefetch=1,
            grid=(1,),
            in_specs=[direct if ins else whole(array.shape) for array in arrays],
            out_specs=[direct if outs else whole(out.shape) for out in out_shape],
            scratch_shapes=list(scratch),
        ),
        out_shape=list(out_shape),
        compiler_params=pltpu.CompilerParams(vmem_limit_bytes=limit << 20),
        cost_estimate=NO_COST,
        name=name,
    )(scalars, *arrays)


def after_kernel(scalars, *refs):
    for index in range(scalars.shape[0]):
        refs[-1][index] = scalars[index]


def after(scalars, arrays, cost):
    return pl.pallas_call(
        after_kernel,
        in_specs=[pl.BlockSpec(memory_space=pltpu.SMEM)]
        + [pl.BlockSpec(memory_space=pl.ANY)] * len(arrays),
        out_specs=pl.BlockSpec(memory_space=pltpu.SMEM),
        out_shape=jax.ShapeDtypeStruct(scalars.shape, scalars.dtype),
        compiler_params=pltpu.CompilerParams(vmem_limit_bytes=1 << 20),
        cost_estimate=cost,
        name="after",
    )(scalars, *arrays)


def norm_kernel(unused, rows_ref, gain_ref, out_ref):
    hat = norm_parts(rows_ref[...].astype(jnp.float32))[0]
    out_ref[...] = (hat * gain_ref[...].reshape(1, -1)).astype(jnp.bfloat16)


def column_choice(chip, heads, size, lanes, width, transposed):
    shape, axis = ((lanes, width), 0) if transposed else ((width, lanes), 1)
    lane = lax.broadcasted_iota(jnp.int32, shape, axis)
    feature = lax.broadcasted_iota(jnp.int32, shape, 1 - axis)
    parts = []
    for head in range(heads):
        here = (feature == lane + (chip * heads + head) * size) & (lane < size)
        parts.append(jnp.where(here, 1.0, 0.0).astype(jnp.bfloat16))
    return jnp.concatenate(parts, axis=axis)


def choose_kernel(heads, size, scalars, wq_ref, wk_ref, wv_ref, *refs):
    query_rows, key_columns, value_rows, key_rows, value_columns, narrow_rows = refs
    width, chip = wq_ref.shape[0], scalars[0]
    tall = column_choice(chip, heads, size, 2 * size, width, True)
    flat = column_choice(chip, heads, size, 2 * size, width, False)
    narrow = column_choice(chip, heads, size, size, width, True)
    query_rows[...] = sent(nt_dot(tall, wq_ref[...]))
    key_columns[...] = sent(nn_dot(wk_ref[...], flat))
    value_columns[...] = sent(nn_dot(wv_ref[...], flat))
    for target, weight in ((value_rows, wv_ref), (key_rows, wk_ref), (narrow_rows, wq_ref)):
        target[...] = sent(nt_dot(narrow, weight[...]))


def choose(scalars, w_query, w_key, w_value, heads, size):
    width = w_query.shape[0]
    shapes = [
        (2 * heads * size, width),
        (width, 2 * heads * size),
        (heads * size, width),
        (heads * size, width),
        (width, 2 * heads * size),
        (heads * size, width),
    ]
    return call_whole(
        partial(choose_kernel, heads, size),
        [jax.ShapeDtypeStruct(shape, jnp.bfloat16) for shape in shapes],
        "choose",
        scalars,
        w_query,
        w_key,
        w_value,
        limit=24,
        ins=False,
    )


def project_kernel(blocks, own, heads, scale, meta, *refs):
    normed = refs[:blocks]
    wq_ref, wk_ref, wv_ref = refs[blocks : blocks + 3]
    q_ref, k_ref, vt_ref = refs[-3:]
    length = normed[0].shape[0]
    lanes = wk_ref.shape[1] // heads
    size = lanes // 2
    first_head = meta[blocks]
    for index in range(blocks):
        rows = normed[index][...]
        start = meta[index]
        span = slice(index * length, (index + 1) * length)
        keys = nn_dot(rows, wk_ref[...])
        vt_ref[:, span] = nt_dot(wv_ref[...], rows).astype(jnp.bfloat16)
        places = start + lax.broadcasted_iota(jnp.int32, (length, 1), 0)
        features = lax.broadcasted_iota(jnp.int32, (1, lanes), 1)
        for head in range(heads):
            wide_rows = slice(head * lanes, (head + 1) * lanes)
            extra = extra_values(places, features, first_head + head, size, False)
            k_ref[span, wide_rows] = (keys[:, wide_rows] + extra).astype(jnp.bfloat16)
        if index < own:
            queries = nt_dot(wq_ref[...], rows).astype(jnp.bfloat16).astype(jnp.float32) * scale
            places = start + lax.broadcasted_iota(jnp.int32, (1, length), 1)
            features = lax.broadcasted_iota(jnp.int32, (lanes, 1), 0)
            for head in range(heads):
                wide_rows = slice(head * lanes, (head + 1) * lanes)
                extra = extra_values(places, features, first_head + head, size, True)
                q_ref[wide_rows, span] = (queries[wide_rows] + extra).astype(jnp.bfloat16)


def project(meta, normed, wq, wk, wv, own, heads, scale, chips, filled=None):
    blocks, length = len(normed), normed[0].shape[0]
    wide_columns, share = wk.shape[1], wv.shape[0]
    last = 0 if filled is None else 2 * chips // blocks - 1
    last_own = 0 if filled is None else chips // own - 1
    aliases = {} if filled is None else {blocks + 4 + index: index for index in range(3)}
    return pl.pallas_call(
        partial(project_kernel, blocks, own, heads, scale),
        grid_spec=pltpu.PrefetchScalarGridSpec(
            num_scalar_prefetch=1,
            grid=(1,),
            in_specs=[whole(array.shape) for array in (*normed, wq, wk, wv)]
            + [pl.BlockSpec(memory_space=pl.ANY)] * (0 if filled is None else 3),
            out_specs=[
                pl.BlockSpec((wide_columns, own * length), lambda i, meta: (0, last_own)),
                pl.BlockSpec((blocks * length, wide_columns), lambda i, meta: (last, 0)),
                pl.BlockSpec((share, blocks * length), lambda i, meta: (0, last)),
            ],
        ),
        out_shape=[
            jax.ShapeDtypeStruct((wide_columns, chips * length), jnp.bfloat16),
            jax.ShapeDtypeStruct((2 * chips * length, wide_columns), jnp.bfloat16),
            jax.ShapeDtypeStruct((share, 2 * chips * length), jnp.bfloat16),
        ],
        input_output_aliases=aliases,
        compiler_params=pltpu.CompilerParams(vmem_limit_bytes=16 << 20),
        cost_estimate=NO_COST,
        name="project",
    )(meta, *normed, wq, wk, wv, *(filled or ()))


def project_back_kernel(blocks, unused, *refs):
    normed = refs[:blocks]
    wk_ref, wv_ref, kt_ref, v_ref = refs[blocks:]
    length = normed[0].shape[0]
    for index in range(blocks):
        rows = normed[index][...]
        span = slice(index * length, (index + 1) * length)
        kt_ref[:, span] = nt_dot(wk_ref[...], rows).astype(jnp.bfloat16)
        v_ref[span, :] = nn_dot(rows, wv_ref[...]).astype(jnp.bfloat16)


def project_back(scalars, normed, wk, wv):
    blocks, length = len(normed), normed[0].shape[0]
    return call_whole(
        partial(project_back_kernel, blocks),
        [
            jax.ShapeDtypeStruct((wk.shape[0], blocks * length), jnp.bfloat16),
            jax.ShapeDtypeStruct((blocks * length, wv.shape[1]), jnp.bfloat16),
        ],
        "project_back",
        scalars,
        *normed,
        wk,
        wv,
    )


def pair_mask(query_start, key_start, doc_line, block):
    query_place = query_start + lax.broadcasted_iota(jnp.int32, (1, block), 1)
    key_place = key_start + lax.broadcasted_iota(jnp.int32, (block, 1), 0)
    return (key_place <= query_place) & (key_place >= doc_line)


def attend_kernel(heads, block, first, steps, key_blocks, meta, doc_ref, q_ref, k_ref, vt_ref, *refs):
    o_ref, m_ref, l_ref = refs[-3:]
    count = (len(refs) - 3) // 3
    mixed_refs, lse_refs, ob_refs = (refs[count * part : count * (part + 1)] for part in range(3))
    step = first + pl.program_id(0)
    query_start = meta[step]
    doc_first, doc_last = meta[steps + key_blocks + step], meta[2 * steps + key_blocks + step]
    doc_line = doc_ref[...]
    size = o_ref.shape[0] // heads
    lanes = q_ref.shape[0] // heads
    m_ref[...] = jnp.full_like(m_ref, big_negative)
    l_ref[...] = jnp.zeros_like(l_ref)
    o_ref[...] = jnp.zeros_like(o_ref)

    def fold(slot, allowed):
        span = pl.ds(pl.multiple_of(slot * block, block), block)
        scores = [
            nn_dot(
                k_ref[span, head * lanes : (head + 1) * lanes],
                q_ref[head * lanes : (head + 1) * lanes, :],
            )
            for head in range(heads)
        ]
        if allowed is not None:
            scores = [jnp.where(allowed, part, big_negative) for part in scores]
        for head in range(heads):
            rows = slice(head * size, (head + 1) * size)
            old_peak = m_ref[head]
            new_peak = jnp.maximum(old_peak, jnp.max(scores[head], axis=0, keepdims=True))
            weights = jnp.exp(scores[head] - new_peak)
            fade = jnp.exp(old_peak - new_peak)
            m_ref[head] = new_peak
            l_ref[head] = l_ref[head] * fade + jnp.sum(weights, axis=0, keepdims=True)
            o_ref[rows, :] = o_ref[rows, :] * fade + nn_dot(
                vt_ref[rows, span], weights.astype(jnp.bfloat16)
            )

    def body(slot, carry):
        key_start = meta[steps + slot]
        live = (key_start <= query_start) & (key_start + block > doc_first)
        full = (key_start < query_start) & (key_start >= doc_last)

        @pl.when(full)
        def _():
            fold(slot, None)

        @pl.when(live & jnp.logical_not(full))
        def _():
            fold(slot, pair_mask(query_start, key_start, doc_line, block))

        return carry

    lax.fori_loop(0, key_blocks, body, 0)
    for index in range(count):

        @pl.when(step == first + index)
        def _(index=index):
            for head in range(heads):
                rows = slice(head * size, (head + 1) * size)
                total = l_ref[head]
                mixed = o_ref[rows, :] / total
                mixed_refs[index][rows, :] = mixed
                ob_refs[index][rows, :] = mixed.astype(jnp.bfloat16)
                lse_refs[index][head] = m_ref[head] + jnp.log(total)


def attend_back_kernel(heads, block, steps, key_blocks, scale, meta, doc_ref, q_ref, k_ref, kt_ref, v_ref, *refs):
    o_refs, lse_refs, g_refs = (refs[steps * part : steps * (part + 1)] for part in range(3))
    dq_ref, mine_ref, other_ref, acc_ref, pair_ref, delta_ref, g_ref, lse_ref = refs[3 * steps :]
    step = pl.program_id(0)
    query_start = meta[step]
    doc_first, doc_last = meta[steps + key_blocks + step], meta[2 * steps + key_blocks + step]
    doc_line = doc_ref[...]
    size = g_ref.shape[0] // heads
    lanes = q_ref.shape[0] // heads
    share = g_ref.shape[0]

    @pl.when(step == 0)
    def _():
        pair_ref[...] = jnp.zeros_like(pair_ref)

    acc_ref[...] = jnp.zeros_like(acc_ref)
    for index in range(steps):

        @pl.when(step == index)
        def _(index=index):
            g_ref[...] = g_refs[index][...]
            lse_ref[...] = lse_refs[index][...]
            for head in range(heads):
                rows = slice(head * size, (head + 1) * size)
                delta_ref[head] = jnp.sum(
                    g_refs[index][rows, :].astype(jnp.float32) * o_refs[index][rows, :],
                    axis=0,
                    keepdims=True,
                )

    def fold(slot, allowed):
        span = pl.ds(pl.multiple_of(slot * block, block), block)
        probs, grad_scores = [], []
        for head in range(heads):
            wide_rows = slice(head * lanes, (head + 1) * lanes)
            rows = slice(head * size, (head + 1) * size)
            probs.append(nn_dot(k_ref[span, wide_rows], q_ref[wide_rows, :]))
            grad_scores.append(
                nn_dot(v_ref[span, head * lanes : head * lanes + size], g_ref[rows, :])
            )
        for head in range(heads):
            part = jnp.exp(probs[head] - lse_ref[head])
            if allowed is not None:
                part = jnp.where(allowed, part, 0.0)
            grad_scores[head] = (part * (grad_scores[head] - delta_ref[head])).astype(jnp.bfloat16)
            probs[head] = part.astype(jnp.bfloat16)
        for head in range(heads):
            rows = slice(head * size, (head + 1) * size)
            value_rows = slice(share + head * size, share + (head + 1) * size)
            query_rows = slice(head * lanes, head * lanes + size)
            pair_ref[value_rows, span] += nt_dot(g_ref[rows, :], probs[head])
            pair_ref[rows, span] += nt_dot(q_ref[query_rows, :], grad_scores[head])
            acc_ref[rows, :] += nn_dot(kt_ref[rows, span], grad_scores[head])

    def body(slot, carry):
        key_start = meta[steps + slot]
        live = (key_start <= query_start) & (key_start + block > doc_first)
        full = (key_start < query_start) & (key_start >= doc_last)

        @pl.when(full)
        def _():
            fold(slot, None)

        @pl.when(live & jnp.logical_not(full))
        def _():
            fold(slot, pair_mask(query_start, key_start, doc_line, block))

        return carry

    lax.fori_loop(0, key_blocks, body, 0)
    dq_ref[...] = (acc_ref[...] * scale).astype(dq_ref.dtype)

    @pl.when(step == steps - 1)
    def _():
        for index in range(steps):
            late = index == steps - 1
            mine = 2 * index if late else index
            other = 2 * index + 1 if late else steps - 1 + index
            span = slice(index * block, (index + 1) * block)
            mine_ref[:, span] = pair_ref[:, mine * block : (mine + 1) * block]
            other_ref[:, span] = pair_ref[:, other * block : (other + 1) * block].astype(
                jnp.bfloat16
            )


def whole(shape):
    return pl.BlockSpec(shape, lambda *index: (0,) * len(shape))


def attend(meta, doc_line, q_ext, k_ext, v_t, heads, block, first, last):
    wide_rows, queries = q_ext.shape
    share, keys = v_t.shape
    steps, key_blocks, count = queries // block, keys // block, last - first
    direct = pl.BlockSpec(memory_space=pltpu.VMEM)
    outs = pl.pallas_call(
        partial(attend_kernel, heads, block, first, steps, key_blocks),
        grid_spec=pltpu.PrefetchScalarGridSpec(
            num_scalar_prefetch=1,
            grid=(count,),
            in_specs=[
                pl.BlockSpec((1, block), lambda i, meta: (0, first + i)),
                pl.BlockSpec((wide_rows, block), lambda i, meta: (0, first + i)),
                direct,
                direct,
            ],
            out_specs=[direct] * (3 * count),
            scratch_shapes=[
                pltpu.VMEM((share, block), jnp.float32),
                pltpu.VMEM((heads, 1, block), jnp.float32),
                pltpu.VMEM((heads, 1, block), jnp.float32),
            ],
        ),
        out_shape=[jax.ShapeDtypeStruct((share, block), jnp.float32)] * count
        + [jax.ShapeDtypeStruct((heads, 1, block), jnp.float32)] * count
        + [jax.ShapeDtypeStruct((share, block), jnp.bfloat16)] * count,
        compiler_params=pltpu.CompilerParams(vmem_limit_bytes=12 << 20),
        cost_estimate=NO_COST,
        name="attend",
    )(meta, doc_line, q_ext, k_ext, v_t)
    return outs[:count], outs[count : 2 * count], outs[2 * count :]


def attend_back(meta, doc_line, q_ext, grads, mixed, lse, k_ext, k_t, v_ext, heads, block, scale):
    wide_rows, queries = q_ext.shape
    share, keys = k_t.shape
    steps, key_blocks = queries // block, keys // block
    direct = pl.BlockSpec(memory_space=pltpu.VMEM)
    return pl.pallas_call(
        partial(attend_back_kernel, heads, block, steps, key_blocks, scale),
        grid_spec=pltpu.PrefetchScalarGridSpec(
            num_scalar_prefetch=1,
            grid=(steps,),
            in_specs=[
                pl.BlockSpec((1, block), lambda i, meta: (0, i)),
                pl.BlockSpec((wide_rows, block), lambda i, meta: (0, i)),
            ]
            + [direct] * (3 + 3 * steps),
            out_specs=[pl.BlockSpec((share, block), lambda i, meta: (0, i)), direct, direct],
            scratch_shapes=[
                pltpu.VMEM((share, block), jnp.float32),
                pltpu.VMEM((2 * share, keys), jnp.float32),
                pltpu.VMEM((heads, 1, block), jnp.float32),
                pltpu.VMEM((share, block), jnp.bfloat16),
                pltpu.VMEM((heads, 1, block), jnp.float32),
            ],
        ),
        out_shape=[
            jax.ShapeDtypeStruct((share, queries), jnp.bfloat16),
            jax.ShapeDtypeStruct((2 * share, keys // 2), jnp.float32),
            jax.ShapeDtypeStruct((2 * share, keys // 2), jnp.bfloat16),
        ],
        compiler_params=pltpu.CompilerParams(vmem_limit_bytes=20 << 20),
        cost_estimate=HIGH_COST,
        name="attend_back",
    )(meta, doc_line, q_ext, k_ext, k_t, v_ext, *mixed, *lse, *grads)


def join_kernel(chips, unused, dq_ref, mine_ref, other_ref, *out_refs):
    share = dq_ref.shape[0]
    block = dq_ref.shape[1] // chips
    for step in range(chips):
        span = slice(step * block, (step + 1) * block)
        pair = (mine_ref[:, span] + other_ref[:, span].astype(jnp.float32)).astype(jnp.bfloat16)
        out_refs[step][:share, :] = dq_ref[:, span]
        out_refs[step][share:, :] = pair


def join_parts(scalars, dq, mine, other, chips):
    rows, block = dq.shape[0] + mine.shape[0], dq.shape[1] // chips
    return call_whole(
        partial(join_kernel, chips),
        [jax.ShapeDtypeStruct((rows, block), jnp.bfloat16)] * chips,
        "join",
        scalars,
        dq,
        mine,
        other,
    )


def head_grads_kernel(chips, per, scalars, *refs):
    normed, grads = refs[:chips], refs[chips : 2 * chips]
    wq_ref, wk_ref, wv_ref, gain_ref, inner_ref, feed_ref, hidden_ref = refs[2 * chips : 2 * chips + 7]
    perm_ref, keep_ref, send_ref = refs[2 * chips + 7 :]
    first_core = scalars[1] == 0
    share, model_width = wq_ref.shape
    own = nn_dot(grads[0][...], normed[0][...])
    for step in range(1, chips):
        own = own + nn_dot(grads[step][...], normed[step][...])
    attend = jnp.zeros((1, model_width), jnp.float32)
    for index, weight in enumerate((wq_ref, wk_ref, wv_ref)):
        part = own[index * share : (index + 1) * share] * weight[...].astype(jnp.float32)
        attend = attend + jnp.sum(part, axis=0, keepdims=True)
    gains = [attend / gain_ref[...], inner_ref[...], feed_ref[...], hidden_ref[...]]
    own = nt_dot(perm_ref[...], own.astype(jnp.bfloat16))
    chunks, _, width = keep_ref.shape
    columns = own.shape[1]
    part = sum(row.shape[1] for row in gains) // (2 * chunks)
    lines = -(-part // 128)
    gains = jnp.concatenate(gains + [jnp.zeros((1, 128), jnp.float32)], axis=1)

    def device_gains(device):
        starts = [device * part + 128 * line for line in range(lines)]
        rows = [gains[:, start : start + 128] for start in starts]
        return jnp.concatenate(rows, axis=0).astype(jnp.bfloat16)

    for target in (keep_ref, send_ref):
        target[:, :, columns:] = jnp.zeros((chunks, per, width - columns), jnp.bfloat16)
    for chunk in range(chunks):
        even, odd = device_gains(2 * chunk), device_gains(2 * chunk + 1)
        keep_ref[chunk, :lines, width - 128 :] = jnp.where(first_core, even, odd)
        send_ref[chunk, :lines, width - 128 :] = jnp.where(first_core, odd, even)
        for which, target in enumerate((keep_ref, send_ref)):
            first = (which * chunks + chunk) * per
            target[chunk, :, :columns] = own[first : first + per].astype(jnp.bfloat16)


def head_grads(scalars, normed, grads, weights, gain, late_gains, perm, per):
    width = perm.shape[0]
    out = jax.ShapeDtypeStruct((width // (2 * per), per, width), jnp.bfloat16)
    return call_whole(
        partial(head_grads_kernel, len(grads), per),
        [out, out],
        "head_grads",
        scalars,
        *normed,
        *grads,
        *weights,
        gain,
        *late_gains,
        perm,
        limit=24,
    )


def norm_parts(values):
    shifted = values - jnp.mean(values, axis=-1, keepdims=True)
    rate = lax.rsqrt(jnp.mean(shifted * shifted, axis=-1, keepdims=True) + 1e-05)
    return shifted * rate, rate


def norm_back(grad, hat, rate, gain):
    scaled = grad * gain
    mean_scaled = jnp.mean(scaled, axis=-1, keepdims=True)
    mean_product = jnp.mean(scaled * hat, axis=-1, keepdims=True)
    return (
        rate * (scaled - mean_scaled - hat * mean_product),
        jnp.sum(grad * hat, axis=0, keepdims=True),
    )


def middle_kernel(chips, tiles, position, *refs):
    mixed = refs[:chips]
    tokens_ref, cot_ref, wout_ref, wup_ref, wdown_ref, ginner_ref, gfeed_ref, ghidden_ref = refs[
        chips : chips + 8
    ]
    result_ref, gmid_ref, gmid_b_ref = refs[chips + 8 : chips + 11]
    go_refs = refs[chips + 11 : 2 * chips + 11]
    (
        z_ref,
        h2_ref,
        bent_out,
        pre_out,
        dinner_ref,
        dfeed_ref,
        dhidden_ref,
        swap_ref,
        work_ref,
        column_ref,
        zhat_ref,
        hat_ref,
        act_ref,
        slope_ref,
        dact_ref,
        acc_ref,
        stat_ref,
    ) = refs[2 * chips + 11 :]
    step = pl.program_id(0)
    chip = position[0]
    block, model_width = tokens_ref.shape
    share = model_width // chips
    tile = wdown_ref.shape[0]
    hidden = tile * tiles
    root = math.sqrt(2.0 / math.pi)
    phase, index = step // tiles, step % tiles
    lanes = stat_ref.shape[2]
    groups = tile // lanes

    def by_rows(body):
        body(slice(None))

    def spread(stat):
        return jnp.concatenate([stat] * groups, axis=1)

    def gathered_lanes(values):
        total = values[:, :lanes]
        for group in range(1, groups):
            total = total + values[:, group * lanes : (group + 1) * lanes]
        return total

    def lane_sum(values):
        return jnp.broadcast_to(jnp.sum(values, axis=-1, keepdims=True), values.shape)

    def column_sums(values):
        total = values[:8]
        for first in range(8, values.shape[0], 8):
            total = total + values[first : first + 8]
        return total

    def norm_rows(values):
        shifted = values - spread(lane_sum(gathered_lanes(values)) / tile)
        rate = lax.rsqrt(lane_sum(gathered_lanes(shifted * shifted)) / tile + 1e-05)
        return shifted * spread(rate), rate

    def norm_rows_back(grad, hat, rate, gain):
        scaled = grad * gain
        mean_scaled = lane_sum(gathered_lanes(scaled)) / tile
        mean_product = lane_sum(gathered_lanes(scaled * hat)) / tile
        return spread(rate) * (scaled - spread(mean_scaled) - hat * spread(mean_product))

    @pl.when(step == 0)
    def _():
        for near in range(chips):
            start = pl.multiple_of(share * lax.rem(chip + near, chips), share)
            swap_ref[pl.ds(start, share), :] = mixed[near][...].astype(jnp.float32)
        work_ref[...] = swap_ref[...].T

        def first_norm(rows):
            zhat, zrate = norm_rows(work_ref[rows, :])
            zhat_ref[rows, :] = zhat
            stat_ref[0, rows, :] = zrate
            z_ref[rows, :] = (zhat * ginner_ref[...]).astype(jnp.bfloat16)

        by_rows(first_norm)
        work_ref[...] = nn_dot(z_ref[...], wout_ref[...])

        def second_norm(rows):
            mid = tokens_ref[rows, :].astype(jnp.float32) + work_ref[rows, :]
            acc_ref[rows, :] = mid
            hat, rate = norm_rows(mid)
            hat_ref[rows, :] = hat
            stat_ref[1, rows, :] = rate
            h2_ref[rows, :] = (hat * gfeed_ref[...]).astype(jnp.bfloat16)

        by_rows(second_norm)
        for stat in range(3, 7):
            stat_ref[stat] = jnp.zeros_like(stat_ref[stat])

    @pl.when(phase == 0)
    def _():
        work_ref[...] = nn_dot(h2_ref[...], wup_ref[...])

        def bend_rows(rows):
            u = work_ref[rows, :]
            squared = u * u
            bend = jnp.tanh(root * (u + 0.044715 * u * squared))
            act_ref[index, rows, :] = 0.5 * u * (1.0 + bend)
            slope_ref[index, rows, :] = 0.5 * (1.0 + bend) + 0.5 * u * (1.0 - bend * bend) * root * (
                1.0 + 3.0 * 0.044715 * squared
            )

        by_rows(bend_rows)

        @pl.when(index == 0)
        def _():
            def pivot(rows):
                stat_ref[2, rows, :] = lane_sum(gathered_lanes(act_ref[0, rows, :])) / tile

            by_rows(pivot)

        def sums(rows):
            off = act_ref[index, rows, :] - spread(stat_ref[2, rows, :])
            stat_ref[3, rows, :] += gathered_lanes(off)
            stat_ref[4, rows, :] += gathered_lanes(off * off)

        by_rows(sums)

    @pl.when(step == tiles)
    def _():
        drift = lane_sum(stat_ref[3]) / hidden
        stat_ref[2] = stat_ref[2] + drift
        stat_ref[4] = lax.rsqrt(
            jnp.maximum(lane_sum(stat_ref[4]) / hidden - drift * drift, 0.0) + 1e-05
        )

    @pl.when(phase == 1)
    def _():
        def hidden_rows(rows):
            hat = (act_ref[index, rows, :] - spread(stat_ref[2, rows, :])) * spread(
                stat_ref[4, rows, :]
            )
            act_ref[index, rows, :] = hat
            bent_out[rows, :] = (hat * ghidden_ref[...]).astype(jnp.bfloat16)

        by_rows(hidden_rows)
        work_ref[...] = nt_dot(cot_ref[...], wdown_ref[...])
        acc_ref[...] += nn_dot(bent_out[...], wdown_ref[...])
        column_ref[...] = jnp.zeros_like(column_ref)

        def grad_rows(rows):
            hat, grad = act_ref[index, rows, :], work_ref[rows, :]
            column_ref[...] += column_sums(grad * hat)
            scaled = grad * ghidden_ref[...]
            dact_ref[index, rows, :] = scaled
            stat_ref[5, rows, :] += gathered_lanes(scaled)
            stat_ref[6, rows, :] += gathered_lanes(scaled * hat)

        by_rows(grad_rows)
        dhidden_ref[...] = jnp.sum(column_ref[...], axis=0, keepdims=True)

    @pl.when(step == 2 * tiles)
    def _():
        result_ref[...] = acc_ref[...].astype(jnp.bfloat16)
        acc_ref[...] = jnp.zeros_like(acc_ref)
        stat_ref[5] = lane_sum(stat_ref[5]) / hidden
        stat_ref[6] = lane_sum(stat_ref[6]) / hidden

    @pl.when(phase == 2)
    def _():
        def pre_rows(rows):
            inner = (
                dact_ref[index, rows, :]
                - spread(stat_ref[5, rows, :])
                - act_ref[index, rows, :] * spread(stat_ref[6, rows, :])
            )
            pre_out[rows, :] = (
                spread(stat_ref[4, rows, :]) * inner * slope_ref[index, rows, :]
            ).astype(jnp.bfloat16)

        by_rows(pre_rows)
        acc_ref[...] += nt_dot(pre_out[...], wup_ref[...])

    @pl.when(step == 3 * tiles - 1)
    def _():
        column_ref[...] = jnp.zeros_like(column_ref)

        def middle_rows(rows):
            grad, hat = acc_ref[rows, :], hat_ref[rows, :]
            column_ref[...] += column_sums(grad * hat)
            gmid = cot_ref[rows, :].astype(jnp.float32) + norm_rows_back(
                grad, hat, stat_ref[1, rows, :], gfeed_ref[...]
            )
            gmid_ref[rows, :] = gmid
            gmid_b_ref[rows, :] = gmid.astype(jnp.bfloat16)

        by_rows(middle_rows)
        dfeed_ref[...] = jnp.sum(column_ref[...], axis=0, keepdims=True)
        work_ref[...] = nt_dot(gmid_b_ref[...], wout_ref[...])
        column_ref[...] = jnp.zeros_like(column_ref)

        def inner_rows(rows):
            grad, hat = work_ref[rows, :], zhat_ref[rows, :]
            column_ref[...] += column_sums(grad * hat)
            work_ref[rows, :] = norm_rows_back(grad, hat, stat_ref[0, rows, :], ginner_ref[...])

        by_rows(inner_rows)
        dinner_ref[...] = jnp.sum(column_ref[...], axis=0, keepdims=True)
        swap_ref[...] = work_ref[...].T
        for near in range(chips):
            start = pl.multiple_of(share * lax.rem(chip + near, chips), share)
            go_refs[near][...] = swap_ref[pl.ds(start, share), :].astype(jnp.bfloat16)


def middle(position, mixed, tokens, cotangent, w_out, w_up, w_down, gains):
    chips = len(mixed)
    block, model_width = tokens.shape
    hidden = w_up.shape[1]
    tile = model_width
    tiles = hidden // tile
    share = model_width // chips
    last = tiles - 1

    def up_index(i, pos):
        return (0, jnp.where(i < tiles, i, jnp.where(i < 2 * tiles, last, i - 2 * tiles)))

    def down_index(i, pos):
        return (jnp.clip(i - tiles, 0, last), 0)

    def hidden_index(i, pos):
        return (0, jnp.clip(i - tiles, 0, last))

    def pre_index(i, pos):
        return (0, jnp.clip(i - 2 * tiles, 0, last))

    def f32(*shape):
        return pltpu.VMEM(shape, jnp.float32)

    row, rows = (1, model_width), (block, model_width)
    narrow = jax.ShapeDtypeStruct(rows, jnp.bfloat16)
    return pl.pallas_call(
        partial(middle_kernel, chips, tiles),
        grid_spec=pltpu.PrefetchScalarGridSpec(
            num_scalar_prefetch=1,
            grid=(3 * tiles,),
            in_specs=[whole((share, block))] * chips
            + [
                whole(rows),
                whole(rows),
                whole((model_width, model_width)),
                pl.BlockSpec((model_width, tile), up_index),
                pl.BlockSpec((tile, model_width), down_index),
                whole(row),
                whole(row),
                pl.BlockSpec((1, tile), hidden_index),
            ],
            out_specs=[whole(rows)] * 3
            + [whole((share, block))] * chips
            + [
                whole(rows),
                whole(rows),
                pl.BlockSpec((block, tile), hidden_index),
                pl.BlockSpec((block, tile), pre_index),
                whole(row),
                whole(row),
                pl.BlockSpec((1, tile), hidden_index),
            ],
            scratch_shapes=[
                f32(model_width, block),
                f32(block, tile),
                f32(8, tile),
                f32(block, model_width),
                f32(block, model_width),
                f32(tiles, block, tile),
                f32(tiles, block, tile),
                f32(tiles, block, tile),
                f32(block, model_width),
                f32(7, block, 128),
            ],
        ),
        out_shape=[narrow, jax.ShapeDtypeStruct(rows, jnp.float32), narrow]
        + [jax.ShapeDtypeStruct((share, block), jnp.bfloat16)] * chips
        + [
            narrow,
            narrow,
            jax.ShapeDtypeStruct((block, hidden), jnp.bfloat16),
            jax.ShapeDtypeStruct((block, hidden), jnp.bfloat16),
            jax.ShapeDtypeStruct(row, jnp.float32),
            jax.ShapeDtypeStruct(row, jnp.float32),
            jax.ShapeDtypeStruct((1, hidden), jnp.float32),
        ],
        compiler_params=pltpu.CompilerParams(vmem_limit_bytes=26 << 20),
        cost_estimate=NO_COST,
        name="middle",
    )(position, *mixed, tokens, cotangent, w_out, w_up, w_down, *gains)


def down_kernel(per, position, bent_ref, cot_ref, keep_ref, send_ref):
    first_core = position[1] == 0
    parts = bent_ref.shape[1] // (2 * per)
    first = pl.program_id(0) * parts
    grad = lax.dot_general(
        bent_ref[...], cot_ref[...], (((0,), (0,)), ((), ())), preferred_element_type=jnp.float32
    ).astype(jnp.bfloat16)
    for part in range(parts):
        even = grad[2 * per * part : 2 * per * part + per]
        odd = grad[2 * per * part + per : 2 * per * (part + 1)]
        keep_ref[first + part] = jnp.where(first_core, even, odd)
        send_ref[first + part] = jnp.where(first_core, odd, even)


def down_grad(position, bent, cotangent, per):
    (block, hidden), model_width = bent.shape, cotangent.shape[1]
    tiles, chunks = hidden // model_width, hidden // (2 * per)
    out = jax.ShapeDtypeStruct((chunks, per, model_width), jnp.bfloat16)
    out_spec = pl.BlockSpec(memory_space=pltpu.VMEM)
    return pl.pallas_call(
        partial(down_kernel, per),
        grid_spec=pltpu.PrefetchScalarGridSpec(
            num_scalar_prefetch=1,
            grid=(tiles,),
            in_specs=[
                pl.BlockSpec((block, model_width), lambda i, pos: (0, i)),
                pl.BlockSpec(memory_space=pltpu.VMEM),
            ],
            out_specs=[out_spec, out_spec],
        ),
        out_shape=[out, out],
        compiler_params=pltpu.CompilerParams(vmem_limit_bytes=20 << 20),
        cost_estimate=NO_COST,
        name="down_grad",
    )(position, bent, cotangent)


def up_out_kernel(tiles, position, h2_ref, pre_ref, z_ref, gmid_ref, perm_ref, keep_ref, send_ref, left_ref):
    step = pl.program_id(0)
    chunks = keep_ref.shape[0]
    per = perm_ref.shape[0] // (2 * chunks)
    place = pl.ds(pl.multiple_of(step * per, per), per)

    @pl.when(step == 0)
    def _():
        left_ref[...] = nt_dot(perm_ref[...], h2_ref[...]).astype(jnp.bfloat16)

    def store(right):
        grad = nn_dot(left_ref[...], right)
        for chunk in range(chunks):
            keep_ref[chunk, place] = grad[chunk * per : (chunk + 1) * per].astype(jnp.bfloat16)
            first = (chunks + chunk) * per
            send_ref[chunk, place] = grad[first : first + per].astype(jnp.bfloat16)

    @pl.when(step < tiles)
    def _():
        store(pre_ref[...])

    @pl.when(step == tiles)
    def _():
        left_ref[...] = nt_dot(perm_ref[...], z_ref[...]).astype(jnp.bfloat16)
        store(gmid_ref[...])


def up_out_grad(position, h2, pre, z, gmid, perm, per):
    (block, hidden), model_width = pre.shape, h2.shape[1]
    tiles, chunks = hidden // model_width, model_width // (2 * per)
    out = jax.ShapeDtypeStruct((chunks, per * (tiles + 1), model_width), jnp.bfloat16)
    out_spec = pl.BlockSpec(memory_space=pltpu.VMEM)
    return pl.pallas_call(
        partial(up_out_kernel, tiles),
        grid_spec=pltpu.PrefetchScalarGridSpec(
            num_scalar_prefetch=1,
            grid=(tiles + 1,),
            in_specs=[
                pl.BlockSpec(memory_space=pltpu.VMEM),
                pl.BlockSpec((block, model_width), lambda i, pos: (0, jnp.minimum(i, tiles - 1))),
            ]
            + [pl.BlockSpec(memory_space=pltpu.VMEM)] * 3,
            out_specs=[out_spec, out_spec],
            scratch_shapes=[pltpu.VMEM((model_width, block), jnp.bfloat16)],
        ),
        out_shape=[out, out],
        compiler_params=pltpu.CompilerParams(vmem_limit_bytes=20 << 20),
        cost_estimate=NO_COST,
        name="up_out_grad",
    )(position, h2, pre, z, gmid, perm)


def final_kernel(chips, position, *refs):
    homes = refs[:chips]
    (
        tokens_ref,
        gmid_ref,
        wq_ref,
        wk_ref,
        wv_ref,
        gain_ref,
        out_ref,
        swap_ref,
    ) = refs[chips:]
    chip = position[0]
    block, model_width = tokens_ref.shape
    share = model_width // chips
    total = jnp.zeros((block, model_width), jnp.float32)
    for index, weight in enumerate((wq_ref, wk_ref, wv_ref)):
        for near in range(chips):
            start = pl.multiple_of(share * lax.rem(chip + near, chips), share)
            swap_ref[pl.ds(start, share), :] = homes[near][
                index * share : (index + 1) * share, :
            ].astype(jnp.float32)
        total = total + nt_dot(swap_ref[...].T.astype(jnp.bfloat16), weight[...])
    hat, rate = norm_parts(tokens_ref[...].astype(jnp.float32))
    back = norm_back(total, hat, rate, gain_ref[...])[0]
    out_ref[...] = (gmid_ref[...] + back).astype(jnp.bfloat16)


def final(position, homes, tokens, gmid, w_query, w_key, w_value, gain):
    block, model_width = tokens.shape
    return call_whole(
        partial(final_kernel, len(homes)),
        [jax.ShapeDtypeStruct((block, model_width), jnp.bfloat16)],
        "final",
        position,
        *homes,
        tokens,
        gmid,
        w_query,
        w_key,
        w_value,
        gain,
        scratch=[pltpu.VMEM((model_width, block), jnp.float32)],
        outs=False,
    )[0]


def chip_shift(value, steps):
    count = lax.axis_size("seq")
    return lax.ppermute(value, "seq", [(i, (i + 2 * steps) % count) for i in range(count)])


def seq_swap(value, bit):
    return lax.ppermute(value, "seq", [(i, i ^ bit) for i in range(lax.axis_size("seq"))])


def row_swap(value, bit):
    return lax.ppermute(value, "row", [(i, i ^ bit) for i in range(lax.axis_size("row"))])


def sent(array):
    return array.astype(jnp.bfloat16)


def wide(array):
    return array.astype(jnp.float32)


def outgoing_kernel(kept, scalars, *refs):
    low_ref, high_ref = refs[-2:]
    low_bit, high_bit = scalars[2], scalars[3]
    if not kept:
        low_bit, high_bit = 1 - low_bit, 1 - high_bit
    half = refs[0].shape[2] // 2
    first = 0
    for group in range(len(refs) // 2 - 1):
        keep, other = refs[2 * group : 2 * group + 2]
        rows = slice(first, first + keep.shape[3])
        for side in range(2):
            low_ref[side, :, rows] = sent(
                wide(keep[side, low_bit, :half]) + wide(other[side, low_bit, :half])
            )
            high_ref[side, :, rows] = sent(
                wide(keep[high_bit, side, half:]) + wide(other[high_bit, side, half:])
            )
        first += keep.shape[3]


def outgoing(scalars, groups, kept=False):
    arrays = [array for group in groups for array in group]
    shape = groups[0][0].shape
    rows = sum(keep.shape[3] for keep, _ in groups)
    out = jax.ShapeDtypeStruct((2, shape[2] // 2, rows, shape[4]), jnp.bfloat16)
    return call_whole(
        partial(outgoing_kernel, kept),
        [out, out],
        "kept" if kept else "outgoing",
        scalars,
        *arrays,
    )


def halfway_kernel(groups, scalars, *refs):
    ins, outs = refs[: 4 * groups], refs[4 * groups :]
    low_bit, high_bit = scalars[2], scalars[3]
    low_keep, low_send, high_keep, high_send = outs
    first = 0
    for group in range(groups):
        low, high, low_in, high_in = ins[4 * group : 4 * group + 4]
        rows = slice(first, first + low.shape[2])
        for target, side in ((low_keep, high_bit), (low_send, 1 - high_bit)):
            target[:, rows] = sent(wide(low[side]) + wide(low_in[side]))
        for target, side in ((high_keep, low_bit), (high_send, 1 - low_bit)):
            target[:, rows] = sent(wide(high[side]) + wide(high_in[side]))
        first += low.shape[2]


def halfway(scalars, groups):
    arrays = [array for group in groups for array in group]
    rows = sum(group[0].shape[2] for group in groups)
    out = jax.ShapeDtypeStruct((arrays[0].shape[1], rows, arrays[0].shape[3]), jnp.bfloat16)
    return call_whole(
        partial(halfway_kernel, len(groups)), [out] * 4, "halfway", scalars, *arrays, limit=12
    )


def split_kernel(chips, groups, scalars, *refs):
    ins, outs = refs[: 4 * groups], refs[4 * groups : 4 * groups + chips]
    all_ref = refs[-1]
    half = chips // 2
    first = 0
    for group in range(groups):
        low_keep, low_in, high_keep, high_in = ins[4 * group : 4 * group + 4]
        rows = slice(first, first + low_in.shape[1])
        all_ref[:half, rows] = sent(wide(low_keep[...]) + wide(low_in[...]))
        all_ref[half:, rows] = sent(wide(high_keep[...]) + wide(high_in[...]))
        first += low_in.shape[1]
    for step in range(chips):
        outs[step][...] = all_ref[lax.rem(scalars[0] + step, chips)]


def split(scalars, groups, chips):
    arrays = [array for group in groups for array in group]
    rows = sum(group[0].shape[1] for group in groups)
    width = arrays[0].shape[2]
    return call_whole(
        partial(split_kernel, chips, len(groups)),
        [jax.ShapeDtypeStruct((rows, width), jnp.bfloat16)] * chips,
        "split",
        scalars,
        *arrays,
        scratch=[pltpu.VMEM((chips, rows, width), jnp.bfloat16)],
    )


def lay_flat(target, values, first, step):
    for piece in range(values.shape[1] // 128):
        target[pl.ds(first + piece, values.shape[0], step), :] = values[
            :, 128 * piece : 128 * (piece + 1)
        ]


def finish_kernel(chips, per, factor, scalars, *refs):
    arrived = refs[:chips]
    down_ref, up_ref, out_ref = refs[chips:]
    width = arrived[0].shape[1]
    pieces = width // 128
    tiles = up_ref.shape[0] * 128 // (per * width)
    down_rows = down_ref.shape[0] * 128 // width

    def total(first, rows):
        result = wide(arrived[0][first : first + rows, :])
        for part in arrived[1:]:
            result = result + wide(part[first : first + rows, :])
        return result * factor

    lay_flat(down_ref, total(0, down_rows), 0, pieces)
    for tile in range(tiles):
        lay_flat(up_ref, total(down_rows + tile * per, per), tile * pieces, tiles * pieces)
    lay_flat(out_ref, total(down_rows + tiles * per, per), 0, pieces)


def finish_heads_kernel(chips, share, factor, scalars, *refs):
    heads_in = refs[:chips]
    query_ref, key_ref, value_ref, gains_ref, heads_ref = refs[chips:]
    chip, pieces = scalars[0], heads_in[0].shape[1] // 128
    gains = wide(heads_in[0][:8, -128:])
    for part in heads_in[1:]:
        gains = gains + wide(part[:8, -128:])
    gains = gains * factor
    part = gains_ref.shape[0]
    for line in range(-(-part // 128)):
        stop = min(part, 128 * (line + 1))
        gains_ref[128 * line : stop] = gains[line, : stop - 128 * line]
    for step in range(chips):
        heads_ref[lax.rem(chip - step + chips, chips)] = wide(heads_in[step][:, : 3 * share])
    for index, target in enumerate((query_ref, key_ref, value_ref)):
        values = jnp.concatenate(
            [heads_ref[near][:, index * share : (index + 1) * share] for near in range(chips)], axis=1
        )
        lay_flat(target, values * factor, 0, pieces)


def finish(scalars, arrived, hidden, gains_part, per, share, factor):
    chips, width = len(arrived) // 2, arrived[0].shape[1]
    square = jax.ShapeDtypeStruct((per * width // 128, 128), jnp.float32)
    large = jax.ShapeDtypeStruct((per * hidden // 128, 128), jnp.float32)
    first = call_whole(
        partial(finish_kernel, chips, per, factor),
        [large, large, square],
        "finish",
        scalars,
        *arrived[:chips],
        outs=False,
    )
    first, heads_in = lax.optimization_barrier((first, list(arrived[chips:])))
    last = call_whole(
        partial(finish_heads_kernel, chips, share, factor),
        [square, square, square, jax.ShapeDtypeStruct((gains_part,), jnp.float32)],
        "finish_heads",
        scalars,
        *heads_in,
        scratch=[pltpu.VMEM((chips, per, 3 * share), jnp.float32)],
        outs=False,
    )
    return [*first, *last]


def gathered(rows):
    behind, ahead = chip_shift(rows, 1), chip_shift(rows, -1)
    up = [(2 * i + core, 2 * i + 2 + core) for i in (1, 2) for core in (0, 1)]
    down = [(2 * i + core, 2 * i - 2 + core) for i in (1, 2) for core in (0, 1)]
    across = (lax.ppermute(ahead, "seq", down), lax.ppermute(behind, "seq", up))
    return behind, ahead, across


def fast_local(
    tokens,
    lengths,
    w_query,
    w_key,
    w_value,
    w_out,
    w_up,
    w_down,
    gain_attend,
    gain_inner,
    gain_feed,
    gain_hidden,
    cotangent,
):
    block, model_width = tokens.shape
    hidden = w_up.shape[1]
    size = model_width // HEADS
    lanes = 2 * size
    scale = size ** (-0.5)
    seq_devices, row_devices = lax.axis_size("seq"), lax.axis_size("row")
    chips = seq_devices // 2
    heads = HEADS // chips
    share = heads * size
    spread = heads * lanes
    parts = row_devices * seq_devices
    position, row = lax.axis_index("seq"), lax.axis_index("row")
    chip, core = position // 2, position % 2
    place = jnp.stack([chip, core, row % 2, row // 2]).astype(jnp.int32)
    bounds = jnp.cumsum(lengths[0])[:-1]
    factor = 1.0 / math.sqrt(block * parts)

    normed_b = call_whole(
        norm_kernel,
        [jax.ShapeDtypeStruct(tokens.shape, jnp.bfloat16)],
        "norm",
        jnp.zeros((1,), jnp.int32),
        tokens,
        gain_attend,
        ins=False,
    )[0]
    behind, ahead, across = gathered(normed_b)

    order = [step for step in range(chips) if step != chips // 2] + [chips // 2]
    slots = [order.index(step) for step in range(chips)]
    chip_ids = (chip - jnp.asarray(order, jnp.int32)) % chips
    query_starts = block * (2 * chip_ids + core)
    other_starts = block * (2 * chip_ids + 1 - core)
    key_starts = jnp.concatenate(
        [query_starts[:-1], other_starts[:-1], query_starts[-1:], other_starts[-1:]]
    )
    in_block = jnp.arange(block, dtype=jnp.int32)[None, :]
    query_places = (query_starts[:, None] + in_block).reshape(-1)
    doc_line = jnp.max(jnp.where(bounds[:, None] <= query_places[None, :], bounds[:, None], 0), axis=0)
    meta = jnp.concatenate(
        [query_starts, key_starts, doc_line.reshape(chips, block)[:, 0], doc_line.reshape(chips, block)[:, -1]]
    )
    doc_line = doc_line[None, :]

    feature = jnp.arange(model_width, dtype=jnp.int32)
    per = model_width // parts
    chunk, inside = feature // per, feature % per
    chunks = parts // 2
    parity = jnp.where(chunk < chunks, core, 1 - core)
    wanted = (2 * (chunk % chunks) + parity) * per + inside
    perm = (wanted[:, None] == feature[None, :]).astype(jnp.bfloat16)

    gains_share = (3 * model_width + hidden) // parts
    gains_rows = -(-gains_share // 128)
    first_head = heads * chip[None]
    small = (
        jnp.concatenate([query_starts[:-1], other_starts[:-1], first_head]),
        jnp.concatenate([query_starts[-1:], other_starts[-1:], first_head]),
        meta,
        doc_line,
        gain_attend[None, :],
        gain_inner[None, :],
        gain_feed[None, :],
        gain_hidden[None, :],
        place,
        perm,
    )
    small = lax.optimization_barrier(small)
    starts, late_starts, meta, doc_line, gain_first, gain_inner, gain_feed, gain_hidden = small[:8]
    place, perm = small[8:]
    early = choose(place, w_query, w_key, w_value, heads, size)
    behind, early = lax.optimization_barrier((behind, early))
    wq_wide, wk_wide, wv_rows, wk_rows, wv_wide, wq_rows = early
    own = [normed_b, behind, ahead]
    early_blocks = own + [seq_swap(rows, 1) for rows in own]
    filled = project(
        starts, early_blocks, wq_wide, wk_wide, wv_rows, chips - 1, heads, scale, chips
    )
    filled, across = lax.optimization_barrier((filled, across))
    own.append(across[0] + across[1])
    late_blocks = [own[-1], seq_swap(own[-1], 1)]
    q_ext, k_ext, v_t = project(
        late_starts, late_blocks, wq_wide, wk_wide, wv_rows, 1, heads, scale, chips, filled
    )
    parts_of = [
        attend(meta, doc_line, q_ext, k_ext, v_t, heads, block, *span) for span in ((0, 1), (1, chips))
    ]
    mixed, lse, mixed_b = (
        list(parts_of[0][item]) + list(parts_of[1][item]) for item in range(3)
    )
    mixed_b[1:], wk_rows = lax.optimization_barrier((mixed_b[1:], wk_rows))
    k_t, v_ext = project_back(place, early_blocks + late_blocks, wk_rows, wv_wide)
    back = [mixed_b[slots[0]]] + [
        chip_shift(mixed_b[slots[step]], -step) for step in range(1, chips)
    ]
    back, k_t, v_ext = lax.optimization_barrier((back, k_t, v_ext))
    outs = middle(
        place, back, tokens, cotangent, w_out, w_up, w_down, (gain_inner, gain_feed, gain_hidden)
    )
    result, grad_middle, gmid_b = outs[:3]
    go = outs[3 : 3 + chips]
    z, h2, bent, pre, dinner, dfeed, dhidden = outs[3 + chips :]
    keep_a, send_a = down_grad(place, bent, cotangent, hidden // parts)
    keep_b, send_b = up_out_grad(place, h2, pre, z, gmid_b, perm, per)
    go, keep_b, send_b = lax.optimization_barrier((go, keep_b, send_b))
    go = [go[0]] + [chip_shift(go[step], step) for step in range(1, chips)]

    def gridded(array):
        return array.reshape((2, 2, chips) + array.shape[1:])

    sums = [
        (gridded(keep), gridded(seq_swap(send, 1)))
        for keep, send in ((keep_a, send_a), (keep_b, send_b))
    ]
    low, high = outgoing(place, sums)
    arrived_sums = [row_swap(low, 1), row_swap(high, 2)]
    dq, pair, other = attend_back(
        meta, doc_line, q_ext, [go[step] for step in order], mixed, lse, k_ext, k_t, v_ext, heads, block, scale
    )
    grads = join_parts(place, dq, pair, seq_swap(other, 1), chips)
    home = [grads[slots[0]]] + [chip_shift(grads[slots[step]], -step) for step in range(1, chips)]
    grads, sums = lax.optimization_barrier((grads, sums))
    kept = outgoing(place, sums, True)
    mine_grad, send_grad = head_grads(
        place,
        own,
        grads,
        (wq_rows, wk_rows, wv_rows),
        gain_first,
        (dinner, dfeed, dhidden),
        perm,
        per,
    )
    arrived_sums, kept, mine_grad, send_grad = lax.optimization_barrier(
        (arrived_sums, kept, mine_grad, send_grad)
    )
    low_keep, low_send, high_keep, high_send = halfway(place, [(*kept, *arrived_sums)])
    low_in, high_in = row_swap(low_send, 2), row_swap(high_send, 1)
    home, mine_grad, send_grad = lax.optimization_barrier((home, mine_grad, send_grad))
    mine_grad, other_grad = gridded(mine_grad), gridded(seq_swap(send_grad, 1))
    stage = split(after(place, home, SOME_COST), [(low_keep, low_in, high_keep, high_in)], chips)
    arrived = [stage[0]] + [chip_shift(stage[step], step) for step in range(1, chips)]
    grad_input = final(
        place, home, tokens, grad_middle, w_query, w_key, w_value, gain_first
    )
    low, high = outgoing(place, [(mine_grad, other_grad)])
    low_keep, low_send, high_keep, high_send = halfway(
        place,
        [(*outgoing(place, [(mine_grad, other_grad)], True), row_swap(low, 1), row_swap(high, 2))],
    )
    stage = split(
        place, [(low_keep, row_swap(low_send, 2), high_keep, row_swap(high_send, 1))], chips
    )
    arrived += [stage[0]] + [chip_shift(stage[step], step) for step in range(1, chips)]
    down, up, out, query, key, value, gains_part = finish(
        place, arrived, hidden, gains_share, per, share, factor
    )
    return (
        result,
        grad_input,
        query.reshape(-1),
        key.reshape(-1),
        value.reshape(-1),
        out.reshape(-1),
        up.reshape(-1),
        down.reshape(-1),
        gains_part,
    )


def local(*arrays):
    seq_devices, row_devices = lax.axis_size("seq"), lax.axis_size("row")
    block = arrays[0].shape[0]
    one_segment = block * seq_devices <= SEGMENT and block % 2 ** (PATTERNS - 1) == 0
    if one_segment and seq_devices == 8 and row_devices == 4:
        return fast_local(*arrays)
    return ring_local(*arrays)


def solution(mesh):
    return jax.shard_map(
        local,
        mesh=mesh,
        in_specs=(
            P(("row", "seq"), None),
            P("row", None),
            P(),
            P(),
            P(),
            P(),
            P(),
            P(),
            P(),
            P(),
            P(),
            P(),
            P(("row", "seq"), None),
        ),
        out_specs=(
            P(("row", "seq"), None),
            P(("row", "seq"), None),
            P(("row", "seq")),
            P(("row", "seq")),
            P(("row", "seq")),
            P(("row", "seq")),
            P(("row", "seq")),
            P(("row", "seq")),
            P(("row", "seq")),
        ),
        check_vma=False,
    )
```
